32 devices in a mesh: dp: 16 (over z, y, x), rep: 2 (over core).
Axes of the slice: x: 2, y: 2, z: 4, core: 2. Of those that a mesh axis runs over, the one named last changes fastest.
Arguments:
- media_tokens: bfloat16 [256, 576, 1024], P(('dp', 'rep')), may hold values from -6 to 6
- patch_counts: int32 [256], P(('dp', 'rep')), may hold values from 256 to 576, as said below
- latents: bfloat16 [256, 64, 1024], P(('dp', 'rep')), may hold values from -6 to 6
- media_gain: bfloat16 [1024], P('dp'), may hold values from 0.3984375 to 1.59375
- media_bias: bfloat16 [1024], P('dp'), may hold values from -3 to 3
- latent_gain: bfloat16 [1024], P('dp'), may hold values from 0.3984375 to 1.59375
- latent_bias: bfloat16 [1024], P('dp'), may hold values from -3 to 3
- query_weight: bfloat16 [1024, 512], P('dp'), may hold values from -0.1875 to 0.1875
- keyval_weight: bfloat16 [1024, 1024], P('dp'), may hold values from -0.1875 to 0.1875
- outproj_weight: bfloat16 [512, 1024], P('dp'), may hold values from -1.5 to 1.5
- ff_gain: bfloat16 [1024], P('dp'), may hold values from 0.3984375 to 1.59375
- ff_bias: bfloat16 [1024], P('dp'), may hold values from -3 to 3
- ff_in_weight: bfloat16 [1024, 4096], P('dp'), may hold values from -0.1875 to 0.1875
- ff_out_weight: bfloat16 [4096, 1024], P('dp'), may hold values from -0.09375 to 0.09375
- cotangent: float32 [256, 64, 1024], P(('dp', 'rep')), may hold values from -6 to 6
Outputs:
- new_latents: float32 [256, 64, 1024], P(('dp', 'rep'))
- media_grad: float32 [256, 576, 1024], P(('dp', 'rep'))
- latent_grad: float32 [256, 64, 1024], P(('dp', 'rep'))
- grad_media_gain: float32 [1024], P('dp')
- grad_media_bias: float32 [1024], P('dp')
- grad_latent_gain: float32 [1024], P('dp')
- grad_latent_bias: float32 [1024], P('dp')
- grad_query: float32 [1024, 512], P('dp')
- grad_keyval: float32 [1024, 1024], P('dp')
- grad_outproj: float32 [512, 1024], P('dp')
- grad_ff_gain: float32 [1024], P('dp')
- grad_ff_bias: float32 [1024], P('dp')
- grad_ff_in: float32 [1024, 4096], P('dp')
- grad_ff_out: float32 [4096, 1024], P('dp')
The draws below stay inside these ranges and needn't reach their ends.
Inputs may be any that keep to these rules, and one draw needn't show every extreme that they name: `patch_counts`: each entry is 256 or 576; some device holds only 576-patch images and some only 256-patch ones.
All inputs are finite; a program needn't handle non-finite values.
Results may differ from the reference program's by a relative error of at most 0.02.
Values may be sent and summed in bfloat16 or wider, within the bound.
No kernel may reach another device: no remote copies, remote signals or barrier semaphores. Data moves between devices by JAX's collectives and lax.ppermute only.
A program may use at most 256 MiB of HBM per device.

```python
import math
import jax
import jax.numpy as jnp
from jax import lax

D = 1024
HEADS = 8
HEAD = 64
FF = 4096
LAT = 64
MEDIA = 576
SHORT = 256
IMG_DEV = 8
INNER = 512
IMAGES = 256


def draw_patch_counts(key, part):
    blocks = IMAGES // IMG_DEV
    count_key, order_key = jax.random.split(jax.random.fold_in(key, 7))
    long_counts = jax.random.randint(count_key, (blocks,), 0, IMG_DEV + 1)
    block_ids = jnp.arange(blocks)
    long_counts = jnp.where(block_ids == 0, IMG_DEV, long_counts)
    long_counts = jnp.where(block_ids == 1, 0, long_counts)
    orders = jax.vmap(lambda sub_key: jax.random.permutation(sub_key, IMG_DEV))(jax.random.split(order_key, blocks))
    is_long = orders < long_counts[:, None]
    return jnp.where(is_long, MEDIA, SHORT).reshape(IMAGES).astype(jnp.int32)


def levels(rng, dims, shards, smallest, largest):
    def one(axis_at, shards_of):
        draws = jax.random.uniform(jax.random.fold_in(jax.random.fold_in(rng, 6), axis_at), (shards_of,), jnp.float32, smallest / len(shards), largest / len(shards))
        return jnp.repeat(jnp.exp(draws), dims[axis_at] // shards_of).reshape((-1,) + (1,) * (len(dims) - axis_at - 1))

    level = one(*shards[0])
    for cut in shards[1:]:
        level = level * one(*cut)
    return level


def scatter_about(own_key, shape, width, bound, pieces=(), held_as=jnp.bfloat16):
    values = width * jax.random.normal(own_key, shape, jnp.float32)
    if pieces:
        values = values * levels(own_key, shape, pieces, -0.22, 0.18)
    return jnp.clip(values, -bound, bound).astype(held_as)


def setup_inputs(seed: int = 0) -> dict:
    keys = jax.random.split(jax.random.key(seed), 16)
    return {
        "media_tokens": scatter_about(keys[0], (IMAGES, MEDIA, D), 1.0, 6.0, ((0, 32),)),
        "patch_counts": draw_patch_counts(jax.random.fold_in(keys[15], 71), 0),
        "latents": scatter_about(keys[2], (IMAGES, LAT, D), 1.0, 6.0, ((0, 32),)),
        "media_gain": jnp.clip(1.0 + 0.12 * jax.random.normal(keys[3], (D,), jnp.float32), 0.3984375, 1.59375).astype(jnp.bfloat16),
        "media_bias": scatter_about(keys[4], (D,), 0.5, 3.0, ((0, 16),)),
        "latent_gain": jnp.clip(1.0 + 0.12 * jax.random.normal(keys[5], (D,), jnp.float32), 0.3984375, 1.59375).astype(jnp.bfloat16),
        "latent_bias": scatter_about(keys[6], (D,), 0.5, 3.0, ((0, 16),)),
        "query_weight": scatter_about(keys[7], (D, INNER), D ** -0.5, 0.1875, ((0, 16),)),
        "keyval_weight": scatter_about(keys[8], (D, 2 * INNER), D ** -0.5, 0.1875, ((0, 16),)),
        "outproj_weight": scatter_about(keys[9], (INNER, D), (INNER // 32) ** -0.5, 1.5, ((0, 16),)),
        "ff_gain": jnp.clip(1.0 + 0.12 * jax.random.normal(keys[10], (D,), jnp.float32), 0.3984375, 1.59375).astype(jnp.bfloat16),
        "ff_bias": scatter_about(keys[11], (D,), 0.5, 3.0, ((0, 16),)),
        "ff_in_weight": scatter_about(keys[12], (D, FF), D ** -0.5, 0.1875, ((0, 16),)),
        "ff_out_weight": scatter_about(keys[13], (FF, D), FF ** -0.5, 0.09375, ((0, 16),)),
        "cotangent": scatter_about(keys[14], (IMAGES, LAT, D), 1.0, 6.0, ((0, 32),), jnp.float32),
    }


@jax.custom_vjp
def low(v):
    return lax.optimization_barrier(v.astype(jnp.bfloat16)).astype(jnp.float32)

@jax.custom_vjp
def low_back(v):
    return v

def low_keep(v):
    return (low(v), None)

def low_pass(kept, grad):
    return (grad,)

def back_keep(v):
    return (v, None)

def back_low(kept, grad):
    return (low(grad),)
low.defvjp(low_keep, low_pass)
low_back.defvjp(back_keep, back_low)
EPS = 1e-05
HIGHEST = lax.Precision.HIGHEST

def layer_norm(values, gain, bias):
    centre = lax.optimization_barrier(jnp.mean(values, -1, keepdims=True))
    centred = values - centre
    spread = lax.optimization_barrier(jnp.mean(centred * centred, -1, keepdims=True))
    return centred * lax.rsqrt(spread + EPS) * gain + bias

def gelu_exact(values):
    return jax.nn.gelu(values, approximate=False)

def group_forward(params, media_group, latent_group, count_group):
    media_gain, media_bias, latent_gain, latent_bias, query_weight, keyval_weight, outproj_weight, ff_gain, ff_bias, ff_in_weight, ff_out_weight = params
    images = latent_group.shape[0]
    keys_len = MEDIA + LAT
    scale = 1.0 / math.sqrt(HEAD)
    media_normed = low(layer_norm(media_group, media_gain, media_bias))
    latent_normed = low(layer_norm(latent_group, latent_gain, latent_bias))
    queries = low(low_back(jnp.einsum('ild,de->ile', latent_normed, query_weight, precision=HIGHEST)))
    key_input = jnp.concatenate([media_normed, latent_normed], axis=1)
    keyvals = low(low_back(jnp.einsum('ikd,de->ike', key_input, keyval_weight, precision=HIGHEST)))
    key_heads = keyvals[:, :, :INNER].reshape(images, keys_len, HEADS, HEAD)
    value_heads = keyvals[:, :, INNER:].reshape(images, keys_len, HEADS, HEAD)
    query_heads = queries.reshape(images, LAT, HEADS, HEAD)
    scores = low_back(jnp.einsum('iqhe,ikhe->ihqk', query_heads, key_heads, precision=HIGHEST) * scale)
    positions = jnp.arange(keys_len, dtype=jnp.int32)
    valid = (positions[None, :] < count_group[:, None]) | (positions[None, :] >= MEDIA)
    scores = jnp.where(valid[:, None, None, :], scores, jnp.float32(-1e+30))
    top = lax.optimization_barrier(jnp.max(scores, -1, keepdims=True))
    expd = jnp.exp(scores - top)
    probs = expd / lax.optimization_barrier(jnp.sum(expd, -1, keepdims=True))
    mixed = jnp.einsum('ihqk,ikhe->iqhe', low(probs), value_heads, precision=HIGHEST)
    mixed = low(low_back(mixed.reshape(images, LAT, INNER)))
    branch = low_back(jnp.einsum('ile,ed->ild', mixed, outproj_weight, precision=HIGHEST))
    resid = latent_group + branch
    ff_normed = low(layer_norm(resid, ff_gain, ff_bias))
    pre_act = low_back(jnp.einsum('ild,df->ilf', ff_normed, ff_in_weight, precision=HIGHEST))
    activ = low(gelu_exact(pre_act))
    ff_branch = low_back(jnp.einsum('ilf,fd->ild', activ, ff_out_weight, precision=HIGHEST))
    return resid + ff_branch

def reference(media_tokens, patch_counts, latents, media_gain, media_bias, latent_gain, latent_bias, query_weight, keyval_weight, outproj_weight, ff_gain, ff_bias, ff_in_weight, ff_out_weight, cotangent):
    params = tuple((weight.astype(jnp.float32) for weight in (media_gain, media_bias, latent_gain, latent_bias, query_weight, keyval_weight, outproj_weight, ff_gain, ff_bias, ff_in_weight, ff_out_weight)))
    groups = media_tokens.shape[0] // IMG_DEV
    media_all = media_tokens.astype(jnp.float32).reshape(groups, IMG_DEV, MEDIA, D)
    latent_all = latents.astype(jnp.float32).reshape(groups, IMG_DEV, LAT, D)
    count_all = patch_counts.astype(jnp.int32).reshape(groups, IMG_DEV)

    def forward(media_in, latent_in, weights):

        def one_group(item):
            return group_forward(weights, item[0], item[1], item[2])
        return lax.map(jax.checkpoint(one_group), (media_in, latent_in, count_all))
    result, pullback = jax.vjp(forward, media_all, latent_all, params)
    media_grad, latent_grad, weight_grads = pullback(cotangent.astype(jnp.float32).reshape(groups, IMG_DEV, LAT, D))
    g_media_gain, g_media_bias, g_latent_gain, g_latent_bias, g_query, g_keyval, g_outproj, g_ff_gain, g_ff_bias, g_ff_in, g_ff_out = weight_grads
    return (result.reshape(-1, LAT, D), media_grad.reshape(-1, MEDIA, D), latent_grad.reshape(-1, LAT, D), g_media_gain, g_media_bias, g_latent_gain, g_latent_bias, g_query, g_keyval, g_outproj, g_ff_gain, g_ff_bias, g_ff_in, g_ff_out)
```

```python
import math

import jax
import jax.numpy as jnp
from jax import lax
from jax.sharding import PartitionSpec as P

HEADS = 8


EPS = 1e-05
F32 = jnp.float32
BF16 = jnp.bfloat16


def norm_parts(values):
    centre = jnp.mean(values, -1, keepdims=True)
    centred = values - centre
    inverse = lax.rsqrt(jnp.mean(centred * centred, -1, keepdims=True) + EPS)
    return centred * inverse, inverse


def norm_grad(grad_normed, unit, inverse, gain):
    scaled = grad_normed * gain
    return inverse * (
        scaled
        - jnp.mean(scaled, -1, keepdims=True)
        - unit * jnp.mean(scaled * unit, -1, keepdims=True)
    )


def row_total(values):
    return jnp.sum(values.reshape(-1, values.shape[-1]), axis=0)


def gelu_exact(values):
    return jax.nn.gelu(values, approximate=False)


def masked_scores(query_heads, key_heads, valid, scale):
    raw = (
        jnp.einsum("iqhe,ikhe->ihqk", query_heads, key_heads, preferred_element_type=F32)
        * scale
    )
    return jnp.where(valid[:, None, None, :], raw, jnp.float32(-1e30))


class Grid:
    def __init__(self, dp, rep):
        self.dp = dp
        self.rep = rep
        self.me = lax.axis_index("dp")
        self.core = lax.axis_index("rep")
        self.column = [1 << b for b in range(2, dp.bit_length() - 1)]

    def swap(self, value, bit):
        return lax.ppermute(value, "dp", [(i, i ^ bit) for i in range(self.dp)])

    def side(self, bit):
        return (self.me & bit) != 0

    def pair(self, own, other, bit, axis):
        return jnp.where(
            self.side(bit), jnp.stack([other, own], axis), jnp.stack([own, other], axis)
        )

    def pick(self, value, bit, axis):
        at = jnp.where(self.side(bit), 1, 0)
        keep = lax.dynamic_index_in_dim(value, at, axis, keepdims=False)
        send = lax.dynamic_index_in_dim(value, 1 - at, axis, keepdims=False)
        return keep, send

    def gather(self, first, second):
        rows = first.shape[0]
        both = jnp.concatenate([first, second], 0)[None]
        for bit in reversed(self.column):
            got = self.swap(both, bit)
            both = self.pair(both, got, bit, 1)
            both = both.reshape((-1,) + both.shape[2:])
        first, second = both[:, :rows], both[:, rows:]
        first_got, second_got = self.swap(first, 2), self.swap(second, 1)
        first = self.pair(first, first_got, 2, 1)
        second = self.pair(second, second_got, 1, 1)
        first_got, second_got = self.swap(first, 1), self.swap(second, 2)
        first = self.pair(first, first_got, 1, 2)
        second = self.pair(second, second_got, 2, 1)
        return (
            first.reshape((self.dp,) + first.shape[3:]),
            second.reshape((self.dp,) + second.shape[3:]),
        )

    def total(self, first, second):
        rows = first.shape[1]
        tail = first.shape[1:]

        def fold(value, bit, axis, last=False):
            keep, send = self.pick(value, bit, axis)
            got = self.swap(send, bit)
            added = keep.astype(F32) + got.astype(F32)
            return added if last else added.astype(BF16)

        first = first.reshape((-1, 2, 2) + tail)
        second = second.reshape((-1, 2, 2) + second.shape[1:])
        first, second = fold(first, 1, 2), fold(second, 2, 1)
        first, second = fold(first, 2, 1), fold(second, 1, 1)
        both = jnp.concatenate([first, second], 1)
        for bit in self.column:
            both = both.reshape((-1, 2) + both.shape[1:])
            both = fold(both, bit, 1, bit == self.column[-1])
        both = both[0]
        return both[:rows], both[rows:]

    def other(self, value):
        return lax.ppermute(value, "rep", [(0, 1), (1, 0)])

    def rep_all(self, value):
        if self.rep != 2:
            return lax.all_gather(value, "rep", axis=0)
        got = self.other(value)
        return jnp.where(self.core == 0, jnp.stack([value, got]), jnp.stack([got, value]))

    def rep_rows(self, value):
        if self.rep != 2:
            return lax.all_gather(value, "rep", axis=0, tiled=True)
        return jnp.concatenate([value, self.other(value)], 0)

    def rep_back(self, value):
        if self.rep != 2:
            return lax.psum_scatter(value, "rep", scatter_dimension=0, tiled=True)
        rows = value.shape[0] // 2
        return value[:rows] + self.other(value[rows:])

    def rep_total(self, value, axis):
        if self.rep != 2:
            value = jnp.moveaxis(value, axis, 0)
            return lax.psum_scatter(value, "rep", scatter_dimension=0).astype(BF16)
        keep = lax.dynamic_index_in_dim(value, self.core, axis, keepdims=False)
        send = lax.dynamic_index_in_dim(value, 1 - self.core, axis, keepdims=False)
        return (keep + self.other(send.astype(BF16)).astype(F32)).astype(BF16)

    def mine(self, value, axis):
        return lax.dynamic_index_in_dim(value, self.core, axis, keepdims=False)


def fold_rows(value):
    half = value.shape[-2] // 2
    return jnp.concatenate([value[..., :half, :], value[..., half:, :]], -1)


def unfold_rows(value):
    half = value.shape[-1] // 2
    return jnp.concatenate([value[..., :half], value[..., half:]], -2)


def shards(
    dp,
    rep,
    media_tokens,
    patch_counts,
    latents,
    media_gain,
    media_bias,
    latent_gain,
    latent_bias,
    query_weight,
    keyval_weight,
    outproj_weight,
    ff_gain,
    ff_bias,
    ff_in_weight,
    ff_out_weight,
    cotangent,
):
    grid = Grid(dp, rep)
    images, media_len, width = media_tokens.shape
    lat_len = latents.shape[1]
    keys_len = media_len + lat_len
    inner_width = query_weight.shape[1]
    head_size = inner_width // HEADS
    hidden = ff_in_weight.shape[1]
    slot = hidden // dp // rep
    part = width // dp
    kv_rows = part // rep
    o_rows = inner_width // dp // rep
    scale = 1.0 / math.sqrt(head_size)

    norms = jnp.stack([media_gain, media_bias, latent_gain, latent_bias, ff_gain, ff_bias])
    norm_row = jnp.pad(norms.reshape(1, -1), ((0, 0), (0, width - norms.size)))
    kv_part = grid.mine(keyval_weight.reshape(rep, kv_rows, width), 0)
    q_part = fold_rows(grid.mine(query_weight.reshape(rep, kv_rows, inner_width), 0))
    q_rows = q_part.shape[0]
    got_kv, got_q = grid.gather(kv_part, jnp.concatenate([q_part, norm_row], 0))
    got_norms = got_q[:, q_rows, : norms.size].reshape(dp, 6, part)
    got_norms = jnp.moveaxis(got_norms, 1, 0).reshape(6, width).astype(F32)
    gain_media, bias_media, gain_latent, bias_latent, gain_ff, bias_ff = got_norms
    w_keyval = jnp.moveaxis(grid.rep_all(got_kv), 0, 1).reshape(width, width)
    w_query = jnp.moveaxis(grid.rep_all(unfold_rows(got_q[:, :q_rows])), 0, 1)
    w_query = w_query.reshape(width, inner_width)

    ffin_part = grid.mine(ff_in_weight.reshape(part, dp, rep, slot), 2).reshape(part, dp * slot)
    cut = ffin_part.shape[1] // 2
    o_part = grid.mine(outproj_weight.reshape(rep, o_rows, width), 0)
    o_part = jnp.pad(o_part, ((0, 0), (0, max(cut - width, 0))))
    got_lo, got_hi = grid.gather(
        ffin_part[:, :cut] if cut >= width else jnp.pad(ffin_part[:, :cut], ((0, 0), (0, width - cut))),
        jnp.concatenate(
            [
                ffin_part[:, cut:] if cut >= width else jnp.pad(ffin_part[:, cut:], ((0, 0), (0, width - cut))),
                o_part,
            ],
            0,
        ),
    )
    w_ffin = jnp.concatenate(
        [
            got_lo[:, :, :cut].reshape(width, cut),
            got_hi[:, :part, :cut].reshape(width, cut),
        ],
        1,
    )
    w_outproj = jnp.moveaxis(grid.rep_all(got_hi[:, part:, :width]), 0, 1).reshape(inner_width, width)
    ffout_part = grid.mine(ff_out_weight.reshape(rep, slot, width), 0)
    w_ffout = lax.all_gather(ffout_part, "dp", axis=0, tiled=True)

    media_unit, media_inv = norm_parts(media_tokens.astype(F32))
    latent_f = latents.astype(F32)
    latent_unit, latent_inv = norm_parts(latent_f)
    grad_out_low = grid.rep_rows(cotangent.astype(BF16).reshape(-1, width))

    media_low = (media_unit * gain_media + bias_media).astype(BF16)
    latent_low = (latent_unit * gain_latent + bias_latent).astype(BF16)
    queries = jnp.einsum("ild,de->ile", latent_low, w_query, preferred_element_type=F32).astype(BF16)
    key_input = jnp.concatenate([media_low, latent_low], axis=1)
    keyvals = jnp.einsum("ikd,de->ike", key_input, w_keyval, preferred_element_type=F32).astype(BF16)
    key_heads = keyvals[:, :, :inner_width].reshape(images, keys_len, HEADS, head_size)
    value_heads = keyvals[:, :, inner_width:].reshape(images, keys_len, HEADS, head_size)
    query_heads = queries.reshape(images, lat_len, HEADS, head_size)
    positions = jnp.arange(keys_len, dtype=jnp.int32)
    valid = (positions[None, :] < patch_counts[:, None]) | (positions[None, :] >= media_len)
    scores = masked_scores(query_heads, key_heads, valid, scale)
    top = jnp.max(scores, -1, keepdims=True)
    expd = jnp.exp(scores - top)
    total = jnp.sum(expd, -1, keepdims=True)
    probs = expd / total
    log_total = top + jnp.log(total)
    mixed = jnp.einsum("ihqk,ikhe->iqhe", probs.astype(BF16), value_heads, preferred_element_type=F32)
    mixed = mixed.reshape(images, lat_len, inner_width).astype(BF16)
    branch = jnp.einsum("ile,ed->ild", mixed, w_outproj, preferred_element_type=F32)
    resid = latent_f + branch
    ff_unit, ff_inv = norm_parts(resid)
    ff_low = grid.rep_rows((ff_unit * gain_ff + bias_ff).astype(BF16).reshape(-1, width))

    pre_act = jnp.dot(ff_low, w_ffin, preferred_element_type=F32)
    activ, gelu_pull = jax.vjp(gelu_exact, pre_act)
    activ_low = activ.astype(BF16)
    grad_ffout = jnp.einsum("rf,rd->fd", activ_low, grad_out_low, preferred_element_type=F32).astype(BF16)
    ff_branch = jnp.dot(activ_low, w_ffout, preferred_element_type=F32)
    grad_activ = jnp.einsum("rd,fd->rf", grad_out_low, w_ffout, preferred_element_type=F32)
    (grad_pre,) = gelu_pull(grad_activ)
    grad_pre_low = grad_pre.astype(BF16)
    grad_ffin = jnp.einsum("rd,rf->df", ff_low, grad_pre_low, preferred_element_type=F32).astype(BF16)
    grad_ffnormed = jnp.einsum("rf,df->rd", grad_pre_low, w_ffin, preferred_element_type=F32)
    grad_ffnormed = grid.rep_back(grad_ffnormed).reshape(resid.shape)
    new_latents = resid + grid.rep_back(ff_branch).reshape(resid.shape)

    grad_ffout = grad_ffout.reshape(dp, slot, width)
    own_lo, own_hi = grid.total(grad_ffout[:, : slot // 2], grad_ffout[:, slot // 2 :])
    own_ffout = grid.rep_all(jnp.concatenate([own_lo, own_hi], 0)).reshape(rep * slot, width)
    grad_ffin = grad_ffin.reshape(dp, part, dp * slot)
    own_lo, own_hi = grid.total(grad_ffin[:, :, :cut], grad_ffin[:, :, cut:])
    own_ffin = grid.rep_all(jnp.concatenate([own_lo, own_hi], 1))
    own_ffin = jnp.moveaxis(own_ffin.reshape(rep, part, dp, slot), 0, 2).reshape(part, hidden)

    grad_gain_ff = row_total(grad_ffnormed * ff_unit)
    grad_bias_ff = row_total(grad_ffnormed)
    grad_resid = cotangent + norm_grad(grad_ffnormed, ff_unit, ff_inv, gain_ff)
    grad_resid_low = grad_resid.astype(BF16)
    grad_outproj = jnp.einsum("ile,ild->ed", mixed, grad_resid_low, preferred_element_type=F32)
    grad_mixed = jnp.einsum("ild,ed->ile", grad_resid_low, w_outproj, preferred_element_type=F32)
    grad_mixed_heads = grad_mixed.astype(BF16).reshape(images, lat_len, HEADS, head_size)
    scores_again = masked_scores(query_heads, key_heads, valid, scale)
    probs_again = jnp.exp(scores_again - log_total)
    grad_probs = jnp.einsum("iqhe,ikhe->ihqk", grad_mixed_heads, value_heads, preferred_element_type=F32)
    grad_scores = probs_again * (grad_probs - jnp.sum(probs_again * grad_probs, -1, keepdims=True))
    grad_scores_low = grad_scores.astype(BF16)
    grad_queries = (
        jnp.einsum("ihqk,ikhe->iqhe", grad_scores_low, key_heads, preferred_element_type=F32) * scale
    )
    grad_queries = grad_queries.reshape(images, lat_len, inner_width).astype(BF16)
    grad_keys = (
        jnp.einsum("ihqk,iqhe->ikhe", grad_scores_low, query_heads, preferred_element_type=F32) * scale
    )
    grad_values = jnp.einsum(
        "ihqk,iqhe->ikhe", probs_again.astype(BF16), grad_mixed_heads, preferred_element_type=F32
    )
    grad_keyvals = jnp.concatenate(
        [
            grad_keys.reshape(images, keys_len, inner_width),
            grad_values.reshape(images, keys_len, inner_width),
        ],
        axis=-1,
    ).astype(BF16)
    grad_qweight = jnp.einsum("ild,ile->de", latent_low, grad_queries, preferred_element_type=F32)
    grad_kvweight = jnp.einsum("ikd,ike->de", key_input, grad_keyvals, preferred_element_type=F32)
    grad_key_input = jnp.einsum("ike,de->ikd", grad_keyvals, w_keyval, preferred_element_type=F32)
    grad_latnormed = jnp.einsum("ile,de->ild", grad_queries, w_query, preferred_element_type=F32)
    grad_latnormed = grad_latnormed + grad_key_input[:, media_len:]
    grad_medianormed = grad_key_input[:, :media_len]
    media_grad = norm_grad(grad_medianormed, media_unit, media_inv, gain_media)
    latent_grad = grad_resid + norm_grad(grad_latnormed, latent_unit, latent_inv, gain_latent)
    vectors = jnp.stack(
        [
            row_total(grad_medianormed * media_unit),
            row_total(grad_medianormed),
            row_total(grad_latnormed * latent_unit),
            row_total(grad_latnormed),
            grad_gain_ff,
            grad_bias_ff,
        ]
    )

    kv_sum = grid.rep_total(grad_kvweight.reshape(dp, rep, kv_rows, width), 1)
    q_sum = fold_rows(grid.rep_total(grad_qweight.reshape(dp, rep, kv_rows, inner_width), 1))
    o_sum = grid.rep_total(grad_outproj.reshape(dp, rep, o_rows, width), 1)
    vec_row = jnp.moveaxis(vectors.reshape(6, dp, part), 1, 0).reshape(dp, 1, 6 * part)
    vec_row = jnp.pad(vec_row, ((0, 0), (0, 0), (0, width - 6 * part))).astype(BF16)
    own_kv, own_rest = grid.total(kv_sum, jnp.concatenate([q_sum, o_sum, vec_row], 1))
    every = grid.rep_all(jnp.concatenate([own_kv, own_rest], 0))
    own_kv = every[:, :kv_rows].reshape(part, width)
    own_q = unfold_rows(every[:, kv_rows : kv_rows + q_rows]).reshape(part, inner_width)
    at = kv_rows + q_rows
    own_o = every[:, at : at + o_rows].reshape(rep * o_rows, width)
    own_vec = jnp.sum(every[:, at + o_rows, : 6 * part], 0).reshape(6, part)
    return (
        new_latents,
        media_grad,
        latent_grad,
        own_vec[0],
        own_vec[1],
        own_vec[2],
        own_vec[3],
        own_q,
        own_kv,
        own_o,
        own_vec[4],
        own_vec[5],
        own_ffin,
        own_ffout,
    )


def solution(mesh):
    dp, rep = mesh.shape["dp"], mesh.shape["rep"]

    def program(*arrays):
        return shards(dp, rep, *arrays)

    return jax.shard_map(
        program,
        mesh=mesh,
        in_specs=(
            P(("dp", "rep"), None, None),
            P(("dp", "rep")),
            P(("dp", "rep"), None, None),
            P("dp"),
            P("dp"),
            P("dp"),
            P("dp"),
            P("dp", None),
            P("dp", None),
            P("dp", None),
            P("dp"),
            P("dp"),
            P("dp", None),
            P("dp", None),
            P(("dp", "rep"), None, None),
        ),
        out_specs=(
            P(("dp", "rep"), None, None),
            P(("dp", "rep"), None, None),
            P(("dp", "rep"), None, None),
            P("dp"),
            P("dp"),
            P("dp"),
            P("dp"),
            P("dp", None),
            P("dp", None),
            P("dp", None),
            P("dp"),
            P("dp"),
            P("dp", None),
            P("dp", None),
        ),
        check_vma=False,
    )
```

```python
import functools
import math

import jax
import jax.numpy as jnp
from jax import lax
from jax.experimental import pallas as pl
from jax.experimental.pallas import tpu as pltpu
from jax.sharding import PartitionSpec as P

HEADS = 8
GROUP = 4
EPS = 1e-05
NEG = -1e30
ROWS = 64
FF_TILE = 512
FF_ROWS = 1024
F32 = jnp.float32
BF16 = jnp.bfloat16


def contract(a, b, over):
    return lax.dot_general(a, b, ((over[:1], over[1:]), ((), ())), preferred_element_type=F32)


def norm_rows(values):
    centred = values - jnp.mean(values, -1, keepdims=True)
    inverse = lax.rsqrt(jnp.mean(centred * centred, -1, keepdims=True) + EPS)
    return centred * inverse, inverse


def norm_back(grad, unit, inverse, gain):
    scaled = grad * gain
    return inverse * (
        scaled
        - jnp.mean(scaled, -1, keepdims=True)
        - unit * jnp.mean(scaled * unit, -1, keepdims=True)
    )


def spread(value, size):
    lane = lax.broadcasted_iota(jnp.int32, value.shape, 1) // size
    value = value.astype(F32)
    return jnp.concatenate([jnp.where(lane == h, value, 0.0) for h in range(GROUP)], 0)


def gathered(value, size):
    rows = value.shape[0] // GROUP
    lane = lax.broadcasted_iota(jnp.int32, (rows, value.shape[1]), 1) // size
    out = jnp.zeros((rows, value.shape[1]), F32)
    for h in range(GROUP):
        out = jnp.where(lane == h, value[h * rows : (h + 1) * rows], out)
    return out


def params(mib):
    return pltpu.CompilerParams(vmem_limit_bytes=mib << 20)


def image_at(i, c):
    return (i, 0, 0)


def fixed_at(*_):
    return (0, 0)


def attend_kernel(counts, media, latent, norms, w_kv, w_q, key_input, keyvals, queries, mixed):
    media_len, lat_len = media.shape[1], latent.shape[1]
    keys_len = media_len + lat_len
    inner = w_q.shape[1]
    size = inner // HEADS
    wide = size * GROUP
    for at in range(0, media_len, ROWS):
        unit, _ = norm_rows(media[0, at : at + ROWS, :].astype(F32))
        key_input[0, at : at + ROWS, :] = (unit * norms[0:1, :] + norms[1:2, :]).astype(BF16)
    unit, _ = norm_rows(latent[0].astype(F32))
    low = (unit * norms[2:3, :] + norms[3:4, :]).astype(BF16)
    key_input[0, media_len:, :] = low
    query = contract(low, w_q[...], (1, 0)).astype(BF16)
    queries[0] = query
    keyvals[0] = contract(key_input[0], w_kv[...], (1, 0)).astype(BF16)
    key_at = lax.broadcasted_iota(jnp.int32, (1, keys_len), 1)
    valid = (key_at < counts[pl.program_id(0)]) | (key_at >= media_len)
    for at in range(0, inner, wide):
        own = spread(query[:, at : at + wide].astype(F32) * (1.0 / math.sqrt(size)), size)
        scores = contract(own.astype(BF16), keyvals[0, :, at : at + wide], (1, 1))
        scores = jnp.where(valid, scores, NEG)
        expd = jnp.exp(scores - jnp.max(scores, -1, keepdims=True))
        probs = (expd * (1.0 / jnp.sum(expd, -1, keepdims=True))).astype(BF16)
        out = contract(probs, keyvals[0, :, inner + at : inner + at + wide], (1, 0))
        mixed[0, :, at : at + wide] = gathered(out, size).astype(BF16)


def attend(counts, media, latent, norms, w_kv, w_q):
    images, media_len, width = media.shape
    lat_len, inner = latent.shape[1], w_q.shape[1]
    keys_len = media_len + lat_len
    flops = 2 * images * (keys_len * width * 2 * inner + lat_len * width * inner)
    return pl.pallas_call(
        attend_kernel,
        grid_spec=pltpu.PrefetchScalarGridSpec(
            num_scalar_prefetch=1,
            grid=(images,),
            in_specs=[
                pl.BlockSpec((1, media_len, width), image_at),
                pl.BlockSpec((1, lat_len, width), image_at),
                pl.BlockSpec(norms.shape, fixed_at),
                pl.BlockSpec(w_kv.shape, fixed_at),
                pl.BlockSpec(w_q.shape, fixed_at),
            ],
            out_specs=[
                pl.BlockSpec((1, keys_len, width), image_at),
                pl.BlockSpec((1, keys_len, 2 * inner), image_at),
                pl.BlockSpec((1, lat_len, inner), image_at),
                pl.BlockSpec((1, lat_len, inner), image_at),
            ],
        ),
        out_shape=[
            jax.ShapeDtypeStruct((images, keys_len, width), BF16),
            jax.ShapeDtypeStruct((images, keys_len, 2 * inner), BF16),
            jax.ShapeDtypeStruct((images, lat_len, inner), BF16),
            jax.ShapeDtypeStruct((images, lat_len, inner), BF16),
        ],
        compiler_params=params(32),
        cost_estimate=pl.CostEstimate(
            flops=2 * flops, bytes_accessed=images * keys_len * width * 6, transcendentals=0
        ),
        name="attend",
    )(counts, media, latent, norms, w_kv, w_q)


def resid_kernel(mixed, latent, w_o, norms, resid, low):
    value = latent[...].astype(F32) + contract(mixed[...], w_o[...], (1, 0))
    resid[...] = value
    unit, _ = norm_rows(value)
    low[...] = (unit * norms[4:5, :] + norms[5:6, :]).astype(BF16)


def add_branch(mixed, latent, w_o, norms):
    rows, width = latent.shape
    inner = mixed.shape[1]
    block = rows // 4
    row_at = lambda i: (i, 0)
    return pl.pallas_call(
        resid_kernel,
        grid=(rows // block,),
        in_specs=[
            pl.BlockSpec((block, inner), row_at),
            pl.BlockSpec((block, width), row_at),
            pl.BlockSpec(w_o.shape, fixed_at),
            pl.BlockSpec(norms.shape, fixed_at),
        ],
        out_specs=[pl.BlockSpec((block, width), row_at), pl.BlockSpec((block, width), row_at)],
        out_shape=[
            jax.ShapeDtypeStruct((rows, width), F32),
            jax.ShapeDtypeStruct((rows, width), BF16),
        ],
        compiler_params=params(16),
        cost_estimate=pl.CostEstimate(
            flops=4 * rows * inner * width, bytes_accessed=rows * width * 9, transcendentals=0
        ),
        name="add_branch",
    )(mixed, latent, w_o, norms)


def ff_kernel(low, dout, w_in, w_out, kept, sent, slope, grad_out, branch):
    step = pl.program_id(0)
    pre = contract(low[...], w_in[...], (1, 0))
    cdf = 0.5 * (1.0 + lax.erf(pre * math.sqrt(0.5)))
    slope[...] = cdf + pre * (jnp.exp(pre * pre * -0.5) * (1.0 / math.sqrt(2.0 * math.pi)))
    activ = (pre * cdf).astype(BF16)
    grad_out[...] = contract(activ, dout[...], (0, 0)).astype(BF16)

    @pl.when(step == 0)
    def _():
        branch[...] = jnp.zeros_like(branch)

    branch[...] += contract(activ, w_out[...], (1, 0))

    @pl.when(step == pl.num_programs(0) - 1)
    def _():
        kept[...] = branch[: kept.shape[0], :]
        sent[...] = branch[kept.shape[0] :, :].astype(BF16)


def feed_forward(low, dout, w_in, w_out):
    rows, width = low.shape
    hidden = w_in.shape[1]
    tile = min(FF_TILE, hidden)
    half = rows // 2
    in_at, out_at = (lambda t: (0, t)), (lambda t: (t, 0))
    return pl.pallas_call(
        ff_kernel,
        grid=(hidden // tile,),
        in_specs=[
            pl.BlockSpec((rows, width), fixed_at),
            pl.BlockSpec((rows, width), fixed_at),
            pl.BlockSpec((width, tile), in_at),
            pl.BlockSpec((tile, width), out_at),
        ],
        out_specs=[
            pl.BlockSpec((half, width), fixed_at),
            pl.BlockSpec((rows - half, width), fixed_at),
            pl.BlockSpec((rows, tile), in_at),
            pl.BlockSpec((tile, width), out_at),
        ],
        out_shape=[
            jax.ShapeDtypeStruct((half, width), F32),
            jax.ShapeDtypeStruct((rows - half, width), BF16),
            jax.ShapeDtypeStruct((rows, hidden), F32),
            jax.ShapeDtypeStruct((hidden, width), BF16),
        ],
        scratch_shapes=[pltpu.VMEM((rows, width), F32)],
        compiler_params=params(48),
        cost_estimate=pl.CostEstimate(
            flops=10 * rows * width * hidden, bytes_accessed=28 << 20, transcendentals=0
        ),
        name="feed_forward",
    )(low, dout, w_in, w_out)


def ff_back_kernel(low, dout, w_in, w_out, slope, grad_in, kept, sent, low_t, grad_low):
    step = pl.program_id(0)

    @pl.when(step == 0)
    def _():
        low_t[...] = low[...].T
        grad_low[...] = jnp.zeros_like(grad_low)

    grad = (contract(dout[...], w_out[...], (1, 1)) * slope[...]).astype(BF16)
    grad_in[...] = contract(low_t[...], grad, (1, 0)).astype(BF16)
    grad_low[...] += contract(grad, w_in[...], (1, 1))

    @pl.when(step == pl.num_programs(0) - 1)
    def _():
        kept[...] = grad_low[: kept.shape[0], :]
        sent[...] = grad_low[kept.shape[0] :, :].astype(BF16)


def feed_back(low, dout, w_in, w_out, slope):
    rows, width = low.shape
    hidden = w_in.shape[1]
    tile = min(FF_TILE, hidden)
    half = rows // 2
    in_at, out_at = (lambda t: (0, t)), (lambda t: (t, 0))
    return pl.pallas_call(
        ff_back_kernel,
        grid=(hidden // tile,),
        in_specs=[
            pl.BlockSpec((rows, width), fixed_at),
            pl.BlockSpec((rows, width), fixed_at),
            pl.BlockSpec((width, tile), in_at),
            pl.BlockSpec((tile, width), out_at),
            pl.BlockSpec((rows, tile), in_at),
        ],
        out_specs=[
            pl.BlockSpec((width, tile), in_at),
            pl.BlockSpec((half, width), fixed_at),
            pl.BlockSpec((rows - half, width), fixed_at),
        ],
        out_shape=[
            jax.ShapeDtypeStruct((width, hidden), BF16),
            jax.ShapeDtypeStruct((half, width), F32),
            jax.ShapeDtypeStruct((rows - half, width), BF16),
        ],
        scratch_shapes=[pltpu.VMEM((width, rows), BF16), pltpu.VMEM((rows, width), F32)],
        compiler_params=params(48),
        cost_estimate=pl.CostEstimate(
            flops=10 * rows * width * hidden, bytes_accessed=28 << 20, transcendentals=0
        ),
        name="feed_back",
    )(low, dout, w_in, w_out, slope)


def resid_back_kernel(
    kept, got, resid, cotangent, mixed, w_o, norms, grad_resid, grad_mixed, grad_o, vectors, total
):
    step = pl.program_id(0)

    @pl.when(step == 0)
    def _():
        vectors[...] = jnp.zeros_like(vectors)
        total[...] = jnp.zeros_like(total)

    grad = kept[...] + got[...].astype(F32)
    unit, inverse = norm_rows(resid[...])
    vectors[0:1, :] += jnp.sum(grad * unit, 0, keepdims=True)
    vectors[1:2, :] += jnp.sum(grad, 0, keepdims=True)
    value = cotangent[...] + norm_back(grad, unit, inverse, norms[4:5, :])
    grad_resid[...] = value
    low = value.astype(BF16)
    grad_mixed[...] = contract(low, w_o[...], (1, 1)).astype(BF16)
    total[...] += contract(mixed[...], low, (0, 0))
    grad_o[...] = total[...].astype(BF16)


def resid_back(kept, got, resid, cotangent, mixed, w_o, norms):
    rows, width = resid.shape
    inner = mixed.shape[1]
    block = rows // 4
    row_at = lambda i: (i, 0)
    wide = pl.BlockSpec((block, width), row_at)
    return pl.pallas_call(
        resid_back_kernel,
        grid=(rows // block,),
        in_specs=[
            wide,
            wide,
            wide,
            wide,
            pl.BlockSpec((block, inner), row_at),
            pl.BlockSpec(w_o.shape, fixed_at),
            pl.BlockSpec(norms.shape, fixed_at),
        ],
        out_specs=[
            wide,
            pl.BlockSpec((block, inner), row_at),
            pl.BlockSpec(w_o.shape, fixed_at),
            pl.BlockSpec((8, width), fixed_at),
        ],
        out_shape=[
            jax.ShapeDtypeStruct((rows, width), F32),
            jax.ShapeDtypeStruct((rows, inner), BF16),
            jax.ShapeDtypeStruct(w_o.shape, BF16),
            jax.ShapeDtypeStruct((8, width), F32),
        ],
        scratch_shapes=[pltpu.VMEM(w_o.shape, F32)],
        compiler_params=params(24),
        cost_estimate=pl.CostEstimate(
            flops=8 * rows * inner * width, bytes_accessed=rows * width * 20, transcendentals=0
        ),
        name="resid_back",
    )(kept, got, resid, cotangent, mixed, w_o, norms)


def attend_back_kernel(
    counts, keyvals, queries, key_input, grad_mixed, grad_kv, grad_q, grad_w, sums
):
    step = pl.program_id(0)
    keys_len = keyvals.shape[1]
    lat_len, inner = queries.shape[1:]
    media_len = keys_len - lat_len
    size = inner // HEADS
    wide = size * GROUP
    scale = 1.0 / math.sqrt(size)
    key_at = lax.broadcasted_iota(jnp.int32, (keys_len, 1), 0)
    valid = (key_at < counts[step]) | (key_at >= media_len)
    for at in range(0, inner, wide):
        keys = keyvals[0, :, at : at + wide]
        values = keyvals[0, :, inner + at : inner + at + wide]
        own = spread(queries[0, :, at : at + wide].astype(F32) * scale, size).astype(BF16)
        grad = spread(grad_mixed[0, :, at : at + wide], size).astype(BF16)
        scores = jnp.where(valid, contract(keys, own, (1, 1)), NEG)
        expd = jnp.exp(scores - jnp.max(scores, 0, keepdims=True))
        probs = expd * (1.0 / jnp.sum(expd, 0, keepdims=True))
        grad_v = contract(probs.astype(BF16), grad, (1, 0)).astype(BF16)
        grad_kv[0, :, inner + at : inner + at + wide] = grad_v
        grad_probs = contract(values, grad, (1, 1))
        held = jnp.sum(probs * grad_probs, 0, keepdims=True)
        low = (probs * (grad_probs - held)).astype(BF16)
        grad_kv[0, :, at : at + wide] = contract(low, own, (1, 0)).astype(BF16)
        back = contract(low, keys, (0, 0))
        grad_q[0, :, at : at + wide] = (gathered(back, size) * scale).astype(BF16)

    @pl.when(step == 0)
    def _():
        grad_w[...] = jnp.zeros_like(grad_w)
        sums[...] = jnp.zeros_like(sums)

    sums[...] += jnp.sum(grad_kv[0, :media_len, :].astype(F32), 0, keepdims=True)
    grad_w[...] += contract(key_input[0], grad_kv[0, :media_len, :], (0, 0))


def attend_back(counts, keyvals, queries, key_input, grad_mixed):
    images, keys_len, width = key_input.shape
    lat_len, inner = queries.shape[1:]
    media_len = keys_len - lat_len
    flops = 2 * images * (media_len * width * 2 * inner + 5 * lat_len * keys_len * inner * GROUP)
    return pl.pallas_call(
        attend_back_kernel,
        grid_spec=pltpu.PrefetchScalarGridSpec(
            num_scalar_prefetch=1,
            grid=(images,),
            in_specs=[
                pl.BlockSpec((1, keys_len, 2 * inner), image_at),
                pl.BlockSpec((1, lat_len, inner), image_at),
                pl.BlockSpec((1, media_len, width), image_at),
                pl.BlockSpec((1, lat_len, inner), image_at),
            ],
            out_specs=[
                pl.BlockSpec((1, keys_len, 2 * inner), image_at),
                pl.BlockSpec((1, lat_len, inner), image_at),
                pl.BlockSpec((width, 2 * inner), fixed_at),
                pl.BlockSpec((8, 2 * inner), fixed_at),
            ],
        ),
        out_shape=[
            jax.ShapeDtypeStruct((images, keys_len, 2 * inner), BF16),
            jax.ShapeDtypeStruct((images, lat_len, inner), BF16),
            jax.ShapeDtypeStruct((width, 2 * inner), F32),
            jax.ShapeDtypeStruct((8, 2 * inner), F32),
        ],
        compiler_params=params(40),
        cost_estimate=pl.CostEstimate(
            flops=2 * flops, bytes_accessed=images * keys_len * width * 8, transcendentals=0
        ),
        name="attend_back",
    )(counts, keyvals, queries, key_input, grad_mixed)


def as_row(column):
    out = []
    size = 128
    same = lax.broadcasted_iota(jnp.int32, (size, size), 0) == lax.broadcasted_iota(
        jnp.int32, (size, size), 1
    )
    for at in range(0, column.shape[0], size):
        out.append(jnp.sum(jnp.where(same, column[at : at + size, :], 0.0), 0, keepdims=True))
    return jnp.concatenate(out, 1)


def latent_back_kernel(
    grad_kv,
    grad_q,
    key_input,
    latent,
    grad_resid,
    w_kv,
    w_q,
    norms,
    media_w,
    media_sums,
    latent_grad,
    grad_wkv,
    grad_wq,
    vectors,
):
    images, lat_len, width = latent.shape
    rows = images * lat_len
    flat_kv = grad_kv[...].reshape(rows, grad_kv.shape[2])
    flat_q = grad_q[...].reshape(rows, grad_q.shape[2])
    low = key_input[...].reshape(rows, width)
    grad = contract(flat_kv, w_kv[...], (1, 1)) + contract(flat_q, w_q[...], (1, 1))
    unit, inverse = norm_rows(latent[...].reshape(rows, width).astype(F32))
    back = norm_back(grad, unit, inverse, norms[2:3, :])
    latent_grad[...] = grad_resid[...] + back.reshape(images, lat_len, width)
    grad_wq[...] = contract(low, flat_q, (0, 0)).astype(BF16)
    grad_wkv[...] = (media_w[...] + contract(low, flat_kv, (0, 0))).astype(BF16)
    parts, left = [], media_sums[0:1, :]
    for _ in range(3):
        parts.append(left.astype(BF16))
        left = left - parts[-1].astype(F32)
    parts.append(jnp.zeros((5, left.shape[1]), BF16))
    bias = jnp.sum(contract(jnp.concatenate(parts, 0), w_kv[...], (1, 1)), 0, keepdims=True)
    both = as_row(jnp.sum(media_w[...] * w_kv[...].astype(F32), 1, keepdims=True))
    vectors[...] = jnp.zeros_like(vectors)
    vectors[0:1, :] = (both - norms[1:2, :] * bias) / norms[0:1, :]
    vectors[1:2, :] = bias
    vectors[2:3, :] = jnp.sum(grad * unit, 0, keepdims=True)
    vectors[3:4, :] = jnp.sum(grad, 0, keepdims=True)


def latent_back(grad_kv, grad_q, key_input, latent, grad_resid, w_kv, w_q, norms, media_w, media_sums):
    images, lat_len, width = latent.shape
    inner = w_q.shape[1]
    tail = grad_kv.shape[1] // lat_len - 1
    tail_at = lambda i: (0, tail, 0)
    whole3 = lambda i: (0, 0, 0)
    return pl.pallas_call(
        latent_back_kernel,
        grid=(1,),
        in_specs=[
            pl.BlockSpec((images, lat_len, 2 * inner), tail_at),
            pl.BlockSpec((images, lat_len, inner), whole3),
            pl.BlockSpec((images, lat_len, width), tail_at),
            pl.BlockSpec((images, lat_len, width), whole3),
            pl.BlockSpec((images, lat_len, width), whole3),
            pl.BlockSpec(w_kv.shape, fixed_at),
            pl.BlockSpec(w_q.shape, fixed_at),
            pl.BlockSpec(norms.shape, fixed_at),
            pl.BlockSpec(media_w.shape, fixed_at),
            pl.BlockSpec(media_sums.shape, fixed_at),
        ],
        out_specs=[
            pl.BlockSpec((images, lat_len, width), whole3),
            pl.BlockSpec(w_kv.shape, fixed_at),
            pl.BlockSpec(w_q.shape, fixed_at),
            pl.BlockSpec((8, width), fixed_at),
        ],
        out_shape=[
            jax.ShapeDtypeStruct((images, lat_len, width), F32),
            jax.ShapeDtypeStruct(w_kv.shape, BF16),
            jax.ShapeDtypeStruct(w_q.shape, BF16),
            jax.ShapeDtypeStruct((8, width), F32),
        ],
        compiler_params=params(48),
        cost_estimate=pl.CostEstimate(
            flops=14 * images * lat_len * inner * width, bytes_accessed=20 << 20, transcendentals=0
        ),
        name="latent_back",
    )(grad_kv, grad_q, key_input, latent, grad_resid, w_kv, w_q, norms, media_w, media_sums)


def media_back_kernel(media, grad_kv, norms, w_kv, out, grad):
    grad[...] = contract(grad_kv[0], w_kv[...], (1, 1))
    for at in range(0, media.shape[1], ROWS):
        unit, inverse = norm_rows(media[0, at : at + ROWS, :].astype(F32))
        out[0, at : at + ROWS, :] = norm_back(grad[at : at + ROWS, :], unit, inverse, norms[0:1, :])


def media_back(media, grad_kv, norms, w_kv):
    images, media_len, width = media.shape
    inner2 = w_kv.shape[1]
    at = lambda i: (i, 0, 0)
    return pl.pallas_call(
        media_back_kernel,
        grid=(images,),
        in_specs=[
            pl.BlockSpec((1, media_len, width), at),
            pl.BlockSpec((1, media_len, inner2), at),
            pl.BlockSpec(norms.shape, fixed_at),
            pl.BlockSpec(w_kv.shape, fixed_at),
        ],
        out_specs=pl.BlockSpec((1, media_len, width), at),
        out_shape=jax.ShapeDtypeStruct((images, media_len, width), F32),
        scratch_shapes=[pltpu.VMEM((media_len, width), F32)],
        compiler_params=params(32),
        cost_estimate=pl.CostEstimate(
            flops=4 * images * media_len * width * inner2,
            bytes_accessed=images * media_len * width * 8,
            transcendentals=0,
        ),
        name="media_back",
    )(media, grad_kv, norms, w_kv)


class Grid:
    def __init__(self, dp, rep):
        self.dp = dp
        self.rep = rep
        self.me = lax.axis_index("dp")
        self.core = lax.axis_index("rep")
        self.column = [1 << b for b in range(2, dp.bit_length() - 1)]

    def swap(self, value, bit):
        return lax.ppermute(value, "dp", [(i, i ^ bit) for i in range(self.dp)])

    def side(self, bit):
        return (self.me & bit) != 0

    def pair(self, own, other, bit, axis):
        return jnp.where(
            self.side(bit), jnp.stack([other, own], axis), jnp.stack([own, other], axis)
        )

    def pick(self, value, bit, axis):
        at = jnp.where(self.side(bit), 1, 0)
        keep = lax.dynamic_index_in_dim(value, at, axis, keepdims=False)
        send = lax.dynamic_index_in_dim(value, 1 - at, axis, keepdims=False)
        return keep, send

    def gather(self, first, second):
        rows = first.shape[0]
        both = jnp.concatenate([first, second], 0)[None]
        for bit in reversed(self.column):
            got = self.swap(both, bit)
            both = self.pair(both, got, bit, 1)
            both = both.reshape((-1,) + both.shape[2:])
        first, second = both[:, :rows], both[:, rows:]
        first_got, second_got = self.swap(first, 2), self.swap(second, 1)
        first = self.pair(first, first_got, 2, 1)
        second = self.pair(second, second_got, 1, 1)
        first_got, second_got = self.swap(first, 1), self.swap(second, 2)
        first = self.pair(first, first_got, 1, 2)
        second = self.pair(second, second_got, 2, 1)
        return (
            first.reshape((self.dp,) + first.shape[3:]),
            second.reshape((self.dp,) + second.shape[3:]),
        )

    def total(self, first, second):
        rows = first.shape[1]
        tail = first.shape[1:]

        def fold(value, bit, axis, last=False):
            keep, send = self.pick(value, bit, axis)
            got = self.swap(send, bit)
            added = keep.astype(F32) + got.astype(F32)
            return added if last else added.astype(BF16)

        first = first.reshape((-1, 2, 2) + tail)
        second = second.reshape((-1, 2, 2) + second.shape[1:])
        first, second = fold(first, 1, 2), fold(second, 2, 1)
        first, second = fold(first, 2, 1), fold(second, 1, 1)
        both = jnp.concatenate([first, second], 1)
        for bit in self.column:
            both = both.reshape((-1, 2) + both.shape[1:])
            both = fold(both, bit, 1, bit == self.column[-1])
        both = both[0]
        return both[:rows], both[rows:]

    def other(self, value):
        return lax.ppermute(value, "rep", [(0, 1), (1, 0)])

    def rep_all(self, value):
        if self.rep != 2:
            return lax.all_gather(value, "rep", axis=0)
        got = self.other(value)
        return jnp.where(self.core == 0, jnp.stack([value, got]), jnp.stack([got, value]))

    def rep_rows(self, value):
        if self.rep != 2:
            return lax.all_gather(value, "rep", axis=0, tiled=True)
        return jnp.concatenate([value, self.other(value)], 0)

    def rep_back(self, pieces):
        if self.rep != 2:
            value = jnp.concatenate([piece.astype(F32) for pair in pieces for piece in pair], 0)
            value = lax.psum_scatter(value, "rep", scatter_dimension=0, tiled=True)
            return value, jnp.zeros(value.shape, BF16)
        ((kept, sent),) = pieces
        return kept, self.other(sent)

    def rep_total(self, value, axis):
        if self.rep != 2:
            value = jnp.moveaxis(value, axis, 0).astype(F32)
            return lax.psum_scatter(value, "rep", scatter_dimension=0).astype(BF16)
        keep = lax.dynamic_index_in_dim(value, self.core, axis, keepdims=False)
        send = lax.dynamic_index_in_dim(value, 1 - self.core, axis, keepdims=False)
        return (keep.astype(F32) + self.other(send).astype(F32)).astype(BF16)

    def mine(self, value, axis):
        return lax.dynamic_index_in_dim(value, self.core, axis, keepdims=False)


def fold_rows(value):
    half = value.shape[-2] // 2
    return jnp.concatenate([value[..., :half, :], value[..., half:, :]], -1)


def unfold_rows(value):
    half = value.shape[-1] // 2
    return jnp.concatenate([value[..., :half], value[..., half:]], -2)


def shards(
    dp,
    rep,
    media_tokens,
    patch_counts,
    latents,
    media_gain,
    media_bias,
    latent_gain,
    latent_bias,
    query_weight,
    keyval_weight,
    outproj_weight,
    ff_gain,
    ff_bias,
    ff_in_weight,
    ff_out_weight,
    cotangent,
):
    grid = Grid(dp, rep)
    images, media_len, width = media_tokens.shape
    lat_len = latents.shape[1]
    inner_width = query_weight.shape[1]
    hidden = ff_in_weight.shape[1]
    slot = hidden // dp // rep
    part = width // dp
    kv_rows = part // rep
    o_rows = inner_width // dp // rep

    norms = jnp.stack([media_gain, media_bias, latent_gain, latent_bias, ff_gain, ff_bias])
    norm_row = jnp.pad(norms.reshape(1, -1), ((0, 0), (0, width - norms.size)))
    kv_part = grid.mine(keyval_weight.reshape(rep, kv_rows, width), 0)
    q_part = fold_rows(grid.mine(query_weight.reshape(rep, kv_rows, inner_width), 0))
    q_rows = q_part.shape[0]
    got_kv, got_q = grid.gather(kv_part, jnp.concatenate([q_part, norm_row], 0))
    got_norms = got_q[:, q_rows, : norms.size].reshape(dp, 6, part)
    got_norms = jnp.moveaxis(got_norms, 1, 0).reshape(6, width).astype(F32)
    norms_all = jnp.concatenate([got_norms, jnp.zeros((2, width), F32)], 0)
    w_keyval = jnp.moveaxis(grid.rep_all(got_kv), 0, 1).reshape(width, width)
    w_query = jnp.moveaxis(grid.rep_all(unfold_rows(got_q[:, :q_rows])), 0, 1)
    w_query = w_query.reshape(width, inner_width)

    ffin_part = grid.mine(ff_in_weight.reshape(part, dp, rep, slot), 2).reshape(part, dp * slot)
    cut = ffin_part.shape[1] // 2
    o_part = grid.mine(outproj_weight.reshape(rep, o_rows, width), 0)
    o_part = jnp.pad(o_part, ((0, 0), (0, max(cut - width, 0))))
    got_lo, got_hi = grid.gather(
        ffin_part[:, :cut] if cut >= width else jnp.pad(ffin_part[:, :cut], ((0, 0), (0, width - cut))),
        jnp.concatenate(
            [
                ffin_part[:, cut:] if cut >= width else jnp.pad(ffin_part[:, cut:], ((0, 0), (0, width - cut))),
                o_part,
            ],
            0,
        ),
    )
    w_ffin = jnp.concatenate(
        [
            got_lo[:, :, :cut].reshape(width, cut),
            got_hi[:, :part, :cut].reshape(width, cut),
        ],
        1,
    )
    w_outproj = jnp.moveaxis(grid.rep_all(got_hi[:, part:, :width]), 0, 1).reshape(inner_width, width)
    ffout_part = grid.mine(ff_out_weight.reshape(rep, slot, width), 0)
    w_ffout = lax.all_gather(ffout_part, "dp", axis=0, tiled=True)

    flat = (images * lat_len, width)
    dout = grid.rep_rows(cotangent.astype(BF16).reshape(flat))
    key_input, keyvals, queries, mixed = attend(
        patch_counts, media_tokens, latents, norms_all, w_keyval, w_query
    )
    mixed = mixed.reshape(-1, inner_width)
    resid, low = add_branch(mixed, latents.reshape(flat), w_outproj, norms_all)

    low = grid.rep_rows(low)
    cuts = [slice(at, at + FF_ROWS) for at in range(0, low.shape[0], FF_ROWS)]
    ahead = [feed_forward(low[cut], dout[cut], w_ffin, w_ffout) for cut in cuts]
    grad_ffout = functools.reduce(jnp.add, [part[3] for part in ahead])
    back = [
        feed_back(low[cut], dout[cut], w_ffin, w_ffout, part[2])
        for cut, part in zip(cuts, ahead, strict=True)
    ]
    grad_ffin = functools.reduce(jnp.add, [part[0] for part in back])
    kept, got = grid.rep_back([part[1:] for part in back])
    share, other_share = grid.rep_back([part[:2] for part in ahead])
    new_latents = (resid + share + other_share.astype(F32)).reshape(latents.shape)

    grad_ffout = grad_ffout.reshape(dp, slot, width)
    own_lo, own_hi = grid.total(grad_ffout[:, : slot // 2], grad_ffout[:, slot // 2 :])
    own_ffout = grid.rep_all(jnp.concatenate([own_lo, own_hi], 0)).reshape(rep * slot, width)
    grad_ffin = grad_ffin.reshape(dp, part, dp * slot)
    own_lo, own_hi = grid.total(grad_ffin[:, :, :cut], grad_ffin[:, :, cut:])
    own_ffin = grid.rep_all(jnp.concatenate([own_lo, own_hi], 1))
    own_ffin = jnp.moveaxis(own_ffin.reshape(rep, part, dp, slot), 0, 2).reshape(part, hidden)

    grad_resid, grad_mixed, grad_outproj, ff_vectors = resid_back(
        kept, got, resid, cotangent.reshape(flat), mixed, w_outproj, norms_all
    )
    grad_kv, grad_q, media_w, media_sums = attend_back(
        patch_counts, keyvals, queries, key_input, grad_mixed.reshape(images, lat_len, inner_width)
    )
    latent_grad, grad_kvweight, grad_qweight, vectors = latent_back(
        grad_kv,
        grad_q,
        key_input,
        latents,
        grad_resid.reshape(latents.shape),
        w_keyval,
        w_query,
        norms_all,
        media_w,
        media_sums,
    )
    media_grad = media_back(media_tokens, grad_kv, norms_all, w_keyval)
    vectors = jnp.concatenate([vectors[:4], ff_vectors[:2]], 0)

    kv_sum = grid.rep_total(grad_kvweight.reshape(dp, rep, kv_rows, width), 1)
    q_sum = fold_rows(grid.rep_total(grad_qweight.reshape(dp, rep, kv_rows, inner_width), 1))
    o_sum = grid.rep_total(grad_outproj.reshape(dp, rep, o_rows, width), 1)
    vec_row = jnp.moveaxis(vectors.reshape(6, dp, part), 1, 0).reshape(dp, 1, 6 * part)
    vec_row = jnp.pad(vec_row, ((0, 0), (0, 0), (0, width - 6 * part))).astype(BF16)
    own_kv, own_rest = grid.total(kv_sum, jnp.concatenate([q_sum, o_sum, vec_row], 1))
    every = grid.rep_all(jnp.concatenate([own_kv, own_rest], 0))
    own_kv = every[:, :kv_rows].reshape(part, width)
    own_q = unfold_rows(every[:, kv_rows : kv_rows + q_rows]).reshape(part, inner_width)
    at = kv_rows + q_rows
    own_o = every[:, at : at + o_rows].reshape(rep * o_rows, width)
    own_vec = jnp.sum(every[:, at + o_rows, : 6 * part], 0).reshape(6, part)
    return (
        new_latents,
        media_grad,
        latent_grad,
        own_vec[0],
        own_vec[1],
        own_vec[2],
        own_vec[3],
        own_q,
        own_kv,
        own_o,
        own_vec[4],
        own_vec[5],
        own_ffin,
        own_ffout,
    )


def solution(mesh):
    dp, rep = mesh.shape["dp"], mesh.shape["rep"]

    def program(*arrays):
        return shards(dp, rep, *arrays)

    return jax.shard_map(
        program,
        mesh=mesh,
        in_specs=(
            P(("dp", "rep"), None, None),
            P(("dp", "rep")),
            P(("dp", "rep"), None, None),
            P("dp"),
            P("dp"),
            P("dp"),
            P("dp"),
            P("dp", None),
            P("dp", None),
            P("dp", None),
            P("dp"),
            P("dp"),
            P("dp", None),
            P("dp", None),
            P(("dp", "rep"), None, None),
        ),
        out_specs=(
            P(("dp", "rep"), None, None),
            P(("dp", "rep"), None, None),
            P(("dp", "rep"), None, None),
            P("dp"),
            P("dp"),
            P("dp"),
            P("dp"),
            P("dp", None),
            P("dp", None),
            P("dp", None),
            P("dp"),
            P("dp"),
            P("dp", None),
            P("dp", None),
        ),
        check_vma=False,
    )
```

```python
import functools
import math

import jax
import jax.numpy as jnp
from jax import lax
from jax.experimental import pallas as pl
from jax.experimental.pallas import tpu as pltpu
from jax.sharding import PartitionSpec as P

HEADS = 8
GROUP = 4
EPS = 1e-05
NEG = -1e30
ROWS = 64
FF_TILE = 512
PLANE = 4
PAD = 8
F32 = jnp.float32
BF16 = jnp.bfloat16


def cost(us):
    return pl.CostEstimate(flops=int(us * 1.1e9), bytes_accessed=1 << 18, transcendentals=0)


def contract(a, b, over):
    return lax.dot_general(a, b, ((over[:1], over[1:]), ((), ())), preferred_element_type=F32)


def norm_rows(values):
    centred = values - jnp.mean(values, -1, keepdims=True)
    inverse = lax.rsqrt(jnp.mean(centred * centred, -1, keepdims=True) + EPS)
    return centred * inverse, inverse


def norm_back(grad, unit, inverse, gain):
    scaled = grad * gain
    return inverse * (
        scaled
        - jnp.mean(scaled, -1, keepdims=True)
        - unit * jnp.mean(scaled * unit, -1, keepdims=True)
    )


def spread(value, size):
    lane = lax.broadcasted_iota(jnp.int32, value.shape, 1) // size
    value = value.astype(F32)
    return jnp.concatenate([jnp.where(lane == h, value, 0.0) for h in range(GROUP)], 0)


def gathered(value, size):
    rows = value.shape[0] // GROUP
    lane = lax.broadcasted_iota(jnp.int32, (rows, value.shape[1]), 1) // size
    out = jnp.zeros((rows, value.shape[1]), F32)
    for h in range(GROUP):
        out = jnp.where(lane == h, value[h * rows : (h + 1) * rows], out)
    return out


def tie(*values):
    return lax.optimization_barrier(values)


def params(mib):
    return pltpu.CompilerParams(vmem_limit_bytes=mib << 20)


def image_at(i, c):
    return (i, 0, 0)


def fixed_at(*_):
    return (0, 0)


def order_kernel(place, *refs):
    sides = refs[:PLANE], refs[PLANE : 2 * PLANE]
    w_kv, w_q, w_o, norms = refs[2 * PLANE :]
    me, core = place[0], place[1]
    columns = sides[0][0].shape[0]
    chips = columns * PLANE
    kv_rows, o_rows = w_kv.shape[0] // chips // 2, w_o.shape[0] // chips // 2
    q_rows, inner = kv_rows // 2, w_q.shape[1]
    total = jnp.zeros(norms.shape, F32)
    for plane in range(PLANE):
        for column in range(columns):
            chip = me ^ (column * PLANE + plane)
            for side in range(2):
                block = sides[side][plane]
                half = core if side == 0 else 1 - core
                at = pl.multiple_of((chip * 2 + half) * kv_rows, kv_rows)
                w_kv[pl.ds(at, kv_rows), :] = block[column, :kv_rows, :]
                rest = block[column, kv_rows : kv_rows + q_rows, :]
                w_q[pl.ds(at, q_rows), :] = rest[:, :inner]
                w_q[pl.ds(pl.multiple_of(at + q_rows, q_rows), q_rows), :] = rest[:, inner:]
                at = pl.multiple_of((chip * 2 + half) * o_rows, o_rows)
                w_o[pl.ds(at, o_rows), :] = block[
                    column, kv_rows + q_rows : kv_rows + q_rows + o_rows, :
                ]
            total += sides[0][plane][column, kv_rows + q_rows + o_rows :, :].astype(F32)
    norms[...] = total


def in_order(place, own, other, inner):
    columns, _, width = own[0].shape
    return pl.pallas_call(
        order_kernel,
        grid_spec=pltpu.PrefetchScalarGridSpec(
            num_scalar_prefetch=1,
            grid=(1,),
            in_specs=[
                pl.BlockSpec(value.shape, lambda t, c: (0, 0, 0)) for value in (*own, *other)
            ],
            out_specs=[
                pl.BlockSpec((width, 2 * inner), fixed_at),
                pl.BlockSpec((width, inner), fixed_at),
                pl.BlockSpec((inner, width), fixed_at),
                pl.BlockSpec((8, width), fixed_at),
            ],
        ),
        out_shape=[
            jax.ShapeDtypeStruct((width, 2 * inner), BF16),
            jax.ShapeDtypeStruct((width, inner), BF16),
            jax.ShapeDtypeStruct((inner, width), BF16),
            jax.ShapeDtypeStruct((8, width), F32),
        ],
        compiler_params=params(24),
        cost_estimate=cost(1),
        name="in_order",
    )(place, *own, *other)


def whole_at(rank):
    return lambda *_: (0,) * rank


def small(kernel, values, outs, us, name):
    return pl.pallas_call(
        kernel,
        grid=(1,),
        in_specs=[pl.BlockSpec(value.shape, whole_at(value.ndim)) for value in values],
        out_specs=[pl.BlockSpec(shape, whole_at(len(shape))) for shape in outs],
        out_shape=[jax.ShapeDtypeStruct(shape, BF16) for shape in outs],
        compiler_params=params(20),
        cost_estimate=cost(us),
        name=name,
    )(*values)


def added(one, two):
    return (one.astype(F32) + two.astype(F32)).astype(BF16)


def fold_kernel(*refs):
    for column in range(len(refs) - PLANE):
        total = refs[0][column].astype(F32)
        for plane in range(1, PLANE):
            total += refs[plane][column].astype(F32)
        refs[PLANE + column][...] = total.astype(BF16)


def fold(values):
    columns = values[0].shape[0]
    return small(fold_kernel, values, [values[0].shape[1:]] * columns, 2, "fold")


def first_kernel(keep0, got0, keep1, got1, held0, pass0, held1, pass1):
    held0[...] = added(keep0[0], got0[0])
    pass0[...] = added(keep0[1], got0[1])
    held1[...] = added(keep1[0], got1[0])
    pass1[...] = added(keep1[1], got1[1])


def fold_first(keep0, got0, keep1, got1):
    values = keep0, got0, keep1, got1
    return small(first_kernel, values, [keep0.shape[1:]] * 4, 2, "fold_first")


def second_kernel(held0, got0, held1, got1, keep, send):
    half = held0.shape[1]
    for i in range(2):
        for out, column in ((keep, 2 * i), (send, 2 * i + 1)):
            out[i, :half, :] = added(held0[column], got0[column])
            out[i, half:, :] = added(held1[column], got1[column])


def fold_second(held0, got0, held1, got1):
    values = held0, got0, held1, got1
    shape = (2, 2 * held0.shape[1], held0.shape[2])
    return small(second_kernel, values, [shape] * 2, 2, "fold_second")


def third_kernel(keep, got, held, passed):
    held[...] = added(keep[0], got[0])
    passed[...] = added(keep[1], got[1])


def fold_third(keep, got):
    return small(third_kernel, (keep, got), [keep.shape[1:]] * 2, 1, "fold_third")


def both_kernel(keep, got, *outs):
    for plane, out in enumerate(outs):
        out[...] = (keep[plane].astype(F32) + got[plane].astype(F32)).astype(BF16)


def add_both(keep, got):
    tail = keep.shape[1:]
    whole = lambda t: (0, 0, 0, 0)
    return pl.pallas_call(
        both_kernel,
        grid=(1,),
        in_specs=[pl.BlockSpec(keep.shape, whole), pl.BlockSpec(keep.shape, whole)],
        out_specs=[pl.BlockSpec(tail, lambda t: (0, 0, 0)) for _ in range(PLANE)],
        out_shape=[jax.ShapeDtypeStruct(tail, BF16) for _ in range(PLANE)],
        compiler_params=params(16),
        cost_estimate=cost(2),
        name="add_both",
    )(keep, got)


def final_ff_kernel(place, own_in, other_in, own_out, other_out, grad_in, grad_out):
    first = place[1] == 0
    slot = own_out.shape[0]
    for chip in range(own_in.shape[1] // slot):
        here = slice(chip * slot, (chip + 1) * slot)
        one, two = own_in[:, here], other_in[:, here]
        at = 2 * chip * slot
        grad_in[:, at : at + slot] = jnp.where(first, one, two)
        grad_in[:, at + slot : at + 2 * slot] = jnp.where(first, two, one)
    grad_out[:slot, :] = jnp.where(first, own_out[...], other_out[...])
    grad_out[slot:, :] = jnp.where(first, other_out[...], own_out[...])


def final_ff(place, own_in, other_in, own_out, other_out):
    values = own_in, other_in, own_out, other_out
    shapes = (own_in.shape[0], 2 * own_in.shape[1]), (2 * own_out.shape[0], own_out.shape[1])
    return pl.pallas_call(
        final_ff_kernel,
        grid_spec=pltpu.PrefetchScalarGridSpec(
            num_scalar_prefetch=1,
            grid=(1,),
            in_specs=[pl.BlockSpec(value.shape, fixed_at) for value in values],
            out_specs=[pl.BlockSpec(shape, fixed_at) for shape in shapes],
        ),
        out_shape=[jax.ShapeDtypeStruct(shape, F32) for shape in shapes],
        compiler_params=params(16),
        cost_estimate=cost(2),
        name="final_ff",
    )(place, *values)


def final_attn_kernel(place, own, other, grad_kv, grad_q, grad_o):
    kv_rows, o_rows = grad_kv.shape[0] // 2, grad_o.shape[0] // 2
    q_rows, inner = kv_rows // 2, grad_q.shape[1]
    first = place[1] == 0
    for half in range(2):
        value = jnp.where(first == (half == 0), own[...], other[...])
        at = half * kv_rows
        grad_kv[at : at + kv_rows, :] = value[:kv_rows]
        rest = value[kv_rows : kv_rows + q_rows]
        grad_q[at : at + q_rows, :] = rest[:, :inner]
        grad_q[at + q_rows : at + kv_rows, :] = rest[:, inner:]
        grad_o[half * o_rows : (half + 1) * o_rows, :] = value[
            kv_rows + q_rows : kv_rows + q_rows + o_rows
        ]


def final_attn(place, own, other, inner, kv_rows, o_rows):
    width = own.shape[1]
    shapes = (2 * kv_rows, width), (2 * kv_rows, inner), (2 * o_rows, width)
    return pl.pallas_call(
        final_attn_kernel,
        grid_spec=pltpu.PrefetchScalarGridSpec(
            num_scalar_prefetch=1,
            grid=(1,),
            in_specs=[pl.BlockSpec(own.shape, fixed_at), pl.BlockSpec(own.shape, fixed_at)],
            out_specs=[pl.BlockSpec(shape, fixed_at) for shape in shapes],
        ),
        out_shape=[jax.ShapeDtypeStruct(shape, F32) for shape in shapes],
        compiler_params=params(16),
        cost_estimate=cost(2),
        name="final_attn",
    )(place, own, other)


def attend_kernel(counts, media, latent, norms, w_kv, w_q, *refs):
    key_input, keyvals, queries, mixed = refs[-4:]
    media_len, lat_len = media.shape[1], latent.shape[1]
    keys_len = media_len + lat_len
    inner = w_q.shape[1]
    size = inner // HEADS
    wide = size * GROUP
    for at in range(0, media_len, ROWS):
        unit, _ = norm_rows(media[0, at : at + ROWS, :].astype(F32))
        key_input[0, at : at + ROWS, :] = (unit * norms[0:1, :] + norms[1:2, :]).astype(BF16)
    unit, _ = norm_rows(latent[0].astype(F32))
    low = (unit * norms[2:3, :] + norms[3:4, :]).astype(BF16)
    key_input[0, media_len:, :] = low
    query = contract(low, w_q[...], (1, 0)).astype(BF16)
    queries[0] = query
    keyvals[0] = contract(key_input[0], w_kv[...], (1, 0)).astype(BF16)
    key_at = lax.broadcasted_iota(jnp.int32, (1, keys_len), 1)
    valid = (key_at < counts[pl.program_id(0)]) | (key_at >= media_len)
    for at in range(0, inner, wide):
        own = spread(query[:, at : at + wide].astype(F32) * (1.0 / math.sqrt(size)), size)
        scores = contract(own.astype(BF16), keyvals[0, :, at : at + wide], (1, 1))
        scores = jnp.where(valid, scores, NEG)
        expd = jnp.exp(scores - jnp.max(scores, -1, keepdims=True))
        probs = (expd * (1.0 / jnp.sum(expd, -1, keepdims=True))).astype(BF16)
        out = contract(probs, keyvals[0, :, inner + at : inner + at + wide], (1, 0))
        mixed[0, :, at : at + wide] = gathered(out, size).astype(BF16)


def attend(counts, media, latent, norms, w_kv, w_q, first, run, into=()):
    images, media_len, width = media.shape
    lat_len, inner = latent.shape[1], w_q.shape[1]
    keys_len = media_len + lat_len
    at = lambda i, c: (i + first, 0, 0)
    shapes = [
        (images, keys_len, width),
        (images, keys_len, 2 * inner),
        (images, lat_len, inner),
        (images, lat_len, inner),
    ]
    return pl.pallas_call(
        attend_kernel,
        grid_spec=pltpu.PrefetchScalarGridSpec(
            num_scalar_prefetch=1,
            grid=(run,),
            in_specs=[
                pl.BlockSpec((1, media_len, width), at),
                pl.BlockSpec((1, lat_len, width), at),
                pl.BlockSpec(norms.shape, fixed_at),
                pl.BlockSpec(w_kv.shape, fixed_at),
                pl.BlockSpec(w_q.shape, fixed_at),
                *[pl.BlockSpec(memory_space=pl.ANY) for _ in into],
            ],
            out_specs=[pl.BlockSpec((1,) + shape[1:], at) for shape in shapes],
        ),
        out_shape=[jax.ShapeDtypeStruct(shape, BF16) for shape in shapes],
        input_output_aliases={6 + i: i for i in range(len(into))},
        compiler_params=params(32),
        cost_estimate=cost(14),
        name="attend",
    )(counts[first : first + run], media, latent, norms, w_kv, w_q, *into)


def resid_kernel(mixed, latent, w_o, norms, resid, low):
    value = latent[...].astype(F32) + contract(mixed[...], w_o[...], (1, 0))
    resid[...] = value
    unit, _ = norm_rows(value)
    low[...] = (unit * norms[4:5, :] + norms[5:6, :]).astype(BF16)


def add_branch(mixed, latent, w_o, norms):
    rows, width = latent.shape
    inner = mixed.shape[1]
    block = rows // 4
    row_at = lambda i: (i, 0)
    return pl.pallas_call(
        resid_kernel,
        grid=(rows // block,),
        in_specs=[
            pl.BlockSpec((block, inner), row_at),
            pl.BlockSpec((block, width), row_at),
            pl.BlockSpec(w_o.shape, fixed_at),
            pl.BlockSpec(norms.shape, fixed_at),
        ],
        out_specs=[pl.BlockSpec((block, width), row_at), pl.BlockSpec((block, width), row_at)],
        out_shape=[
            jax.ShapeDtypeStruct((rows, width), F32),
            jax.ShapeDtypeStruct((rows, width), BF16),
        ],
        compiler_params=params(16),
        cost_estimate=cost(3),
        name="add_branch",
    )(mixed, latent, w_o, norms)


def ff_kernel(place, *refs):
    low0, low1, dout0, dout1 = refs[:4]
    lo, hi = refs[4:8], refs[8:12]
    activ, slope, low_t, dout, w_in = refs[12:17]
    keep0, send0, keep1, send1 = refs[17:21]
    low, grad = refs[21:]
    step, steps = pl.program_id(0), pl.num_programs(0)
    me = place[0]
    half = low0.shape[0]
    part = lo[0].shape[1]
    slot = grad.shape[0] // PLANE
    cut = slot // 2

    @pl.when(step == 0)
    def _():
        low[:half, :] = low0[...]
        low[half:, :] = low1[...]
        dout[:half, :] = dout0[...]
        dout[half:, :] = dout1[...]
        low_t[...] = low[...].T

    def put(pieces):
        for plane in range(PLANE):
            for column in range(pieces[0].shape[0]):
                at = pl.multiple_of((me ^ (column * PLANE + plane)) * part, part)
                w_in[pl.ds(at, part), :] = pieces[plane][column]

    pl.when(step < steps // 2)(lambda: put(lo))
    pl.when(step >= steps // 2)(lambda: put(hi))
    pre = contract(low[...], w_in[...], (1, 0))
    cdf = 0.5 * (1.0 + lax.erf(pre * math.sqrt(0.5)))
    slope[...] = cdf + pre * (jnp.exp(pre * pre * -0.5) * (1.0 / math.sqrt(2.0 * math.pi)))
    value = (pre * cdf).astype(BF16)
    activ[...] = value
    grad[...] = contract(value, dout[...], (0, 0)).astype(BF16)

    def block(plane, at):
        at = pl.multiple_of((plane ^ (me % PLANE)) * slot + at, cut)
        return grad[pl.ds(at, cut), :]

    for i in range(2):
        keep0[i, 0] = block(2 * i, 0)
        send0[i, 0] = block(2 * i + 1, 0)
        keep1[i, 0] = block(i, cut)
        send1[i, 0] = block(2 + i, cut)


def feed_forward(place, lows, douts, lo, hi, slot):
    half, width = lows[0].shape
    rows = 2 * half
    columns, part, cut = lo[0].shape
    tile = PLANE * slot
    steps = 2 * cut // tile
    in_at = lambda t, c: (0, t)
    lo_at = lambda t, c: (0, 0, jnp.minimum(t, steps // 2 - 1))
    hi_at = lambda t, c: (0, 0, jnp.maximum(t - steps // 2, 0))
    once = pl.Buffered(1)
    return pl.pallas_call(
        ff_kernel,
        grid_spec=pltpu.PrefetchScalarGridSpec(
            num_scalar_prefetch=1,
            grid=(steps,),
            in_specs=[
                *[pl.BlockSpec((half, width), fixed_at, pipeline_mode=once) for _ in range(4)],
                *[pl.BlockSpec((columns, part, tile), lo_at) for _ in lo],
                *[pl.BlockSpec((columns, part, tile), hi_at) for _ in hi],
            ],
            out_specs=[
                pl.BlockSpec((rows, tile), in_at),
                pl.BlockSpec((rows, tile), in_at),
                pl.BlockSpec((width, rows), fixed_at),
                pl.BlockSpec((rows, width), fixed_at),
                pl.BlockSpec((width, tile), in_at),
                *[
                    pl.BlockSpec(
                        (2, 1, slot // 2, width), lambda t, c: (0, t ^ (c[0] // PLANE), 0, 0)
                    )
                    for _ in range(4)
                ],
            ],
            scratch_shapes=[pltpu.VMEM((rows, width), BF16), pltpu.VMEM((tile, width), BF16)],
        ),
        out_shape=[
            jax.ShapeDtypeStruct((rows, 2 * cut), BF16),
            jax.ShapeDtypeStruct((rows, 2 * cut), F32),
            jax.ShapeDtypeStruct((width, rows), BF16),
            jax.ShapeDtypeStruct((rows, width), BF16),
            jax.ShapeDtypeStruct((width, 2 * cut), BF16),
            *[jax.ShapeDtypeStruct((2, columns, slot // 2, width), BF16) for _ in range(4)],
        ],
        compiler_params=params(44),
        cost_estimate=cost(18),
        name="feed_forward",
    )(place, *lows, *douts, *lo, *hi)


def ff_back_kernel(
    place, dout, low_t, w_in, w_out, slope, keep0, send0, keep1, send1, kept, sent, total, grad_in
):
    step, steps = pl.program_id(0), pl.num_programs(0)
    columns, cut = keep0.shape[1:3]

    @pl.when(step == 0)
    def _():
        total[...] = jnp.zeros_like(total)

    grad = (contract(dout[...], w_out[...], (1, 1)) * slope[...]).astype(BF16)
    grad_in[...] = contract(low_t[...], grad, (1, 0)).astype(BF16)

    def block(plane, column, at):
        at = pl.multiple_of((place[0] ^ (column * PLANE + plane)) * 2 * cut + at, cut)
        return grad_in[pl.ds(at, cut), :]

    for column in range(columns):
        for i in range(2):
            keep0[i, column] = block(2 * i, column, 0)
            send0[i, column] = block(2 * i + 1, column, 0)
            keep1[i, column] = block(i, column, cut)
            send1[i, column] = block(2 + i, column, cut)
    total[...] += contract(grad, w_in[...], (1, 1))

    @pl.when(step == steps - 1)
    def _():
        half = kept.shape[0]
        kept[...] = total[:half, :]
        sent[...] = total[half:, :].astype(BF16)


def feed_back(place, dout, low_t, w_in, w_out, slope, columns, part):
    rows, width = dout.shape
    hidden = w_in.shape[1]
    tile = min(FF_TILE, hidden)
    half = rows // 2
    in_at, out_at = (lambda t, c: (0, t)), (lambda t, c: (t, 0))
    once = pl.Buffered(1)
    return pl.pallas_call(
        ff_back_kernel,
        grid_spec=pltpu.PrefetchScalarGridSpec(
            num_scalar_prefetch=1,
            grid=(hidden // tile,),
            in_specs=[
                pl.BlockSpec((rows, width), fixed_at, pipeline_mode=once),
                pl.BlockSpec((width, rows), fixed_at, pipeline_mode=once),
                pl.BlockSpec((width, tile), in_at),
                pl.BlockSpec((tile, width), out_at),
                pl.BlockSpec((rows, tile), in_at),
            ],
            out_specs=[
                *[
                    pl.BlockSpec((2, columns, part // 2, tile), lambda t, c: (0, 0, 0, t))
                    for _ in range(4)
                ],
                pl.BlockSpec((half, width), fixed_at, pipeline_mode=once),
                pl.BlockSpec((half, width), fixed_at, pipeline_mode=once),
            ],
            scratch_shapes=[pltpu.VMEM((rows, width), F32), pltpu.VMEM((width, tile), BF16)],
        ),
        out_shape=[
            *[jax.ShapeDtypeStruct((2, columns, part // 2, hidden), BF16) for _ in range(4)],
            jax.ShapeDtypeStruct((half, width), F32),
            jax.ShapeDtypeStruct((half, width), BF16),
        ],
        compiler_params=params(48),
        cost_estimate=cost(21),
        name="feed_back",
    )(place, dout, low_t, w_in, w_out, slope)


def ff_out_kernel(activ, w_out, kept, sent, total):
    step = pl.program_id(0)

    @pl.when(step == 0)
    def _():
        total[...] = jnp.zeros_like(total)

    total[...] += contract(activ[...], w_out[...], (1, 0))

    @pl.when(step == pl.num_programs(0) - 1)
    def _():
        half = kept.shape[0]
        kept[...] = total[:half, :]
        sent[...] = total[half:, :].astype(BF16)


def feed_out(activ, w_out):
    rows, hidden = activ.shape
    width = w_out.shape[1]
    tile = min(FF_TILE, hidden)
    half = rows // 2
    once = pl.Buffered(1)
    return pl.pallas_call(
        ff_out_kernel,
        grid=(hidden // tile,),
        in_specs=[
            pl.BlockSpec((rows, tile), lambda t: (0, t)),
            pl.BlockSpec((tile, width), lambda t: (t, 0)),
        ],
        out_specs=[pl.BlockSpec((half, width), fixed_at, pipeline_mode=once)] * 2,
        out_shape=[
            jax.ShapeDtypeStruct((half, width), F32),
            jax.ShapeDtypeStruct((half, width), BF16),
        ],
        scratch_shapes=[pltpu.VMEM((rows, width), F32)],
        compiler_params=params(24),
        cost_estimate=cost(7),
        name="feed_out",
    )(activ, w_out)


def resid_back_kernel(
    kept,
    got,
    resid,
    cotangent,
    mixed,
    w_o,
    norms,
    grad_resid,
    grad_mixed,
    grad_o,
    vectors,
    total,
):
    step = pl.program_id(0)

    @pl.when(step == 0)
    def _():
        vectors[...] = jnp.zeros_like(vectors)
        total[...] = jnp.zeros_like(total)

    grad = kept[...] + got[...].astype(F32)
    unit, inverse = norm_rows(resid[...])
    vectors[0:1, :] += jnp.sum(grad * unit, 0, keepdims=True)
    vectors[1:2, :] += jnp.sum(grad, 0, keepdims=True)
    value = cotangent[...] + norm_back(grad, unit, inverse, norms[4:5, :])
    grad_resid[...] = value
    low = value.astype(BF16)
    grad_mixed[...] = contract(low, w_o[...], (1, 1)).astype(BF16)
    total[...] += contract(mixed[...], low, (0, 0))
    grad_o[...] = total[...].astype(BF16)


def resid_back(kept, got, resid, cotangent, mixed, w_o, norms):
    rows, width = resid.shape
    inner = mixed.shape[1]
    block = rows // 4
    row_at = lambda i: (i, 0)
    wide = pl.BlockSpec((block, width), row_at)
    return pl.pallas_call(
        resid_back_kernel,
        grid=(rows // block,),
        in_specs=[
            *[wide] * 4,
            pl.BlockSpec((block, inner), row_at),
            pl.BlockSpec(w_o.shape, fixed_at),
            pl.BlockSpec(norms.shape, fixed_at),
        ],
        out_specs=[
            wide,
            pl.BlockSpec((block, inner), row_at),
            pl.BlockSpec(w_o.shape, fixed_at),
            pl.BlockSpec((8, width), fixed_at),
        ],
        out_shape=[
            jax.ShapeDtypeStruct((rows, width), F32),
            jax.ShapeDtypeStruct((rows, inner), BF16),
            jax.ShapeDtypeStruct(w_o.shape, BF16),
            jax.ShapeDtypeStruct((8, width), F32),
        ],
        scratch_shapes=[pltpu.VMEM(w_o.shape, F32)],
        compiler_params=params(24),
        cost_estimate=cost(6),
        name="resid_back",
    )(kept, got, resid, cotangent, mixed, w_o, norms)


def as_row(column):
    out = []
    size = 128
    same = lax.broadcasted_iota(jnp.int32, (size, size), 0) == lax.broadcasted_iota(
        jnp.int32, (size, size), 1
    )
    for at in range(0, column.shape[0], size):
        out.append(jnp.sum(jnp.where(same, column[at : at + size, :], 0.0), 0, keepdims=True))
    return jnp.concatenate(out, 1)


def in_bf16(row):
    parts = []
    for _ in range(3):
        parts.append(row.astype(BF16))
        row = row - parts[-1].astype(F32)
    return parts


def attend_back_kernel(counts, keyvals, queries, grad_mixed, grad_kv, grad_q):
    step = pl.program_id(0)
    keys_len = keyvals.shape[1]
    lat_len, inner = queries.shape[1:]
    media_len = keys_len - lat_len
    size = inner // HEADS
    wide = size * GROUP
    scale = 1.0 / math.sqrt(size)
    key_at = lax.broadcasted_iota(jnp.int32, (keys_len, 1), 0)
    valid = (key_at < counts[step]) | (key_at >= media_len)
    for at in range(0, inner, wide):
        keys = keyvals[0, :, at : at + wide]
        values = keyvals[0, :, inner + at : inner + at + wide]
        own = spread(queries[0, :, at : at + wide].astype(F32) * scale, size).astype(BF16)
        grad = spread(grad_mixed[0, :, at : at + wide], size).astype(BF16)
        scores = jnp.where(valid, contract(keys, own, (1, 1)), NEG)
        expd = jnp.exp(scores - jnp.max(scores, 0, keepdims=True))
        probs = expd * (1.0 / jnp.sum(expd, 0, keepdims=True))
        grad_v = contract(probs.astype(BF16), grad, (1, 0)).astype(BF16)
        grad_kv[0, :, inner + at : inner + at + wide] = grad_v
        grad_probs = contract(values, grad, (1, 1))
        held = jnp.sum(probs * grad_probs, 0, keepdims=True)
        low = (probs * (grad_probs - held)).astype(BF16)
        grad_kv[0, :, at : at + wide] = contract(low, own, (1, 0)).astype(BF16)
        back = contract(low, keys, (0, 0))
        grad_q[0, :, at : at + wide] = (gathered(back, size) * scale).astype(BF16)


def weight_back_kernel(
    place,
    grad_kv,
    grad_q,
    key_input,
    w_kv,
    w_q,
    norms,
    grad_o,
    ff_vectors,
    keep,
    send,
    media_w,
    sums,
    lat_low,
    lat_kv,
    lat_q,
    total_q,
):
    step, steps = pl.program_id(0), pl.num_programs(0)
    lat_len, inner = grad_q.shape[1:]
    media_len = grad_kv.shape[1] - lat_len

    @pl.when(step == 0)
    def _():
        media_w[...] = jnp.zeros_like(media_w)
        sums[...] = jnp.zeros_like(sums)

    sums[...] += jnp.sum(grad_kv[0, :media_len, :].astype(F32), 0, keepdims=True)
    media_w[...] += contract(key_input[0, :media_len, :], grad_kv[0, :media_len, :], (0, 0))
    here = pl.ds(pl.multiple_of(step * lat_len, lat_len), lat_len)
    lat_low[here, :] = key_input[0, media_len:, :]
    lat_kv[here, :] = grad_kv[0, media_len:, :]
    lat_q[here, :] = grad_q[0]

    @pl.when(step == steps - 1)
    def _():
        lat_w = contract(lat_low[...], lat_kv[...], (0, 0))
        lat_wq = contract(lat_low[...], lat_q[...], (0, 0))
        weight, weight_q = w_kv[...].astype(F32), w_q[...].astype(F32)
        lat_sum = jnp.sum(lat_kv[...].astype(F32), 0, keepdims=True)
        lat_sum_q = jnp.sum(lat_q[...].astype(F32), 0, keepdims=True)
        rows = in_bf16(sums[0:1, :]) + in_bf16(lat_sum) + [jnp.zeros((2, 2 * inner), BF16)]
        rows_q = in_bf16(lat_sum_q) + [jnp.zeros((5, inner), BF16)]
        biases = contract(jnp.concatenate(rows, 0), w_kv[...], (1, 1))
        biases_q = contract(jnp.concatenate(rows_q, 0), w_q[...], (1, 1))
        media_bias = jnp.sum(biases[0:3], 0, keepdims=True)
        lat_bias = jnp.sum(biases[3:6], 0, keepdims=True) + jnp.sum(biases_q, 0, keepdims=True)
        media_both = as_row(jnp.sum(media_w[...] * weight, 1, keepdims=True))
        lat_both = as_row(
            jnp.sum(lat_w * weight, 1, keepdims=True)
            + jnp.sum(lat_wq * weight_q, 1, keepdims=True)
        )
        vectors = [
            (media_both - norms[1:2, :] * media_bias) / norms[0:1, :],
            media_bias,
            (lat_both - norms[3:4, :] * lat_bias) / norms[2:3, :],
            lat_bias,
            ff_vectors[0:2, :],
            jnp.zeros((2, ff_vectors.shape[1]), F32),
        ]
        vectors = jnp.concatenate(vectors, 0).astype(BF16)
        media_w[...] += lat_w
        total_q[...] = lat_wq
        me, core = place[0], place[1]
        columns = keep.shape[1]
        kv_rows = media_w.shape[0] // (2 * columns * PLANE)
        o_rows = grad_o.shape[0] // (2 * columns * PLANE)
        q_rows = kv_rows // 2
        for plane in range(PLANE):
            for column in range(columns):
                chip = me ^ (column * PLANE + plane)
                for out, half in ((keep, core), (send, 1 - core)):
                    at = pl.multiple_of((chip * 2 + half) * kv_rows, kv_rows)
                    out[plane, column, :kv_rows, :] = media_w[pl.ds(at, kv_rows), :].astype(BF16)
                    value = total_q[pl.ds(at, kv_rows), :].astype(BF16)
                    row = kv_rows
                    out[plane, column, row : row + q_rows, :inner] = value[:q_rows]
                    out[plane, column, row : row + q_rows, inner:] = value[q_rows:]
                    row += q_rows
                    at = pl.multiple_of((chip * 2 + half) * o_rows, o_rows)
                    out[plane, column, row : row + o_rows, :] = grad_o[pl.ds(at, o_rows), :]
                    out[plane, column, row + o_rows :, :] = vectors


def attend_back(counts, keyvals, queries, grad_mixed):
    images, keys_len, wide = keyvals.shape
    lat_len, inner = queries.shape[1:]
    at = lambda i, c: (i, 0, 0)
    return pl.pallas_call(
        attend_back_kernel,
        grid_spec=pltpu.PrefetchScalarGridSpec(
            num_scalar_prefetch=1,
            grid=(images,),
            in_specs=[
                pl.BlockSpec((1, keys_len, wide), at),
                pl.BlockSpec((1, lat_len, inner), at),
                pl.BlockSpec((1, lat_len, inner), at),
            ],
            out_specs=[
                pl.BlockSpec((1, keys_len, wide), at),
                pl.BlockSpec((1, lat_len, inner), at),
            ],
        ),
        out_shape=[
            jax.ShapeDtypeStruct((images, keys_len, wide), BF16),
            jax.ShapeDtypeStruct((images, lat_len, inner), BF16),
        ],
        compiler_params=params(32),
        cost_estimate=cost(27),
        name="attend_back",
    )(counts, keyvals, queries, grad_mixed)


def weight_back(place, grad_kv, grad_q, key_input, w_kv, w_q, norms, grad_o, ff_vectors, columns):
    images, keys_len, width = key_input.shape
    lat_len, inner = grad_q.shape[1:]
    rows = images * lat_len
    chips = columns * PLANE
    kv_rows, o_rows = width // chips // 2, inner // chips // 2
    pack = (PLANE, columns, kv_rows + kv_rows // 2 + o_rows + PAD, width)
    at = lambda i, c: (i, 0, 0)
    once = pl.Buffered(1)
    return pl.pallas_call(
        weight_back_kernel,
        grid_spec=pltpu.PrefetchScalarGridSpec(
            num_scalar_prefetch=1,
            grid=(images,),
            in_specs=[
                pl.BlockSpec((1, keys_len, 2 * inner), at),
                pl.BlockSpec((1, lat_len, inner), at),
                pl.BlockSpec((1, keys_len, width), at),
                pl.BlockSpec(w_kv.shape, fixed_at, pipeline_mode=once),
                pl.BlockSpec(w_q.shape, fixed_at, pipeline_mode=once),
                pl.BlockSpec(norms.shape, fixed_at),
                pl.BlockSpec(grad_o.shape, fixed_at, pipeline_mode=once),
                pl.BlockSpec(ff_vectors.shape, fixed_at),
            ],
            out_specs=[
                pl.BlockSpec(pack, whole_at(4), pipeline_mode=once),
                pl.BlockSpec(pack, whole_at(4), pipeline_mode=once),
            ],
            scratch_shapes=[
                pltpu.VMEM(w_kv.shape, F32),
                pltpu.VMEM((8, 2 * inner), F32),
                pltpu.VMEM((rows, width), BF16),
                pltpu.VMEM((rows, 2 * inner), BF16),
                pltpu.VMEM((rows, inner), BF16),
                pltpu.VMEM(w_q.shape, F32),
            ],
        ),
        out_shape=[jax.ShapeDtypeStruct(pack, BF16), jax.ShapeDtypeStruct(pack, BF16)],
        compiler_params=params(48),
        cost_estimate=cost(17),
        name="weight_back",
    )(place, grad_kv, grad_q, key_input, w_kv, w_q, norms, grad_o, ff_vectors)


def latent_back_kernel(grad_kv, grad_q, latent, grad_resid, w_kv, w_q, norms, latent_grad):
    images, lat_len, width = latent.shape
    rows = images * lat_len
    grad = contract(grad_kv[...].reshape(rows, grad_kv.shape[2]), w_kv[...], (1, 1))
    grad += contract(grad_q[...].reshape(rows, grad_q.shape[2]), w_q[...], (1, 1))
    unit, inverse = norm_rows(latent[...].reshape(rows, width).astype(F32))
    back = norm_back(grad, unit, inverse, norms[2:3, :])
    latent_grad[...] = grad_resid[...] + back.reshape(images, lat_len, width)


def latent_back(grad_kv, grad_q, latent, grad_resid, w_kv, w_q, norms):
    images, lat_len, width = latent.shape
    inner = w_q.shape[1]
    tail = grad_kv.shape[1] // lat_len - 1
    block = images // 2
    at = lambda i: (i, 0, 0)
    return pl.pallas_call(
        latent_back_kernel,
        grid=(images // block,),
        in_specs=[
            pl.BlockSpec((block, lat_len, 2 * inner), lambda i: (i, tail, 0)),
            pl.BlockSpec((block, lat_len, inner), at),
            pl.BlockSpec((block, lat_len, width), at),
            pl.BlockSpec((block, lat_len, width), at),
            pl.BlockSpec(w_kv.shape, fixed_at),
            pl.BlockSpec(w_q.shape, fixed_at),
            pl.BlockSpec(norms.shape, fixed_at),
        ],
        out_specs=pl.BlockSpec((block, lat_len, width), at),
        out_shape=jax.ShapeDtypeStruct((images, lat_len, width), F32),
        compiler_params=params(32),
        cost_estimate=cost(4),
        name="latent_back",
    )(grad_kv, grad_q, latent, grad_resid, w_kv, w_q, norms)


def media_back_kernel(media, grad_kv, norms, w_kv, *refs):
    out, grad = refs[-2:]
    grad[...] = contract(grad_kv[0], w_kv[...], (1, 1))
    for at in range(0, media.shape[1], ROWS):
        unit, inverse = norm_rows(media[0, at : at + ROWS, :].astype(F32))
        out[0, at : at + ROWS, :] = norm_back(grad[at : at + ROWS, :], unit, inverse, norms[0:1, :])


def media_back(media, grad_kv, norms, w_kv, first, run, into=()):
    images, media_len, width = media.shape
    inner2 = w_kv.shape[1]
    at = lambda i: (i + first, 0, 0)
    return pl.pallas_call(
        media_back_kernel,
        grid=(run,),
        in_specs=[
            pl.BlockSpec((1, media_len, width), at),
            pl.BlockSpec((1, media_len, inner2), at),
            pl.BlockSpec(norms.shape, fixed_at),
            pl.BlockSpec(w_kv.shape, fixed_at),
            *[pl.BlockSpec(memory_space=pl.ANY) for _ in into],
        ],
        out_specs=pl.BlockSpec((1, media_len, width), at),
        out_shape=jax.ShapeDtypeStruct((images, media_len, width), F32),
        input_output_aliases={4 + i: i for i in range(len(into))},
        scratch_shapes=[pltpu.VMEM((media_len, width), F32)],
        compiler_params=params(32),
        cost_estimate=cost(19),
        name="media_back",
    )(media, grad_kv, norms, w_kv, *into)


def fold_rows(value):
    half = value.shape[0] // 2
    return jnp.concatenate([value[:half], value[half:]], 1)


def shards(
    dp,
    media_tokens,
    patch_counts,
    latents,
    media_gain,
    media_bias,
    latent_gain,
    latent_bias,
    query_weight,
    keyval_weight,
    outproj_weight,
    ff_gain,
    ff_bias,
    ff_in_weight,
    ff_out_weight,
    cotangent,
):
    me, core = lax.axis_index("dp"), lax.axis_index("rep")
    place = jnp.stack([me, core]).astype(jnp.int32)
    columns = dp // PLANE
    images, _, width = media_tokens.shape
    lat_len = latents.shape[1]
    inner = query_weight.shape[1]
    part = width // dp
    slot = ff_in_weight.shape[1] // dp // 2
    kv_rows, o_rows = part // 2, inner // dp // 2
    flat = (images * lat_len, width)

    def swap(value, bits):
        return lax.ppermute(value, "dp", [(i, i ^ bits) for i in range(dp)])

    def other(value):
        return lax.ppermute(value, "rep", [(0, 1), (1, 0)])

    def mine(value, axis):
        return lax.dynamic_index_in_dim(value, core, axis, keepdims=False)

    def down(value):
        return [value] + [swap(value, c * PLANE) for c in range(1, columns)]

    def across(values):
        return [values[0]] + [swap(values[p], p) for p in range(1, PLANE)]

    def total(values):
        got = [values[0]] + [swap(values[c], c * PLANE) for c in range(1, columns)]
        return functools.reduce(jnp.add, [value.astype(F32) for value in got])

    norms = jnp.stack([media_gain, media_bias, latent_gain, latent_bias, ff_gain, ff_bias])
    norms = lax.dynamic_update_slice(jnp.zeros((PAD, width), BF16), norms, (0, me * part))
    attn = [
        mine(keyval_weight.reshape(2, kv_rows, width), 0),
        fold_rows(mine(query_weight.reshape(2, kv_rows, inner), 0)),
        mine(outproj_weight.reshape(2, o_rows, width), 0),
        norms,
    ]
    attn = jnp.stack(down(jnp.concatenate(attn, 0)))
    ffout = mine(ff_out_weight.reshape(2, slot, width), 0)
    ffin = mine(ff_in_weight.reshape(part, dp, 2, slot), 2).reshape(part, dp * slot)
    cut = ffin.shape[1] // 2
    ffin = jnp.concatenate([ffin[:, :cut], ffin[:, cut:]], 0)
    attn, ffout, ffin = tie(attn, ffout, ffin)
    attn = [attn] + [swap(attn, p) for p in range(1, PLANE)]
    w_ffout = lax.all_gather(ffout, "dp", axis=0, tiled=True)
    ffin = jnp.stack([ffin, swap(ffin, 2 * PLANE)])
    got = swap(ffin, PLANE)
    w_kv, w_q, w_o, norms = in_order(place, attn, [other(value) for value in attn], inner)
    lo, hi = [
        jnp.stack([ffin[0, rows], got[0, rows], ffin[1, rows], got[1, rows]])
        for rows in (slice(0, part), slice(part, 2 * part))
    ]
    dout = cotangent.astype(BF16).reshape(flat)
    douts = dout, other(dout)

    w_kv, lo, hi = tie(w_kv, lo, hi)
    lo, hi = {0: lo, 2: swap(lo, 2)}, {0: hi, 1: swap(hi, 1)}
    run = images // 2
    held = attend(patch_counts, media_tokens, latents, norms, w_kv, w_q, 0, run)
    held, lo, hi = tie(held, lo, hi)
    lo[1], lo[3] = swap(lo[0], 1), swap(lo[2], 1)
    hi[2], hi[3] = swap(hi[0], 2), swap(hi[1], 2)
    key_input, keyvals, queries, mixed = attend(
        patch_counts, media_tokens, latents, norms, w_kv, w_q, run, images - run, held
    )
    mixed, lo, hi = tie(mixed.reshape(-1, inner), lo, hi)
    lo, hi = [lo[p] for p in range(PLANE)], [hi[p] for p in range(PLANE)]
    resid, low = add_branch(mixed, latents.reshape(flat), w_o, norms)

    activ, slope, low_t, dout, w_ffin, *grads = feed_forward(
        place, (low, other(low)), douts, lo, hi, slot
    )
    out_sum = grads[0], swap(grads[1], 1), grads[2], swap(grads[3], 2)
    *grads, kept, sent = feed_back(place, dout, low_t, w_ffin, w_ffout, slope, columns, part)
    kept, sent, out_sum = tie(kept, sent, out_sum)
    out_sum = fold_first(*out_sum)
    out_sum = out_sum[0], swap(out_sum[1], 2), out_sum[2], swap(out_sum[3], 1)
    grad_resid, grad_mixed, grad_o, ff_vectors = resid_back(
        kept, other(sent), resid, cotangent.reshape(flat), mixed, w_o, norms
    )
    grad_mixed, out_sum = tie(grad_mixed, out_sum)
    keep, send = fold_second(*out_sum)
    grad_mixed, keep, send = tie(grad_mixed, keep, send)
    out_sum = keep, swap(send, PLANE)
    in_sum = grads[0], swap(grads[1], 1), grads[2], swap(grads[3], 2)
    grad_kv, grad_q = attend_back(
        patch_counts, keyvals, queries, grad_mixed.reshape(images, lat_len, inner)
    )
    grad_kv, grad_q, out_sum, in_sum = tie(grad_kv, grad_q, out_sum, in_sum)
    held, passed = fold_third(*out_sum)
    in_sum = fold_first(*in_sum)
    grad_q, held, passed, in_sum = tie(grad_q, held, passed, in_sum)
    out_sum = held, swap(passed, 2 * PLANE)
    in_sum = in_sum[0], swap(in_sum[1], 2), in_sum[2], swap(in_sum[3], 1)
    keep, send = weight_back(
        place, grad_kv, grad_q, key_input, w_kv, w_q, norms, grad_o, ff_vectors, columns
    )
    keep, send, out_sum, in_sum = tie(keep, send, out_sum, in_sum)
    got = other(send)
    in_keep, in_send = fold_second(*in_sum)
    keep, in_send = tie(keep, in_send)
    in_sum = in_keep, swap(in_send, PLANE)
    attn = add_both(keep, got)
    grad_kv, attn = tie(grad_kv, attn)
    attn = across(attn)
    media_grad = media_back(media_tokens, grad_kv, norms, w_kv, 0, images)
    media_grad, attn, in_sum = tie(media_grad, attn, in_sum)
    attn = fold(attn)
    attn, in_sum = tie(attn, in_sum)
    held, passed = fold_third(*in_sum)
    in_sum = held, swap(passed, 2 * PLANE)
    activ, grad_q, attn, passed = tie(activ, grad_q, attn, passed)
    latent_grad = latent_back(
        grad_kv, grad_q, latents, grad_resid.reshape(latents.shape), w_kv, w_q, norms
    )
    share, sent = feed_out(activ, w_ffout)
    new_latents = resid + (share + other(sent).astype(F32))
    own_in, own_out = [value[0].astype(F32) + value[1].astype(F32) for value in (in_sum, out_sum)]
    grad_ffin, grad_ffout = final_ff(place, own_in, other(own_in), own_out, other(own_out))
    own = total(attn)
    rows = own.shape[0] - PAD
    vectors = lax.dynamic_slice(own[rows:], (0, me * part), (6, part))
    own = own[:rows]
    grad_wkv, grad_wq, grad_wo = final_attn(place, own, other(own), inner, kv_rows, o_rows)
    return (
        new_latents.reshape(latents.shape),
        media_grad,
        latent_grad,
        vectors[0],
        vectors[1],
        vectors[2],
        vectors[3],
        grad_wq,
        grad_wkv,
        grad_wo,
        vectors[4],
        vectors[5],
        grad_ffin,
        grad_ffout,
    )


def norm_apply(values, gain, bias):
    centre = jnp.mean(values, -1, keepdims=True)
    centred = values - centre
    inverse = lax.rsqrt(jnp.mean(centred * centred, -1, keepdims=True) + EPS)
    unit = centred * inverse
    return (unit * gain.astype(jnp.float32) + bias.astype(jnp.float32), unit, inverse)


def plain_norm_grad(grad_normed, unit, inverse, gain):
    scaled = grad_normed * gain.astype(jnp.float32)
    return inverse * (
        scaled
        - jnp.mean(scaled, -1, keepdims=True)
        - unit * jnp.mean(scaled * unit, -1, keepdims=True)
    )


def row_total(values):
    return jnp.sum(values.reshape(-1, values.shape[-1]), axis=0)


def gelu_exact(values):
    return jax.nn.gelu(values, approximate=False)


def masked_scores(query_heads, key_heads, valid, scale):
    raw = (
        jnp.einsum("iqhe,ikhe->ihqk", query_heads, key_heads, preferred_element_type=jnp.float32)
        * scale
    )
    return jnp.where(valid[:, None, None, :], raw, jnp.float32(-1e30))


def plain_shards(
    media_tokens,
    patch_counts,
    latents,
    media_gain,
    media_bias,
    latent_gain,
    latent_bias,
    query_weight,
    keyval_weight,
    outproj_weight,
    ff_gain,
    ff_bias,
    ff_in_weight,
    ff_out_weight,
    cotangent,
):
    f32 = jnp.float32
    bf16 = jnp.bfloat16
    whole = (
        lax.all_gather(media_gain, "dp", axis=0, tiled=True),
        lax.all_gather(media_bias, "dp", axis=0, tiled=True),
        lax.all_gather(latent_gain, "dp", axis=0, tiled=True),
        lax.all_gather(latent_bias, "dp", axis=0, tiled=True),
        lax.all_gather(query_weight, "dp", axis=0, tiled=True),
        lax.all_gather(keyval_weight, "dp", axis=0, tiled=True),
        lax.all_gather(outproj_weight, "dp", axis=0, tiled=True),
        lax.all_gather(ff_gain, "dp", axis=0, tiled=True),
        lax.all_gather(ff_bias, "dp", axis=0, tiled=True),
        lax.all_gather(ff_in_weight, "dp", axis=0, tiled=True),
        lax.all_gather(ff_out_weight, "dp", axis=0, tiled=True),
    )
    (
        gain_media,
        bias_media,
        gain_latent,
        bias_latent,
        w_query,
        w_keyval,
        w_outproj,
        gain_ff,
        bias_ff,
        w_ffin,
        w_ffout,
    ) = whole
    images, media_len, width = media_tokens.shape
    lat_len = latents.shape[1]
    keys_len = media_len + lat_len
    inner_width = w_query.shape[1]
    head_size = inner_width // HEADS
    scale = 1.0 / math.sqrt(head_size)
    media_f = media_tokens.astype(f32)
    latent_f = latents.astype(f32)
    media_normed, media_unit, media_inv = norm_apply(media_f, gain_media, bias_media)
    latent_normed, latent_unit, latent_inv = norm_apply(latent_f, gain_latent, bias_latent)
    media_low = media_normed.astype(bf16)
    latent_low = latent_normed.astype(bf16)
    queries = jnp.einsum("ild,de->ile", latent_low, w_query, preferred_element_type=f32).astype(
        bf16
    )
    key_input = jnp.concatenate([media_low, latent_low], axis=1)
    keyvals = jnp.einsum("ikd,de->ike", key_input, w_keyval, preferred_element_type=f32).astype(
        bf16
    )
    key_heads = keyvals[:, :, :inner_width].reshape(images, keys_len, HEADS, head_size)
    value_heads = keyvals[:, :, inner_width:].reshape(images, keys_len, HEADS, head_size)
    query_heads = queries.reshape(images, lat_len, HEADS, head_size)
    positions = jnp.arange(keys_len, dtype=jnp.int32)
    valid = (positions[None, :] < patch_counts[:, None]) | (positions[None, :] >= media_len)
    scores = masked_scores(query_heads, key_heads, valid, scale)
    top = jnp.max(scores, -1, keepdims=True)
    expd = jnp.exp(scores - top)
    total = jnp.sum(expd, -1, keepdims=True)
    probs = expd / total
    log_total = top + jnp.log(total)
    mixed = jnp.einsum(
        "ihqk,ikhe->iqhe", probs.astype(bf16), value_heads, preferred_element_type=f32
    )
    mixed = mixed.reshape(images, lat_len, inner_width).astype(bf16)
    branch = jnp.einsum("ile,ed->ild", mixed, w_outproj, preferred_element_type=f32)
    resid = latent_f + branch
    ff_normed, ff_unit, ff_inv = norm_apply(resid, gain_ff, bias_ff)
    ff_low = ff_normed.astype(bf16)
    pre_act = jnp.einsum("ild,df->ilf", ff_low, w_ffin, preferred_element_type=f32)
    activ, gelu_pull = jax.vjp(gelu_exact, pre_act)
    activ_low = activ.astype(bf16)
    new_latents = resid + jnp.einsum("ilf,fd->ild", activ_low, w_ffout, preferred_element_type=f32)
    again = (
        lax.all_gather(media_gain, "dp", axis=0, tiled=True),
        lax.all_gather(media_bias, "dp", axis=0, tiled=True),
        lax.all_gather(latent_gain, "dp", axis=0, tiled=True),
        lax.all_gather(latent_bias, "dp", axis=0, tiled=True),
        lax.all_gather(query_weight, "dp", axis=0, tiled=True),
        lax.all_gather(keyval_weight, "dp", axis=0, tiled=True),
        lax.all_gather(outproj_weight, "dp", axis=0, tiled=True),
        lax.all_gather(ff_gain, "dp", axis=0, tiled=True),
        lax.all_gather(ff_bias, "dp", axis=0, tiled=True),
        lax.all_gather(ff_in_weight, "dp", axis=0, tiled=True),
        lax.all_gather(ff_out_weight, "dp", axis=0, tiled=True),
    )
    (
        gain_media_b,
        bias_media_b,
        gain_latent_b,
        bias_latent_b,
        w_query_b,
        w_keyval_b,
        w_outproj_b,
        gain_ff_b,
        bias_ff_b,
        w_ffin_b,
        w_ffout_b,
    ) = again
    grad_out_low = cotangent.astype(bf16)
    grad_ffout = jnp.einsum("ilf,ild->fd", activ_low, grad_out_low, preferred_element_type=f32)
    grad_activ = jnp.einsum("ild,fd->ilf", grad_out_low, w_ffout_b, preferred_element_type=f32)
    (grad_pre,) = gelu_pull(grad_activ)
    grad_pre_low = grad_pre.astype(bf16)
    grad_ffin = jnp.einsum("ild,ilf->df", ff_low, grad_pre_low, preferred_element_type=f32)
    grad_ffnormed = jnp.einsum("ilf,df->ild", grad_pre_low, w_ffin_b, preferred_element_type=f32)
    grad_gain_ff = row_total(grad_ffnormed * ff_unit)
    grad_bias_ff = row_total(grad_ffnormed)
    grad_resid = cotangent + plain_norm_grad(grad_ffnormed, ff_unit, ff_inv, gain_ff_b)
    grad_resid_low = grad_resid.astype(bf16)
    grad_outproj = jnp.einsum("ile,ild->ed", mixed, grad_resid_low, preferred_element_type=f32)
    grad_mixed = jnp.einsum(
        "ild,ed->ile", grad_resid_low, w_outproj_b, preferred_element_type=f32
    ).astype(bf16)
    grad_mixed_heads = grad_mixed.reshape(images, lat_len, HEADS, head_size)
    scores_again = masked_scores(query_heads, key_heads, valid, scale)
    probs_again = jnp.exp(scores_again - log_total)
    grad_probs = jnp.einsum(
        "iqhe,ikhe->ihqk", grad_mixed_heads, value_heads, preferred_element_type=f32
    )
    grad_scores = probs_again * (grad_probs - jnp.sum(probs_again * grad_probs, -1, keepdims=True))
    grad_scores_low = grad_scores.astype(bf16)
    grad_queries = (
        jnp.einsum("ihqk,ikhe->iqhe", grad_scores_low, key_heads, preferred_element_type=f32)
        * scale
    )
    grad_queries = grad_queries.reshape(images, lat_len, inner_width).astype(bf16)
    grad_keys = (
        jnp.einsum("ihqk,iqhe->ikhe", grad_scores_low, query_heads, preferred_element_type=f32)
        * scale
    )
    grad_values = jnp.einsum(
        "ihqk,iqhe->ikhe", probs_again.astype(bf16), grad_mixed_heads, preferred_element_type=f32
    )
    grad_keyvals = jnp.concatenate(
        [
            grad_keys.reshape(images, keys_len, inner_width),
            grad_values.reshape(images, keys_len, inner_width),
        ],
        axis=-1,
    ).astype(bf16)
    grad_qweight = jnp.einsum("ild,ile->de", latent_low, grad_queries, preferred_element_type=f32)
    grad_kvweight = jnp.einsum("ikd,ike->de", key_input, grad_keyvals, preferred_element_type=f32)
    grad_key_input = jnp.einsum("ike,de->ikd", grad_keyvals, w_keyval_b, preferred_element_type=f32)
    grad_latnormed = jnp.einsum("ile,de->ild", grad_queries, w_query_b, preferred_element_type=f32)
    grad_latnormed = grad_latnormed + grad_key_input[:, media_len:]
    grad_medianormed = grad_key_input[:, :media_len]
    media_grad = plain_norm_grad(grad_medianormed, media_unit, media_inv, gain_media_b)
    latent_grad = grad_resid + plain_norm_grad(grad_latnormed, latent_unit, latent_inv, gain_latent_b)
    grad_gain_media = row_total(grad_medianormed * media_unit)
    grad_bias_media = row_total(grad_medianormed)
    grad_gain_latent = row_total(grad_latnormed * latent_unit)
    grad_bias_latent = row_total(grad_latnormed)
    owned = (
        lax.psum_scatter(
            grad_gain_media.astype(jnp.bfloat16), "dp", scatter_dimension=0, tiled=True
        ).astype(jnp.float32),
        lax.psum_scatter(
            grad_bias_media.astype(jnp.bfloat16), "dp", scatter_dimension=0, tiled=True
        ).astype(jnp.float32),
        lax.psum_scatter(
            grad_gain_latent.astype(jnp.bfloat16), "dp", scatter_dimension=0, tiled=True
        ).astype(jnp.float32),
        lax.psum_scatter(
            grad_bias_latent.astype(jnp.bfloat16), "dp", scatter_dimension=0, tiled=True
        ).astype(jnp.float32),
        lax.psum_scatter(
            grad_qweight.astype(jnp.bfloat16), "dp", scatter_dimension=0, tiled=True
        ).astype(jnp.float32),
        lax.psum_scatter(
            grad_kvweight.astype(jnp.bfloat16), "dp", scatter_dimension=0, tiled=True
        ).astype(jnp.float32),
        lax.psum_scatter(
            grad_outproj.astype(jnp.bfloat16), "dp", scatter_dimension=0, tiled=True
        ).astype(jnp.float32),
        lax.psum_scatter(
            grad_gain_ff.astype(jnp.bfloat16), "dp", scatter_dimension=0, tiled=True
        ).astype(jnp.float32),
        lax.psum_scatter(
            grad_bias_ff.astype(jnp.bfloat16), "dp", scatter_dimension=0, tiled=True
        ).astype(jnp.float32),
        lax.psum_scatter(
            grad_ffin.astype(jnp.bfloat16), "dp", scatter_dimension=0, tiled=True
        ).astype(jnp.float32),
        lax.psum_scatter(
            grad_ffout.astype(jnp.bfloat16), "dp", scatter_dimension=0, tiled=True
        ).astype(jnp.float32),
    )
    summed = (
        lax.psum(owned[0].astype(jnp.bfloat16), "rep").astype(jnp.float32),
        lax.psum(owned[1].astype(jnp.bfloat16), "rep").astype(jnp.float32),
        lax.psum(owned[2].astype(jnp.bfloat16), "rep").astype(jnp.float32),
        lax.psum(owned[3].astype(jnp.bfloat16), "rep").astype(jnp.float32),
        lax.psum(owned[4].astype(jnp.bfloat16), "rep").astype(jnp.float32),
        lax.psum(owned[5].astype(jnp.bfloat16), "rep").astype(jnp.float32),
        lax.psum(owned[6].astype(jnp.bfloat16), "rep").astype(jnp.float32),
        lax.psum(owned[7].astype(jnp.bfloat16), "rep").astype(jnp.float32),
        lax.psum(owned[8].astype(jnp.bfloat16), "rep").astype(jnp.float32),
        lax.psum(owned[9].astype(jnp.bfloat16), "rep").astype(jnp.float32),
        lax.psum(owned[10].astype(jnp.bfloat16), "rep").astype(jnp.float32),
    )
    (
        sum_gain_media,
        sum_bias_media,
        sum_gain_latent,
        sum_bias_latent,
        sum_query,
        sum_keyval,
        sum_outproj,
        sum_gain_ff,
        sum_bias_ff,
        sum_ffin,
        sum_ffout,
    ) = summed
    return (
        new_latents,
        media_grad,
        latent_grad,
        sum_gain_media,
        sum_bias_media,
        sum_gain_latent,
        sum_bias_latent,
        sum_query,
        sum_keyval,
        sum_outproj,
        sum_gain_ff,
        sum_bias_ff,
        sum_ffin,
        sum_ffout,
    )


def solution(mesh):
    dp, rep = mesh.shape["dp"], mesh.shape["rep"]

    def program(*arrays):
        if rep != 2 or dp != PLANE * PLANE:
            return plain_shards(*arrays)
        return shards(dp, *arrays)

    return jax.shard_map(
        program,
        mesh=mesh,
        in_specs=(
            P(("dp", "rep"), None, None),
            P(("dp", "rep")),
            P(("dp", "rep"), None, None),
            P("dp"),
            P("dp"),
            P("dp"),
            P("dp"),
            P("dp", None),
            P("dp", None),
            P("dp", None),
            P("dp"),
            P("dp"),
            P("dp", None),
            P("dp", None),
            P(("dp", "rep"), None, None),
        ),
        out_specs=(
            P(("dp", "rep"), None, None),
            P(("dp", "rep"), None, None),
            P(("dp", "rep"), None, None),
            P("dp"),
            P("dp"),
            P("dp"),
            P("dp"),
            P("dp", None),
            P("dp", None),
            P("dp", None),
            P("dp"),
            P("dp"),
            P("dp", None),
            P("dp", None),
        ),
        check_vma=False,
    )
```

```python
import functools
import math

import jax
import jax.numpy as jnp
from jax import lax
from jax.experimental import pallas as pl
from jax.experimental.pallas import tpu as pltpu
from jax.sharding import PartitionSpec as P

HEADS = 8
GROUP = 4
EPS = 1e-05
NEG = -1e30
ROWS = 64
FF_TILE = 512
PLANE = 4
PAD = 8
F32 = jnp.float32
BF16 = jnp.bfloat16


def cost(us):
    return pl.CostEstimate(flops=int(us * 1.1e9), bytes_accessed=1 << 18, transcendentals=0)


def contract(a, b, over):
    return lax.dot_general(a, b, ((over[:1], over[1:]), ((), ())), preferred_element_type=F32)


def norm_rows(values):
    centred = values - jnp.mean(values, -1, keepdims=True)
    inverse = lax.rsqrt(jnp.mean(centred * centred, -1, keepdims=True) + EPS)
    return centred * inverse, inverse


def norm_back(grad, unit, inverse, gain):
    scaled = grad * gain
    return inverse * (
        scaled
        - jnp.mean(scaled, -1, keepdims=True)
        - unit * jnp.mean(scaled * unit, -1, keepdims=True)
    )


def spread(value, size):
    lane = lax.broadcasted_iota(jnp.int32, value.shape, 1) // size
    value = value.astype(F32)
    return jnp.concatenate([jnp.where(lane == h, value, 0.0) for h in range(GROUP)], 0)


def gathered(value, size):
    rows = value.shape[0] // GROUP
    lane = lax.broadcasted_iota(jnp.int32, (rows, value.shape[1]), 1) // size
    out = jnp.zeros((rows, value.shape[1]), F32)
    for h in range(GROUP):
        out = jnp.where(lane == h, value[h * rows : (h + 1) * rows], out)
    return out


def tie(*values):
    return lax.optimization_barrier(values)


def params(mib):
    return pltpu.CompilerParams(vmem_limit_bytes=mib << 20)


def image_at(i, c):
    return (i, 0, 0)


def fixed_at(*_):
    return (0, 0)


def order_kernel(place, *refs):
    sides = refs[:PLANE], refs[PLANE : 2 * PLANE]
    w_kv, w_q, w_o, norms = refs[2 * PLANE :]
    me, core = place[0], place[1]
    columns = sides[0][0].shape[0]
    chips = columns * PLANE
    kv_rows, o_rows = w_kv.shape[0] // chips // 2, w_o.shape[0] // chips // 2
    q_rows, inner = kv_rows // 2, w_q.shape[1]
    total = jnp.zeros(norms.shape, F32)
    for plane in range(PLANE):
        for column in range(columns):
            chip = me ^ (column * PLANE + plane)
            for side in range(2):
                block = sides[side][plane]
                half = core if side == 0 else 1 - core
                at = pl.multiple_of((chip * 2 + half) * kv_rows, kv_rows)
                w_kv[pl.ds(at, kv_rows), :] = block[column, :kv_rows, :]
                rest = block[column, kv_rows : kv_rows + q_rows, :]
                w_q[pl.ds(at, q_rows), :] = rest[:, :inner]
                w_q[pl.ds(pl.multiple_of(at + q_rows, q_rows), q_rows), :] = rest[:, inner:]
                at = pl.multiple_of((chip * 2 + half) * o_rows, o_rows)
                w_o[pl.ds(at, o_rows), :] = block[
                    column, kv_rows + q_rows : kv_rows + q_rows + o_rows, :
                ]
            total += sides[0][plane][column, kv_rows + q_rows + o_rows :, :].astype(F32)
    norms[...] = total


def in_order(place, own, other, inner):
    columns, _, width = own[0].shape
    return pl.pallas_call(
        order_kernel,
        grid_spec=pltpu.PrefetchScalarGridSpec(
            num_scalar_prefetch=1,
            grid=(1,),
            in_specs=[
                pl.BlockSpec(value.shape, lambda t, c: (0, 0, 0)) for value in (*own, *other)
            ],
            out_specs=[
                pl.BlockSpec((width, 2 * inner), fixed_at),
                pl.BlockSpec((width, inner), fixed_at),
                pl.BlockSpec((inner, width), fixed_at),
                pl.BlockSpec((8, width), fixed_at),
            ],
        ),
        out_shape=[
            jax.ShapeDtypeStruct((width, 2 * inner), BF16),
            jax.ShapeDtypeStruct((width, inner), BF16),
            jax.ShapeDtypeStruct((inner, width), BF16),
            jax.ShapeDtypeStruct((8, width), F32),
        ],
        compiler_params=params(24),
        cost_estimate=cost(1),
        name="in_order",
    )(place, *own, *other)


def whole_at(rank):
    return lambda *_: (0,) * rank


def small(kernel, values, outs, us, name):
    return pl.pallas_call(
        kernel,
        grid=(1,),
        in_specs=[pl.BlockSpec(value.shape, whole_at(value.ndim)) for value in values],
        out_specs=[pl.BlockSpec(shape, whole_at(len(shape))) for shape in outs],
        out_shape=[jax.ShapeDtypeStruct(shape, BF16) for shape in outs],
        compiler_params=params(20),
        cost_estimate=cost(us),
        name=name,
    )(*values)


def added(one, two):
    return (one.astype(F32) + two.astype(F32)).astype(BF16)


def fold_kernel(*refs):
    for column in range(len(refs) - PLANE):
        total = refs[0][column].astype(F32)
        for plane in range(1, PLANE):
            total += refs[plane][column].astype(F32)
        refs[PLANE + column][...] = total.astype(BF16)


def fold(values):
    columns = values[0].shape[0]
    return small(fold_kernel, values, [values[0].shape[1:]] * columns, 2, "fold")


def first_kernel(keep0, got0, keep1, got1, held0, pass0, held1, pass1):
    held0[...] = added(keep0[0], got0[0])
    pass0[...] = added(keep0[1], got0[1])
    held1[...] = added(keep1[0], got1[0])
    pass1[...] = added(keep1[1], got1[1])


def fold_first(keep0, got0, keep1, got1):
    values = keep0, got0, keep1, got1
    return small(first_kernel, values, [keep0.shape[1:]] * 4, 2, "fold_first")


def second_kernel(held0, got0, held1, got1, keep, send):
    half = held0.shape[1]
    for i in range(2):
        for out, column in ((keep, 2 * i), (send, 2 * i + 1)):
            out[i, :half, :] = added(held0[column], got0[column])
            out[i, half:, :] = added(held1[column], got1[column])


def fold_second(held0, got0, held1, got1):
    values = held0, got0, held1, got1
    shape = (2, 2 * held0.shape[1], held0.shape[2])
    return small(second_kernel, values, [shape] * 2, 2, "fold_second")


def third_kernel(keep, got, held, passed):
    held[...] = added(keep[0], got[0])
    passed[...] = added(keep[1], got[1])


def fold_third(keep, got):
    return small(third_kernel, (keep, got), [keep.shape[1:]] * 2, 0.5, "fold_third")


def both_kernel(keep, got, *outs):
    for plane, out in enumerate(outs):
        out[...] = (keep[plane].astype(F32) + got[plane].astype(F32)).astype(BF16)


def add_both(keep, got):
    tail = keep.shape[1:]
    whole = lambda t: (0, 0, 0, 0)
    return pl.pallas_call(
        both_kernel,
        grid=(1,),
        in_specs=[pl.BlockSpec(keep.shape, whole), pl.BlockSpec(keep.shape, whole)],
        out_specs=[pl.BlockSpec(tail, lambda t: (0, 0, 0)) for _ in range(PLANE)],
        out_shape=[jax.ShapeDtypeStruct(tail, BF16) for _ in range(PLANE)],
        compiler_params=params(16),
        cost_estimate=cost(2),
        name="add_both",
    )(keep, got)


def final_ff_kernel(place, own_in, other_in, own_out, other_out, grad_in, grad_out):
    first = place[1] == 0
    slot = own_out.shape[0]
    for chip in range(own_in.shape[1] // slot):
        here = slice(chip * slot, (chip + 1) * slot)
        one, two = own_in[:, here], other_in[:, here]
        at = 2 * chip * slot
        grad_in[:, at : at + slot] = jnp.where(first, one, two)
        grad_in[:, at + slot : at + 2 * slot] = jnp.where(first, two, one)
    grad_out[:slot, :] = jnp.where(first, own_out[...], other_out[...])
    grad_out[slot:, :] = jnp.where(first, other_out[...], own_out[...])


def final_ff(place, own_in, other_in, own_out, other_out):
    values = own_in, other_in, own_out, other_out
    shapes = (own_in.shape[0], 2 * own_in.shape[1]), (2 * own_out.shape[0], own_out.shape[1])
    return pl.pallas_call(
        final_ff_kernel,
        grid_spec=pltpu.PrefetchScalarGridSpec(
            num_scalar_prefetch=1,
            grid=(1,),
            in_specs=[pl.BlockSpec(value.shape, fixed_at) for value in values],
            out_specs=[pl.BlockSpec(shape, fixed_at) for shape in shapes],
        ),
        out_shape=[jax.ShapeDtypeStruct(shape, F32) for shape in shapes],
        compiler_params=params(16),
        cost_estimate=cost(2),
        name="final_ff",
    )(place, *values)


def final_attn_kernel(place, own, other, grad_kv, grad_q, grad_o):
    kv_rows, o_rows = grad_kv.shape[0] // 2, grad_o.shape[0] // 2
    q_rows, inner = kv_rows // 2, grad_q.shape[1]
    first = place[1] == 0
    for half in range(2):
        value = jnp.where(first == (half == 0), own[...], other[...])
        at = half * kv_rows
        grad_kv[at : at + kv_rows, :] = value[:kv_rows]
        rest = value[kv_rows : kv_rows + q_rows]
        grad_q[at : at + q_rows, :] = rest[:, :inner]
        grad_q[at + q_rows : at + kv_rows, :] = rest[:, inner:]
        grad_o[half * o_rows : (half + 1) * o_rows, :] = value[
            kv_rows + q_rows : kv_rows + q_rows + o_rows
        ]


def final_attn(place, own, other, inner, kv_rows, o_rows):
    width = own.shape[1]
    shapes = (2 * kv_rows, width), (2 * kv_rows, inner), (2 * o_rows, width)
    return pl.pallas_call(
        final_attn_kernel,
        grid_spec=pltpu.PrefetchScalarGridSpec(
            num_scalar_prefetch=1,
            grid=(1,),
            in_specs=[pl.BlockSpec(own.shape, fixed_at), pl.BlockSpec(own.shape, fixed_at)],
            out_specs=[pl.BlockSpec(shape, fixed_at) for shape in shapes],
        ),
        out_shape=[jax.ShapeDtypeStruct(shape, F32) for shape in shapes],
        compiler_params=params(16),
        cost_estimate=cost(2),
        name="final_attn",
    )(place, own, other)


def attend_kernel(counts, media, latent, norms, w_kv, w_q, *refs):
    turned, lat_low, keyvals, queries, mixed, key_input = refs[-6:]
    media_len, lat_len = media.shape[1], latent.shape[1]
    keys_len = media_len + lat_len
    inner = w_q.shape[1]
    size = inner // HEADS
    wide = size * GROUP
    for at in range(0, media_len, ROWS):
        unit, _ = norm_rows(media[0, at : at + ROWS, :].astype(F32))
        key_input[at : at + ROWS, :] = (unit * norms[0:1, :] + norms[1:2, :]).astype(BF16)
    unit, _ = norm_rows(latent[0].astype(F32))
    low = (unit * norms[2:3, :] + norms[3:4, :]).astype(BF16)
    key_input[media_len:, :] = low
    lat_low[0] = low
    query = contract(low, w_q[...], (1, 0)).astype(BF16)
    queries[0] = query
    keyvals[0] = contract(key_input[...], w_kv[...], (1, 0)).astype(BF16)
    for side in range(2):

        @pl.when(pl.program_id(0) % 2 == side)
        def _(side=side):
            turned[0, :, side * keys_len : (side + 1) * keys_len] = key_input[...].T

    key_at = lax.broadcasted_iota(jnp.int32, (1, keys_len), 1)
    valid = (key_at < counts[pl.program_id(0)]) | (key_at >= media_len)
    for at in range(0, inner, wide):
        own = spread(query[:, at : at + wide].astype(F32) * (1.0 / math.sqrt(size)), size)
        scores = contract(own.astype(BF16), keyvals[0, :, at : at + wide], (1, 1))
        scores = jnp.where(valid, scores, NEG)
        expd = jnp.exp(scores - jnp.max(scores, -1, keepdims=True))
        probs = (expd * (1.0 / jnp.sum(expd, -1, keepdims=True))).astype(BF16)
        out = contract(probs, keyvals[0, :, inner + at : inner + at + wide], (1, 0))
        mixed[0, :, at : at + wide] = gathered(out, size).astype(BF16)


def attend(counts, media, latent, norms, w_kv, w_q, first, run, into=()):
    images, media_len, width = media.shape
    lat_len, inner = latent.shape[1], w_q.shape[1]
    keys_len = media_len + lat_len
    at = lambda i, c: (i + first, 0, 0)
    shapes = [
        (images, lat_len, width),
        (images, keys_len, 2 * inner),
        (images, lat_len, inner),
        (images, lat_len, inner),
    ]
    return pl.pallas_call(
        attend_kernel,
        grid_spec=pltpu.PrefetchScalarGridSpec(
            num_scalar_prefetch=1,
            grid=(run,),
            in_specs=[
                pl.BlockSpec((1, media_len, width), at),
                pl.BlockSpec((1, lat_len, width), at),
                pl.BlockSpec(norms.shape, fixed_at),
                pl.BlockSpec(w_kv.shape, fixed_at),
                pl.BlockSpec(w_q.shape, fixed_at),
                *[pl.BlockSpec(memory_space=pl.ANY) for _ in into],
            ],
            out_specs=[
                pl.BlockSpec((1, width, 2 * keys_len), lambda i, c: ((i + first) // 2, 0, 0)),
                *[pl.BlockSpec((1,) + shape[1:], at) for shape in shapes],
            ],
            scratch_shapes=[pltpu.VMEM((keys_len, width), BF16)],
        ),
        out_shape=[
            jax.ShapeDtypeStruct((images // 2, width, 2 * keys_len), BF16),
            *[jax.ShapeDtypeStruct(shape, BF16) for shape in shapes],
        ],
        input_output_aliases={6 + i: i for i in range(len(into))},
        compiler_params=params(32),
        cost_estimate=cost(14),
        name="attend",
    )(counts[first : first + run], media, latent, norms, w_kv, w_q, *into)


def resid_kernel(mixed, latent, w_o, norms, resid, low):
    value = latent[...].astype(F32) + contract(mixed[...], w_o[...], (1, 0))
    resid[...] = value
    unit, _ = norm_rows(value)
    low[...] = (unit * norms[4:5, :] + norms[5:6, :]).astype(BF16)


def add_branch(mixed, latent, w_o, norms):
    rows, width = latent.shape
    inner = mixed.shape[1]
    block = rows // 4
    row_at = lambda i: (i, 0)
    return pl.pallas_call(
        resid_kernel,
        grid=(rows // block,),
        in_specs=[
            pl.BlockSpec((block, inner), row_at),
            pl.BlockSpec((block, width), row_at),
            pl.BlockSpec(w_o.shape, fixed_at),
            pl.BlockSpec(norms.shape, fixed_at),
        ],
        out_specs=[pl.BlockSpec((block, width), row_at), pl.BlockSpec((block, width), row_at)],
        out_shape=[
            jax.ShapeDtypeStruct((rows, width), F32),
            jax.ShapeDtypeStruct((rows, width), BF16),
        ],
        compiler_params=params(16),
        cost_estimate=cost(3),
        name="add_branch",
    )(mixed, latent, w_o, norms)


def ff_kernel(place, *refs):
    low0, low1, dout0, dout1 = refs[:4]
    lo, hi = refs[4:8], refs[8:12]
    activ, slope, low_t, dout, w_in = refs[12:17]
    keep0, send0, keep1, send1 = refs[17:21]
    low, grad = refs[21:]
    step, steps = pl.program_id(0), pl.num_programs(0)
    me = place[0]
    half = low0.shape[0]
    part = lo[0].shape[1]
    slot = grad.shape[0] // PLANE
    cut = slot // 2

    @pl.when(step == 0)
    def _():
        low[:half, :] = low0[...]
        low[half:, :] = low1[...]
        dout[:half, :] = dout0[...]
        dout[half:, :] = dout1[...]
        low_t[...] = low[...].T

    def put(pieces):
        for plane in range(PLANE):
            for column in range(pieces[0].shape[0]):
                at = pl.multiple_of((me ^ (column * PLANE + plane)) * part, part)
                w_in[pl.ds(at, part), :] = pieces[plane][column]

    pl.when(step < steps // 2)(lambda: put(lo))
    pl.when(step >= steps // 2)(lambda: put(hi))
    pre = contract(low[...], w_in[...], (1, 0))
    cdf = 0.5 * (1.0 + lax.erf(pre * math.sqrt(0.5)))
    slope[...] = cdf + pre * (jnp.exp(pre * pre * -0.5) * (1.0 / math.sqrt(2.0 * math.pi)))
    value = (pre * cdf).astype(BF16)
    activ[...] = value
    grad[...] = contract(value, dout[...], (0, 0)).astype(BF16)

    def block(plane, at):
        at = pl.multiple_of((plane ^ (me % PLANE)) * slot + at, cut)
        return grad[pl.ds(at, cut), :]

    for i in range(2):
        keep0[i, 0] = block(2 * i, 0)
        send0[i, 0] = block(2 * i + 1, 0)
        keep1[i, 0] = block(i, cut)
        send1[i, 0] = block(2 + i, cut)


def feed_forward(place, lows, douts, lo, hi, slot):
    half, width = lows[0].shape
    rows = 2 * half
    columns, part, cut = lo[0].shape
    tile = PLANE * slot
    steps = 2 * cut // tile
    in_at = lambda t, c: (0, t)
    lo_at = lambda t, c: (0, 0, jnp.minimum(t, steps // 2 - 1))
    hi_at = lambda t, c: (0, 0, jnp.maximum(t - steps // 2, 0))
    once = pl.Buffered(1)
    return pl.pallas_call(
        ff_kernel,
        grid_spec=pltpu.PrefetchScalarGridSpec(
            num_scalar_prefetch=1,
            grid=(steps,),
            in_specs=[
                *[pl.BlockSpec((half, width), fixed_at, pipeline_mode=once) for _ in range(4)],
                *[pl.BlockSpec((columns, part, tile), lo_at) for _ in lo],
                *[pl.BlockSpec((columns, part, tile), hi_at) for _ in hi],
            ],
            out_specs=[
                pl.BlockSpec((rows, tile), in_at),
                pl.BlockSpec((rows, tile), in_at),
                pl.BlockSpec((width, rows), fixed_at),
                pl.BlockSpec((rows, width), fixed_at),
                pl.BlockSpec((width, tile), in_at),
                *[
                    pl.BlockSpec(
                        (2, 1, slot // 2, width), lambda t, c: (0, t ^ (c[0] // PLANE), 0, 0)
                    )
                    for _ in range(4)
                ],
            ],
            scratch_shapes=[pltpu.VMEM((rows, width), BF16), pltpu.VMEM((tile, width), BF16)],
        ),
        out_shape=[
            jax.ShapeDtypeStruct((rows, 2 * cut), BF16),
            jax.ShapeDtypeStruct((rows, 2 * cut), F32),
            jax.ShapeDtypeStruct((width, rows), BF16),
            jax.ShapeDtypeStruct((rows, width), BF16),
            jax.ShapeDtypeStruct((width, 2 * cut), BF16),
            *[jax.ShapeDtypeStruct((2, columns, slot // 2, width), BF16) for _ in range(4)],
        ],
        compiler_params=params(44),
        cost_estimate=cost(18),
        name="feed_forward",
    )(place, *lows, *douts, *lo, *hi)


def ff_back_kernel(
    place, dout, low_t, w_in, w_out, slope, keep0, send0, keep1, send1, kept, sent, total, grad_in
):
    step, steps = pl.program_id(0), pl.num_programs(0)
    columns, cut = keep0.shape[1:3]

    @pl.when(step == 0)
    def _():
        total[...] = jnp.zeros_like(total)

    grad = (contract(dout[...], w_out[...], (1, 1)) * slope[...]).astype(BF16)
    grad_in[...] = contract(low_t[...], grad, (1, 0)).astype(BF16)

    def block(plane, column, at):
        at = pl.multiple_of((place[0] ^ (column * PLANE + plane)) * 2 * cut + at, cut)
        return grad_in[pl.ds(at, cut), :]

    for column in range(columns):
        for i in range(2):
            keep0[i, column] = block(2 * i, column, 0)
            send0[i, column] = block(2 * i + 1, column, 0)
            keep1[i, column] = block(i, column, cut)
            send1[i, column] = block(2 + i, column, cut)
    total[...] += contract(grad, w_in[...], (1, 1))

    @pl.when(step == steps - 1)
    def _():
        half = kept.shape[0]
        kept[...] = total[:half, :]
        sent[...] = total[half:, :].astype(BF16)


def feed_back(place, dout, low_t, w_in, w_out, slope, columns, part):
    rows, width = dout.shape
    hidden = w_in.shape[1]
    tile = min(FF_TILE, hidden)
    half = rows // 2
    in_at, out_at = (lambda t, c: (0, t)), (lambda t, c: (t, 0))
    once = pl.Buffered(1)
    return pl.pallas_call(
        ff_back_kernel,
        grid_spec=pltpu.PrefetchScalarGridSpec(
            num_scalar_prefetch=1,
            grid=(hidden // tile,),
            in_specs=[
                pl.BlockSpec((rows, width), fixed_at, pipeline_mode=once),
                pl.BlockSpec((width, rows), fixed_at, pipeline_mode=once),
                pl.BlockSpec((width, tile), in_at),
                pl.BlockSpec((tile, width), out_at),
                pl.BlockSpec((rows, tile), in_at),
            ],
            out_specs=[
                *[
                    pl.BlockSpec((2, columns, part // 2, tile), lambda t, c: (0, 0, 0, t))
                    for _ in range(4)
                ],
                pl.BlockSpec((half, width), fixed_at, pipeline_mode=once),
                pl.BlockSpec((half, width), fixed_at, pipeline_mode=once),
            ],
            scratch_shapes=[pltpu.VMEM((rows, width), F32), pltpu.VMEM((width, tile), BF16)],
        ),
        out_shape=[
            *[jax.ShapeDtypeStruct((2, columns, part // 2, hidden), BF16) for _ in range(4)],
            jax.ShapeDtypeStruct((half, width), F32),
            jax.ShapeDtypeStruct((half, width), BF16),
        ],
        compiler_params=params(48),
        cost_estimate=cost(21),
        name="feed_back",
    )(place, dout, low_t, w_in, w_out, slope)


def ff_out_kernel(activ, w_out, kept, sent, total):
    step = pl.program_id(0)

    @pl.when(step == 0)
    def _():
        total[...] = jnp.zeros_like(total)

    total[...] += contract(activ[...], w_out[...], (1, 0))

    @pl.when(step == pl.num_programs(0) - 1)
    def _():
        half = kept.shape[0]
        kept[...] = total[:half, :]
        sent[...] = total[half:, :].astype(BF16)


def feed_out(activ, w_out):
    rows, hidden = activ.shape
    width = w_out.shape[1]
    tile = min(FF_TILE, hidden)
    half = rows // 2
    once = pl.Buffered(1)
    return pl.pallas_call(
        ff_out_kernel,
        grid=(hidden // tile,),
        in_specs=[
            pl.BlockSpec((rows, tile), lambda t: (0, t)),
            pl.BlockSpec((tile, width), lambda t: (t, 0)),
        ],
        out_specs=[pl.BlockSpec((half, width), fixed_at, pipeline_mode=once)] * 2,
        out_shape=[
            jax.ShapeDtypeStruct((half, width), F32),
            jax.ShapeDtypeStruct((half, width), BF16),
        ],
        scratch_shapes=[pltpu.VMEM((rows, width), F32)],
        compiler_params=params(24),
        cost_estimate=cost(7),
        name="feed_out",
    )(activ, w_out)


def resid_back_kernel(
    kept,
    got,
    resid,
    cotangent,
    mixed,
    w_o,
    norms,
    grad_resid,
    grad_mixed,
    grad_o,
    vectors,
    total,
):
    step = pl.program_id(0)

    @pl.when(step == 0)
    def _():
        vectors[...] = jnp.zeros_like(vectors)
        total[...] = jnp.zeros_like(total)

    grad = kept[...] + got[...].astype(F32)
    unit, inverse = norm_rows(resid[...])
    vectors[0:1, :] += jnp.sum(grad * unit, 0, keepdims=True)
    vectors[1:2, :] += jnp.sum(grad, 0, keepdims=True)
    value = cotangent[...] + norm_back(grad, unit, inverse, norms[4:5, :])
    grad_resid[...] = value
    low = value.astype(BF16)
    grad_mixed[...] = contract(low, w_o[...], (1, 1)).astype(BF16)
    total[...] += contract(mixed[...], low, (0, 0))
    grad_o[...] = total[...].astype(BF16)


def resid_back(kept, got, resid, cotangent, mixed, w_o, norms):
    rows, width = resid.shape
    inner = mixed.shape[1]
    block = rows // 4
    row_at = lambda i: (i, 0)
    wide = pl.BlockSpec((block, width), row_at)
    return pl.pallas_call(
        resid_back_kernel,
        grid=(rows // block,),
        in_specs=[
            *[wide] * 4,
            pl.BlockSpec((block, inner), row_at),
            pl.BlockSpec(w_o.shape, fixed_at),
            pl.BlockSpec(norms.shape, fixed_at),
        ],
        out_specs=[
            wide,
            pl.BlockSpec((block, inner), row_at),
            pl.BlockSpec(w_o.shape, fixed_at),
            pl.BlockSpec((8, width), fixed_at),
        ],
        out_shape=[
            jax.ShapeDtypeStruct((rows, width), F32),
            jax.ShapeDtypeStruct((rows, inner), BF16),
            jax.ShapeDtypeStruct(w_o.shape, BF16),
            jax.ShapeDtypeStruct((8, width), F32),
        ],
        scratch_shapes=[pltpu.VMEM(w_o.shape, F32)],
        compiler_params=params(24),
        cost_estimate=cost(6),
        name="resid_back",
    )(kept, got, resid, cotangent, mixed, w_o, norms)


def as_row(column):
    out = []
    size = 128
    same = lax.broadcasted_iota(jnp.int32, (size, size), 0) == lax.broadcasted_iota(
        jnp.int32, (size, size), 1
    )
    for at in range(0, column.shape[0], size):
        out.append(jnp.sum(jnp.where(same, column[at : at + size, :], 0.0), 0, keepdims=True))
    return jnp.concatenate(out, 1)


def in_bf16(row):
    parts = []
    for _ in range(3):
        parts.append(row.astype(BF16))
        row = row - parts[-1].astype(F32)
    return parts


def attend_back_kernel(counts, keyvals, queries, grad_mixed, grad_kv, grad_q):
    step = pl.program_id(0)
    keys_len = keyvals.shape[1]
    lat_len, inner = queries.shape[1:]
    media_len = keys_len - lat_len
    size = inner // HEADS
    wide = size * GROUP
    scale = 1.0 / math.sqrt(size)
    key_at = lax.broadcasted_iota(jnp.int32, (keys_len, 1), 0)
    valid = (key_at < counts[step]) | (key_at >= media_len)
    for at in range(0, inner, wide):
        keys = keyvals[0, :, at : at + wide]
        values = keyvals[0, :, inner + at : inner + at + wide]
        own = spread(queries[0, :, at : at + wide].astype(F32) * scale, size).astype(BF16)
        grad = spread(grad_mixed[0, :, at : at + wide], size).astype(BF16)
        scores = jnp.where(valid, contract(keys, own, (1, 1)), NEG)
        expd = jnp.exp(scores - jnp.max(scores, 0, keepdims=True))
        probs = expd * (1.0 / jnp.sum(expd, 0, keepdims=True))
        grad_v = contract(probs.astype(BF16), grad, (1, 0)).astype(BF16)
        grad_kv[0, :, inner + at : inner + at + wide] = grad_v
        grad_probs = contract(values, grad, (1, 1))
        held = jnp.sum(probs * grad_probs, 0, keepdims=True)
        low = (probs * (grad_probs - held)).astype(BF16)
        grad_kv[0, :, at : at + wide] = contract(low, own, (1, 0)).astype(BF16)
        back = contract(low, keys, (0, 0))
        grad_q[0, :, at : at + wide] = (gathered(back, size) * scale).astype(BF16)


def weight_back_kernel(
    place,
    grad_kv,
    grad_q,
    turned,
    lat_low,
    w_kv,
    w_q,
    norms,
    grad_o,
    ff_vectors,
    keep,
    send,
    total,
    sums,
    lat_kv,
    lat_q,
    total_q,
):
    step, steps = pl.program_id(0), pl.num_programs(0)
    lat_len, inner = grad_q.shape[1:]
    keys_len = grad_kv.shape[1]
    media_len = keys_len - lat_len

    @pl.when(step == 0)
    def _():
        total[...] = jnp.zeros_like(total)
        sums[...] = jnp.zeros_like(sums)

    both = grad_kv[...].reshape(2 * keys_len, 2 * inner)
    total[...] += contract(turned[0], both, (1, 0))
    sums[...] += jnp.sum(both.astype(F32), 0, keepdims=True)
    for side in range(2):
        here = pl.ds(pl.multiple_of((2 * step + side) * lat_len, lat_len), lat_len)
        lat_kv[here, :] = grad_kv[side, media_len:, :]
        lat_q[here, :] = grad_q[side]

    @pl.when(step == steps - 1)
    def _():
        lat_w = contract(lat_low[...], lat_kv[...], (0, 0))
        lat_wq = contract(lat_low[...], lat_q[...], (0, 0))
        weight, weight_q = w_kv[...].astype(F32), w_q[...].astype(F32)
        lat_sum = jnp.sum(lat_kv[...].astype(F32), 0, keepdims=True)
        lat_sum_q = jnp.sum(lat_q[...].astype(F32), 0, keepdims=True)
        rows = in_bf16(sums[0:1, :] - lat_sum) + in_bf16(lat_sum) + [jnp.zeros((2, 2 * inner), BF16)]
        rows_q = in_bf16(lat_sum_q) + [jnp.zeros((5, inner), BF16)]
        biases = contract(jnp.concatenate(rows, 0), w_kv[...], (1, 1))
        biases_q = contract(jnp.concatenate(rows_q, 0), w_q[...], (1, 1))
        media_bias = jnp.sum(biases[0:3], 0, keepdims=True)
        lat_bias = jnp.sum(biases[3:6], 0, keepdims=True) + jnp.sum(biases_q, 0, keepdims=True)
        media_both = as_row(jnp.sum((total[...] - lat_w) * weight, 1, keepdims=True))
        lat_both = as_row(
            jnp.sum(lat_w * weight, 1, keepdims=True)
            + jnp.sum(lat_wq * weight_q, 1, keepdims=True)
        )
        vectors = [
            (media_both - norms[1:2, :] * media_bias) / norms[0:1, :],
            media_bias,
            (lat_both - norms[3:4, :] * lat_bias) / norms[2:3, :],
            lat_bias,
            ff_vectors[0:2, :],
            jnp.zeros((2, ff_vectors.shape[1]), F32),
        ]
        vectors = jnp.concatenate(vectors, 0).astype(BF16)
        total_q[...] = lat_wq
        me, core = place[0], place[1]
        columns = keep.shape[1]
        kv_rows = total.shape[0] // (2 * columns * PLANE)
        o_rows = grad_o.shape[0] // (2 * columns * PLANE)
        q_rows = kv_rows // 2
        for plane in range(PLANE):
            for column in range(columns):
                chip = me ^ (column * PLANE + plane)
                for out, half in ((keep, core), (send, 1 - core)):
                    at = pl.multiple_of((chip * 2 + half) * kv_rows, kv_rows)
                    out[plane, column, :kv_rows, :] = total[pl.ds(at, kv_rows), :].astype(BF16)
                    value = total_q[pl.ds(at, kv_rows), :].astype(BF16)
                    row = kv_rows
                    out[plane, column, row : row + q_rows, :inner] = value[:q_rows]
                    out[plane, column, row : row + q_rows, inner:] = value[q_rows:]
                    row += q_rows
                    at = pl.multiple_of((chip * 2 + half) * o_rows, o_rows)
                    out[plane, column, row : row + o_rows, :] = grad_o[pl.ds(at, o_rows), :]
                    out[plane, column, row + o_rows :, :] = vectors


def attend_back(counts, keyvals, queries, grad_mixed):
    images, keys_len, wide = keyvals.shape
    lat_len, inner = queries.shape[1:]
    at = lambda i, c: (i, 0, 0)
    return pl.pallas_call(
        attend_back_kernel,
        grid_spec=pltpu.PrefetchScalarGridSpec(
            num_scalar_prefetch=1,
            grid=(images,),
            in_specs=[
                pl.BlockSpec((1, keys_len, wide), at),
                pl.BlockSpec((1, lat_len, inner), at),
                pl.BlockSpec((1, lat_len, inner), at),
            ],
            out_specs=[
                pl.BlockSpec((1, keys_len, wide), at),
                pl.BlockSpec((1, lat_len, inner), at),
            ],
        ),
        out_shape=[
            jax.ShapeDtypeStruct((images, keys_len, wide), BF16),
            jax.ShapeDtypeStruct((images, lat_len, inner), BF16),
        ],
        compiler_params=params(58),
        cost_estimate=cost(27),
        name="attend_back",
    )(counts, keyvals, queries, grad_mixed)


def weight_back(
    place, grad_kv, grad_q, turned, lat_low, w_kv, w_q, norms, grad_o, ff_vectors, columns
):
    images, keys_len, _ = grad_kv.shape
    width = turned.shape[1]
    lat_len, inner = grad_q.shape[1:]
    rows = images * lat_len
    chips = columns * PLANE
    kv_rows, o_rows = width // chips // 2, inner // chips // 2
    pack = (PLANE, columns, kv_rows + kv_rows // 2 + o_rows + PAD, width)
    at = lambda i, c: (i, 0, 0)
    once = pl.Buffered(1)
    return pl.pallas_call(
        weight_back_kernel,
        grid_spec=pltpu.PrefetchScalarGridSpec(
            num_scalar_prefetch=1,
            grid=(images // 2,),
            in_specs=[
                pl.BlockSpec((2, keys_len, 2 * inner), at),
                pl.BlockSpec((2, lat_len, inner), at),
                pl.BlockSpec((1, width, 2 * keys_len), at),
                pl.BlockSpec(lat_low.shape, fixed_at, pipeline_mode=once),
                pl.BlockSpec(w_kv.shape, fixed_at, pipeline_mode=once),
                pl.BlockSpec(w_q.shape, fixed_at, pipeline_mode=once),
                pl.BlockSpec(norms.shape, fixed_at),
                pl.BlockSpec(grad_o.shape, fixed_at, pipeline_mode=once),
                pl.BlockSpec(ff_vectors.shape, fixed_at),
            ],
            out_specs=[
                pl.BlockSpec(pack, whole_at(4), pipeline_mode=once),
                pl.BlockSpec(pack, whole_at(4), pipeline_mode=once),
            ],
            scratch_shapes=[
                pltpu.VMEM(w_kv.shape, F32),
                pltpu.VMEM((8, 2 * inner), F32),
                pltpu.VMEM((rows, 2 * inner), BF16),
                pltpu.VMEM((rows, inner), BF16),
                pltpu.VMEM(w_q.shape, F32),
            ],
        ),
        out_shape=[jax.ShapeDtypeStruct(pack, BF16), jax.ShapeDtypeStruct(pack, BF16)],
        compiler_params=params(58),
        cost_estimate=cost(17),
        name="weight_back",
    )(place, grad_kv, grad_q, turned, lat_low, w_kv, w_q, norms, grad_o, ff_vectors)


def latent_back_kernel(grad_kv, grad_q, latent, grad_resid, w_kv, w_q, norms, latent_grad):
    images, lat_len, width = latent.shape
    rows = images * lat_len
    grad = contract(grad_kv[...].reshape(rows, grad_kv.shape[2]), w_kv[...], (1, 1))
    grad += contract(grad_q[...].reshape(rows, grad_q.shape[2]), w_q[...], (1, 1))
    unit, inverse = norm_rows(latent[...].reshape(rows, width).astype(F32))
    back = norm_back(grad, unit, inverse, norms[2:3, :])
    latent_grad[...] = grad_resid[...] + back.reshape(images, lat_len, width)


def latent_back(grad_kv, grad_q, latent, grad_resid, w_kv, w_q, norms):
    images, lat_len, width = latent.shape
    inner = w_q.shape[1]
    tail = grad_kv.shape[1] // lat_len - 1
    block = images // 2
    at = lambda i: (i, 0, 0)
    return pl.pallas_call(
        latent_back_kernel,
        grid=(images // block,),
        in_specs=[
            pl.BlockSpec((block, lat_len, 2 * inner), lambda i: (i, tail, 0)),
            pl.BlockSpec((block, lat_len, inner), at),
            pl.BlockSpec((block, lat_len, width), at),
            pl.BlockSpec((block, lat_len, width), at),
            pl.BlockSpec(w_kv.shape, fixed_at),
            pl.BlockSpec(w_q.shape, fixed_at),
            pl.BlockSpec(norms.shape, fixed_at),
        ],
        out_specs=pl.BlockSpec((block, lat_len, width), at),
        out_shape=jax.ShapeDtypeStruct((images, lat_len, width), F32),
        compiler_params=params(32),
        cost_estimate=cost(4),
        name="latent_back",
    )(grad_kv, grad_q, latent, grad_resid, w_kv, w_q, norms)


def media_back_kernel(media, grad_kv, norms, w_kv, *refs):
    out, grad = refs[-2:]
    grad[...] = contract(grad_kv[0], w_kv[...], (1, 1))
    for at in range(0, media.shape[1], ROWS):
        unit, inverse = norm_rows(media[0, at : at + ROWS, :].astype(F32))
        out[0, at : at + ROWS, :] = norm_back(grad[at : at + ROWS, :], unit, inverse, norms[0:1, :])


def media_back(media, grad_kv, norms, w_kv, first, run, into=()):
    images, media_len, width = media.shape
    inner2 = w_kv.shape[1]
    at = lambda i: (i + first, 0, 0)
    return pl.pallas_call(
        media_back_kernel,
        grid=(run,),
        in_specs=[
            pl.BlockSpec((1, media_len, width), at),
            pl.BlockSpec((1, media_len, inner2), at),
            pl.BlockSpec(norms.shape, fixed_at),
            pl.BlockSpec(w_kv.shape, fixed_at),
            *[pl.BlockSpec(memory_space=pl.ANY) for _ in into],
        ],
        out_specs=pl.BlockSpec((1, media_len, width), at),
        out_shape=jax.ShapeDtypeStruct((images, media_len, width), F32),
        input_output_aliases={4 + i: i for i in range(len(into))},
        scratch_shapes=[pltpu.VMEM((media_len, width), F32)],
        compiler_params=params(32),
        cost_estimate=cost(0.5),
        name="media_back",
    )(media, grad_kv, norms, w_kv, *into)


def fold_rows(value):
    half = value.shape[0] // 2
    return jnp.concatenate([value[:half], value[half:]], 1)


def shards(
    dp,
    media_tokens,
    patch_counts,
    latents,
    media_gain,
    media_bias,
    latent_gain,
    latent_bias,
    query_weight,
    keyval_weight,
    outproj_weight,
    ff_gain,
    ff_bias,
    ff_in_weight,
    ff_out_weight,
    cotangent,
):
    me, core = lax.axis_index("dp"), lax.axis_index("rep")
    place = jnp.stack([me, core]).astype(jnp.int32)
    columns = dp // PLANE
    images, _, width = media_tokens.shape
    lat_len = latents.shape[1]
    inner = query_weight.shape[1]
    part = width // dp
    slot = ff_in_weight.shape[1] // dp // 2
    kv_rows, o_rows = part // 2, inner // dp // 2
    flat = (images * lat_len, width)

    def swap(value, bits):
        return lax.ppermute(value, "dp", [(i, i ^ bits) for i in range(dp)])

    def other(value):
        return lax.ppermute(value, "rep", [(0, 1), (1, 0)])

    def mine(value, axis):
        return lax.dynamic_index_in_dim(value, core, axis, keepdims=False)

    def down(value):
        return [value] + [swap(value, c * PLANE) for c in range(1, columns)]

    def across(values):
        return [values[0]] + [swap(values[p], p) for p in range(1, PLANE)]

    def down_sums(values):
        return [values[0]] + [swap(values[c], c * PLANE) for c in range(1, columns)]

    norms = jnp.stack([media_gain, media_bias, latent_gain, latent_bias, ff_gain, ff_bias])
    norms = lax.dynamic_update_slice(jnp.zeros((PAD, width), BF16), norms, (0, me * part))
    attn = [
        mine(keyval_weight.reshape(2, kv_rows, width), 0),
        fold_rows(mine(query_weight.reshape(2, kv_rows, inner), 0)),
        mine(outproj_weight.reshape(2, o_rows, width), 0),
        norms,
    ]
    attn = jnp.stack(down(jnp.concatenate(attn, 0)))
    ffout = mine(ff_out_weight.reshape(2, slot, width), 0)
    ffin = mine(ff_in_weight.reshape(part, dp, 2, slot), 2).reshape(part, dp * slot)
    cut = ffin.shape[1] // 2
    ffin = jnp.concatenate([ffin[:, :cut], ffin[:, cut:]], 0)
    attn, ffout, ffin = tie(attn, ffout, ffin)
    attn = [attn] + [swap(attn, p) for p in range(1, PLANE)]
    w_ffout = lax.all_gather(ffout, "dp", axis=0, tiled=True)
    ffin = jnp.stack([ffin, swap(ffin, 2 * PLANE)])
    got = swap(ffin, PLANE)
    w_kv, w_q, w_o, norms = in_order(place, attn, [other(value) for value in attn], inner)
    lo, hi = [
        jnp.stack([ffin[0, rows], got[0, rows], ffin[1, rows], got[1, rows]])
        for rows in (slice(0, part), slice(part, 2 * part))
    ]
    dout = cotangent.astype(BF16).reshape(flat)
    douts = dout, other(dout)

    w_kv, lo, hi = tie(w_kv, lo, hi)
    lo, hi = {0: lo, 2: swap(lo, 2)}, {0: hi, 1: swap(hi, 1)}
    run = images // 2
    held = attend(patch_counts, media_tokens, latents, norms, w_kv, w_q, 0, run)
    held, lo, hi = tie(held, lo, hi)
    lo[1], lo[3] = swap(lo[0], 1), swap(lo[2], 1)
    hi[2], hi[3] = swap(hi[0], 2), swap(hi[1], 2)
    turned, lat_low, keyvals, queries, mixed = attend(
        patch_counts, media_tokens, latents, norms, w_kv, w_q, run, images - run, held
    )
    mixed, lo, hi = tie(mixed.reshape(-1, inner), lo, hi)
    lo, hi = [lo[p] for p in range(PLANE)], [hi[p] for p in range(PLANE)]
    resid, low = add_branch(mixed, latents.reshape(flat), w_o, norms)

    activ, slope, low_t, dout, w_ffin, *grads = feed_forward(
        place, (low, other(low)), douts, lo, hi, slot
    )
    out_sum = grads[0], swap(grads[1], 1), grads[2], swap(grads[3], 2)
    *grads, kept, sent = feed_back(place, dout, low_t, w_ffin, w_ffout, slope, columns, part)
    kept, sent, out_sum = tie(kept, sent, out_sum)
    out_sum = fold_first(*out_sum)
    out_sum = out_sum[0], swap(out_sum[1], 2), out_sum[2], swap(out_sum[3], 1)
    grad_resid, grad_mixed, grad_o, ff_vectors = resid_back(
        kept, other(sent), resid, cotangent.reshape(flat), mixed, w_o, norms
    )
    in_sum = grads[0], swap(grads[1], 1), grads[2], swap(grads[3], 2)
    grad_kv, grad_q = attend_back(
        patch_counts, keyvals, queries, grad_mixed.reshape(images, lat_len, inner)
    )
    grad_kv, grad_q, out_sum, in_sum = tie(grad_kv, grad_q, out_sum, in_sum)
    keep, send = fold_second(*out_sum)
    in_sum = fold_first(*in_sum)
    grad_q, keep, send, in_sum = tie(grad_q, keep, send, in_sum)
    out_sum = keep, swap(send, PLANE)
    in_sum = in_sum[0], swap(in_sum[1], 2), in_sum[2], swap(in_sum[3], 1)
    keep, send = weight_back(
        place,
        grad_kv,
        grad_q,
        turned,
        lat_low.reshape(flat),
        w_kv,
        w_q,
        norms,
        grad_o,
        ff_vectors,
        columns,
    )
    keep, send, out_sum, in_sum = tie(keep, send, out_sum, in_sum)
    got = other(send)
    in_keep, in_send = fold_second(*in_sum)
    held, passed = fold_third(*out_sum)
    keep, in_send, passed = tie(keep, in_send, passed)
    in_sum = in_keep, swap(in_send, PLANE)
    out_sum = held, swap(passed, 2 * PLANE)
    attn = add_both(keep, got)
    attn = across(attn)
    grad_kv, attn[0] = tie(grad_kv, attn[0])
    done = media_back(media_tokens, grad_kv, norms, w_kv, 0, run)
    done, in_sum = tie(done, in_sum)
    held, passed = fold_third(*in_sum)
    done, held, passed = tie(done, held, passed)
    in_sum = held, swap(passed, 2 * PLANE)
    media_grad = media_back(media_tokens, grad_kv, norms, w_kv, run, images - run, (done,))
    media_grad, attn = tie(media_grad, attn)
    attn = fold(attn)
    attn, activ, grad_q, in_sum, out_sum = tie(attn, activ, grad_q, in_sum, out_sum)
    attn = down_sums(attn)
    latent_grad = latent_back(
        grad_kv, grad_q, latents, grad_resid.reshape(latents.shape), w_kv, w_q, norms
    )
    share, sent = feed_out(activ, w_ffout)
    own_in, own_out = [value[0].astype(F32) + value[1].astype(F32) for value in (in_sum, out_sum)]
    grad_ffin, grad_ffout = final_ff(place, own_in, other(own_in), own_out, other(own_out))
    sent, attn, grad_ffin, latent_grad = tie(sent, attn, grad_ffin, latent_grad)
    own = functools.reduce(jnp.add, [value.astype(F32) for value in attn])
    new_latents = resid + (share + other(sent).astype(F32))
    rows = own.shape[0] - PAD
    vectors = lax.dynamic_slice(own[rows:], (0, me * part), (6, part))
    own = own[:rows]
    grad_wkv, grad_wq, grad_wo = final_attn(place, own, other(own), inner, kv_rows, o_rows)
    return (
        new_latents.reshape(latents.shape),
        media_grad,
        latent_grad,
        vectors[0],
        vectors[1],
        vectors[2],
        vectors[3],
        grad_wq,
        grad_wkv,
        grad_wo,
        vectors[4],
        vectors[5],
        grad_ffin,
        grad_ffout,
    )


def norm_apply(values, gain, bias):
    centre = jnp.mean(values, -1, keepdims=True)
    centred = values - centre
    inverse = lax.rsqrt(jnp.mean(centred * centred, -1, keepdims=True) + EPS)
    unit = centred * inverse
    return (unit * gain.astype(jnp.float32) + bias.astype(jnp.float32), unit, inverse)


def plain_norm_grad(grad_normed, unit, inverse, gain):
    scaled = grad_normed * gain.astype(jnp.float32)
    return inverse * (
        scaled
        - jnp.mean(scaled, -1, keepdims=True)
        - unit * jnp.mean(scaled * unit, -1, keepdims=True)
    )


def row_total(values):
    return jnp.sum(values.reshape(-1, values.shape[-1]), axis=0)


def gelu_exact(values):
    return jax.nn.gelu(values, approximate=False)


def masked_scores(query_heads, key_heads, valid, scale):
    raw = (
        jnp.einsum("iqhe,ikhe->ihqk", query_heads, key_heads, preferred_element_type=jnp.float32)
        * scale
    )
    return jnp.where(valid[:, None, None, :], raw, jnp.float32(-1e30))


def plain_shards(
    media_tokens,
    patch_counts,
    latents,
    media_gain,
    media_bias,
    latent_gain,
    latent_bias,
    query_weight,
    keyval_weight,
    outproj_weight,
    ff_gain,
    ff_bias,
    ff_in_weight,
    ff_out_weight,
    cotangent,
):
    f32 = jnp.float32
    bf16 = jnp.bfloat16
    whole = (
        lax.all_gather(media_gain, "dp", axis=0, tiled=True),
        lax.all_gather(media_bias, "dp", axis=0, tiled=True),
        lax.all_gather(latent_gain, "dp", axis=0, tiled=True),
        lax.all_gather(latent_bias, "dp", axis=0, tiled=True),
        lax.all_gather(query_weight, "dp", axis=0, tiled=True),
        lax.all_gather(keyval_weight, "dp", axis=0, tiled=True),
        lax.all_gather(outproj_weight, "dp", axis=0, tiled=True),
        lax.all_gather(ff_gain, "dp", axis=0, tiled=True),
        lax.all_gather(ff_bias, "dp", axis=0, tiled=True),
        lax.all_gather(ff_in_weight, "dp", axis=0, tiled=True),
        lax.all_gather(ff_out_weight, "dp", axis=0, tiled=True),
    )
    (
        gain_media,
        bias_media,
        gain_latent,
        bias_latent,
        w_query,
        w_keyval,
        w_outproj,
        gain_ff,
        bias_ff,
        w_ffin,
        w_ffout,
    ) = whole
    images, media_len, width = media_tokens.shape
    lat_len = latents.shape[1]
    keys_len = media_len + lat_len
    inner_width = w_query.shape[1]
    head_size = inner_width // HEADS
    scale = 1.0 / math.sqrt(head_size)
    media_f = media_tokens.astype(f32)
    latent_f = latents.astype(f32)
    media_normed, media_unit, media_inv = norm_apply(media_f, gain_media, bias_media)
    latent_normed, latent_unit, latent_inv = norm_apply(latent_f, gain_latent, bias_latent)
    media_low = media_normed.astype(bf16)
    latent_low = latent_normed.astype(bf16)
    queries = jnp.einsum("ild,de->ile", latent_low, w_query, preferred_element_type=f32).astype(
        bf16
    )
    key_input = jnp.concatenate([media_low, latent_low], axis=1)
    keyvals = jnp.einsum("ikd,de->ike", key_input, w_keyval, preferred_element_type=f32).astype(
        bf16
    )
    key_heads = keyvals[:, :, :inner_width].reshape(images, keys_len, HEADS, head_size)
    value_heads = keyvals[:, :, inner_width:].reshape(images, keys_len, HEADS, head_size)
    query_heads = queries.reshape(images, lat_len, HEADS, head_size)
    positions = jnp.arange(keys_len, dtype=jnp.int32)
    valid = (positions[None, :] < patch_counts[:, None]) | (positions[None, :] >= media_len)
    scores = masked_scores(query_heads, key_heads, valid, scale)
    top = jnp.max(scores, -1, keepdims=True)
    expd = jnp.exp(scores - top)
    total = jnp.sum(expd, -1, keepdims=True)
    probs = expd / total
    log_total = top + jnp.log(total)
    mixed = jnp.einsum(
        "ihqk,ikhe->iqhe", probs.astype(bf16), value_heads, preferred_element_type=f32
    )
    mixed = mixed.reshape(images, lat_len, inner_width).astype(bf16)
    branch = jnp.einsum("ile,ed->ild", mixed, w_outproj, preferred_element_type=f32)
    resid = latent_f + branch
    ff_normed, ff_unit, ff_inv = norm_apply(resid, gain_ff, bias_ff)
    ff_low = ff_normed.astype(bf16)
    pre_act = jnp.einsum("ild,df->ilf", ff_low, w_ffin, preferred_element_type=f32)
    activ, gelu_pull = jax.vjp(gelu_exact, pre_act)
    activ_low = activ.astype(bf16)
    new_latents = resid + jnp.einsum("ilf,fd->ild", activ_low, w_ffout, preferred_element_type=f32)
    again = (
        lax.all_gather(media_gain, "dp", axis=0, tiled=True),
        lax.all_gather(media_bias, "dp", axis=0, tiled=True),
        lax.all_gather(latent_gain, "dp", axis=0, tiled=True),
        lax.all_gather(latent_bias, "dp", axis=0, tiled=True),
        lax.all_gather(query_weight, "dp", axis=0, tiled=True),
        lax.all_gather(keyval_weight, "dp", axis=0, tiled=True),
        lax.all_gather(outproj_weight, "dp", axis=0, tiled=True),
        lax.all_gather(ff_gain, "dp", axis=0, tiled=True),
        lax.all_gather(ff_bias, "dp", axis=0, tiled=True),
        lax.all_gather(ff_in_weight, "dp", axis=0, tiled=True),
        lax.all_gather(ff_out_weight, "dp", axis=0, tiled=True),
    )
    (
        gain_media_b,
        bias_media_b,
        gain_latent_b,
        bias_latent_b,
        w_query_b,
        w_keyval_b,
        w_outproj_b,
        gain_ff_b,
        bias_ff_b,
        w_ffin_b,
        w_ffout_b,
    ) = again
    grad_out_low = cotangent.astype(bf16)
    grad_ffout = jnp.einsum("ilf,ild->fd", activ_low, grad_out_low, preferred_element_type=f32)
    grad_activ = jnp.einsum("ild,fd->ilf", grad_out_low, w_ffout_b, preferred_element_type=f32)
    (grad_pre,) = gelu_pull(grad_activ)
    grad_pre_low = grad_pre.astype(bf16)
    grad_ffin = jnp.einsum("ild,ilf->df", ff_low, grad_pre_low, preferred_element_type=f32)
    grad_ffnormed = jnp.einsum("ilf,df->ild", grad_pre_low, w_ffin_b, preferred_element_type=f32)
    grad_gain_ff = row_total(grad_ffnormed * ff_unit)
    grad_bias_ff = row_total(grad_ffnormed)
    grad_resid = cotangent + plain_norm_grad(grad_ffnormed, ff_unit, ff_inv, gain_ff_b)
    grad_resid_low = grad_resid.astype(bf16)
    grad_outproj = jnp.einsum("ile,ild->ed", mixed, grad_resid_low, preferred_element_type=f32)
    grad_mixed = jnp.einsum(
        "ild,ed->ile", grad_resid_low, w_outproj_b, preferred_element_type=f32
    ).astype(bf16)
    grad_mixed_heads = grad_mixed.reshape(images, lat_len, HEADS, head_size)
    scores_again = masked_scores(query_heads, key_heads, valid, scale)
    probs_again = jnp.exp(scores_again - log_total)
    grad_probs = jnp.einsum(
        "iqhe,ikhe->ihqk", grad_mixed_heads, value_heads, preferred_element_type=f32
    )
    grad_scores = probs_again * (grad_probs - jnp.sum(probs_again * grad_probs, -1, keepdims=True))
    grad_scores_low = grad_scores.astype(bf16)
    grad_queries = (
        jnp.einsum("ihqk,ikhe->iqhe", grad_scores_low, key_heads, preferred_element_type=f32)
        * scale
    )
    grad_queries = grad_queries.reshape(images, lat_len, inner_width).astype(bf16)
    grad_keys = (
        jnp.einsum("ihqk,iqhe->ikhe", grad_scores_low, query_heads, preferred_element_type=f32)
        * scale
    )
    grad_values = jnp.einsum(
        "ihqk,iqhe->ikhe", probs_again.astype(bf16), grad_mixed_heads, preferred_element_type=f32
    )
    grad_keyvals = jnp.concatenate(
        [
            grad_keys.reshape(images, keys_len, inner_width),
            grad_values.reshape(images, keys_len, inner_width),
        ],
        axis=-1,
    ).astype(bf16)
    grad_qweight = jnp.einsum("ild,ile->de", latent_low, grad_queries, preferred_element_type=f32)
    grad_kvweight = jnp.einsum("ikd,ike->de", key_input, grad_keyvals, preferred_element_type=f32)
    grad_key_input = jnp.einsum("ike,de->ikd", grad_keyvals, w_keyval_b, preferred_element_type=f32)
    grad_latnormed = jnp.einsum("ile,de->ild", grad_queries, w_query_b, preferred_element_type=f32)
    grad_latnormed = grad_latnormed + grad_key_input[:, media_len:]
    grad_medianormed = grad_key_input[:, :media_len]
    media_grad = plain_norm_grad(grad_medianormed, media_unit, media_inv, gain_media_b)
    latent_grad = grad_resid + plain_norm_grad(grad_latnormed, latent_unit, latent_inv, gain_latent_b)
    grad_gain_media = row_total(grad_medianormed * media_unit)
    grad_bias_media = row_total(grad_medianormed)
    grad_gain_latent = row_total(grad_latnormed * latent_unit)
    grad_bias_latent = row_total(grad_latnormed)
    owned = (
        lax.psum_scatter(
            grad_gain_media.astype(jnp.bfloat16), "dp", scatter_dimension=0, tiled=True
        ).astype(jnp.float32),
        lax.psum_scatter(
            grad_bias_media.astype(jnp.bfloat16), "dp", scatter_dimension=0, tiled=True
        ).astype(jnp.float32),
        lax.psum_scatter(
            grad_gain_latent.astype(jnp.bfloat16), "dp", scatter_dimension=0, tiled=True
        ).astype(jnp.float32),
        lax.psum_scatter(
            grad_bias_latent.astype(jnp.bfloat16), "dp", scatter_dimension=0, tiled=True
        ).astype(jnp.float32),
        lax.psum_scatter(
            grad_qweight.astype(jnp.bfloat16), "dp", scatter_dimension=0, tiled=True
        ).astype(jnp.float32),
        lax.psum_scatter(
            grad_kvweight.astype(jnp.bfloat16), "dp", scatter_dimension=0, tiled=True
        ).astype(jnp.float32),
        lax.psum_scatter(
            grad_outproj.astype(jnp.bfloat16), "dp", scatter_dimension=0, tiled=True
        ).astype(jnp.float32),
        lax.psum_scatter(
            grad_gain_ff.astype(jnp.bfloat16), "dp", scatter_dimension=0, tiled=True
        ).astype(jnp.float32),
        lax.psum_scatter(
            grad_bias_ff.astype(jnp.bfloat16), "dp", scatter_dimension=0, tiled=True
        ).astype(jnp.float32),
        lax.psum_scatter(
            grad_ffin.astype(jnp.bfloat16), "dp", scatter_dimension=0, tiled=True
        ).astype(jnp.float32),
        lax.psum_scatter(
            grad_ffout.astype(jnp.bfloat16), "dp", scatter_dimension=0, tiled=True
        ).astype(jnp.float32),
    )
    summed = (
        lax.psum(owned[0].astype(jnp.bfloat16), "rep").astype(jnp.float32),
        lax.psum(owned[1].astype(jnp.bfloat16), "rep").astype(jnp.float32),
        lax.psum(owned[2].astype(jnp.bfloat16), "rep").astype(jnp.float32),
        lax.psum(owned[3].astype(jnp.bfloat16), "rep").astype(jnp.float32),
        lax.psum(owned[4].astype(jnp.bfloat16), "rep").astype(jnp.float32),
        lax.psum(owned[5].astype(jnp.bfloat16), "rep").astype(jnp.float32),
        lax.psum(owned[6].astype(jnp.bfloat16), "rep").astype(jnp.float32),
        lax.psum(owned[7].astype(jnp.bfloat16), "rep").astype(jnp.float32),
        lax.psum(owned[8].astype(jnp.bfloat16), "rep").astype(jnp.float32),
        lax.psum(owned[9].astype(jnp.bfloat16), "rep").astype(jnp.float32),
        lax.psum(owned[10].astype(jnp.bfloat16), "rep").astype(jnp.float32),
    )
    (
        sum_gain_media,
        sum_bias_media,
        sum_gain_latent,
        sum_bias_latent,
        sum_query,
        sum_keyval,
        sum_outproj,
        sum_gain_ff,
        sum_bias_ff,
        sum_ffin,
        sum_ffout,
    ) = summed
    return (
        new_latents,
        media_grad,
        latent_grad,
        sum_gain_media,
        sum_bias_media,
        sum_gain_latent,
        sum_bias_latent,
        sum_query,
        sum_keyval,
        sum_outproj,
        sum_gain_ff,
        sum_bias_ff,
        sum_ffin,
        sum_ffout,
    )


def solution(mesh):
    dp, rep = mesh.shape["dp"], mesh.shape["rep"]

    def program(*arrays):
        if rep != 2 or dp != PLANE * PLANE:
            return plain_shards(*arrays)
        return shards(dp, *arrays)

    return jax.shard_map(
        program,
        mesh=mesh,
        in_specs=(
            P(("dp", "rep"), None, None),
            P(("dp", "rep")),
            P(("dp", "rep"), None, None),
            P("dp"),
            P("dp"),
            P("dp"),
            P("dp"),
            P("dp", None),
            P("dp", None),
            P("dp", None),
            P("dp"),
            P("dp"),
            P("dp", None),
            P("dp", None),
            P(("dp", "rep"), None, None),
        ),
        out_specs=(
            P(("dp", "rep"), None, None),
            P(("dp", "rep"), None, None),
            P(("dp", "rep"), None, None),
            P("dp"),
            P("dp"),
            P("dp"),
            P("dp"),
            P("dp", None),
            P("dp", None),
            P("dp", None),
            P("dp"),
            P("dp"),
            P("dp", None),
            P("dp", None),
        ),
        check_vma=False,
    )
```

```python
import functools
import math

import jax
import jax.numpy as jnp
from jax import lax
from jax.experimental import pallas as pl
from jax.experimental.pallas import tpu as pltpu
from jax.sharding import PartitionSpec as P

HEADS = 8
GROUP = 4
EPS = 1e-05
NEG = -1e30
ROWS = 64
FF_TILE = 512
PLANE = 4
PAD = 8
F32 = jnp.float32
BF16 = jnp.bfloat16


def cost(us):
    return pl.CostEstimate(flops=int(us * 1.1e9), bytes_accessed=1 << 18, transcendentals=0)


def contract(a, b, over):
    return lax.dot_general(a, b, ((over[:1], over[1:]), ((), ())), preferred_element_type=F32)


def norm_rows(values):
    centred = values - jnp.mean(values, -1, keepdims=True)
    inverse = lax.rsqrt(jnp.mean(centred * centred, -1, keepdims=True) + EPS)
    return centred * inverse, inverse


def norm_back(grad, unit, inverse, gain):
    scaled = grad * gain
    return inverse * (
        scaled
        - jnp.mean(scaled, -1, keepdims=True)
        - unit * jnp.mean(scaled * unit, -1, keepdims=True)
    )


def spread(value, size):
    lane = lax.broadcasted_iota(jnp.int32, value.shape, 1) // size
    value = value.astype(F32)
    return jnp.concatenate([jnp.where(lane == h, value, 0.0) for h in range(GROUP)], 0)


def gathered(value, size):
    rows = value.shape[0] // GROUP
    lane = lax.broadcasted_iota(jnp.int32, (rows, value.shape[1]), 1) // size
    out = jnp.zeros((rows, value.shape[1]), F32)
    for h in range(GROUP):
        out = jnp.where(lane == h, value[h * rows : (h + 1) * rows], out)
    return out


def tie(*values):
    return lax.optimization_barrier(values)


def params(mib):
    return pltpu.CompilerParams(vmem_limit_bytes=mib << 20)


def image_at(i, c):
    return (i, 0, 0)


def fixed_at(*_):
    return (0, 0)


def order_kernel(place, *refs):
    sides = refs[:PLANE], refs[PLANE : 2 * PLANE]
    w_kv, w_q, w_o, norms = refs[2 * PLANE :]
    me, core = place[0], place[1]
    columns = sides[0][0].shape[0]
    chips = columns * PLANE
    kv_rows, o_rows = w_kv.shape[0] // chips // 2, w_o.shape[0] // chips // 2
    q_rows, inner = kv_rows // 2, w_q.shape[1]
    total = jnp.zeros(norms.shape, F32)
    for plane in range(PLANE):
        for column in range(columns):
            chip = me ^ (column * PLANE + plane)
            for side in range(2):
                block = sides[side][plane]
                half = core if side == 0 else 1 - core
                at = pl.multiple_of((chip * 2 + half) * kv_rows, kv_rows)
                w_kv[pl.ds(at, kv_rows), :] = block[column, :kv_rows, :]
                rest = block[column, kv_rows : kv_rows + q_rows, :]
                w_q[pl.ds(at, q_rows), :] = rest[:, :inner]
                w_q[pl.ds(pl.multiple_of(at + q_rows, q_rows), q_rows), :] = rest[:, inner:]
                at = pl.multiple_of((chip * 2 + half) * o_rows, o_rows)
                w_o[pl.ds(at, o_rows), :] = block[
                    column, kv_rows + q_rows : kv_rows + q_rows + o_rows, :
                ]
            total += sides[0][plane][column, kv_rows + q_rows + o_rows :, :].astype(F32)
    norms[...] = total


def in_order(place, own, other, inner):
    columns, _, width = own[0].shape
    return pl.pallas_call(
        order_kernel,
        grid_spec=pltpu.PrefetchScalarGridSpec(
            num_scalar_prefetch=1,
            grid=(1,),
            in_specs=[
                pl.BlockSpec(value.shape, lambda t, c: (0, 0, 0)) for value in (*own, *other)
            ],
            out_specs=[
                pl.BlockSpec((width, 2 * inner), fixed_at),
                pl.BlockSpec((width, inner), fixed_at),
                pl.BlockSpec((inner, width), fixed_at),
                pl.BlockSpec((8, width), fixed_at),
            ],
        ),
        out_shape=[
            jax.ShapeDtypeStruct((width, 2 * inner), BF16),
            jax.ShapeDtypeStruct((width, inner), BF16),
            jax.ShapeDtypeStruct((inner, width), BF16),
            jax.ShapeDtypeStruct((8, width), F32),
        ],
        compiler_params=params(24),
        cost_estimate=cost(1),
        name="in_order",
    )(place, *own, *other)


def whole_at(rank):
    return lambda *_: (0,) * rank


def small(kernel, values, outs, us, name):
    return pl.pallas_call(
        kernel,
        grid=(1,),
        in_specs=[pl.BlockSpec(value.shape, whole_at(value.ndim)) for value in values],
        out_specs=[pl.BlockSpec(shape, whole_at(len(shape))) for shape in outs],
        out_shape=[jax.ShapeDtypeStruct(shape, BF16) for shape in outs],
        compiler_params=params(20),
        cost_estimate=cost(us),
        name=name,
    )(*values)


def added(one, two):
    return (one.astype(F32) + two.astype(F32)).astype(BF16)


def fold_kernel(*refs):
    for column in range(len(refs) - PLANE):
        total = refs[0][column].astype(F32)
        for plane in range(1, PLANE):
            total += refs[plane][column].astype(F32)
        refs[PLANE + column][...] = total.astype(BF16)


def fold(values):
    columns = values[0].shape[0]
    return small(fold_kernel, values, [values[0].shape[1:]] * columns, 2, "fold")


def first_kernel(keep0, got0, keep1, got1, held0, pass0, held1, pass1):
    held0[...] = added(keep0[0], got0[0])
    pass0[...] = added(keep0[1], got0[1])
    held1[...] = added(keep1[0], got1[0])
    pass1[...] = added(keep1[1], got1[1])


def fold_first(keep0, got0, keep1, got1):
    values = keep0, got0, keep1, got1
    return small(first_kernel, values, [keep0.shape[1:]] * 4, 2, "fold_first")


def second_kernel(held0, got0, held1, got1, keep, send):
    half = held0.shape[1]
    for i in range(2):
        for out, column in ((keep, 2 * i), (send, 2 * i + 1)):
            out[i, :half, :] = added(held0[column], got0[column])
            out[i, half:, :] = added(held1[column], got1[column])


def fold_second(held0, got0, held1, got1):
    values = held0, got0, held1, got1
    shape = (2, 2 * held0.shape[1], held0.shape[2])
    return small(second_kernel, values, [shape] * 2, 2, "fold_second")


def third_kernel(keep, got, held, passed):
    held[...] = added(keep[0], got[0])
    passed[...] = added(keep[1], got[1])


def fold_third(keep, got):
    return small(third_kernel, (keep, got), [keep.shape[1:]] * 2, 0.5, "fold_third")


def both_kernel(keep, got, *outs):
    for plane, out in enumerate(outs):
        out[...] = (keep[plane].astype(F32) + got[plane].astype(F32)).astype(BF16)


def add_both(keep, got):
    tail = keep.shape[1:]
    whole = lambda t: (0, 0, 0, 0)
    return pl.pallas_call(
        both_kernel,
        grid=(1,),
        in_specs=[pl.BlockSpec(keep.shape, whole), pl.BlockSpec(keep.shape, whole)],
        out_specs=[pl.BlockSpec(tail, lambda t: (0, 0, 0)) for _ in range(PLANE)],
        out_shape=[jax.ShapeDtypeStruct(tail, BF16) for _ in range(PLANE)],
        compiler_params=params(16),
        cost_estimate=cost(2),
        name="add_both",
    )(keep, got)


def final_ff_kernel(place, own_in, other_in, own_out, other_out, grad_in, grad_out):
    first = place[1] == 0
    slot = own_out.shape[0]
    for chip in range(own_in.shape[1] // slot):
        here = slice(chip * slot, (chip + 1) * slot)
        one, two = own_in[:, here], other_in[:, here]
        at = 2 * chip * slot
        grad_in[:, at : at + slot] = jnp.where(first, one, two)
        grad_in[:, at + slot : at + 2 * slot] = jnp.where(first, two, one)
    grad_out[:slot, :] = jnp.where(first, own_out[...], other_out[...])
    grad_out[slot:, :] = jnp.where(first, other_out[...], own_out[...])


def final_ff(place, own_in, other_in, own_out, other_out):
    values = own_in, other_in, own_out, other_out
    shapes = (own_in.shape[0], 2 * own_in.shape[1]), (2 * own_out.shape[0], own_out.shape[1])
    return pl.pallas_call(
        final_ff_kernel,
        grid_spec=pltpu.PrefetchScalarGridSpec(
            num_scalar_prefetch=1,
            grid=(1,),
            in_specs=[pl.BlockSpec(value.shape, fixed_at) for value in values],
            out_specs=[pl.BlockSpec(shape, fixed_at) for shape in shapes],
        ),
        out_shape=[jax.ShapeDtypeStruct(shape, F32) for shape in shapes],
        compiler_params=params(16),
        cost_estimate=cost(2),
        name="final_ff",
    )(place, *values)


def final_attn_kernel(place, own, other, grad_kv, grad_q, grad_o):
    kv_rows, o_rows = grad_kv.shape[0] // 2, grad_o.shape[0] // 2
    q_rows, inner = kv_rows // 2, grad_q.shape[1]
    first = place[1] == 0
    for half in range(2):
        value = jnp.where(first == (half == 0), own[...], other[...])
        at = half * kv_rows
        grad_kv[at : at + kv_rows, :] = value[:kv_rows]
        rest = value[kv_rows : kv_rows + q_rows]
        grad_q[at : at + q_rows, :] = rest[:, :inner]
        grad_q[at + q_rows : at + kv_rows, :] = rest[:, inner:]
        grad_o[half * o_rows : (half + 1) * o_rows, :] = value[
            kv_rows + q_rows : kv_rows + q_rows + o_rows
        ]


def final_attn(place, own, other, inner, kv_rows, o_rows):
    width = own.shape[1]
    shapes = (2 * kv_rows, width), (2 * kv_rows, inner), (2 * o_rows, width)
    return pl.pallas_call(
        final_attn_kernel,
        grid_spec=pltpu.PrefetchScalarGridSpec(
            num_scalar_prefetch=1,
            grid=(1,),
            in_specs=[pl.BlockSpec(own.shape, fixed_at), pl.BlockSpec(own.shape, fixed_at)],
            out_specs=[pl.BlockSpec(shape, fixed_at) for shape in shapes],
        ),
        out_shape=[jax.ShapeDtypeStruct(shape, F32) for shape in shapes],
        compiler_params=params(16),
        cost_estimate=cost(2),
        name="final_attn",
    )(place, own, other)


def attend_kernel(counts, media, latent, norms, w_kv, w_q, *refs):
    turned, lat_low, keyvals, queries, mixed, key_input = refs[-6:]
    media_len, lat_len = media.shape[1], latent.shape[1]
    keys_len = media_len + lat_len
    inner = w_q.shape[1]
    size = inner // HEADS
    wide = size * GROUP
    for at in range(0, media_len, ROWS):
        unit, _ = norm_rows(media[0, at : at + ROWS, :].astype(F32))
        key_input[at : at + ROWS, :] = (unit * norms[0:1, :] + norms[1:2, :]).astype(BF16)
    unit, _ = norm_rows(latent[0].astype(F32))
    low = (unit * norms[2:3, :] + norms[3:4, :]).astype(BF16)
    key_input[media_len:, :] = low
    lat_low[0] = low
    query = contract(low, w_q[...], (1, 0)).astype(BF16)
    queries[0] = query
    keyvals[0] = contract(key_input[...], w_kv[...], (1, 0)).astype(BF16)
    for side in range(2):

        @pl.when(pl.program_id(0) % 2 == side)
        def _(side=side):
            turned[0, :, side * keys_len : (side + 1) * keys_len] = key_input[...].T

    key_at = lax.broadcasted_iota(jnp.int32, (1, keys_len), 1)
    valid = (key_at < counts[pl.program_id(0)]) | (key_at >= media_len)
    for at in range(0, inner, wide):
        own = spread(query[:, at : at + wide].astype(F32) * (1.0 / math.sqrt(size)), size)
        scores = contract(own.astype(BF16), keyvals[0, :, at : at + wide], (1, 1))
        scores = jnp.where(valid, scores, NEG)
        expd = jnp.exp(scores - jnp.max(scores, -1, keepdims=True))
        probs = (expd * (1.0 / jnp.sum(expd, -1, keepdims=True))).astype(BF16)
        out = contract(probs, keyvals[0, :, inner + at : inner + at + wide], (1, 0))
        mixed[0, :, at : at + wide] = gathered(out, size).astype(BF16)


def attend(counts, media, latent, norms, w_kv, w_q, first, run, into=()):
    images, media_len, width = media.shape
    lat_len, inner = latent.shape[1], w_q.shape[1]
    keys_len = media_len + lat_len
    at = lambda i, c: (i + first, 0, 0)
    shapes = [
        (images, lat_len, width),
        (images, keys_len, 2 * inner),
        (images, lat_len, inner),
        (images, lat_len, inner),
    ]
    return pl.pallas_call(
        attend_kernel,
        grid_spec=pltpu.PrefetchScalarGridSpec(
            num_scalar_prefetch=1,
            grid=(run,),
            in_specs=[
                pl.BlockSpec((1, media_len, width), at),
                pl.BlockSpec((1, lat_len, width), at),
                pl.BlockSpec(norms.shape, fixed_at),
                pl.BlockSpec(w_kv.shape, fixed_at),
                pl.BlockSpec(w_q.shape, fixed_at),
                *[pl.BlockSpec(memory_space=pl.ANY) for _ in into],
            ],
            out_specs=[
                pl.BlockSpec((1, width, 2 * keys_len), lambda i, c: ((i + first) // 2, 0, 0)),
                *[pl.BlockSpec((1,) + shape[1:], at) for shape in shapes],
            ],
            scratch_shapes=[pltpu.VMEM((keys_len, width), BF16)],
        ),
        out_shape=[
            jax.ShapeDtypeStruct((images // 2, width, 2 * keys_len), BF16),
            *[jax.ShapeDtypeStruct(shape, BF16) for shape in shapes],
        ],
        input_output_aliases={6 + i: i for i in range(len(into))},
        compiler_params=params(32),
        cost_estimate=cost(14),
        name="attend",
    )(counts[first : first + run], media, latent, norms, w_kv, w_q, *into)


def resid_kernel(mixed, latent, w_o, norms, resid, low):
    value = latent[...].astype(F32) + contract(mixed[...], w_o[...], (1, 0))
    resid[...] = value
    unit, _ = norm_rows(value)
    low[...] = (unit * norms[4:5, :] + norms[5:6, :]).astype(BF16)


def add_branch(mixed, latent, w_o, norms):
    rows, width = latent.shape
    inner = mixed.shape[1]
    block = rows // 4
    row_at = lambda i: (i, 0)
    return pl.pallas_call(
        resid_kernel,
        grid=(rows // block,),
        in_specs=[
            pl.BlockSpec((block, inner), row_at),
            pl.BlockSpec((block, width), row_at),
            pl.BlockSpec(w_o.shape, fixed_at),
            pl.BlockSpec(norms.shape, fixed_at),
        ],
        out_specs=[pl.BlockSpec((block, width), row_at), pl.BlockSpec((block, width), row_at)],
        out_shape=[
            jax.ShapeDtypeStruct((rows, width), F32),
            jax.ShapeDtypeStruct((rows, width), BF16),
        ],
        compiler_params=params(16),
        cost_estimate=cost(3),
        name="add_branch",
    )(mixed, latent, w_o, norms)


def ff_kernel(place, *refs):
    low0, low1, dout0, dout1 = refs[:4]
    lo, hi = refs[4:8], refs[8:12]
    activ, slope, low_t, dout, w_in = refs[12:17]
    keep0, send0, keep1, send1 = refs[17:21]
    low, grad = refs[21:]
    step, steps = pl.program_id(0), pl.num_programs(0)
    me = place[0]
    half = low0.shape[0]
    part = lo[0].shape[1]
    slot = grad.shape[0] // PLANE
    cut = slot // 2

    @pl.when(step == 0)
    def _():
        low[:half, :] = low0[...]
        low[half:, :] = low1[...]
        dout[:half, :] = dout0[...]
        dout[half:, :] = dout1[...]
        low_t[...] = low[...].T

    def put(pieces):
        for plane in range(PLANE):
            for column in range(pieces[0].shape[0]):
                at = pl.multiple_of((me ^ (column * PLANE + plane)) * part, part)
                w_in[pl.ds(at, part), :] = pieces[plane][column]

    pl.when(step < steps // 2)(lambda: put(lo))
    pl.when(step >= steps // 2)(lambda: put(hi))
    pre = contract(low[...], w_in[...], (1, 0))
    cdf = 0.5 * (1.0 + lax.erf(pre * math.sqrt(0.5)))
    slope[...] = cdf + pre * (jnp.exp(pre * pre * -0.5) * (1.0 / math.sqrt(2.0 * math.pi)))
    value = (pre * cdf).astype(BF16)
    activ[...] = value
    grad[...] = contract(value, dout[...], (0, 0)).astype(BF16)

    def block(plane, at):
        at = pl.multiple_of((plane ^ (me % PLANE)) * slot + at, cut)
        return grad[pl.ds(at, cut), :]

    for i in range(2):
        keep0[i, 0] = block(2 * i, 0)
        send0[i, 0] = block(2 * i + 1, 0)
        keep1[i, 0] = block(i, cut)
        send1[i, 0] = block(2 + i, cut)


def feed_forward(place, lows, douts, lo, hi, slot):
    half, width = lows[0].shape
    rows = 2 * half
    columns, part, cut = lo[0].shape
    tile = PLANE * slot
    steps = 2 * cut // tile
    in_at = lambda t, c: (0, t)
    lo_at = lambda t, c: (0, 0, jnp.minimum(t, steps // 2 - 1))
    hi_at = lambda t, c: (0, 0, jnp.maximum(t - steps // 2, 0))
    once = pl.Buffered(1)
    return pl.pallas_call(
        ff_kernel,
        grid_spec=pltpu.PrefetchScalarGridSpec(
            num_scalar_prefetch=1,
            grid=(steps,),
            in_specs=[
                *[pl.BlockSpec((half, width), fixed_at, pipeline_mode=once) for _ in range(4)],
                *[pl.BlockSpec((columns, part, tile), lo_at) for _ in lo],
                *[pl.BlockSpec((columns, part, tile), hi_at) for _ in hi],
            ],
            out_specs=[
                pl.BlockSpec((rows, tile), in_at),
                pl.BlockSpec((rows, tile), in_at),
                pl.BlockSpec((width, rows), fixed_at),
                pl.BlockSpec((rows, width), fixed_at),
                pl.BlockSpec((width, tile), in_at),
                *[
                    pl.BlockSpec(
                        (2, 1, slot // 2, width), lambda t, c: (0, t ^ (c[0] // PLANE), 0, 0)
                    )
                    for _ in range(4)
                ],
            ],
            scratch_shapes=[pltpu.VMEM((rows, width), BF16), pltpu.VMEM((tile, width), BF16)],
        ),
        out_shape=[
            jax.ShapeDtypeStruct((rows, 2 * cut), BF16),
            jax.ShapeDtypeStruct((rows, 2 * cut), F32),
            jax.ShapeDtypeStruct((width, rows), BF16),
            jax.ShapeDtypeStruct((rows, width), BF16),
            jax.ShapeDtypeStruct((width, 2 * cut), BF16),
            *[jax.ShapeDtypeStruct((2, columns, slot // 2, width), BF16) for _ in range(4)],
        ],
        compiler_params=params(44),
        cost_estimate=cost(18),
        name="feed_forward",
    )(place, *lows, *douts, *lo, *hi)


def ff_back_kernel(
    place, dout, low_t, w_in, w_out, slope, keep0, send0, keep1, send1, kept, sent, total, grad_in
):
    step, steps = pl.program_id(0), pl.num_programs(0)
    columns, cut = keep0.shape[1:3]

    @pl.when(step == 0)
    def _():
        total[...] = jnp.zeros_like(total)

    grad = (contract(dout[...], w_out[...], (1, 1)) * slope[...]).astype(BF16)
    grad_in[...] = contract(low_t[...], grad, (1, 0)).astype(BF16)

    def block(plane, column, at):
        at = pl.multiple_of((place[0] ^ (column * PLANE + plane)) * 2 * cut + at, cut)
        return grad_in[pl.ds(at, cut), :]

    for column in range(columns):
        for i in range(2):
            keep0[i, column] = block(2 * i, column, 0)
            send0[i, column] = block(2 * i + 1, column, 0)
            keep1[i, column] = block(i, column, cut)
            send1[i, column] = block(2 + i, column, cut)
    total[...] += contract(grad, w_in[...], (1, 1))

    @pl.when(step == steps - 1)
    def _():
        half = kept.shape[0]
        kept[...] = total[:half, :]
        sent[...] = total[half:, :].astype(BF16)


def feed_back(place, dout, low_t, w_in, w_out, slope, columns, part):
    rows, width = dout.shape
    hidden = w_in.shape[1]
    tile = min(FF_TILE, hidden)
    half = rows // 2
    in_at, out_at = (lambda t, c: (0, t)), (lambda t, c: (t, 0))
    once = pl.Buffered(1)
    return pl.pallas_call(
        ff_back_kernel,
        grid_spec=pltpu.PrefetchScalarGridSpec(
            num_scalar_prefetch=1,
            grid=(hidden // tile,),
            in_specs=[
                pl.BlockSpec((rows, width), fixed_at, pipeline_mode=once),
                pl.BlockSpec((width, rows), fixed_at, pipeline_mode=once),
                pl.BlockSpec((width, tile), in_at),
                pl.BlockSpec((tile, width), out_at),
                pl.BlockSpec((rows, tile), in_at),
            ],
            out_specs=[
                *[
                    pl.BlockSpec((2, columns, part // 2, tile), lambda t, c: (0, 0, 0, t))
                    for _ in range(4)
                ],
                pl.BlockSpec((half, width), fixed_at, pipeline_mode=once),
                pl.BlockSpec((half, width), fixed_at, pipeline_mode=once),
            ],
            scratch_shapes=[pltpu.VMEM((rows, width), F32), pltpu.VMEM((width, tile), BF16)],
        ),
        out_shape=[
            *[jax.ShapeDtypeStruct((2, columns, part // 2, hidden), BF16) for _ in range(4)],
            jax.ShapeDtypeStruct((half, width), F32),
            jax.ShapeDtypeStruct((half, width), BF16),
        ],
        compiler_params=params(48),
        cost_estimate=cost(21),
        name="feed_back",
    )(place, dout, low_t, w_in, w_out, slope)


def ff_out_kernel(activ, w_out, kept, sent, total):
    step = pl.program_id(0)

    @pl.when(step == 0)
    def _():
        total[...] = jnp.zeros_like(total)

    total[...] += contract(activ[...], w_out[...], (1, 0))

    @pl.when(step == pl.num_programs(0) - 1)
    def _():
        half = kept.shape[0]
        kept[...] = total[:half, :]
        sent[...] = total[half:, :].astype(BF16)


def feed_out(activ, w_out):
    rows, hidden = activ.shape
    width = w_out.shape[1]
    tile = min(FF_TILE, hidden)
    half = rows // 2
    once = pl.Buffered(1)
    return pl.pallas_call(
        ff_out_kernel,
        grid=(hidden // tile,),
        in_specs=[
            pl.BlockSpec((rows, tile), lambda t: (0, t)),
            pl.BlockSpec((tile, width), lambda t: (t, 0)),
        ],
        out_specs=[pl.BlockSpec((half, width), fixed_at, pipeline_mode=once)] * 2,
        out_shape=[
            jax.ShapeDtypeStruct((half, width), F32),
            jax.ShapeDtypeStruct((half, width), BF16),
        ],
        scratch_shapes=[pltpu.VMEM((rows, width), F32)],
        compiler_params=params(24),
        cost_estimate=cost(7),
        name="feed_out",
    )(activ, w_out)


def resid_back_kernel(
    kept,
    got,
    resid,
    cotangent,
    mixed,
    w_o,
    norms,
    grad_resid,
    grad_mixed,
    grad_o,
    vectors,
    total,
):
    step = pl.program_id(0)

    @pl.when(step == 0)
    def _():
        vectors[...] = jnp.zeros_like(vectors)
        total[...] = jnp.zeros_like(total)

    grad = kept[...] + got[...].astype(F32)
    unit, inverse = norm_rows(resid[...])
    vectors[0:1, :] += jnp.sum(grad * unit, 0, keepdims=True)
    vectors[1:2, :] += jnp.sum(grad, 0, keepdims=True)
    value = cotangent[...] + norm_back(grad, unit, inverse, norms[4:5, :])
    grad_resid[...] = value
    low = value.astype(BF16)
    grad_mixed[...] = contract(low, w_o[...], (1, 1)).astype(BF16)
    total[...] += contract(mixed[...], low, (0, 0))
    grad_o[...] = total[...].astype(BF16)


def resid_back(kept, got, resid, cotangent, mixed, w_o, norms):
    rows, width = resid.shape
    inner = mixed.shape[1]
    block = rows // 4
    row_at = lambda i: (i, 0)
    wide = pl.BlockSpec((block, width), row_at)
    return pl.pallas_call(
        resid_back_kernel,
        grid=(rows // block,),
        in_specs=[
            *[wide] * 4,
            pl.BlockSpec((block, inner), row_at),
            pl.BlockSpec(w_o.shape, fixed_at),
            pl.BlockSpec(norms.shape, fixed_at),
        ],
        out_specs=[
            wide,
            pl.BlockSpec((block, inner), row_at),
            pl.BlockSpec(w_o.shape, fixed_at),
            pl.BlockSpec((8, width), fixed_at),
        ],
        out_shape=[
            jax.ShapeDtypeStruct((rows, width), F32),
            jax.ShapeDtypeStruct((rows, inner), BF16),
            jax.ShapeDtypeStruct(w_o.shape, BF16),
            jax.ShapeDtypeStruct((8, width), F32),
        ],
        scratch_shapes=[pltpu.VMEM(w_o.shape, F32)],
        compiler_params=params(24),
        cost_estimate=cost(6),
        name="resid_back",
    )(kept, got, resid, cotangent, mixed, w_o, norms)


def as_row(column):
    out = []
    size = 128
    same = lax.broadcasted_iota(jnp.int32, (size, size), 0) == lax.broadcasted_iota(
        jnp.int32, (size, size), 1
    )
    for at in range(0, column.shape[0], size):
        out.append(jnp.sum(jnp.where(same, column[at : at + size, :], 0.0), 0, keepdims=True))
    return jnp.concatenate(out, 1)


def in_bf16(row):
    parts = []
    for _ in range(3):
        parts.append(row.astype(BF16))
        row = row - parts[-1].astype(F32)
    return parts


def attend_back_kernel(counts, keyvals, queries, grad_mixed, grad_kv, grad_q):
    taken, keys_len = keyvals.shape[:2]
    lat_len, inner = queries.shape[1:]
    media_len = keys_len - lat_len
    size = inner // HEADS
    wide = size * GROUP
    scale = 1.0 / math.sqrt(size)
    key_at = lax.broadcasted_iota(jnp.int32, (keys_len, 1), 0)

    def begin(i, at):
        own = spread(queries[i, :, at : at + wide].astype(F32) * scale, size).astype(BF16)
        grad = spread(grad_mixed[i, :, at : at + wide], size).astype(BF16)
        scores = contract(keyvals[i, :, at : at + wide], own, (1, 1))
        grad_probs = contract(keyvals[i, :, inner + at : inner + at + wide], grad, (1, 1))
        return own, grad, scores, grad_probs

    def weigh(i, scores, grad_probs):
        valid = (key_at < counts[pl.program_id(0) * taken + i]) | (key_at >= media_len)
        scores = jnp.where(valid, scores, NEG)
        expd = jnp.exp(scores - jnp.max(scores, 0, keepdims=True))
        probs = expd * (1.0 / jnp.sum(expd, 0, keepdims=True))
        held = jnp.sum(probs * grad_probs, 0, keepdims=True)
        return probs.astype(BF16), (probs * (grad_probs - held)).astype(BF16)

    def end(i, at, own, grad, probs, low):
        grad_v = contract(probs, grad, (1, 0)).astype(BF16)
        grad_kv[i, :, inner + at : inner + at + wide] = grad_v
        grad_kv[i, :, at : at + wide] = contract(low, own, (1, 0)).astype(BF16)
        back = contract(low, keyvals[i, :, at : at + wide], (0, 0))
        grad_q[i, :, at : at + wide] = (gathered(back, size) * scale).astype(BF16)

    items = [(i, at) for i in range(taken) for at in range(0, inner, wide)]
    ahead, behind = begin(*items[0]), None
    for n, item in enumerate(items):
        own, grad, scores, grad_probs = ahead
        if n + 1 < len(items):
            ahead = begin(*items[n + 1])
        weights = weigh(item[0], scores, grad_probs)
        if behind:
            end(*behind)
        behind = (*item, own, grad, *weights)
    end(*behind)


def weight_back_kernel(
    place,
    grad_kv,
    grad_q,
    turned,
    lat_low,
    w_kv,
    w_q,
    norms,
    grad_o,
    ff_vectors,
    keep,
    send,
    total,
    sums,
    lat_kv,
    lat_q,
    total_q,
):
    step, steps = pl.program_id(0), pl.num_programs(0)
    lat_len, inner = grad_q.shape[1:]
    keys_len = grad_kv.shape[1]
    media_len = keys_len - lat_len

    @pl.when(step == 0)
    def _():
        total[...] = jnp.zeros_like(total)
        sums[...] = jnp.zeros_like(sums)

    both = grad_kv[...].reshape(2 * keys_len, 2 * inner)
    total[...] += contract(turned[0], both, (1, 0))
    sums[...] += jnp.sum(both.astype(F32), 0, keepdims=True)
    for side in range(2):
        here = pl.ds(pl.multiple_of((2 * step + side) * lat_len, lat_len), lat_len)
        lat_kv[here, :] = grad_kv[side, media_len:, :]
        lat_q[here, :] = grad_q[side]

    @pl.when(step == steps - 1)
    def _():
        lat_w = contract(lat_low[...], lat_kv[...], (0, 0))
        lat_wq = contract(lat_low[...], lat_q[...], (0, 0))
        weight, weight_q = w_kv[...].astype(F32), w_q[...].astype(F32)
        lat_sum = jnp.sum(lat_kv[...].astype(F32), 0, keepdims=True)
        lat_sum_q = jnp.sum(lat_q[...].astype(F32), 0, keepdims=True)
        rows = in_bf16(sums[0:1, :] - lat_sum) + in_bf16(lat_sum) + [jnp.zeros((2, 2 * inner), BF16)]
        rows_q = in_bf16(lat_sum_q) + [jnp.zeros((5, inner), BF16)]
        biases = contract(jnp.concatenate(rows, 0), w_kv[...], (1, 1))
        biases_q = contract(jnp.concatenate(rows_q, 0), w_q[...], (1, 1))
        media_bias = jnp.sum(biases[0:3], 0, keepdims=True)
        lat_bias = jnp.sum(biases[3:6], 0, keepdims=True) + jnp.sum(biases_q, 0, keepdims=True)
        media_both = as_row(jnp.sum((total[...] - lat_w) * weight, 1, keepdims=True))
        lat_both = as_row(
            jnp.sum(lat_w * weight, 1, keepdims=True)
            + jnp.sum(lat_wq * weight_q, 1, keepdims=True)
        )
        vectors = [
            (media_both - norms[1:2, :] * media_bias) / norms[0:1, :],
            media_bias,
            (lat_both - norms[3:4, :] * lat_bias) / norms[2:3, :],
            lat_bias,
            ff_vectors[0:2, :],
            jnp.zeros((2, ff_vectors.shape[1]), F32),
        ]
        vectors = jnp.concatenate(vectors, 0).astype(BF16)
        total_q[...] = lat_wq
        me, core = place[0], place[1]
        columns = keep.shape[1]
        kv_rows = total.shape[0] // (2 * columns * PLANE)
        o_rows = grad_o.shape[0] // (2 * columns * PLANE)
        q_rows = kv_rows // 2
        for plane in range(PLANE):
            for column in range(columns):
                chip = me ^ (column * PLANE + plane)
                for out, half in ((keep, core), (send, 1 - core)):
                    at = pl.multiple_of((chip * 2 + half) * kv_rows, kv_rows)
                    out[plane, column, :kv_rows, :] = total[pl.ds(at, kv_rows), :].astype(BF16)
                    value = total_q[pl.ds(at, kv_rows), :].astype(BF16)
                    row = kv_rows
                    out[plane, column, row : row + q_rows, :inner] = value[:q_rows]
                    out[plane, column, row : row + q_rows, inner:] = value[q_rows:]
                    row += q_rows
                    at = pl.multiple_of((chip * 2 + half) * o_rows, o_rows)
                    out[plane, column, row : row + o_rows, :] = grad_o[pl.ds(at, o_rows), :]
                    out[plane, column, row + o_rows :, :] = vectors


def attend_back(counts, keyvals, queries, grad_mixed):
    images, keys_len, wide = keyvals.shape
    lat_len, inner = queries.shape[1:]
    taken = 2
    at = lambda i, c: (i, 0, 0)
    return pl.pallas_call(
        attend_back_kernel,
        grid_spec=pltpu.PrefetchScalarGridSpec(
            num_scalar_prefetch=1,
            grid=(images // taken,),
            in_specs=[
                pl.BlockSpec((taken, keys_len, wide), at),
                pl.BlockSpec((taken, lat_len, inner), at),
                pl.BlockSpec((taken, lat_len, inner), at),
            ],
            out_specs=[
                pl.BlockSpec((taken, keys_len, wide), at),
                pl.BlockSpec((taken, lat_len, inner), at),
            ],
        ),
        out_shape=[
            jax.ShapeDtypeStruct((images, keys_len, wide), BF16),
            jax.ShapeDtypeStruct((images, lat_len, inner), BF16),
        ],
        compiler_params=params(58),
        cost_estimate=cost(15),
        name="attend_back",
    )(counts, keyvals, queries, grad_mixed)


def weight_back(
    place, grad_kv, grad_q, turned, lat_low, w_kv, w_q, norms, grad_o, ff_vectors, columns
):
    images, keys_len, _ = grad_kv.shape
    width = turned.shape[1]
    lat_len, inner = grad_q.shape[1:]
    rows = images * lat_len
    chips = columns * PLANE
    kv_rows, o_rows = width // chips // 2, inner // chips // 2
    pack = (PLANE, columns, kv_rows + kv_rows // 2 + o_rows + PAD, width)
    at = lambda i, c: (i, 0, 0)
    once = pl.Buffered(1)
    return pl.pallas_call(
        weight_back_kernel,
        grid_spec=pltpu.PrefetchScalarGridSpec(
            num_scalar_prefetch=1,
            grid=(images // 2,),
            in_specs=[
                pl.BlockSpec((2, keys_len, 2 * inner), at),
                pl.BlockSpec((2, lat_len, inner), at),
                pl.BlockSpec((1, width, 2 * keys_len), at),
                pl.BlockSpec(lat_low.shape, fixed_at, pipeline_mode=once),
                pl.BlockSpec(w_kv.shape, fixed_at, pipeline_mode=once),
                pl.BlockSpec(w_q.shape, fixed_at, pipeline_mode=once),
                pl.BlockSpec(norms.shape, fixed_at),
                pl.BlockSpec(grad_o.shape, fixed_at, pipeline_mode=once),
                pl.BlockSpec(ff_vectors.shape, fixed_at),
            ],
            out_specs=[
                pl.BlockSpec(pack, whole_at(4), pipeline_mode=once),
                pl.BlockSpec(pack, whole_at(4), pipeline_mode=once),
            ],
            scratch_shapes=[
                pltpu.VMEM(w_kv.shape, F32),
                pltpu.VMEM((8, 2 * inner), F32),
                pltpu.VMEM((rows, 2 * inner), BF16),
                pltpu.VMEM((rows, inner), BF16),
                pltpu.VMEM(w_q.shape, F32),
            ],
        ),
        out_shape=[jax.ShapeDtypeStruct(pack, BF16), jax.ShapeDtypeStruct(pack, BF16)],
        compiler_params=params(58),
        cost_estimate=cost(17),
        name="weight_back",
    )(place, grad_kv, grad_q, turned, lat_low, w_kv, w_q, norms, grad_o, ff_vectors)


def latent_back_kernel(grad_kv, grad_q, latent, grad_resid, w_kv, w_q, norms, latent_grad):
    images, lat_len, width = latent.shape
    rows = images * lat_len
    grad = contract(grad_kv[...].reshape(rows, grad_kv.shape[2]), w_kv[...], (1, 1))
    grad += contract(grad_q[...].reshape(rows, grad_q.shape[2]), w_q[...], (1, 1))
    unit, inverse = norm_rows(latent[...].reshape(rows, width).astype(F32))
    back = norm_back(grad, unit, inverse, norms[2:3, :])
    latent_grad[...] = grad_resid[...] + back.reshape(images, lat_len, width)


def latent_back(grad_kv, grad_q, latent, grad_resid, w_kv, w_q, norms):
    images, lat_len, width = latent.shape
    inner = w_q.shape[1]
    tail = grad_kv.shape[1] // lat_len - 1
    block = images // 2
    at = lambda i: (i, 0, 0)
    return pl.pallas_call(
        latent_back_kernel,
        grid=(images // block,),
        in_specs=[
            pl.BlockSpec((block, lat_len, 2 * inner), lambda i: (i, tail, 0)),
            pl.BlockSpec((block, lat_len, inner), at),
            pl.BlockSpec((block, lat_len, width), at),
            pl.BlockSpec((block, lat_len, width), at),
            pl.BlockSpec(w_kv.shape, fixed_at),
            pl.BlockSpec(w_q.shape, fixed_at),
            pl.BlockSpec(norms.shape, fixed_at),
        ],
        out_specs=pl.BlockSpec((block, lat_len, width), at),
        out_shape=jax.ShapeDtypeStruct((images, lat_len, width), F32),
        compiler_params=params(32),
        cost_estimate=cost(4),
        name="latent_back",
    )(grad_kv, grad_q, latent, grad_resid, w_kv, w_q, norms)


def media_back_kernel(media, grad_kv, norms, w_kv, *refs):
    out, grad = refs[-2:]
    grad[...] = contract(grad_kv[0], w_kv[...], (1, 1))
    for at in range(0, media.shape[1], ROWS):
        unit, inverse = norm_rows(media[0, at : at + ROWS, :].astype(F32))
        out[0, at : at + ROWS, :] = norm_back(grad[at : at + ROWS, :], unit, inverse, norms[0:1, :])


def media_back(media, grad_kv, norms, w_kv, first, run, into=()):
    images, media_len, width = media.shape
    inner2 = w_kv.shape[1]
    at = lambda i: (i + first, 0, 0)
    return pl.pallas_call(
        media_back_kernel,
        grid=(run,),
        in_specs=[
            pl.BlockSpec((1, media_len, width), at),
            pl.BlockSpec((1, media_len, inner2), at),
            pl.BlockSpec(norms.shape, fixed_at),
            pl.BlockSpec(w_kv.shape, fixed_at),
            *[pl.BlockSpec(memory_space=pl.ANY) for _ in into],
        ],
        out_specs=pl.BlockSpec((1, media_len, width), at),
        out_shape=jax.ShapeDtypeStruct((images, media_len, width), F32),
        input_output_aliases={4 + i: i for i in range(len(into))},
        scratch_shapes=[pltpu.VMEM((media_len, width), F32)],
        compiler_params=params(32),
        cost_estimate=cost(0.5),
        name="media_back",
    )(media, grad_kv, norms, w_kv, *into)


def fold_rows(value):
    half = value.shape[0] // 2
    return jnp.concatenate([value[:half], value[half:]], 1)


def shards(
    dp,
    media_tokens,
    patch_counts,
    latents,
    media_gain,
    media_bias,
    latent_gain,
    latent_bias,
    query_weight,
    keyval_weight,
    outproj_weight,
    ff_gain,
    ff_bias,
    ff_in_weight,
    ff_out_weight,
    cotangent,
):
    me, core = lax.axis_index("dp"), lax.axis_index("rep")
    place = jnp.stack([me, core]).astype(jnp.int32)
    columns = dp // PLANE
    images, _, width = media_tokens.shape
    lat_len = latents.shape[1]
    inner = query_weight.shape[1]
    part = width // dp
    slot = ff_in_weight.shape[1] // dp // 2
    kv_rows, o_rows = part // 2, inner // dp // 2
    flat = (images * lat_len, width)

    def swap(value, bits):
        return lax.ppermute(value, "dp", [(i, i ^ bits) for i in range(dp)])

    def other(value):
        return lax.ppermute(value, "rep", [(0, 1), (1, 0)])

    def mine(value, axis):
        return lax.dynamic_index_in_dim(value, core, axis, keepdims=False)

    def down(value):
        return [value] + [swap(value, c * PLANE) for c in range(1, columns)]

    def across(values):
        return [values[0]] + [swap(values[p], p) for p in range(1, PLANE)]

    def down_sums(values):
        return [values[0]] + [swap(values[c], c * PLANE) for c in range(1, columns)]

    norms = jnp.stack([media_gain, media_bias, latent_gain, latent_bias, ff_gain, ff_bias])
    norms = lax.dynamic_update_slice(jnp.zeros((PAD, width), BF16), norms, (0, me * part))
    attn = [
        mine(keyval_weight.reshape(2, kv_rows, width), 0),
        fold_rows(mine(query_weight.reshape(2, kv_rows, inner), 0)),
        mine(outproj_weight.reshape(2, o_rows, width), 0),
        norms,
    ]
    attn = jnp.stack(down(jnp.concatenate(attn, 0)))
    ffout = mine(ff_out_weight.reshape(2, slot, width), 0)
    ffin = mine(ff_in_weight.reshape(part, dp, 2, slot), 2).reshape(part, dp * slot)
    cut = ffin.shape[1] // 2
    ffin = jnp.concatenate([ffin[:, :cut], ffin[:, cut:]], 0)
    attn, ffout, ffin = tie(attn, ffout, ffin)
    attn = [attn] + [swap(attn, p) for p in range(1, PLANE)]
    w_ffout = lax.all_gather(ffout, "dp", axis=0, tiled=True)
    ffin = jnp.stack([ffin, swap(ffin, 2 * PLANE)])
    got = swap(ffin, PLANE)
    w_kv, w_q, w_o, norms = in_order(place, attn, [other(value) for value in attn], inner)
    lo, hi = [
        jnp.stack([ffin[0, rows], got[0, rows], ffin[1, rows], got[1, rows]])
        for rows in (slice(0, part), slice(part, 2 * part))
    ]
    dout = cotangent.astype(BF16).reshape(flat)
    douts = dout, other(dout)

    w_kv, lo, hi = tie(w_kv, lo, hi)
    lo, hi = {0: lo, 2: swap(lo, 2)}, {0: hi, 1: swap(hi, 1)}
    run = images // 2
    held = attend(patch_counts, media_tokens, latents, norms, w_kv, w_q, 0, run)
    held, lo, hi = tie(held, lo, hi)
    lo[1], lo[3] = swap(lo[0], 1), swap(lo[2], 1)
    hi[2], hi[3] = swap(hi[0], 2), swap(hi[1], 2)
    turned, lat_low, keyvals, queries, mixed = attend(
        patch_counts, media_tokens, latents, norms, w_kv, w_q, run, images - run, held
    )
    mixed, lo, hi = tie(mixed.reshape(-1, inner), lo, hi)
    lo, hi = [lo[p] for p in range(PLANE)], [hi[p] for p in range(PLANE)]
    resid, low = add_branch(mixed, latents.reshape(flat), w_o, norms)

    activ, slope, low_t, dout, w_ffin, *grads = feed_forward(
        place, (low, other(low)), douts, lo, hi, slot
    )
    out_sum = grads[0], swap(grads[1], 1), grads[2], swap(grads[3], 2)
    *grads, kept, sent = feed_back(place, dout, low_t, w_ffin, w_ffout, slope, columns, part)
    kept, out_sum = tie(kept, out_sum)
    grad_resid, grad_mixed, grad_o, ff_vectors = resid_back(
        kept, other(sent), resid, cotangent.reshape(flat), mixed, w_o, norms
    )
    grad_mixed, out_sum = tie(grad_mixed, out_sum)
    out_sum = fold_first(*out_sum)
    grad_mixed, out_sum = tie(grad_mixed, out_sum)
    out_sum = out_sum[0], swap(out_sum[1], 2), out_sum[2], swap(out_sum[3], 1)
    in_sum = grads[0], swap(grads[1], 1), grads[2], swap(grads[3], 2)
    grad_kv, grad_q = attend_back(
        patch_counts, keyvals, queries, grad_mixed.reshape(images, lat_len, inner)
    )
    grad_kv, grad_q, out_sum, in_sum = tie(grad_kv, grad_q, out_sum, in_sum)
    keep, send = fold_second(*out_sum)
    in_sum = fold_first(*in_sum)
    grad_q, keep, send, in_sum = tie(grad_q, keep, send, in_sum)
    out_sum = keep, swap(send, PLANE)
    in_sum = in_sum[0], swap(in_sum[1], 2), in_sum[2], swap(in_sum[3], 1)
    keep, send = weight_back(
        place,
        grad_kv,
        grad_q,
        turned,
        lat_low.reshape(flat),
        w_kv,
        w_q,
        norms,
        grad_o,
        ff_vectors,
        columns,
    )
    keep, send, out_sum, in_sum = tie(keep, send, out_sum, in_sum)
    got = other(send)
    in_keep, in_send = fold_second(*in_sum)
    held, passed = fold_third(*out_sum)
    keep, in_send, passed = tie(keep, in_send, passed)
    in_sum = in_keep, swap(in_send, PLANE)
    out_sum = held, swap(passed, 2 * PLANE)
    attn = add_both(keep, got)
    attn = across(attn)
    grad_kv, attn[0] = tie(grad_kv, attn[0])
    done = media_back(media_tokens, grad_kv, norms, w_kv, 0, run)
    done, in_sum = tie(done, in_sum)
    held, passed = fold_third(*in_sum)
    done, held, passed = tie(done, held, passed)
    in_sum = held, swap(passed, 2 * PLANE)
    media_grad = media_back(media_tokens, grad_kv, norms, w_kv, run, images - run, (done,))
    media_grad, attn = tie(media_grad, attn)
    attn = fold(attn)
    attn, activ, grad_q, in_sum, out_sum = tie(attn, activ, grad_q, in_sum, out_sum)
    attn = down_sums(attn)
    latent_grad = latent_back(
        grad_kv, grad_q, latents, grad_resid.reshape(latents.shape), w_kv, w_q, norms
    )
    share, sent = feed_out(activ, w_ffout)
    own_in, own_out = [value[0].astype(F32) + value[1].astype(F32) for value in (in_sum, out_sum)]
    grad_ffin, grad_ffout = final_ff(place, own_in, other(own_in), own_out, other(own_out))
    sent, attn, grad_ffin, latent_grad = tie(sent, attn, grad_ffin, latent_grad)
    own = functools.reduce(jnp.add, [value.astype(F32) for value in attn])
    new_latents = resid + (share + other(sent).astype(F32))
    rows = own.shape[0] - PAD
    vectors = lax.dynamic_slice(own[rows:], (0, me * part), (6, part))
    own = own[:rows]
    grad_wkv, grad_wq, grad_wo = final_attn(place, own, other(own), inner, kv_rows, o_rows)
    return (
        new_latents.reshape(latents.shape),
        media_grad,
        latent_grad,
        vectors[0],
        vectors[1],
        vectors[2],
        vectors[3],
        grad_wq,
        grad_wkv,
        grad_wo,
        vectors[4],
        vectors[5],
        grad_ffin,
        grad_ffout,
    )


def norm_apply(values, gain, bias):
    centre = jnp.mean(values, -1, keepdims=True)
    centred = values - centre
    inverse = lax.rsqrt(jnp.mean(centred * centred, -1, keepdims=True) + EPS)
    unit = centred * inverse
    return (unit * gain.astype(jnp.float32) + bias.astype(jnp.float32), unit, inverse)


def plain_norm_grad(grad_normed, unit, inverse, gain):
    scaled = grad_normed * gain.astype(jnp.float32)
    return inverse * (
        scaled
        - jnp.mean(scaled, -1, keepdims=True)
        - unit * jnp.mean(scaled * unit, -1, keepdims=True)
    )


def row_total(values):
    return jnp.sum(values.reshape(-1, values.shape[-1]), axis=0)


def gelu_exact(values):
    return jax.nn.gelu(values, approximate=False)


def masked_scores(query_heads, key_heads, valid, scale):
    raw = (
        jnp.einsum("iqhe,ikhe->ihqk", query_heads, key_heads, preferred_element_type=jnp.float32)
        * scale
    )
    return jnp.where(valid[:, None, None, :], raw, jnp.float32(-1e30))


def plain_shards(
    media_tokens,
    patch_counts,
    latents,
    media_gain,
    media_bias,
    latent_gain,
    latent_bias,
    query_weight,
    keyval_weight,
    outproj_weight,
    ff_gain,
    ff_bias,
    ff_in_weight,
    ff_out_weight,
    cotangent,
):
    f32 = jnp.float32
    bf16 = jnp.bfloat16
    whole = (
        lax.all_gather(media_gain, "dp", axis=0, tiled=True),
        lax.all_gather(media_bias, "dp", axis=0, tiled=True),
        lax.all_gather(latent_gain, "dp", axis=0, tiled=True),
        lax.all_gather(latent_bias, "dp", axis=0, tiled=True),
        lax.all_gather(query_weight, "dp", axis=0, tiled=True),
        lax.all_gather(keyval_weight, "dp", axis=0, tiled=True),
        lax.all_gather(outproj_weight, "dp", axis=0, tiled=True),
        lax.all_gather(ff_gain, "dp", axis=0, tiled=True),
        lax.all_gather(ff_bias, "dp", axis=0, tiled=True),
        lax.all_gather(ff_in_weight, "dp", axis=0, tiled=True),
        lax.all_gather(ff_out_weight, "dp", axis=0, tiled=True),
    )
    (
        gain_media,
        bias_media,
        gain_latent,
        bias_latent,
        w_query,
        w_keyval,
        w_outproj,
        gain_ff,
        bias_ff,
        w_ffin,
        w_ffout,
    ) = whole
    images, media_len, width = media_tokens.shape
    lat_len = latents.shape[1]
    keys_len = media_len + lat_len
    inner_width = w_query.shape[1]
    head_size = inner_width // HEADS
    scale = 1.0 / math.sqrt(head_size)
    media_f = media_tokens.astype(f32)
    latent_f = latents.astype(f32)
    media_normed, media_unit, media_inv = norm_apply(media_f, gain_media, bias_media)
    latent_normed, latent_unit, latent_inv = norm_apply(latent_f, gain_latent, bias_latent)
    media_low = media_normed.astype(bf16)
    latent_low = latent_normed.astype(bf16)
    queries = jnp.einsum("ild,de->ile", latent_low, w_query, preferred_element_type=f32).astype(
        bf16
    )
    key_input = jnp.concatenate([media_low, latent_low], axis=1)
    keyvals = jnp.einsum("ikd,de->ike", key_input, w_keyval, preferred_element_type=f32).astype(
        bf16
    )
    key_heads = keyvals[:, :, :inner_width].reshape(images, keys_len, HEADS, head_size)
    value_heads = keyvals[:, :, inner_width:].reshape(images, keys_len, HEADS, head_size)
    query_heads = queries.reshape(images, lat_len, HEADS, head_size)
    positions = jnp.arange(keys_len, dtype=jnp.int32)
    valid = (positions[None, :] < patch_counts[:, None]) | (positions[None, :] >= media_len)
    scores = masked_scores(query_heads, key_heads, valid, scale)
    top = jnp.max(scores, -1, keepdims=True)
    expd = jnp.exp(scores - top)
    total = jnp.sum(expd, -1, keepdims=True)
    probs = expd / total
    log_total = top + jnp.log(total)
    mixed = jnp.einsum(
        "ihqk,ikhe->iqhe", probs.astype(bf16), value_heads, preferred_element_type=f32
    )
    mixed = mixed.reshape(images, lat_len, inner_width).astype(bf16)
    branch = jnp.einsum("ile,ed->ild", mixed, w_outproj, preferred_element_type=f32)
    resid = latent_f + branch
    ff_normed, ff_unit, ff_inv = norm_apply(resid, gain_ff, bias_ff)
    ff_low = ff_normed.astype(bf16)
    pre_act = jnp.einsum("ild,df->ilf", ff_low, w_ffin, preferred_element_type=f32)
    activ, gelu_pull = jax.vjp(gelu_exact, pre_act)
    activ_low = activ.astype(bf16)
    new_latents = resid + jnp.einsum("ilf,fd->ild", activ_low, w_ffout, preferred_element_type=f32)
    again = (
        lax.all_gather(media_gain, "dp", axis=0, tiled=True),
        lax.all_gather(media_bias, "dp", axis=0, tiled=True),
        lax.all_gather(latent_gain, "dp", axis=0, tiled=True),
        lax.all_gather(latent_bias, "dp", axis=0, tiled=True),
        lax.all_gather(query_weight, "dp", axis=0, tiled=True),
        lax.all_gather(keyval_weight, "dp", axis=0, tiled=True),
        lax.all_gather(outproj_weight, "dp", axis=0, tiled=True),
        lax.all_gather(ff_gain, "dp", axis=0, tiled=True),
        lax.all_gather(ff_bias, "dp", axis=0, tiled=True),
        lax.all_gather(ff_in_weight, "dp", axis=0, tiled=True),
        lax.all_gather(ff_out_weight, "dp", axis=0, tiled=True),
    )
    (
        gain_media_b,
        bias_media_b,
        gain_latent_b,
        bias_latent_b,
        w_query_b,
        w_keyval_b,
        w_outproj_b,
        gain_ff_b,
        bias_ff_b,
        w_ffin_b,
        w_ffout_b,
    ) = again
    grad_out_low = cotangent.astype(bf16)
    grad_ffout = jnp.einsum("ilf,ild->fd", activ_low, grad_out_low, preferred_element_type=f32)
    grad_activ = jnp.einsum("ild,fd->ilf", grad_out_low, w_ffout_b, preferred_element_type=f32)
    (grad_pre,) = gelu_pull(grad_activ)
    grad_pre_low = grad_pre.astype(bf16)
    grad_ffin = jnp.einsum("ild,ilf->df", ff_low, grad_pre_low, preferred_element_type=f32)
    grad_ffnormed = jnp.einsum("ilf,df->ild", grad_pre_low, w_ffin_b, preferred_element_type=f32)
    grad_gain_ff = row_total(grad_ffnormed * ff_unit)
    grad_bias_ff = row_total(grad_ffnormed)
    grad_resid = cotangent + plain_norm_grad(grad_ffnormed, ff_unit, ff_inv, gain_ff_b)
    grad_resid_low = grad_resid.astype(bf16)
    grad_outproj = jnp.einsum("ile,ild->ed", mixed, grad_resid_low, preferred_element_type=f32)
    grad_mixed = jnp.einsum(
        "ild,ed->ile", grad_resid_low, w_outproj_b, preferred_element_type=f32
    ).astype(bf16)
    grad_mixed_heads = grad_mixed.reshape(images, lat_len, HEADS, head_size)
    scores_again = masked_scores(query_heads, key_heads, valid, scale)
    probs_again = jnp.exp(scores_again - log_total)
    grad_probs = jnp.einsum(
        "iqhe,ikhe->ihqk", grad_mixed_heads, value_heads, preferred_element_type=f32
    )
    grad_scores = probs_again * (grad_probs - jnp.sum(probs_again * grad_probs, -1, keepdims=True))
    grad_scores_low = grad_scores.astype(bf16)
    grad_queries = (
        jnp.einsum("ihqk,ikhe->iqhe", grad_scores_low, key_heads, preferred_element_type=f32)
        * scale
    )
    grad_queries = grad_queries.reshape(images, lat_len, inner_width).astype(bf16)
    grad_keys = (
        jnp.einsum("ihqk,iqhe->ikhe", grad_scores_low, query_heads, preferred_element_type=f32)
        * scale
    )
    grad_values = jnp.einsum(
        "ihqk,iqhe->ikhe", probs_again.astype(bf16), grad_mixed_heads, preferred_element_type=f32
    )
    grad_keyvals = jnp.concatenate(
        [
            grad_keys.reshape(images, keys_len, inner_width),
            grad_values.reshape(images, keys_len, inner_width),
        ],
        axis=-1,
    ).astype(bf16)
    grad_qweight = jnp.einsum("ild,ile->de", latent_low, grad_queries, preferred_element_type=f32)
    grad_kvweight = jnp.einsum("ikd,ike->de", key_input, grad_keyvals, preferred_element_type=f32)
    grad_key_input = jnp.einsum("ike,de->ikd", grad_keyvals, w_keyval_b, preferred_element_type=f32)
    grad_latnormed = jnp.einsum("ile,de->ild", grad_queries, w_query_b, preferred_element_type=f32)
    grad_latnormed = grad_latnormed + grad_key_input[:, media_len:]
    grad_medianormed = grad_key_input[:, :media_len]
    media_grad = plain_norm_grad(grad_medianormed, media_unit, media_inv, gain_media_b)
    latent_grad = grad_resid + plain_norm_grad(grad_latnormed, latent_unit, latent_inv, gain_latent_b)
    grad_gain_media = row_total(grad_medianormed * media_unit)
    grad_bias_media = row_total(grad_medianormed)
    grad_gain_latent = row_total(grad_latnormed * latent_unit)
    grad_bias_latent = row_total(grad_latnormed)
    owned = (
        lax.psum_scatter(
            grad_gain_media.astype(jnp.bfloat16), "dp", scatter_dimension=0, tiled=True
        ).astype(jnp.float32),
        lax.psum_scatter(
            grad_bias_media.astype(jnp.bfloat16), "dp", scatter_dimension=0, tiled=True
        ).astype(jnp.float32),
        lax.psum_scatter(
            grad_gain_latent.astype(jnp.bfloat16), "dp", scatter_dimension=0, tiled=True
        ).astype(jnp.float32),
        lax.psum_scatter(
            grad_bias_latent.astype(jnp.bfloat16), "dp", scatter_dimension=0, tiled=True
        ).astype(jnp.float32),
        lax.psum_scatter(
            grad_qweight.astype(jnp.bfloat16), "dp", scatter_dimension=0, tiled=True
        ).astype(jnp.float32),
        lax.psum_scatter(
            grad_kvweight.astype(jnp.bfloat16), "dp", scatter_dimension=0, tiled=True
        ).astype(jnp.float32),
        lax.psum_scatter(
            grad_outproj.astype(jnp.bfloat16), "dp", scatter_dimension=0, tiled=True
        ).astype(jnp.float32),
        lax.psum_scatter(
            grad_gain_ff.astype(jnp.bfloat16), "dp", scatter_dimension=0, tiled=True
        ).astype(jnp.float32),
        lax.psum_scatter(
            grad_bias_ff.astype(jnp.bfloat16), "dp", scatter_dimension=0, tiled=True
        ).astype(jnp.float32),
        lax.psum_scatter(
            grad_ffin.astype(jnp.bfloat16), "dp", scatter_dimension=0, tiled=True
        ).astype(jnp.float32),
        lax.psum_scatter(
            grad_ffout.astype(jnp.bfloat16), "dp", scatter_dimension=0, tiled=True
        ).astype(jnp.float32),
    )
    summed = (
        lax.psum(owned[0].astype(jnp.bfloat16), "rep").astype(jnp.float32),
        lax.psum(owned[1].astype(jnp.bfloat16), "rep").astype(jnp.float32),
        lax.psum(owned[2].astype(jnp.bfloat16), "rep").astype(jnp.float32),
        lax.psum(owned[3].astype(jnp.bfloat16), "rep").astype(jnp.float32),
        lax.psum(owned[4].astype(jnp.bfloat16), "rep").astype(jnp.float32),
        lax.psum(owned[5].astype(jnp.bfloat16), "rep").astype(jnp.float32),
        lax.psum(owned[6].astype(jnp.bfloat16), "rep").astype(jnp.float32),
        lax.psum(owned[7].astype(jnp.bfloat16), "rep").astype(jnp.float32),
        lax.psum(owned[8].astype(jnp.bfloat16), "rep").astype(jnp.float32),
        lax.psum(owned[9].astype(jnp.bfloat16), "rep").astype(jnp.float32),
        lax.psum(owned[10].astype(jnp.bfloat16), "rep").astype(jnp.float32),
    )
    (
        sum_gain_media,
        sum_bias_media,
        sum_gain_latent,
        sum_bias_latent,
        sum_query,
        sum_keyval,
        sum_outproj,
        sum_gain_ff,
        sum_bias_ff,
        sum_ffin,
        sum_ffout,
    ) = summed
    return (
        new_latents,
        media_grad,
        latent_grad,
        sum_gain_media,
        sum_bias_media,
        sum_gain_latent,
        sum_bias_latent,
        sum_query,
        sum_keyval,
        sum_outproj,
        sum_gain_ff,
        sum_bias_ff,
        sum_ffin,
        sum_ffout,
    )


def solution(mesh):
    dp, rep = mesh.shape["dp"], mesh.shape["rep"]

    def program(*arrays):
        if rep != 2 or dp != PLANE * PLANE:
            return plain_shards(*arrays)
        return shards(dp, *arrays)

    return jax.shard_map(
        program,
        mesh=mesh,
        in_specs=(
            P(("dp", "rep"), None, None),
            P(("dp", "rep")),
            P(("dp", "rep"), None, None),
            P("dp"),
            P("dp"),
            P("dp"),
            P("dp"),
            P("dp", None),
            P("dp", None),
            P("dp", None),
            P("dp"),
            P("dp"),
            P("dp", None),
            P("dp", None),
            P(("dp", "rep"), None, None),
        ),
        out_specs=(
            P(("dp", "rep"), None, None),
            P(("dp", "rep"), None, None),
            P(("dp", "rep"), None, None),
            P("dp"),
            P("dp"),
            P("dp"),
            P("dp"),
            P("dp", None),
            P("dp", None),
            P("dp", None),
            P("dp"),
            P("dp"),
            P("dp", None),
            P("dp", None),
        ),
        check_vma=False,
    )
```

```python
import functools
import math

import jax
import jax.numpy as jnp
from jax import lax
from jax.experimental import pallas as pl
from jax.experimental.pallas import tpu as pltpu
from jax.sharding import PartitionSpec as P

HEADS = 8
GROUP = 4
EPS = 1e-05
NEG = -1e30
ROWS = 64
FF_TILE = 512
PLANE = 4
PAD = 8
F32 = jnp.float32
BF16 = jnp.bfloat16


def cost(us):
    return pl.CostEstimate(flops=int(us * 1.1e9), bytes_accessed=1 << 18, transcendentals=0)


def contract(a, b, over):
    return lax.dot_general(a, b, ((over[:1], over[1:]), ((), ())), preferred_element_type=F32)


def norm_rows(values):
    centred = values - jnp.mean(values, -1, keepdims=True)
    inverse = lax.rsqrt(jnp.mean(centred * centred, -1, keepdims=True) + EPS)
    return centred * inverse, inverse


def norm_back(grad, unit, inverse, gain):
    scaled = grad * gain
    return inverse * (
        scaled
        - jnp.mean(scaled, -1, keepdims=True)
        - unit * jnp.mean(scaled * unit, -1, keepdims=True)
    )


def spread(value, size):
    lane = lax.broadcasted_iota(jnp.int32, value.shape, 1) // size
    value = value.astype(F32)
    return jnp.concatenate([jnp.where(lane == h, value, 0.0) for h in range(GROUP)], 0)


def gathered(value, size):
    rows = value.shape[0] // GROUP
    lane = lax.broadcasted_iota(jnp.int32, (rows, value.shape[1]), 1) // size
    out = jnp.zeros((rows, value.shape[1]), F32)
    for h in range(GROUP):
        out = jnp.where(lane == h, value[h * rows : (h + 1) * rows], out)
    return out


def tie(*values):
    return lax.optimization_barrier(values)


def params(mib):
    return pltpu.CompilerParams(vmem_limit_bytes=mib << 20)


def image_at(i, c):
    return (i, 0, 0)


def fixed_at(*_):
    return (0, 0)


def order_kernel(place, *refs):
    sides = refs[:PLANE], refs[PLANE : 2 * PLANE]
    w_kv, w_q, w_o, norms = refs[2 * PLANE :]
    me, core = place[0], place[1]
    columns = sides[0][0].shape[0]
    chips = columns * PLANE
    kv_rows, o_rows = w_kv.shape[0] // chips // 2, w_o.shape[0] // chips // 2
    q_rows, inner = kv_rows // 2, w_q.shape[1]
    total = jnp.zeros(norms.shape, F32)
    for plane in range(PLANE):
        for column in range(columns):
            chip = me ^ (column * PLANE + plane)
            for side in range(2):
                block = sides[side][plane]
                half = core if side == 0 else 1 - core
                at = pl.multiple_of((chip * 2 + half) * kv_rows, kv_rows)
                w_kv[pl.ds(at, kv_rows), :] = block[column, :kv_rows, :]
                rest = block[column, kv_rows : kv_rows + q_rows, :]
                w_q[pl.ds(at, q_rows), :] = rest[:, :inner]
                w_q[pl.ds(pl.multiple_of(at + q_rows, q_rows), q_rows), :] = rest[:, inner:]
                at = pl.multiple_of((chip * 2 + half) * o_rows, o_rows)
                w_o[pl.ds(at, o_rows), :] = block[
                    column, kv_rows + q_rows : kv_rows + q_rows + o_rows, :
                ]
            total += sides[0][plane][column, kv_rows + q_rows + o_rows :, :].astype(F32)
    norms[...] = total


def in_order(place, own, other, inner):
    columns, _, width = own[0].shape
    return pl.pallas_call(
        order_kernel,
        grid_spec=pltpu.PrefetchScalarGridSpec(
            num_scalar_prefetch=1,
            grid=(1,),
            in_specs=[
                pl.BlockSpec(value.shape, lambda t, c: (0, 0, 0)) for value in (*own, *other)
            ],
            out_specs=[
                pl.BlockSpec((width, 2 * inner), fixed_at),
                pl.BlockSpec((width, inner), fixed_at),
                pl.BlockSpec((inner, width), fixed_at),
                pl.BlockSpec((8, width), fixed_at),
            ],
        ),
        out_shape=[
            jax.ShapeDtypeStruct((width, 2 * inner), BF16),
            jax.ShapeDtypeStruct((width, inner), BF16),
            jax.ShapeDtypeStruct((inner, width), BF16),
            jax.ShapeDtypeStruct((8, width), F32),
        ],
        compiler_params=params(24),
        cost_estimate=cost(1),
        name="in_order",
    )(place, *own, *other)


def whole_at(rank):
    return lambda *_: (0,) * rank


def small(kernel, values, outs, us, name):
    return pl.pallas_call(
        kernel,
        grid=(1,),
        in_specs=[pl.BlockSpec(value.shape, whole_at(value.ndim)) for value in values],
        out_specs=[pl.BlockSpec(shape, whole_at(len(shape))) for shape in outs],
        out_shape=[jax.ShapeDtypeStruct(shape, BF16) for shape in outs],
        compiler_params=params(20),
        cost_estimate=cost(us),
        name=name,
    )(*values)


def added(one, two):
    return (one.astype(F32) + two.astype(F32)).astype(BF16)


def fold_kernel(*refs):
    for column in range(len(refs) - PLANE):
        total = refs[0][column].astype(F32)
        for plane in range(1, PLANE):
            total += refs[plane][column].astype(F32)
        refs[PLANE + column][...] = total.astype(BF16)


def fold(values):
    columns = values[0].shape[0]
    return small(fold_kernel, values, [values[0].shape[1:]] * columns, 2, "fold")


def first_kernel(keep0, got0, keep1, got1, held0, pass0, held1, pass1):
    held0[...] = added(keep0[0], got0[0])
    pass0[...] = added(keep0[1], got0[1])
    held1[...] = added(keep1[0], got1[0])
    pass1[...] = added(keep1[1], got1[1])


def fold_first(keep0, got0, keep1, got1):
    values = keep0, got0, keep1, got1
    return small(first_kernel, values, [keep0.shape[1:]] * 4, 2, "fold_first")


def second_kernel(held0, got0, held1, got1, keep, send):
    half = held0.shape[1]
    for i in range(2):
        for out, column in ((keep, 2 * i), (send, 2 * i + 1)):
            out[i, :half, :] = added(held0[column], got0[column])
            out[i, half:, :] = added(held1[column], got1[column])


def fold_second(held0, got0, held1, got1):
    values = held0, got0, held1, got1
    shape = (2, 2 * held0.shape[1], held0.shape[2])
    return small(second_kernel, values, [shape] * 2, 2, "fold_second")


def third_kernel(keep, got, held, passed):
    held[...] = added(keep[0], got[0])
    passed[...] = added(keep[1], got[1])


def fold_third(keep, got):
    return small(third_kernel, (keep, got), [keep.shape[1:]] * 2, 0.5, "fold_third")


def both_kernel(keep, got, *outs):
    for plane, out in enumerate(outs):
        out[...] = (keep[plane].astype(F32) + got[plane].astype(F32)).astype(BF16)


def add_both(keep, got):
    tail = keep.shape[1:]
    whole = lambda t: (0, 0, 0, 0)
    return pl.pallas_call(
        both_kernel,
        grid=(1,),
        in_specs=[pl.BlockSpec(keep.shape, whole), pl.BlockSpec(keep.shape, whole)],
        out_specs=[pl.BlockSpec(tail, lambda t: (0, 0, 0)) for _ in range(PLANE)],
        out_shape=[jax.ShapeDtypeStruct(tail, BF16) for _ in range(PLANE)],
        compiler_params=params(16),
        cost_estimate=cost(2),
        name="add_both",
    )(keep, got)


def final_ff_kernel(place, own_in, other_in, own_out, other_out, grad_in, grad_out):
    first = place[1] == 0
    slot = own_out.shape[0]
    for chip in range(own_in.shape[1] // slot):
        here = slice(chip * slot, (chip + 1) * slot)
        one, two = own_in[:, here], other_in[:, here]
        at = 2 * chip * slot
        grad_in[:, at : at + slot] = jnp.where(first, one, two)
        grad_in[:, at + slot : at + 2 * slot] = jnp.where(first, two, one)
    grad_out[:slot, :] = jnp.where(first, own_out[...], other_out[...])
    grad_out[slot:, :] = jnp.where(first, other_out[...], own_out[...])


def final_ff(place, own_in, other_in, own_out, other_out):
    values = own_in, other_in, own_out, other_out
    shapes = (own_in.shape[0], 2 * own_in.shape[1]), (2 * own_out.shape[0], own_out.shape[1])
    return pl.pallas_call(
        final_ff_kernel,
        grid_spec=pltpu.PrefetchScalarGridSpec(
            num_scalar_prefetch=1,
            grid=(1,),
            in_specs=[pl.BlockSpec(value.shape, fixed_at) for value in values],
            out_specs=[pl.BlockSpec(shape, fixed_at) for shape in shapes],
        ),
        out_shape=[jax.ShapeDtypeStruct(shape, F32) for shape in shapes],
        compiler_params=params(16),
        cost_estimate=cost(2),
        name="final_ff",
    )(place, *values)


def final_attn_kernel(place, own, other, grad_kv, grad_q, grad_o):
    kv_rows, o_rows = grad_kv.shape[0] // 2, grad_o.shape[0] // 2
    q_rows, inner = kv_rows // 2, grad_q.shape[1]
    first = place[1] == 0
    for half in range(2):
        value = jnp.where(first == (half == 0), own[...], other[...])
        at = half * kv_rows
        grad_kv[at : at + kv_rows, :] = value[:kv_rows]
        rest = value[kv_rows : kv_rows + q_rows]
        grad_q[at : at + q_rows, :] = rest[:, :inner]
        grad_q[at + q_rows : at + kv_rows, :] = rest[:, inner:]
        grad_o[half * o_rows : (half + 1) * o_rows, :] = value[
            kv_rows + q_rows : kv_rows + q_rows + o_rows
        ]


def final_attn(place, own, other, inner, kv_rows, o_rows):
    width = own.shape[1]
    shapes = (2 * kv_rows, width), (2 * kv_rows, inner), (2 * o_rows, width)
    return pl.pallas_call(
        final_attn_kernel,
        grid_spec=pltpu.PrefetchScalarGridSpec(
            num_scalar_prefetch=1,
            grid=(1,),
            in_specs=[pl.BlockSpec(own.shape, fixed_at), pl.BlockSpec(own.shape, fixed_at)],
            out_specs=[pl.BlockSpec(shape, fixed_at) for shape in shapes],
        ),
        out_shape=[jax.ShapeDtypeStruct(shape, F32) for shape in shapes],
        compiler_params=params(16),
        cost_estimate=cost(2),
        name="final_attn",
    )(place, own, other)


def attend_kernel(counts, media, latent, norms, w_kv, w_q, *refs):
    turned, lat_low, keyvals, queries, mixed, key_input = refs[-6:]
    media_len, lat_len = media.shape[1], latent.shape[1]
    keys_len = media_len + lat_len
    inner = w_q.shape[1]
    size = inner // HEADS
    wide = size * GROUP
    for at in range(0, media_len, ROWS):
        unit, _ = norm_rows(media[0, at : at + ROWS, :].astype(F32))
        key_input[at : at + ROWS, :] = (unit * norms[0:1, :] + norms[1:2, :]).astype(BF16)
    unit, _ = norm_rows(latent[0].astype(F32))
    low = (unit * norms[2:3, :] + norms[3:4, :]).astype(BF16)
    key_input[media_len:, :] = low
    lat_low[0] = low
    query = contract(low, w_q[...], (1, 0)).astype(BF16)
    queries[0] = query
    keyvals[0] = contract(key_input[...], w_kv[...], (1, 0)).astype(BF16)
    for side in range(2):

        @pl.when(pl.program_id(0) % 2 == side)
        def _(side=side):
            turned[0, :, side * keys_len : (side + 1) * keys_len] = key_input[...].T

    key_at = lax.broadcasted_iota(jnp.int32, (1, keys_len), 1)
    valid = (key_at < counts[pl.program_id(0)]) | (key_at >= media_len)
    for at in range(0, inner, wide):
        own = spread(query[:, at : at + wide].astype(F32) * (1.0 / math.sqrt(size)), size)
        scores = contract(own.astype(BF16), keyvals[0, :, at : at + wide], (1, 1))
        scores = jnp.where(valid, scores, NEG)
        expd = jnp.exp(scores - jnp.max(scores, -1, keepdims=True))
        probs = (expd * (1.0 / jnp.sum(expd, -1, keepdims=True))).astype(BF16)
        out = contract(probs, keyvals[0, :, inner + at : inner + at + wide], (1, 0))
        mixed[0, :, at : at + wide] = gathered(out, size).astype(BF16)


def attend(counts, media, latent, norms, w_kv, w_q, first, run, into=()):
    images, media_len, width = media.shape
    lat_len, inner = latent.shape[1], w_q.shape[1]
    keys_len = media_len + lat_len
    at = lambda i, c: (i + first, 0, 0)
    shapes = [
        (images, lat_len, width),
        (images, keys_len, 2 * inner),
        (images, lat_len, inner),
        (images, lat_len, inner),
    ]
    return pl.pallas_call(
        attend_kernel,
        grid_spec=pltpu.PrefetchScalarGridSpec(
            num_scalar_prefetch=1,
            grid=(run,),
            in_specs=[
                pl.BlockSpec((1, media_len, width), at),
                pl.BlockSpec((1, lat_len, width), at),
                pl.BlockSpec(norms.shape, fixed_at),
                pl.BlockSpec(w_kv.shape, fixed_at),
                pl.BlockSpec(w_q.shape, fixed_at),
                *[pl.BlockSpec(memory_space=pl.ANY) for _ in into],
            ],
            out_specs=[
                pl.BlockSpec((1, width, 2 * keys_len), lambda i, c: ((i + first) // 2, 0, 0)),
                *[pl.BlockSpec((1,) + shape[1:], at) for shape in shapes],
            ],
            scratch_shapes=[pltpu.VMEM((keys_len, width), BF16)],
        ),
        out_shape=[
            jax.ShapeDtypeStruct((images // 2, width, 2 * keys_len), BF16),
            *[jax.ShapeDtypeStruct(shape, BF16) for shape in shapes],
        ],
        input_output_aliases={6 + i: i for i in range(len(into))},
        compiler_params=params(32),
        cost_estimate=cost(14),
        name="attend",
    )(counts[first : first + run], media, latent, norms, w_kv, w_q, *into)


def resid_kernel(mixed, latent, w_o, norms, resid, low):
    value = latent[...].astype(F32) + contract(mixed[...], w_o[...], (1, 0))
    resid[...] = value
    unit, _ = norm_rows(value)
    low[...] = (unit * norms[4:5, :] + norms[5:6, :]).astype(BF16)


def add_branch(mixed, latent, w_o, norms):
    rows, width = latent.shape
    inner = mixed.shape[1]
    block = rows // 4
    row_at = lambda i: (i, 0)
    return pl.pallas_call(
        resid_kernel,
        grid=(rows // block,),
        in_specs=[
            pl.BlockSpec((block, inner), row_at),
            pl.BlockSpec((block, width), row_at),
            pl.BlockSpec(w_o.shape, fixed_at),
            pl.BlockSpec(norms.shape, fixed_at),
        ],
        out_specs=[pl.BlockSpec((block, width), row_at), pl.BlockSpec((block, width), row_at)],
        out_shape=[
            jax.ShapeDtypeStruct((rows, width), F32),
            jax.ShapeDtypeStruct((rows, width), BF16),
        ],
        compiler_params=params(16),
        cost_estimate=cost(3),
        name="add_branch",
    )(mixed, latent, w_o, norms)


def ff_kernel(place, *refs):
    low0, low1, dout0, dout1 = refs[:4]
    lo, hi = refs[4:8], refs[8:12]
    activ, slope, low_t, dout, w_in = refs[12:17]
    keep0, send0, keep1, send1 = refs[17:21]
    low, grad = refs[21:]
    step, steps = pl.program_id(0), pl.num_programs(0)
    me = place[0]
    half = low0.shape[0]
    part = lo[0].shape[1]
    slot = grad.shape[0] // PLANE
    cut = slot // 2

    @pl.when(step == 0)
    def _():
        low[:half, :] = low0[...]
        low[half:, :] = low1[...]
        dout[:half, :] = dout0[...]
        dout[half:, :] = dout1[...]
        low_t[...] = low[...].T

    def put(pieces):
        for plane in range(PLANE):
            for column in range(pieces[0].shape[0]):
                at = pl.multiple_of((me ^ (column * PLANE + plane)) * part, part)
                w_in[pl.ds(at, part), :] = pieces[plane][column]

    pl.when(step < steps // 2)(lambda: put(lo))
    pl.when(step >= steps // 2)(lambda: put(hi))
    pre = contract(low[...], w_in[...], (1, 0))
    cdf = 0.5 * (1.0 + lax.erf(pre * math.sqrt(0.5)))
    slope[...] = cdf + pre * (jnp.exp(pre * pre * -0.5) * (1.0 / math.sqrt(2.0 * math.pi)))
    value = (pre * cdf).astype(BF16)
    activ[...] = value
    grad[...] = contract(value, dout[...], (0, 0)).astype(BF16)

    def block(plane, at):
        at = pl.multiple_of((plane ^ (me % PLANE)) * slot + at, cut)
        return grad[pl.ds(at, cut), :]

    for i in range(2):
        keep0[i, 0] = block(2 * i, 0)
        send0[i, 0] = block(2 * i + 1, 0)
        keep1[i, 0] = block(i, cut)
        send1[i, 0] = block(2 + i, cut)


def feed_forward(place, lows, douts, lo, hi, slot):
    half, width = lows[0].shape
    rows = 2 * half
    columns, part, cut = lo[0].shape
    tile = PLANE * slot
    steps = 2 * cut // tile
    in_at = lambda t, c: (0, t)
    lo_at = lambda t, c: (0, 0, jnp.minimum(t, steps // 2 - 1))
    hi_at = lambda t, c: (0, 0, jnp.maximum(t - steps // 2, 0))
    once = pl.Buffered(1)
    return pl.pallas_call(
        ff_kernel,
        grid_spec=pltpu.PrefetchScalarGridSpec(
            num_scalar_prefetch=1,
            grid=(steps,),
            in_specs=[
                *[pl.BlockSpec((half, width), fixed_at, pipeline_mode=once) for _ in range(4)],
                *[pl.BlockSpec((columns, part, tile), lo_at) for _ in lo],
                *[pl.BlockSpec((columns, part, tile), hi_at) for _ in hi],
            ],
            out_specs=[
                pl.BlockSpec((rows, tile), in_at),
                pl.BlockSpec((rows, tile), in_at),
                pl.BlockSpec((width, rows), fixed_at),
                pl.BlockSpec((rows, width), fixed_at),
                pl.BlockSpec((width, tile), in_at),
                *[
                    pl.BlockSpec(
                        (2, 1, slot // 2, width), lambda t, c: (0, t ^ (c[0] // PLANE), 0, 0)
                    )
                    for _ in range(4)
                ],
            ],
            scratch_shapes=[pltpu.VMEM((rows, width), BF16), pltpu.VMEM((tile, width), BF16)],
        ),
        out_shape=[
            jax.ShapeDtypeStruct((rows, 2 * cut), BF16),
            jax.ShapeDtypeStruct((rows, 2 * cut), F32),
            jax.ShapeDtypeStruct((width, rows), BF16),
            jax.ShapeDtypeStruct((rows, width), BF16),
            jax.ShapeDtypeStruct((width, 2 * cut), BF16),
            *[
                kind((2, columns, slot // 2, width), BF16)
                for kind in (jax.ShapeDtypeStruct, pltpu.HBM) * 2
            ],
        ],
        compiler_params=params(44),
        cost_estimate=cost(18),
        name="feed_forward",
    )(place, *lows, *douts, *lo, *hi)


def ff_back_kernel(
    place, dout, low_t, w_in, w_out, slope, keep0, send0, keep1, send1, kept, sent, total, grad_in
):
    step, steps = pl.program_id(0), pl.num_programs(0)
    columns, cut = keep0.shape[1:3]

    @pl.when(step == 0)
    def _():
        total[...] = jnp.zeros_like(total)

    grad = (contract(dout[...], w_out[...], (1, 1)) * slope[...]).astype(BF16)
    grad_in[...] = contract(low_t[...], grad, (1, 0)).astype(BF16)

    def block(plane, column, at):
        at = pl.multiple_of((place[0] ^ (column * PLANE + plane)) * 2 * cut + at, cut)
        return grad_in[pl.ds(at, cut), :]

    for column in range(columns):
        for i in range(2):
            keep0[i, column] = block(2 * i, column, 0)
            send0[i, column] = block(2 * i + 1, column, 0)
            keep1[i, column] = block(i, column, cut)
            send1[i, column] = block(2 + i, column, cut)
    total[...] += contract(grad, w_in[...], (1, 1))

    @pl.when(step == steps - 1)
    def _():
        half = kept.shape[0]
        kept[...] = total[:half, :]
        sent[...] = total[half:, :].astype(BF16)


def feed_back(place, dout, low_t, w_in, w_out, slope, columns, part):
    rows, width = dout.shape
    hidden = w_in.shape[1]
    tile = min(FF_TILE, hidden)
    half = rows // 2
    in_at, out_at = (lambda t, c: (0, t)), (lambda t, c: (t, 0))
    once = pl.Buffered(1)
    return pl.pallas_call(
        ff_back_kernel,
        grid_spec=pltpu.PrefetchScalarGridSpec(
            num_scalar_prefetch=1,
            grid=(hidden // tile,),
            in_specs=[
                pl.BlockSpec((rows, width), fixed_at, pipeline_mode=once),
                pl.BlockSpec((width, rows), fixed_at, pipeline_mode=once),
                pl.BlockSpec((width, tile), in_at),
                pl.BlockSpec((tile, width), out_at),
                pl.BlockSpec((rows, tile), in_at),
            ],
            out_specs=[
                *[
                    pl.BlockSpec((2, columns, part // 2, tile), lambda t, c: (0, 0, 0, t))
                    for _ in range(4)
                ],
                pl.BlockSpec((half, width), fixed_at, pipeline_mode=once),
                pl.BlockSpec((half, width), fixed_at, pipeline_mode=once),
            ],
            scratch_shapes=[pltpu.VMEM((rows, width), F32), pltpu.VMEM((width, tile), BF16)],
        ),
        out_shape=[
            *[
                kind((2, columns, part // 2, hidden), BF16)
                for kind in (jax.ShapeDtypeStruct, pltpu.HBM) * 2
            ],
            jax.ShapeDtypeStruct((half, width), F32),
            jax.ShapeDtypeStruct((half, width), BF16),
        ],
        compiler_params=params(48),
        cost_estimate=cost(21),
        name="feed_back",
    )(place, dout, low_t, w_in, w_out, slope)


def ff_out_kernel(activ, w_out, kept, sent, total):
    step = pl.program_id(0)

    @pl.when(step == 0)
    def _():
        total[...] = jnp.zeros_like(total)

    total[...] += contract(activ[...], w_out[...], (1, 0))

    @pl.when(step == pl.num_programs(0) - 1)
    def _():
        half = kept.shape[0]
        kept[...] = total[:half, :]
        sent[...] = total[half:, :].astype(BF16)


def feed_out(activ, w_out):
    rows, hidden = activ.shape
    width = w_out.shape[1]
    tile = min(FF_TILE, hidden)
    half = rows // 2
    once = pl.Buffered(1)
    return pl.pallas_call(
        ff_out_kernel,
        grid=(hidden // tile,),
        in_specs=[
            pl.BlockSpec((rows, tile), lambda t: (0, t)),
            pl.BlockSpec((tile, width), lambda t: (t, 0)),
        ],
        out_specs=[pl.BlockSpec((half, width), fixed_at, pipeline_mode=once)] * 2,
        out_shape=[
            jax.ShapeDtypeStruct((half, width), F32),
            jax.ShapeDtypeStruct((half, width), BF16),
        ],
        scratch_shapes=[pltpu.VMEM((rows, width), F32)],
        compiler_params=params(24),
        cost_estimate=cost(7),
        name="feed_out",
    )(activ, w_out)


def resid_back_kernel(
    kept,
    got,
    resid,
    cotangent,
    mixed,
    w_o,
    norms,
    grad_resid,
    grad_mixed,
    grad_o,
    vectors,
    total,
):
    step = pl.program_id(0)

    @pl.when(step == 0)
    def _():
        vectors[...] = jnp.zeros_like(vectors)
        total[...] = jnp.zeros_like(total)

    grad = kept[...] + got[...].astype(F32)
    unit, inverse = norm_rows(resid[...])
    vectors[0:1, :] += jnp.sum(grad * unit, 0, keepdims=True)
    vectors[1:2, :] += jnp.sum(grad, 0, keepdims=True)
    value = cotangent[...] + norm_back(grad, unit, inverse, norms[4:5, :])
    grad_resid[...] = value
    low = value.astype(BF16)
    grad_mixed[...] = contract(low, w_o[...], (1, 1)).astype(BF16)
    total[...] += contract(mixed[...], low, (0, 0))
    grad_o[...] = total[...].astype(BF16)


def resid_back(kept, got, resid, cotangent, mixed, w_o, norms):
    rows, width = resid.shape
    inner = mixed.shape[1]
    block = rows // 4
    row_at = lambda i: (i, 0)
    wide = pl.BlockSpec((block, width), row_at)
    return pl.pallas_call(
        resid_back_kernel,
        grid=(rows // block,),
        in_specs=[
            *[wide] * 4,
            pl.BlockSpec((block, inner), row_at),
            pl.BlockSpec(w_o.shape, fixed_at),
            pl.BlockSpec(norms.shape, fixed_at),
        ],
        out_specs=[
            wide,
            pl.BlockSpec((block, inner), row_at),
            pl.BlockSpec(w_o.shape, fixed_at),
            pl.BlockSpec((8, width), fixed_at),
        ],
        out_shape=[
            jax.ShapeDtypeStruct((rows, width), F32),
            jax.ShapeDtypeStruct((rows, inner), BF16),
            jax.ShapeDtypeStruct(w_o.shape, BF16),
            jax.ShapeDtypeStruct((8, width), F32),
        ],
        scratch_shapes=[pltpu.VMEM(w_o.shape, F32)],
        compiler_params=params(24),
        cost_estimate=cost(6),
        name="resid_back",
    )(kept, got, resid, cotangent, mixed, w_o, norms)


def as_row(column):
    out = []
    size = 128
    same = lax.broadcasted_iota(jnp.int32, (size, size), 0) == lax.broadcasted_iota(
        jnp.int32, (size, size), 1
    )
    for at in range(0, column.shape[0], size):
        out.append(jnp.sum(jnp.where(same, column[at : at + size, :], 0.0), 0, keepdims=True))
    return jnp.concatenate(out, 1)


def in_bf16(row):
    parts = []
    for _ in range(3):
        parts.append(row.astype(BF16))
        row = row - parts[-1].astype(F32)
    return parts


def attend_back_kernel(counts, keyvals, queries, grad_mixed, grad_kv, grad_q):
    taken, keys_len = keyvals.shape[:2]
    lat_len, inner = queries.shape[1:]
    media_len = keys_len - lat_len
    size = inner // HEADS
    wide = size * GROUP
    scale = 1.0 / math.sqrt(size)
    key_at = lax.broadcasted_iota(jnp.int32, (keys_len, 1), 0)

    def begin(i, at):
        own = spread(queries[i, :, at : at + wide].astype(F32) * scale, size).astype(BF16)
        grad = spread(grad_mixed[i, :, at : at + wide], size).astype(BF16)
        scores = contract(keyvals[i, :, at : at + wide], own, (1, 1))
        grad_probs = contract(keyvals[i, :, inner + at : inner + at + wide], grad, (1, 1))
        return own, grad, scores, grad_probs

    def weigh(i, scores, grad_probs):
        valid = (key_at < counts[pl.program_id(0) * taken + i]) | (key_at >= media_len)
        scores = jnp.where(valid, scores, NEG)
        expd = jnp.exp(scores - jnp.max(scores, 0, keepdims=True))
        probs = expd * (1.0 / jnp.sum(expd, 0, keepdims=True))
        held = jnp.sum(probs * grad_probs, 0, keepdims=True)
        return probs.astype(BF16), (probs * (grad_probs - held)).astype(BF16)

    def end(i, at, own, grad, probs, low):
        grad_v = contract(probs, grad, (1, 0)).astype(BF16)
        grad_kv[i, :, inner + at : inner + at + wide] = grad_v
        grad_kv[i, :, at : at + wide] = contract(low, own, (1, 0)).astype(BF16)
        back = contract(low, keyvals[i, :, at : at + wide], (0, 0))
        grad_q[i, :, at : at + wide] = (gathered(back, size) * scale).astype(BF16)

    items = [(i, at) for i in range(taken) for at in range(0, inner, wide)]
    ahead, behind = begin(*items[0]), None
    for n, item in enumerate(items):
        own, grad, scores, grad_probs = ahead
        if n + 1 < len(items):
            ahead = begin(*items[n + 1])
        weights = weigh(item[0], scores, grad_probs)
        if behind:
            end(*behind)
        behind = (*item, own, grad, *weights)
    end(*behind)


def weight_back_kernel(
    place,
    grad_kv,
    grad_q,
    turned,
    lat_low,
    w_kv,
    w_q,
    norms,
    grad_o,
    ff_vectors,
    keep,
    send,
    total,
    sums,
    lat_kv,
    lat_q,
    total_q,
):
    step, steps = pl.program_id(0), pl.num_programs(0)
    lat_len, inner = grad_q.shape[1:]
    keys_len = grad_kv.shape[1]
    media_len = keys_len - lat_len

    @pl.when(step == 0)
    def _():
        total[...] = jnp.zeros_like(total)
        sums[...] = jnp.zeros_like(sums)

    both = grad_kv[...].reshape(2 * keys_len, 2 * inner)
    total[...] += contract(turned[0], both, (1, 0))
    sums[...] += jnp.sum(both.astype(F32), 0, keepdims=True)
    for side in range(2):
        here = pl.ds(pl.multiple_of((2 * step + side) * lat_len, lat_len), lat_len)
        lat_kv[here, :] = grad_kv[side, media_len:, :]
        lat_q[here, :] = grad_q[side]

    @pl.when(step == steps - 1)
    def _():
        lat_w = contract(lat_low[...], lat_kv[...], (0, 0))
        lat_wq = contract(lat_low[...], lat_q[...], (0, 0))
        weight, weight_q = w_kv[...].astype(F32), w_q[...].astype(F32)
        lat_sum = jnp.sum(lat_kv[...].astype(F32), 0, keepdims=True)
        lat_sum_q = jnp.sum(lat_q[...].astype(F32), 0, keepdims=True)
        rows = in_bf16(sums[0:1, :] - lat_sum) + in_bf16(lat_sum) + [jnp.zeros((2, 2 * inner), BF16)]
        rows_q = in_bf16(lat_sum_q) + [jnp.zeros((5, inner), BF16)]
        biases = contract(jnp.concatenate(rows, 0), w_kv[...], (1, 1))
        biases_q = contract(jnp.concatenate(rows_q, 0), w_q[...], (1, 1))
        media_bias = jnp.sum(biases[0:3], 0, keepdims=True)
        lat_bias = jnp.sum(biases[3:6], 0, keepdims=True) + jnp.sum(biases_q, 0, keepdims=True)
        media_both = as_row(jnp.sum((total[...] - lat_w) * weight, 1, keepdims=True))
        lat_both = as_row(
            jnp.sum(lat_w * weight, 1, keepdims=True)
            + jnp.sum(lat_wq * weight_q, 1, keepdims=True)
        )
        vectors = [
            (media_both - norms[1:2, :] * media_bias) / norms[0:1, :],
            media_bias,
            (lat_both - norms[3:4, :] * lat_bias) / norms[2:3, :],
            lat_bias,
            ff_vectors[0:2, :],
            jnp.zeros((2, ff_vectors.shape[1]), F32),
        ]
        vectors = jnp.concatenate(vectors, 0).astype(BF16)
        total_q[...] = lat_wq
        me, core = place[0], place[1]
        columns = keep.shape[1]
        kv_rows = total.shape[0] // (2 * columns * PLANE)
        o_rows = grad_o.shape[0] // (2 * columns * PLANE)
        q_rows = kv_rows // 2
        for plane in range(PLANE):
            for column in range(columns):
                chip = me ^ (column * PLANE + plane)
                for out, half in ((keep, core), (send, 1 - core)):
                    at = pl.multiple_of((chip * 2 + half) * kv_rows, kv_rows)
                    out[plane, column, :kv_rows, :] = total[pl.ds(at, kv_rows), :].astype(BF16)
                    value = total_q[pl.ds(at, kv_rows), :].astype(BF16)
                    row = kv_rows
                    out[plane, column, row : row + q_rows, :inner] = value[:q_rows]
                    out[plane, column, row : row + q_rows, inner:] = value[q_rows:]
                    row += q_rows
                    at = pl.multiple_of((chip * 2 + half) * o_rows, o_rows)
                    out[plane, column, row : row + o_rows, :] = grad_o[pl.ds(at, o_rows), :]
                    out[plane, column, row + o_rows :, :] = vectors


def attend_back(counts, keyvals, queries, grad_mixed):
    images, keys_len, wide = keyvals.shape
    lat_len, inner = queries.shape[1:]
    taken = 2
    at = lambda i, c: (i, 0, 0)
    return pl.pallas_call(
        attend_back_kernel,
        grid_spec=pltpu.PrefetchScalarGridSpec(
            num_scalar_prefetch=1,
            grid=(images // taken,),
            in_specs=[
                pl.BlockSpec((taken, keys_len, wide), at),
                pl.BlockSpec((taken, lat_len, inner), at),
                pl.BlockSpec((taken, lat_len, inner), at),
            ],
            out_specs=[
                pl.BlockSpec((taken, keys_len, wide), at),
                pl.BlockSpec((taken, lat_len, inner), at),
            ],
        ),
        out_shape=[
            jax.ShapeDtypeStruct((images, keys_len, wide), BF16),
            jax.ShapeDtypeStruct((images, lat_len, inner), BF16),
        ],
        compiler_params=params(58),
        cost_estimate=cost(15),
        name="attend_back",
    )(counts, keyvals, queries, grad_mixed)


def weight_back(
    place, grad_kv, grad_q, turned, lat_low, w_kv, w_q, norms, grad_o, ff_vectors, columns
):
    images, keys_len, _ = grad_kv.shape
    width = turned.shape[1]
    lat_len, inner = grad_q.shape[1:]
    rows = images * lat_len
    chips = columns * PLANE
    kv_rows, o_rows = width // chips // 2, inner // chips // 2
    pack = (PLANE, columns, kv_rows + kv_rows // 2 + o_rows + PAD, width)
    at = lambda i, c: (i, 0, 0)
    once = pl.Buffered(1)
    return pl.pallas_call(
        weight_back_kernel,
        grid_spec=pltpu.PrefetchScalarGridSpec(
            num_scalar_prefetch=1,
            grid=(images // 2,),
            in_specs=[
                pl.BlockSpec((2, keys_len, 2 * inner), at),
                pl.BlockSpec((2, lat_len, inner), at),
                pl.BlockSpec((1, width, 2 * keys_len), at),
                pl.BlockSpec(lat_low.shape, fixed_at, pipeline_mode=once),
                pl.BlockSpec(w_kv.shape, fixed_at, pipeline_mode=once),
                pl.BlockSpec(w_q.shape, fixed_at, pipeline_mode=once),
                pl.BlockSpec(norms.shape, fixed_at),
                pl.BlockSpec(grad_o.shape, fixed_at, pipeline_mode=once),
                pl.BlockSpec(ff_vectors.shape, fixed_at),
            ],
            out_specs=[
                pl.BlockSpec(pack, whole_at(4), pipeline_mode=once),
                pl.BlockSpec(pack, whole_at(4), pipeline_mode=once),
            ],
            scratch_shapes=[
                pltpu.VMEM(w_kv.shape, F32),
                pltpu.VMEM((8, 2 * inner), F32),
                pltpu.VMEM((rows, 2 * inner), BF16),
                pltpu.VMEM((rows, inner), BF16),
                pltpu.VMEM(w_q.shape, F32),
            ],
        ),
        out_shape=[jax.ShapeDtypeStruct(pack, BF16), jax.ShapeDtypeStruct(pack, BF16)],
        compiler_params=params(58),
        cost_estimate=cost(17),
        name="weight_back",
    )(place, grad_kv, grad_q, turned, lat_low, w_kv, w_q, norms, grad_o, ff_vectors)


def latent_back_kernel(grad_kv, grad_q, latent, grad_resid, w_kv, w_q, norms, latent_grad):
    images, lat_len, width = latent.shape
    rows = images * lat_len
    grad = contract(grad_kv[...].reshape(rows, grad_kv.shape[2]), w_kv[...], (1, 1))
    grad += contract(grad_q[...].reshape(rows, grad_q.shape[2]), w_q[...], (1, 1))
    unit, inverse = norm_rows(latent[...].reshape(rows, width).astype(F32))
    back = norm_back(grad, unit, inverse, norms[2:3, :])
    latent_grad[...] = grad_resid[...] + back.reshape(images, lat_len, width)


def latent_back(grad_kv, grad_q, latent, grad_resid, w_kv, w_q, norms):
    images, lat_len, width = latent.shape
    inner = w_q.shape[1]
    tail = grad_kv.shape[1] // lat_len - 1
    block = images // 2
    at = lambda i: (i, 0, 0)
    return pl.pallas_call(
        latent_back_kernel,
        grid=(images // block,),
        in_specs=[
            pl.BlockSpec((block, lat_len, 2 * inner), lambda i: (i, tail, 0)),
            pl.BlockSpec((block, lat_len, inner), at),
            pl.BlockSpec((block, lat_len, width), at),
            pl.BlockSpec((block, lat_len, width), at),
            pl.BlockSpec(w_kv.shape, fixed_at),
            pl.BlockSpec(w_q.shape, fixed_at),
            pl.BlockSpec(norms.shape, fixed_at),
        ],
        out_specs=pl.BlockSpec((block, lat_len, width), at),
        out_shape=jax.ShapeDtypeStruct((images, lat_len, width), F32),
        compiler_params=params(32),
        cost_estimate=cost(4),
        name="latent_back",
    )(grad_kv, grad_q, latent, grad_resid, w_kv, w_q, norms)


def media_back_kernel(media, grad_kv, norms, w_kv, *refs):
    out, grad = refs[-2:]
    grad[...] = contract(grad_kv[0], w_kv[...], (1, 1))
    for at in range(0, media.shape[1], ROWS):
        unit, inverse = norm_rows(media[0, at : at + ROWS, :].astype(F32))
        out[0, at : at + ROWS, :] = norm_back(grad[at : at + ROWS, :], unit, inverse, norms[0:1, :])


def media_back(media, grad_kv, norms, w_kv, first, run, into=()):
    images, media_len, width = media.shape
    inner2 = w_kv.shape[1]
    at = lambda i: (i + first, 0, 0)
    return pl.pallas_call(
        media_back_kernel,
        grid=(run,),
        in_specs=[
            pl.BlockSpec((1, media_len, width), at),
            pl.BlockSpec((1, media_len, inner2), at),
            pl.BlockSpec(norms.shape, fixed_at),
            pl.BlockSpec(w_kv.shape, fixed_at),
            *[pl.BlockSpec(memory_space=pl.ANY) for _ in into],
        ],
        out_specs=pl.BlockSpec((1, media_len, width), at),
        out_shape=jax.ShapeDtypeStruct((images, media_len, width), F32),
        input_output_aliases={4 + i: i for i in range(len(into))},
        scratch_shapes=[pltpu.VMEM((media_len, width), F32)],
        compiler_params=params(32),
        cost_estimate=cost(0.5),
        name="media_back",
    )(media, grad_kv, norms, w_kv, *into)


def fold_rows(value):
    half = value.shape[0] // 2
    return jnp.concatenate([value[:half], value[half:]], 1)


def shards(
    dp,
    media_tokens,
    patch_counts,
    latents,
    media_gain,
    media_bias,
    latent_gain,
    latent_bias,
    query_weight,
    keyval_weight,
    outproj_weight,
    ff_gain,
    ff_bias,
    ff_in_weight,
    ff_out_weight,
    cotangent,
):
    me, core = lax.axis_index("dp"), lax.axis_index("rep")
    place = jnp.stack([me, core]).astype(jnp.int32)
    columns = dp // PLANE
    images, _, width = media_tokens.shape
    lat_len = latents.shape[1]
    inner = query_weight.shape[1]
    part = width // dp
    slot = ff_in_weight.shape[1] // dp // 2
    kv_rows, o_rows = part // 2, inner // dp // 2
    flat = (images * lat_len, width)

    def swap(value, bits):
        return lax.ppermute(value, "dp", [(i, i ^ bits) for i in range(dp)])

    def other(value):
        return lax.ppermute(value, "rep", [(0, 1), (1, 0)])

    def mine(value, axis):
        return lax.dynamic_index_in_dim(value, core, axis, keepdims=False)

    def down(value):
        return [value] + [swap(value, c * PLANE) for c in range(1, columns)]

    def across(values):
        return [values[0]] + [swap(values[p], p) for p in range(1, PLANE)]

    def down_sums(values):
        return [values[0]] + [swap(values[c], c * PLANE) for c in range(1, columns)]

    norms = jnp.stack([media_gain, media_bias, latent_gain, latent_bias, ff_gain, ff_bias])
    norms = lax.dynamic_update_slice(jnp.zeros((PAD, width), BF16), norms, (0, me * part))
    attn = [
        mine(keyval_weight.reshape(2, kv_rows, width), 0),
        fold_rows(mine(query_weight.reshape(2, kv_rows, inner), 0)),
        mine(outproj_weight.reshape(2, o_rows, width), 0),
        norms,
    ]
    attn = jnp.stack(down(jnp.concatenate(attn, 0)))
    ffout = mine(ff_out_weight.reshape(2, slot, width), 0)
    ffin = mine(ff_in_weight.reshape(part, dp, 2, slot), 2).reshape(part, dp * slot)
    cut = ffin.shape[1] // 2
    ffin = jnp.concatenate([ffin[:, :cut], ffin[:, cut:]], 0)
    attn, ffout, ffin = tie(attn, ffout, ffin)
    attn = [attn] + [swap(attn, p) for p in range(1, PLANE)]
    w_ffout = lax.all_gather(ffout, "dp", axis=0, tiled=True)
    ffin = jnp.stack([ffin, swap(ffin, 2 * PLANE)])
    got = swap(ffin, PLANE)
    w_kv, w_q, w_o, norms = in_order(place, attn, [other(value) for value in attn], inner)
    lo, hi = [
        jnp.stack([ffin[0, rows], got[0, rows], ffin[1, rows], got[1, rows]])
        for rows in (slice(0, part), slice(part, 2 * part))
    ]
    dout = cotangent.astype(BF16).reshape(flat)
    douts = dout, other(dout)

    w_kv, lo, hi = tie(w_kv, lo, hi)
    lo, hi = {0: lo, 2: swap(lo, 2)}, {0: hi, 1: swap(hi, 1)}
    run = images // 2
    held = attend(patch_counts, media_tokens, latents, norms, w_kv, w_q, 0, run)
    held, lo, hi = tie(held, lo, hi)
    lo[1], lo[3] = swap(lo[0], 1), swap(lo[2], 1)
    hi[2], hi[3] = swap(hi[0], 2), swap(hi[1], 2)
    turned, lat_low, keyvals, queries, mixed = attend(
        patch_counts, media_tokens, latents, norms, w_kv, w_q, run, images - run, held
    )
    mixed, lo, hi = tie(mixed.reshape(-1, inner), lo, hi)
    lo, hi = [lo[p] for p in range(PLANE)], [hi[p] for p in range(PLANE)]
    resid, low = add_branch(mixed, latents.reshape(flat), w_o, norms)

    activ, slope, low_t, dout, w_ffin, *grads = feed_forward(
        place, (low, other(low)), douts, lo, hi, slot
    )
    out_sum = grads[0], swap(grads[1], 1), grads[2], swap(grads[3], 2)
    *grads, kept, sent = feed_back(place, dout, low_t, w_ffin, w_ffout, slope, columns, part)
    kept, out_sum = tie(kept, out_sum)
    grad_resid, grad_mixed, grad_o, ff_vectors = resid_back(
        kept, other(sent), resid, cotangent.reshape(flat), mixed, w_o, norms
    )
    grad_mixed, out_sum = tie(grad_mixed, out_sum)
    out_sum = fold_first(*out_sum)
    grad_mixed, out_sum = tie(grad_mixed, out_sum)
    out_sum = out_sum[0], swap(out_sum[1], 2), out_sum[2], swap(out_sum[3], 1)
    in_sum = grads[0], swap(grads[1], 1), grads[2], swap(grads[3], 2)
    grad_kv, grad_q = attend_back(
        patch_counts, keyvals, queries, grad_mixed.reshape(images, lat_len, inner)
    )
    grad_kv, grad_q, out_sum, in_sum = tie(grad_kv, grad_q, out_sum, in_sum)
    keep, send = fold_second(*out_sum)
    in_sum = fold_first(*in_sum)
    grad_q, keep, send, in_sum = tie(grad_q, keep, send, in_sum)
    out_sum = keep, swap(send, PLANE)
    in_sum = in_sum[0], swap(in_sum[1], 2), in_sum[2], swap(in_sum[3], 1)
    keep, send = weight_back(
        place,
        grad_kv,
        grad_q,
        turned,
        lat_low.reshape(flat),
        w_kv,
        w_q,
        norms,
        grad_o,
        ff_vectors,
        columns,
    )
    keep, send, out_sum, in_sum = tie(keep, send, out_sum, in_sum)
    got = other(send)
    in_keep, in_send = fold_second(*in_sum)
    held, passed = fold_third(*out_sum)
    keep, in_send, passed = tie(keep, in_send, passed)
    in_sum = in_keep, swap(in_send, PLANE)
    out_sum = held, swap(passed, 2 * PLANE)
    attn = add_both(keep, got)
    attn = across(attn)
    grad_kv, attn[0] = tie(grad_kv, attn[0])
    done = media_back(media_tokens, grad_kv, norms, w_kv, 0, run)
    done, in_sum = tie(done, in_sum)
    held, passed = fold_third(*in_sum)
    done, held, passed = tie(done, held, passed)
    in_sum = held, swap(passed, 2 * PLANE)
    media_grad = media_back(media_tokens, grad_kv, norms, w_kv, run, images - run, (done,))
    media_grad, attn = tie(media_grad, attn)
    attn = fold(attn)
    attn, activ, grad_q, in_sum = tie(attn, activ, grad_q, in_sum)
    attn = down_sums(attn)
    latent_grad = latent_back(
        grad_kv, grad_q, latents, grad_resid.reshape(latents.shape), w_kv, w_q, norms
    )
    share, sent = feed_out(activ, w_ffout)
    own_in, own_out = [value[0].astype(F32) + value[1].astype(F32) for value in (in_sum, out_sum)]
    grad_ffin, grad_ffout = final_ff(place, own_in, other(own_in), own_out, other(own_out))
    sent, attn, grad_ffin, latent_grad = tie(sent, attn, grad_ffin, latent_grad)
    own = functools.reduce(jnp.add, [value.astype(F32) for value in attn])
    new_latents = resid + (share + other(sent).astype(F32))
    rows = own.shape[0] - PAD
    vectors = lax.dynamic_slice(own[rows:], (0, me * part), (6, part))
    own = own[:rows]
    grad_wkv, grad_wq, grad_wo = final_attn(place, own, other(own), inner, kv_rows, o_rows)
    return (
        new_latents.reshape(latents.shape),
        media_grad,
        latent_grad,
        vectors[0],
        vectors[1],
        vectors[2],
        vectors[3],
        grad_wq,
        grad_wkv,
        grad_wo,
        vectors[4],
        vectors[5],
        grad_ffin,
        grad_ffout,
    )


def norm_apply(values, gain, bias):
    centre = jnp.mean(values, -1, keepdims=True)
    centred = values - centre
    inverse = lax.rsqrt(jnp.mean(centred * centred, -1, keepdims=True) + EPS)
    unit = centred * inverse
    return (unit * gain.astype(jnp.float32) + bias.astype(jnp.float32), unit, inverse)


def plain_norm_grad(grad_normed, unit, inverse, gain):
    scaled = grad_normed * gain.astype(jnp.float32)
    return inverse * (
        scaled
        - jnp.mean(scaled, -1, keepdims=True)
        - unit * jnp.mean(scaled * unit, -1, keepdims=True)
    )


def row_total(values):
    return jnp.sum(values.reshape(-1, values.shape[-1]), axis=0)


def gelu_exact(values):
    return jax.nn.gelu(values, approximate=False)


def masked_scores(query_heads, key_heads, valid, scale):
    raw = (
        jnp.einsum("iqhe,ikhe->ihqk", query_heads, key_heads, preferred_element_type=jnp.float32)
        * scale
    )
    return jnp.where(valid[:, None, None, :], raw, jnp.float32(-1e30))


def plain_shards(
    media_tokens,
    patch_counts,
    latents,
    media_gain,
    media_bias,
    latent_gain,
    latent_bias,
    query_weight,
    keyval_weight,
    outproj_weight,
    ff_gain,
    ff_bias,
    ff_in_weight,
    ff_out_weight,
    cotangent,
):
    f32 = jnp.float32
    bf16 = jnp.bfloat16
    whole = (
        lax.all_gather(media_gain, "dp", axis=0, tiled=True),
        lax.all_gather(media_bias, "dp", axis=0, tiled=True),
        lax.all_gather(latent_gain, "dp", axis=0, tiled=True),
        lax.all_gather(latent_bias, "dp", axis=0, tiled=True),
        lax.all_gather(query_weight, "dp", axis=0, tiled=True),
        lax.all_gather(keyval_weight, "dp", axis=0, tiled=True),
        lax.all_gather(outproj_weight, "dp", axis=0, tiled=True),
        lax.all_gather(ff_gain, "dp", axis=0, tiled=True),
        lax.all_gather(ff_bias, "dp", axis=0, tiled=True),
        lax.all_gather(ff_in_weight, "dp", axis=0, tiled=True),
        lax.all_gather(ff_out_weight, "dp", axis=0, tiled=True),
    )
    (
        gain_media,
        bias_media,
        gain_latent,
        bias_latent,
        w_query,
        w_keyval,
        w_outproj,
        gain_ff,
        bias_ff,
        w_ffin,
        w_ffout,
    ) = whole
    images, media_len, width = media_tokens.shape
    lat_len = latents.shape[1]
    keys_len = media_len + lat_len
    inner_width = w_query.shape[1]
    head_size = inner_width // HEADS
    scale = 1.0 / math.sqrt(head_size)
    media_f = media_tokens.astype(f32)
    latent_f = latents.astype(f32)
    media_normed, media_unit, media_inv = norm_apply(media_f, gain_media, bias_media)
    latent_normed, latent_unit, latent_inv = norm_apply(latent_f, gain_latent, bias_latent)
    media_low = media_normed.astype(bf16)
    latent_low = latent_normed.astype(bf16)
    queries = jnp.einsum("ild,de->ile", latent_low, w_query, preferred_element_type=f32).astype(
        bf16
    )
    key_input = jnp.concatenate([media_low, latent_low], axis=1)
    keyvals = jnp.einsum("ikd,de->ike", key_input, w_keyval, preferred_element_type=f32).astype(
        bf16
    )
    key_heads = keyvals[:, :, :inner_width].reshape(images, keys_len, HEADS, head_size)
    value_heads = keyvals[:, :, inner_width:].reshape(images, keys_len, HEADS, head_size)
    query_heads = queries.reshape(images, lat_len, HEADS, head_size)
    positions = jnp.arange(keys_len, dtype=jnp.int32)
    valid = (positions[None, :] < patch_counts[:, None]) | (positions[None, :] >= media_len)
    scores = masked_scores(query_heads, key_heads, valid, scale)
    top = jnp.max(scores, -1, keepdims=True)
    expd = jnp.exp(scores - top)
    total = jnp.sum(expd, -1, keepdims=True)
    probs = expd / total
    log_total = top + jnp.log(total)
    mixed = jnp.einsum(
        "ihqk,ikhe->iqhe", probs.astype(bf16), value_heads, preferred_element_type=f32
    )
    mixed = mixed.reshape(images, lat_len, inner_width).astype(bf16)
    branch = jnp.einsum("ile,ed->ild", mixed, w_outproj, preferred_element_type=f32)
    resid = latent_f + branch
    ff_normed, ff_unit, ff_inv = norm_apply(resid, gain_ff, bias_ff)
    ff_low = ff_normed.astype(bf16)
    pre_act = jnp.einsum("ild,df->ilf", ff_low, w_ffin, preferred_element_type=f32)
    activ, gelu_pull = jax.vjp(gelu_exact, pre_act)
    activ_low = activ.astype(bf16)
    new_latents = resid + jnp.einsum("ilf,fd->ild", activ_low, w_ffout, preferred_element_type=f32)
    again = (
        lax.all_gather(media_gain, "dp", axis=0, tiled=True),
        lax.all_gather(media_bias, "dp", axis=0, tiled=True),
        lax.all_gather(latent_gain, "dp", axis=0, tiled=True),
        lax.all_gather(latent_bias, "dp", axis=0, tiled=True),
        lax.all_gather(query_weight, "dp", axis=0, tiled=True),
        lax.all_gather(keyval_weight, "dp", axis=0, tiled=True),
        lax.all_gather(outproj_weight, "dp", axis=0, tiled=True),
        lax.all_gather(ff_gain, "dp", axis=0, tiled=True),
        lax.all_gather(ff_bias, "dp", axis=0, tiled=True),
        lax.all_gather(ff_in_weight, "dp", axis=0, tiled=True),
        lax.all_gather(ff_out_weight, "dp", axis=0, tiled=True),
    )
    (
        gain_media_b,
        bias_media_b,
        gain_latent_b,
        bias_latent_b,
        w_query_b,
        w_keyval_b,
        w_outproj_b,
        gain_ff_b,
        bias_ff_b,
        w_ffin_b,
        w_ffout_b,
    ) = again
    grad_out_low = cotangent.astype(bf16)
    grad_ffout = jnp.einsum("ilf,ild->fd", activ_low, grad_out_low, preferred_element_type=f32)
    grad_activ = jnp.einsum("ild,fd->ilf", grad_out_low, w_ffout_b, preferred_element_type=f32)
    (grad_pre,) = gelu_pull(grad_activ)
    grad_pre_low = grad_pre.astype(bf16)
    grad_ffin = jnp.einsum("ild,ilf->df", ff_low, grad_pre_low, preferred_element_type=f32)
    grad_ffnormed = jnp.einsum("ilf,df->ild", grad_pre_low, w_ffin_b, preferred_element_type=f32)
    grad_gain_ff = row_total(grad_ffnormed * ff_unit)
    grad_bias_ff = row_total(grad_ffnormed)
    grad_resid = cotangent + plain_norm_grad(grad_ffnormed, ff_unit, ff_inv, gain_ff_b)
    grad_resid_low = grad_resid.astype(bf16)
    grad_outproj = jnp.einsum("ile,ild->ed", mixed, grad_resid_low, preferred_element_type=f32)
    grad_mixed = jnp.einsum(
        "ild,ed->ile", grad_resid_low, w_outproj_b, preferred_element_type=f32
    ).astype(bf16)
    grad_mixed_heads = grad_mixed.reshape(images, lat_len, HEADS, head_size)
    scores_again = masked_scores(query_heads, key_heads, valid, scale)
    probs_again = jnp.exp(scores_again - log_total)
    grad_probs = jnp.einsum(
        "iqhe,ikhe->ihqk", grad_mixed_heads, value_heads, preferred_element_type=f32
    )
    grad_scores = probs_again * (grad_probs - jnp.sum(probs_again * grad_probs, -1, keepdims=True))
    grad_scores_low = grad_scores.astype(bf16)
    grad_queries = (
        jnp.einsum("ihqk,ikhe->iqhe", grad_scores_low, key_heads, preferred_element_type=f32)
        * scale
    )
    grad_queries = grad_queries.reshape(images, lat_len, inner_width).astype(bf16)
    grad_keys = (
        jnp.einsum("ihqk,iqhe->ikhe", grad_scores_low, query_heads, preferred_element_type=f32)
        * scale
    )
    grad_values = jnp.einsum(
        "ihqk,iqhe->ikhe", probs_again.astype(bf16), grad_mixed_heads, preferred_element_type=f32
    )
    grad_keyvals = jnp.concatenate(
        [
            grad_keys.reshape(images, keys_len, inner_width),
            grad_values.reshape(images, keys_len, inner_width),
        ],
        axis=-1,
    ).astype(bf16)
    grad_qweight = jnp.einsum("ild,ile->de", latent_low, grad_queries, preferred_element_type=f32)
    grad_kvweight = jnp.einsum("ikd,ike->de", key_input, grad_keyvals, preferred_element_type=f32)
    grad_key_input = jnp.einsum("ike,de->ikd", grad_keyvals, w_keyval_b, preferred_element_type=f32)
    grad_latnormed = jnp.einsum("ile,de->ild", grad_queries, w_query_b, preferred_element_type=f32)
    grad_latnormed = grad_latnormed + grad_key_input[:, media_len:]
    grad_medianormed = grad_key_input[:, :media_len]
    media_grad = plain_norm_grad(grad_medianormed, media_unit, media_inv, gain_media_b)
    latent_grad = grad_resid + plain_norm_grad(grad_latnormed, latent_unit, latent_inv, gain_latent_b)
    grad_gain_media = row_total(grad_medianormed * media_unit)
    grad_bias_media = row_total(grad_medianormed)
    grad_gain_latent = row_total(grad_latnormed * latent_unit)
    grad_bias_latent = row_total(grad_latnormed)
    owned = (
        lax.psum_scatter(
            grad_gain_media.astype(jnp.bfloat16), "dp", scatter_dimension=0, tiled=True
        ).astype(jnp.float32),
        lax.psum_scatter(
            grad_bias_media.astype(jnp.bfloat16), "dp", scatter_dimension=0, tiled=True
        ).astype(jnp.float32),
        lax.psum_scatter(
            grad_gain_latent.astype(jnp.bfloat16), "dp", scatter_dimension=0, tiled=True
        ).astype(jnp.float32),
        lax.psum_scatter(
            grad_bias_latent.astype(jnp.bfloat16), "dp", scatter_dimension=0, tiled=True
        ).astype(jnp.float32),
        lax.psum_scatter(
            grad_qweight.astype(jnp.bfloat16), "dp", scatter_dimension=0, tiled=True
        ).astype(jnp.float32),
        lax.psum_scatter(
            grad_kvweight.astype(jnp.bfloat16), "dp", scatter_dimension=0, tiled=True
        ).astype(jnp.float32),
        lax.psum_scatter(
            grad_outproj.astype(jnp.bfloat16), "dp", scatter_dimension=0, tiled=True
        ).astype(jnp.float32),
        lax.psum_scatter(
            grad_gain_ff.astype(jnp.bfloat16), "dp", scatter_dimension=0, tiled=True
        ).astype(jnp.float32),
        lax.psum_scatter(
            grad_bias_ff.astype(jnp.bfloat16), "dp", scatter_dimension=0, tiled=True
        ).astype(jnp.float32),
        lax.psum_scatter(
            grad_ffin.astype(jnp.bfloat16), "dp", scatter_dimension=0, tiled=True
        ).astype(jnp.float32),
        lax.psum_scatter(
            grad_ffout.astype(jnp.bfloat16), "dp", scatter_dimension=0, tiled=True
        ).astype(jnp.float32),
    )
    summed = (
        lax.psum(owned[0].astype(jnp.bfloat16), "rep").astype(jnp.float32),
        lax.psum(owned[1].astype(jnp.bfloat16), "rep").astype(jnp.float32),
        lax.psum(owned[2].astype(jnp.bfloat16), "rep").astype(jnp.float32),
        lax.psum(owned[3].astype(jnp.bfloat16), "rep").astype(jnp.float32),
        lax.psum(owned[4].astype(jnp.bfloat16), "rep").astype(jnp.float32),
        lax.psum(owned[5].astype(jnp.bfloat16), "rep").astype(jnp.float32),
        lax.psum(owned[6].astype(jnp.bfloat16), "rep").astype(jnp.float32),
        lax.psum(owned[7].astype(jnp.bfloat16), "rep").astype(jnp.float32),
        lax.psum(owned[8].astype(jnp.bfloat16), "rep").astype(jnp.float32),
        lax.psum(owned[9].astype(jnp.bfloat16), "rep").astype(jnp.float32),
        lax.psum(owned[10].astype(jnp.bfloat16), "rep").astype(jnp.float32),
    )
    (
        sum_gain_media,
        sum_bias_media,
        sum_gain_latent,
        sum_bias_latent,
        sum_query,
        sum_keyval,
        sum_outproj,
        sum_gain_ff,
        sum_bias_ff,
        sum_ffin,
        sum_ffout,
    ) = summed
    return (
        new_latents,
        media_grad,
        latent_grad,
        sum_gain_media,
        sum_bias_media,
        sum_gain_latent,
        sum_bias_latent,
        sum_query,
        sum_keyval,
        sum_outproj,
        sum_gain_ff,
        sum_bias_ff,
        sum_ffin,
        sum_ffout,
    )


def solution(mesh):
    dp, rep = mesh.shape["dp"], mesh.shape["rep"]

    def program(*arrays):
        if rep != 2 or dp != PLANE * PLANE:
            return plain_shards(*arrays)
        return shards(dp, *arrays)

    return jax.shard_map(
        program,
        mesh=mesh,
        in_specs=(
            P(("dp", "rep"), None, None),
            P(("dp", "rep")),
            P(("dp", "rep"), None, None),
            P("dp"),
            P("dp"),
            P("dp"),
            P("dp"),
            P("dp", None),
            P("dp", None),
            P("dp", None),
            P("dp"),
            P("dp"),
            P("dp", None),
            P("dp", None),
            P(("dp", "rep"), None, None),
        ),
        out_specs=(
            P(("dp", "rep"), None, None),
            P(("dp", "rep"), None, None),
            P(("dp", "rep"), None, None),
            P("dp"),
            P("dp"),
            P("dp"),
            P("dp"),
            P("dp", None),
            P("dp", None),
            P("dp", None),
            P("dp"),
            P("dp"),
            P("dp", None),
            P("dp", None),
        ),
        check_vma=False,
    )
```

```python
import functools
import math

import jax
import jax.numpy as jnp
from jax import lax
from jax.experimental import pallas as pl
from jax.experimental.pallas import tpu as pltpu
from jax.sharding import PartitionSpec as P

HEADS = 8
GROUP = 4
EPS = 1e-05
NEG = -1e30
ROWS = 64
FF_TILE = 512
PLANE = 4
PAD = 8
F32 = jnp.float32
BF16 = jnp.bfloat16


def cost(us):
    return pl.CostEstimate(flops=int(us * 1.1e9), bytes_accessed=1 << 18, transcendentals=0)


def contract(a, b, over):
    return lax.dot_general(a, b, ((over[:1], over[1:]), ((), ())), preferred_element_type=F32)


def norm_rows(values):
    centred = values - jnp.mean(values, -1, keepdims=True)
    inverse = lax.rsqrt(jnp.mean(centred * centred, -1, keepdims=True) + EPS)
    return centred * inverse, inverse


def norm_back(grad, unit, inverse, gain):
    scaled = grad * gain
    return inverse * (
        scaled
        - jnp.mean(scaled, -1, keepdims=True)
        - unit * jnp.mean(scaled * unit, -1, keepdims=True)
    )


def spread(value, size):
    lane = lax.broadcasted_iota(jnp.int32, value.shape, 1) // size
    value = value.astype(F32)
    return jnp.concatenate([jnp.where(lane == h, value, 0.0) for h in range(GROUP)], 0)


def gathered(value, size):
    rows = value.shape[0] // GROUP
    lane = lax.broadcasted_iota(jnp.int32, (rows, value.shape[1]), 1) // size
    out = jnp.zeros((rows, value.shape[1]), F32)
    for h in range(GROUP):
        out = jnp.where(lane == h, value[h * rows : (h + 1) * rows], out)
    return out


def tie(*values):
    return lax.optimization_barrier(values)


def params(mib):
    return pltpu.CompilerParams(vmem_limit_bytes=mib << 20)


def image_at(i, c):
    return (i, 0, 0)


def fixed_at(*_):
    return (0, 0)


def order_kernel(place, *refs):
    sides = refs[:PLANE], refs[PLANE : 2 * PLANE]
    w_kv, w_q, w_o, norms = refs[2 * PLANE :]
    me, core = place[0], place[1]
    columns = sides[0][0].shape[0]
    chips = columns * PLANE
    kv_rows, o_rows = w_kv.shape[0] // chips // 2, w_o.shape[0] // chips // 2
    q_rows, inner = kv_rows // 2, w_q.shape[1]
    total = jnp.zeros(norms.shape, F32)
    for plane in range(PLANE):
        for column in range(columns):
            chip = me ^ (column * PLANE + plane)
            for side in range(2):
                block = sides[side][plane]
                half = core if side == 0 else 1 - core
                at = pl.multiple_of((chip * 2 + half) * kv_rows, kv_rows)
                w_kv[pl.ds(at, kv_rows), :] = block[column, :kv_rows, :]
                rest = block[column, kv_rows : kv_rows + q_rows, :]
                w_q[pl.ds(at, q_rows), :] = rest[:, :inner]
                w_q[pl.ds(pl.multiple_of(at + q_rows, q_rows), q_rows), :] = rest[:, inner:]
                at = pl.multiple_of((chip * 2 + half) * o_rows, o_rows)
                w_o[pl.ds(at, o_rows), :] = block[
                    column, kv_rows + q_rows : kv_rows + q_rows + o_rows, :
                ]
            total += sides[0][plane][column, kv_rows + q_rows + o_rows :, :].astype(F32)
    norms[...] = total


def in_order(place, own, other, inner):
    columns, _, width = own[0].shape
    return pl.pallas_call(
        order_kernel,
        grid_spec=pltpu.PrefetchScalarGridSpec(
            num_scalar_prefetch=1,
            grid=(1,),
            in_specs=[
                pl.BlockSpec(value.shape, lambda t, c: (0, 0, 0)) for value in (*own, *other)
            ],
            out_specs=[
                pl.BlockSpec((width, 2 * inner), fixed_at),
                pl.BlockSpec((width, inner), fixed_at),
                pl.BlockSpec((inner, width), fixed_at),
                pl.BlockSpec((8, width), fixed_at),
            ],
        ),
        out_shape=[
            jax.ShapeDtypeStruct((width, 2 * inner), BF16),
            jax.ShapeDtypeStruct((width, inner), BF16),
            jax.ShapeDtypeStruct((inner, width), BF16),
            jax.ShapeDtypeStruct((8, width), F32),
        ],
        compiler_params=params(24),
        cost_estimate=cost(1),
        name="in_order",
    )(place, *own, *other)


def whole_at(rank):
    return lambda *_: (0,) * rank


def small(kernel, values, outs, us, name):
    return pl.pallas_call(
        kernel,
        grid=(1,),
        in_specs=[pl.BlockSpec(value.shape, whole_at(value.ndim)) for value in values],
        out_specs=[pl.BlockSpec(shape, whole_at(len(shape))) for shape in outs],
        out_shape=[jax.ShapeDtypeStruct(shape, BF16) for shape in outs],
        compiler_params=params(20),
        cost_estimate=cost(us),
        name=name,
    )(*values)


def added(one, two):
    return (one.astype(F32) + two.astype(F32)).astype(BF16)


def fold_kernel(*refs):
    for column in range(len(refs) - PLANE):
        total = refs[0][column].astype(F32)
        for plane in range(1, PLANE):
            total += refs[plane][column].astype(F32)
        refs[PLANE + column][...] = total.astype(BF16)


def fold(values):
    columns = values[0].shape[0]
    return small(fold_kernel, values, [values[0].shape[1:]] * columns, 2, "fold")


def first_kernel(keep0, got0, keep1, got1, held0, pass0, held1, pass1):
    held0[...] = added(keep0[0], got0[0])
    pass0[...] = added(keep0[1], got0[1])
    held1[...] = added(keep1[0], got1[0])
    pass1[...] = added(keep1[1], got1[1])


def fold_first(keep0, got0, keep1, got1):
    values = keep0, got0, keep1, got1
    return small(first_kernel, values, [keep0.shape[1:]] * 4, 2, "fold_first")


def second_kernel(held0, got0, held1, got1, keep, send):
    half = held0.shape[1]
    for i in range(2):
        for out, column in ((keep, 2 * i), (send, 2 * i + 1)):
            out[i, :half, :] = added(held0[column], got0[column])
            out[i, half:, :] = added(held1[column], got1[column])


def fold_second(held0, got0, held1, got1):
    values = held0, got0, held1, got1
    shape = (2, 2 * held0.shape[1], held0.shape[2])
    return small(second_kernel, values, [shape] * 2, 2, "fold_second")


def third_kernel(keep, got, held, passed):
    held[...] = added(keep[0], got[0])
    passed[...] = added(keep[1], got[1])


def fold_third(keep, got):
    return small(third_kernel, (keep, got), [keep.shape[1:]] * 2, 0.5, "fold_third")


def both_kernel(keep, got, *outs):
    for plane, out in enumerate(outs):
        out[...] = (keep[plane].astype(F32) + got[plane].astype(F32)).astype(BF16)


def add_both(keep, got):
    tail = keep.shape[1:]
    whole = lambda t: (0, 0, 0, 0)
    return pl.pallas_call(
        both_kernel,
        grid=(1,),
        in_specs=[pl.BlockSpec(keep.shape, whole), pl.BlockSpec(keep.shape, whole)],
        out_specs=[pl.BlockSpec(tail, lambda t: (0, 0, 0)) for _ in range(PLANE)],
        out_shape=[jax.ShapeDtypeStruct(tail, BF16) for _ in range(PLANE)],
        compiler_params=params(16),
        cost_estimate=cost(2),
        name="add_both",
    )(keep, got)


def final_ff_kernel(place, own_in, other_in, own_out, other_out, grad_in, grad_out):
    first = place[1] == 0
    slot = own_out.shape[0]
    for chip in range(own_in.shape[1] // slot):
        here = slice(chip * slot, (chip + 1) * slot)
        one, two = own_in[:, here], other_in[:, here]
        at = 2 * chip * slot
        grad_in[:, at : at + slot] = jnp.where(first, one, two)
        grad_in[:, at + slot : at + 2 * slot] = jnp.where(first, two, one)
    grad_out[:slot, :] = jnp.where(first, own_out[...], other_out[...])
    grad_out[slot:, :] = jnp.where(first, other_out[...], own_out[...])


def final_ff(place, own_in, other_in, own_out, other_out):
    values = own_in, other_in, own_out, other_out
    shapes = (own_in.shape[0], 2 * own_in.shape[1]), (2 * own_out.shape[0], own_out.shape[1])
    return pl.pallas_call(
        final_ff_kernel,
        grid_spec=pltpu.PrefetchScalarGridSpec(
            num_scalar_prefetch=1,
            grid=(1,),
            in_specs=[pl.BlockSpec(value.shape, fixed_at) for value in values],
            out_specs=[pl.BlockSpec(shape, fixed_at) for shape in shapes],
        ),
        out_shape=[jax.ShapeDtypeStruct(shape, F32) for shape in shapes],
        compiler_params=params(16),
        cost_estimate=cost(2),
        name="final_ff",
    )(place, *values)


def final_attn_kernel(place, own, other, grad_kv, grad_q, grad_o):
    kv_rows, o_rows = grad_kv.shape[0] // 2, grad_o.shape[0] // 2
    q_rows, inner = kv_rows // 2, grad_q.shape[1]
    first = place[1] == 0
    for half in range(2):
        value = jnp.where(first == (half == 0), own[...], other[...])
        at = half * kv_rows
        grad_kv[at : at + kv_rows, :] = value[:kv_rows]
        rest = value[kv_rows : kv_rows + q_rows]
        grad_q[at : at + q_rows, :] = rest[:, :inner]
        grad_q[at + q_rows : at + kv_rows, :] = rest[:, inner:]
        grad_o[half * o_rows : (half + 1) * o_rows, :] = value[
            kv_rows + q_rows : kv_rows + q_rows + o_rows
        ]


def final_attn(place, own, other, inner, kv_rows, o_rows):
    width = own.shape[1]
    shapes = (2 * kv_rows, width), (2 * kv_rows, inner), (2 * o_rows, width)
    return pl.pallas_call(
        final_attn_kernel,
        grid_spec=pltpu.PrefetchScalarGridSpec(
            num_scalar_prefetch=1,
            grid=(1,),
            in_specs=[pl.BlockSpec(own.shape, fixed_at), pl.BlockSpec(own.shape, fixed_at)],
            out_specs=[pl.BlockSpec(shape, fixed_at) for shape in shapes],
        ),
        out_shape=[jax.ShapeDtypeStruct(shape, F32) for shape in shapes],
        compiler_params=params(16),
        cost_estimate=cost(2),
        name="final_attn",
    )(place, own, other)


def attend_kernel(counts, media, latent, norms, w_kv, w_q, *refs):
    turned, lat_low, keyvals, queries, mixed, key_input = refs[-6:]
    media_len, lat_len = media.shape[1], latent.shape[1]
    keys_len = media_len + lat_len
    inner = w_q.shape[1]
    size = inner // HEADS
    wide = size * GROUP
    for at in range(0, media_len, ROWS):
        unit, _ = norm_rows(media[0, at : at + ROWS, :].astype(F32))
        key_input[at : at + ROWS, :] = (unit * norms[0:1, :] + norms[1:2, :]).astype(BF16)
    unit, _ = norm_rows(latent[0].astype(F32))
    low = (unit * norms[2:3, :] + norms[3:4, :]).astype(BF16)
    key_input[media_len:, :] = low
    lat_low[0] = low
    query = contract(low, w_q[...], (1, 0)).astype(BF16)
    queries[0] = query
    keyvals[0] = contract(key_input[...], w_kv[...], (1, 0)).astype(BF16)
    for side in range(2):

        @pl.when(pl.program_id(0) % 2 == side)
        def _(side=side):
            turned[0, :, side * keys_len : (side + 1) * keys_len] = key_input[...].T

    key_at = lax.broadcasted_iota(jnp.int32, (1, keys_len), 1)
    valid = (key_at < counts[pl.program_id(0)]) | (key_at >= media_len)
    for at in range(0, inner, wide):
        own = spread(query[:, at : at + wide].astype(F32) * (1.0 / math.sqrt(size)), size)
        scores = contract(own.astype(BF16), keyvals[0, :, at : at + wide], (1, 1))
        scores = jnp.where(valid, scores, NEG)
        expd = jnp.exp(scores - jnp.max(scores, -1, keepdims=True))
        probs = (expd * (1.0 / jnp.sum(expd, -1, keepdims=True))).astype(BF16)
        out = contract(probs, keyvals[0, :, inner + at : inner + at + wide], (1, 0))
        mixed[0, :, at : at + wide] = gathered(out, size).astype(BF16)


def attend(counts, media, latent, norms, w_kv, w_q, first, run, into=()):
    images, media_len, width = media.shape
    lat_len, inner = latent.shape[1], w_q.shape[1]
    keys_len = media_len + lat_len
    at = lambda i, c: (i + first, 0, 0)
    shapes = [
        (images, lat_len, width),
        (images, keys_len, 2 * inner),
        (images, lat_len, inner),
        (images, lat_len, inner),
    ]
    return pl.pallas_call(
        attend_kernel,
        grid_spec=pltpu.PrefetchScalarGridSpec(
            num_scalar_prefetch=1,
            grid=(run,),
            in_specs=[
                pl.BlockSpec((1, media_len, width), at),
                pl.BlockSpec((1, lat_len, width), at),
                pl.BlockSpec(norms.shape, fixed_at),
                pl.BlockSpec(w_kv.shape, fixed_at),
                pl.BlockSpec(w_q.shape, fixed_at),
                *[pl.BlockSpec(memory_space=pl.ANY) for _ in into],
            ],
            out_specs=[
                pl.BlockSpec((1, width, 2 * keys_len), lambda i, c: ((i + first) // 2, 0, 0)),
                *[pl.BlockSpec((1,) + shape[1:], at) for shape in shapes],
            ],
            scratch_shapes=[pltpu.VMEM((keys_len, width), BF16)],
        ),
        out_shape=[
            jax.ShapeDtypeStruct((images // 2, width, 2 * keys_len), BF16),
            *[jax.ShapeDtypeStruct(shape, BF16) for shape in shapes],
        ],
        input_output_aliases={6 + i: i for i in range(len(into))},
        compiler_params=params(32),
        cost_estimate=cost(14),
        name="attend",
    )(counts[first : first + run], media, latent, norms, w_kv, w_q, *into)


def resid_kernel(mixed, latent, w_o, norms, resid, low):
    value = latent[...].astype(F32) + contract(mixed[...], w_o[...], (1, 0))
    resid[...] = value
    unit, _ = norm_rows(value)
    low[...] = (unit * norms[4:5, :] + norms[5:6, :]).astype(BF16)


def add_branch(mixed, latent, w_o, norms):
    rows, width = latent.shape
    inner = mixed.shape[1]
    block = rows // 4
    row_at = lambda i: (i, 0)
    return pl.pallas_call(
        resid_kernel,
        grid=(rows // block,),
        in_specs=[
            pl.BlockSpec((block, inner), row_at),
            pl.BlockSpec((block, width), row_at),
            pl.BlockSpec(w_o.shape, fixed_at),
            pl.BlockSpec(norms.shape, fixed_at),
        ],
        out_specs=[pl.BlockSpec((block, width), row_at), pl.BlockSpec((block, width), row_at)],
        out_shape=[
            jax.ShapeDtypeStruct((rows, width), F32),
            jax.ShapeDtypeStruct((rows, width), BF16),
        ],
        compiler_params=params(16),
        cost_estimate=cost(3),
        name="add_branch",
    )(mixed, latent, w_o, norms)


def ff_kernel(place, *refs):
    low0, low1, dout0, dout1 = refs[:4]
    lo, hi = refs[4:8], refs[8:12]
    activ, slope, low_t, dout, w_in = refs[12:17]
    keep0, send0, keep1, send1 = refs[17:21]
    low, grad = refs[21:]
    step, steps = pl.program_id(0), pl.num_programs(0)
    me = place[0]
    half = low0.shape[0]
    part = lo[0].shape[1]
    slot = grad.shape[0] // PLANE
    cut = slot // 2

    @pl.when(step == 0)
    def _():
        low[:half, :] = low0[...]
        low[half:, :] = low1[...]
        dout[:half, :] = dout0[...]
        dout[half:, :] = dout1[...]
        low_t[...] = low[...].T

    def put(pieces):
        for plane in range(PLANE):
            for column in range(pieces[0].shape[0]):
                at = pl.multiple_of((me ^ (column * PLANE + plane)) * part, part)
                w_in[pl.ds(at, part), :] = pieces[plane][column]

    pl.when(step < steps // 2)(lambda: put(lo))
    pl.when(step >= steps // 2)(lambda: put(hi))
    pre = contract(low[...], w_in[...], (1, 0))
    cdf = 0.5 * (1.0 + lax.erf(pre * math.sqrt(0.5)))
    slope[...] = cdf + pre * (jnp.exp(pre * pre * -0.5) * (1.0 / math.sqrt(2.0 * math.pi)))
    value = (pre * cdf).astype(BF16)
    activ[...] = value
    grad[...] = contract(value, dout[...], (0, 0)).astype(BF16)

    def block(plane, at):
        at = pl.multiple_of((plane ^ (me % PLANE)) * slot + at, cut)
        return grad[pl.ds(at, cut), :]

    for i in range(2):
        keep0[i, 0] = block(2 * i, 0)
        send0[i, 0] = block(2 * i + 1, 0)
        keep1[i, 0] = block(i, cut)
        send1[i, 0] = block(2 + i, cut)


def feed_forward(place, lows, douts, lo, hi, slot):
    half, width = lows[0].shape
    rows = 2 * half
    columns, part, cut = lo[0].shape
    tile = PLANE * slot
    steps = 2 * cut // tile
    in_at = lambda t, c: (0, t)
    lo_at = lambda t, c: (0, 0, jnp.minimum(t, steps // 2 - 1))
    hi_at = lambda t, c: (0, 0, jnp.maximum(t - steps // 2, 0))
    once = pl.Buffered(1)
    return pl.pallas_call(
        ff_kernel,
        grid_spec=pltpu.PrefetchScalarGridSpec(
            num_scalar_prefetch=1,
            grid=(steps,),
            in_specs=[
                *[pl.BlockSpec((half, width), fixed_at, pipeline_mode=once) for _ in range(4)],
                *[pl.BlockSpec((columns, part, tile), lo_at) for _ in lo],
                *[pl.BlockSpec((columns, part, tile), hi_at) for _ in hi],
            ],
            out_specs=[
                pl.BlockSpec((rows, tile), in_at),
                pl.BlockSpec((rows, tile), in_at),
                pl.BlockSpec((width, rows), fixed_at),
                pl.BlockSpec((rows, width), fixed_at),
                pl.BlockSpec((width, tile), in_at),
                *[
                    pl.BlockSpec(
                        (2, 1, slot // 2, width), lambda t, c: (0, t ^ (c[0] // PLANE), 0, 0)
                    )
                    for _ in range(4)
                ],
            ],
            scratch_shapes=[pltpu.VMEM((rows, width), BF16), pltpu.VMEM((tile, width), BF16)],
        ),
        out_shape=[
            jax.ShapeDtypeStruct((rows, 2 * cut), BF16),
            jax.ShapeDtypeStruct((rows, 2 * cut), F32),
            jax.ShapeDtypeStruct((width, rows), BF16),
            jax.ShapeDtypeStruct((rows, width), BF16),
            jax.ShapeDtypeStruct((width, 2 * cut), BF16),
            *[
                kind((2, columns, slot // 2, width), BF16)
                for kind in (jax.ShapeDtypeStruct, pltpu.HBM) * 2
            ],
        ],
        compiler_params=params(44),
        cost_estimate=cost(18),
        name="feed_forward",
    )(place, *lows, *douts, *lo, *hi)


def ff_back_kernel(
    place, dout, low_t, w_in, w_out, slope, keep0, send0, keep1, send1, kept, sent, total, grad_in
):
    step, steps = pl.program_id(0), pl.num_programs(0)
    columns, cut = keep0.shape[1:3]

    @pl.when(step == 0)
    def _():
        total[...] = jnp.zeros_like(total)

    grad = (contract(dout[...], w_out[...], (1, 1)) * slope[...]).astype(BF16)
    grad_in[...] = contract(low_t[...], grad, (1, 0)).astype(BF16)

    def block(plane, column, at):
        at = pl.multiple_of((place[0] ^ (column * PLANE + plane)) * 2 * cut + at, cut)
        return grad_in[pl.ds(at, cut), :]

    for column in range(columns):
        for i in range(2):
            keep0[i, column] = block(2 * i, column, 0)
            send0[i, column] = block(2 * i + 1, column, 0)
            keep1[i, column] = block(i, column, cut)
            send1[i, column] = block(2 + i, column, cut)
    total[...] += contract(grad, w_in[...], (1, 1))

    @pl.when(step == steps - 1)
    def _():
        half = kept.shape[0]
        kept[...] = total[:half, :]
        sent[...] = total[half:, :].astype(BF16)


def feed_back(place, dout, low_t, w_in, w_out, slope, columns, part):
    rows, width = dout.shape
    hidden = w_in.shape[1]
    tile = min(FF_TILE, hidden)
    half = rows // 2
    in_at, out_at = (lambda t, c: (0, t)), (lambda t, c: (t, 0))
    once = pl.Buffered(1)
    return pl.pallas_call(
        ff_back_kernel,
        grid_spec=pltpu.PrefetchScalarGridSpec(
            num_scalar_prefetch=1,
            grid=(hidden // tile,),
            in_specs=[
                pl.BlockSpec((rows, width), fixed_at, pipeline_mode=once),
                pl.BlockSpec((width, rows), fixed_at, pipeline_mode=once),
                pl.BlockSpec((width, tile), in_at),
                pl.BlockSpec((tile, width), out_at),
                pl.BlockSpec((rows, tile), in_at),
            ],
            out_specs=[
                *[
                    pl.BlockSpec((2, columns, part // 2, tile), lambda t, c: (0, 0, 0, t))
                    for _ in range(4)
                ],
                pl.BlockSpec((half, width), fixed_at, pipeline_mode=once),
                pl.BlockSpec((half, width), fixed_at, pipeline_mode=once),
            ],
            scratch_shapes=[pltpu.VMEM((rows, width), F32), pltpu.VMEM((width, tile), BF16)],
        ),
        out_shape=[
            *[
                kind((2, columns, part // 2, hidden), BF16)
                for kind in (jax.ShapeDtypeStruct, pltpu.HBM) * 2
            ],
            jax.ShapeDtypeStruct((half, width), F32),
            jax.ShapeDtypeStruct((half, width), BF16),
        ],
        compiler_params=params(48),
        cost_estimate=cost(21),
        name="feed_back",
    )(place, dout, low_t, w_in, w_out, slope)


def ff_out_kernel(activ, w_out, kept, sent, total):
    step = pl.program_id(0)

    @pl.when(step == 0)
    def _():
        total[...] = jnp.zeros_like(total)

    total[...] += contract(activ[...], w_out[...], (1, 0))

    @pl.when(step == pl.num_programs(0) - 1)
    def _():
        half = kept.shape[0]
        kept[...] = total[:half, :]
        sent[...] = total[half:, :].astype(BF16)


def feed_out(activ, w_out):
    rows, hidden = activ.shape
    width = w_out.shape[1]
    tile = min(FF_TILE, hidden)
    half = rows // 2
    once = pl.Buffered(1)
    return pl.pallas_call(
        ff_out_kernel,
        grid=(hidden // tile,),
        in_specs=[
            pl.BlockSpec((rows, tile), lambda t: (0, t)),
            pl.BlockSpec((tile, width), lambda t: (t, 0)),
        ],
        out_specs=[pl.BlockSpec((half, width), fixed_at, pipeline_mode=once)] * 2,
        out_shape=[
            jax.ShapeDtypeStruct((half, width), F32),
            jax.ShapeDtypeStruct((half, width), BF16),
        ],
        scratch_shapes=[pltpu.VMEM((rows, width), F32)],
        compiler_params=params(24),
        cost_estimate=cost(7),
        name="feed_out",
    )(activ, w_out)


def resid_back_kernel(
    kept,
    got,
    resid,
    cotangent,
    mixed,
    w_o,
    norms,
    grad_resid,
    grad_mixed,
    grad_o,
    vectors,
    total,
):
    step = pl.program_id(0)

    @pl.when(step == 0)
    def _():
        vectors[...] = jnp.zeros_like(vectors)
        total[...] = jnp.zeros_like(total)

    grad = kept[...] + got[...].astype(F32)
    unit, inverse = norm_rows(resid[...])
    vectors[0:1, :] += jnp.sum(grad * unit, 0, keepdims=True)
    vectors[1:2, :] += jnp.sum(grad, 0, keepdims=True)
    value = cotangent[...] + norm_back(grad, unit, inverse, norms[4:5, :])
    grad_resid[...] = value
    low = value.astype(BF16)
    grad_mixed[...] = contract(low, w_o[...], (1, 1)).astype(BF16)
    total[...] += contract(mixed[...], low, (0, 0))
    grad_o[...] = total[...].astype(BF16)


def resid_back(kept, got, resid, cotangent, mixed, w_o, norms):
    rows, width = resid.shape
    inner = mixed.shape[1]
    block = rows // 4
    row_at = lambda i: (i, 0)
    wide = pl.BlockSpec((block, width), row_at)
    return pl.pallas_call(
        resid_back_kernel,
        grid=(rows // block,),
        in_specs=[
            *[wide] * 4,
            pl.BlockSpec((block, inner), row_at),
            pl.BlockSpec(w_o.shape, fixed_at),
            pl.BlockSpec(norms.shape, fixed_at),
        ],
        out_specs=[
            wide,
            pl.BlockSpec((block, inner), row_at),
            pl.BlockSpec(w_o.shape, fixed_at),
            pl.BlockSpec((8, width), fixed_at),
        ],
        out_shape=[
            jax.ShapeDtypeStruct((rows, width), F32),
            jax.ShapeDtypeStruct((rows, inner), BF16),
            jax.ShapeDtypeStruct(w_o.shape, BF16),
            jax.ShapeDtypeStruct((8, width), F32),
        ],
        scratch_shapes=[pltpu.VMEM(w_o.shape, F32)],
        compiler_params=params(24),
        cost_estimate=cost(6),
        name="resid_back",
    )(kept, got, resid, cotangent, mixed, w_o, norms)


def as_row(column):
    out = []
    size = 128
    same = lax.broadcasted_iota(jnp.int32, (size, size), 0) == lax.broadcasted_iota(
        jnp.int32, (size, size), 1
    )
    for at in range(0, column.shape[0], size):
        out.append(jnp.sum(jnp.where(same, column[at : at + size, :], 0.0), 0, keepdims=True))
    return jnp.concatenate(out, 1)


def in_bf16(row):
    parts = []
    for _ in range(3):
        parts.append(row.astype(BF16))
        row = row - parts[-1].astype(F32)
    return parts


def attend_back_kernel(counts, keyvals, queries, grad_mixed, grad_kv, grad_q):
    taken, keys_len = keyvals.shape[:2]
    lat_len, inner = queries.shape[1:]
    media_len = keys_len - lat_len
    size = inner // HEADS
    wide = size * GROUP
    scale = 1.0 / math.sqrt(size)
    key_at = lax.broadcasted_iota(jnp.int32, (keys_len, 1), 0)

    def begin(i, at):
        own = spread(queries[i, :, at : at + wide].astype(F32) * scale, size).astype(BF16)
        grad = spread(grad_mixed[i, :, at : at + wide], size).astype(BF16)
        scores = contract(keyvals[i, :, at : at + wide], own, (1, 1))
        grad_probs = contract(keyvals[i, :, inner + at : inner + at + wide], grad, (1, 1))
        return own, grad, scores, grad_probs

    def weigh(i, scores, grad_probs):
        valid = (key_at < counts[pl.program_id(0) * taken + i]) | (key_at >= media_len)
        scores = jnp.where(valid, scores, NEG)
        expd = jnp.exp(scores - jnp.max(scores, 0, keepdims=True))
        probs = expd * (1.0 / jnp.sum(expd, 0, keepdims=True))
        held = jnp.sum(probs * grad_probs, 0, keepdims=True)
        return probs.astype(BF16), (probs * (grad_probs - held)).astype(BF16)

    def end(i, at, own, grad, probs, low):
        grad_v = contract(probs, grad, (1, 0)).astype(BF16)
        grad_kv[i, :, inner + at : inner + at + wide] = grad_v
        grad_kv[i, :, at : at + wide] = contract(low, own, (1, 0)).astype(BF16)
        back = contract(low, keyvals[i, :, at : at + wide], (0, 0))
        grad_q[i, :, at : at + wide] = (gathered(back, size) * scale).astype(BF16)

    items = [(i, at) for i in range(taken) for at in range(0, inner, wide)]
    ahead, behind = begin(*items[0]), None
    for n, item in enumerate(items):
        own, grad, scores, grad_probs = ahead
        if n + 1 < len(items):
            ahead = begin(*items[n + 1])
        weights = weigh(item[0], scores, grad_probs)
        if behind:
            end(*behind)
        behind = (*item, own, grad, *weights)
    end(*behind)


def weight_back_kernel(
    place,
    grad_kv,
    grad_q,
    turned,
    lat_low,
    w_kv,
    w_q,
    norms,
    grad_o,
    ff_vectors,
    keep,
    send,
    total,
    sums,
    lat_kv,
    lat_q,
    total_q,
):
    step, steps = pl.program_id(0), pl.num_programs(0)
    lat_len, inner = grad_q.shape[1:]
    keys_len = grad_kv.shape[1]
    media_len = keys_len - lat_len

    @pl.when(step == 0)
    def _():
        total[...] = jnp.zeros_like(total)
        sums[...] = jnp.zeros_like(sums)

    both = grad_kv[...].reshape(2 * keys_len, 2 * inner)
    total[...] += contract(turned[0], both, (1, 0))
    sums[...] += jnp.sum(both.astype(F32), 0, keepdims=True)
    for side in range(2):
        here = pl.ds(pl.multiple_of((2 * step + side) * lat_len, lat_len), lat_len)
        lat_kv[here, :] = grad_kv[side, media_len:, :]
        lat_q[here, :] = grad_q[side]

    @pl.when(step == steps - 1)
    def _():
        lat_w = contract(lat_low[...], lat_kv[...], (0, 0))
        lat_wq = contract(lat_low[...], lat_q[...], (0, 0))
        weight, weight_q = w_kv[...].astype(F32), w_q[...].astype(F32)
        lat_sum = jnp.sum(lat_kv[...].astype(F32), 0, keepdims=True)
        lat_sum_q = jnp.sum(lat_q[...].astype(F32), 0, keepdims=True)
        rows = in_bf16(sums[0:1, :] - lat_sum) + in_bf16(lat_sum) + [jnp.zeros((2, 2 * inner), BF16)]
        rows_q = in_bf16(lat_sum_q) + [jnp.zeros((5, inner), BF16)]
        biases = contract(jnp.concatenate(rows, 0), w_kv[...], (1, 1))
        biases_q = contract(jnp.concatenate(rows_q, 0), w_q[...], (1, 1))
        media_bias = jnp.sum(biases[0:3], 0, keepdims=True)
        lat_bias = jnp.sum(biases[3:6], 0, keepdims=True) + jnp.sum(biases_q, 0, keepdims=True)
        media_both = as_row(jnp.sum((total[...] - lat_w) * weight, 1, keepdims=True))
        lat_both = as_row(
            jnp.sum(lat_w * weight, 1, keepdims=True)
            + jnp.sum(lat_wq * weight_q, 1, keepdims=True)
        )
        vectors = [
            (media_both - norms[1:2, :] * media_bias) / norms[0:1, :],
            media_bias,
            (lat_both - norms[3:4, :] * lat_bias) / norms[2:3, :],
            lat_bias,
            ff_vectors[0:2, :],
            jnp.zeros((2, ff_vectors.shape[1]), F32),
        ]
        vectors = jnp.concatenate(vectors, 0).astype(BF16)
        total_q[...] = lat_wq
        me, core = place[0], place[1]
        columns = keep.shape[1]
        kv_rows = total.shape[0] // (2 * columns * PLANE)
        o_rows = grad_o.shape[0] // (2 * columns * PLANE)
        q_rows = kv_rows // 2
        for plane in range(PLANE):
            for column in range(columns):
                chip = me ^ (column * PLANE + plane)
                for out, half in ((keep, core), (send, 1 - core)):
                    at = pl.multiple_of((chip * 2 + half) * kv_rows, kv_rows)
                    out[plane, column, :kv_rows, :] = total[pl.ds(at, kv_rows), :].astype(BF16)
                    value = total_q[pl.ds(at, kv_rows), :].astype(BF16)
                    row = kv_rows
                    out[plane, column, row : row + q_rows, :inner] = value[:q_rows]
                    out[plane, column, row : row + q_rows, inner:] = value[q_rows:]
                    row += q_rows
                    at = pl.multiple_of((chip * 2 + half) * o_rows, o_rows)
                    out[plane, column, row : row + o_rows, :] = grad_o[pl.ds(at, o_rows), :]
                    out[plane, column, row + o_rows :, :] = vectors


def attend_back(counts, keyvals, queries, grad_mixed):
    images, keys_len, wide = keyvals.shape
    lat_len, inner = queries.shape[1:]
    taken = 2
    at = lambda i, c: (i, 0, 0)
    return pl.pallas_call(
        attend_back_kernel,
        grid_spec=pltpu.PrefetchScalarGridSpec(
            num_scalar_prefetch=1,
            grid=(images // taken,),
            in_specs=[
                pl.BlockSpec((taken, keys_len, wide), at),
                pl.BlockSpec((taken, lat_len, inner), at),
                pl.BlockSpec((taken, lat_len, inner), at),
            ],
            out_specs=[
                pl.BlockSpec((taken, keys_len, wide), at),
                pl.BlockSpec((taken, lat_len, inner), at),
            ],
        ),
        out_shape=[
            jax.ShapeDtypeStruct((images, keys_len, wide), BF16),
            jax.ShapeDtypeStruct((images, lat_len, inner), BF16),
        ],
        compiler_params=params(58),
        cost_estimate=cost(15),
        name="attend_back",
    )(counts, keyvals, queries, grad_mixed)


def weight_back(
    place, grad_kv, grad_q, turned, lat_low, w_kv, w_q, norms, grad_o, ff_vectors, columns
):
    images, keys_len, _ = grad_kv.shape
    width = turned.shape[1]
    lat_len, inner = grad_q.shape[1:]
    rows = images * lat_len
    chips = columns * PLANE
    kv_rows, o_rows = width // chips // 2, inner // chips // 2
    pack = (PLANE, columns, kv_rows + kv_rows // 2 + o_rows + PAD, width)
    at = lambda i, c: (i, 0, 0)
    once = pl.Buffered(1)
    return pl.pallas_call(
        weight_back_kernel,
        grid_spec=pltpu.PrefetchScalarGridSpec(
            num_scalar_prefetch=1,
            grid=(images // 2,),
            in_specs=[
                pl.BlockSpec((2, keys_len, 2 * inner), at),
                pl.BlockSpec((2, lat_len, inner), at),
                pl.BlockSpec((1, width, 2 * keys_len), at),
                pl.BlockSpec(lat_low.shape, fixed_at, pipeline_mode=once),
                pl.BlockSpec(w_kv.shape, fixed_at, pipeline_mode=once),
                pl.BlockSpec(w_q.shape, fixed_at, pipeline_mode=once),
                pl.BlockSpec(norms.shape, fixed_at),
                pl.BlockSpec(grad_o.shape, fixed_at, pipeline_mode=once),
                pl.BlockSpec(ff_vectors.shape, fixed_at),
            ],
            out_specs=[
                pl.BlockSpec(pack, whole_at(4), pipeline_mode=once),
                pl.BlockSpec(pack, whole_at(4), pipeline_mode=once),
            ],
            scratch_shapes=[
                pltpu.VMEM(w_kv.shape, F32),
                pltpu.VMEM((8, 2 * inner), F32),
                pltpu.VMEM((rows, 2 * inner), BF16),
                pltpu.VMEM((rows, inner), BF16),
                pltpu.VMEM(w_q.shape, F32),
            ],
        ),
        out_shape=[jax.ShapeDtypeStruct(pack, BF16), jax.ShapeDtypeStruct(pack, BF16)],
        compiler_params=params(58),
        cost_estimate=cost(17),
        name="weight_back",
    )(place, grad_kv, grad_q, turned, lat_low, w_kv, w_q, norms, grad_o, ff_vectors)


def latent_back_kernel(grad_kv, grad_q, latent, grad_resid, w_kv, w_q, norms, latent_grad):
    images, lat_len, width = latent.shape
    rows = images * lat_len
    grad = contract(grad_kv[...].reshape(rows, grad_kv.shape[2]), w_kv[...], (1, 1))
    grad += contract(grad_q[...].reshape(rows, grad_q.shape[2]), w_q[...], (1, 1))
    unit, inverse = norm_rows(latent[...].reshape(rows, width).astype(F32))
    back = norm_back(grad, unit, inverse, norms[2:3, :])
    latent_grad[...] = grad_resid[...] + back.reshape(images, lat_len, width)


def latent_back(grad_kv, grad_q, latent, grad_resid, w_kv, w_q, norms):
    images, lat_len, width = latent.shape
    inner = w_q.shape[1]
    tail = grad_kv.shape[1] // lat_len - 1
    block = images // 2
    at = lambda i: (i, 0, 0)
    return pl.pallas_call(
        latent_back_kernel,
        grid=(images // block,),
        in_specs=[
            pl.BlockSpec((block, lat_len, 2 * inner), lambda i: (i, tail, 0)),
            pl.BlockSpec((block, lat_len, inner), at),
            pl.BlockSpec((block, lat_len, width), at),
            pl.BlockSpec((block, lat_len, width), at),
            pl.BlockSpec(w_kv.shape, fixed_at),
            pl.BlockSpec(w_q.shape, fixed_at),
            pl.BlockSpec(norms.shape, fixed_at),
        ],
        out_specs=pl.BlockSpec((block, lat_len, width), at),
        out_shape=jax.ShapeDtypeStruct((images, lat_len, width), F32),
        compiler_params=params(32),
        cost_estimate=cost(4),
        name="latent_back",
    )(grad_kv, grad_q, latent, grad_resid, w_kv, w_q, norms)


def media_back_kernel(media, grad_kv, norms, w_kv, *refs):
    out, grad = refs[-2:]
    grad[...] = contract(grad_kv[0], w_kv[...], (1, 1))
    for at in range(0, media.shape[1], ROWS):
        unit, inverse = norm_rows(media[0, at : at + ROWS, :].astype(F32))
        out[0, at : at + ROWS, :] = norm_back(grad[at : at + ROWS, :], unit, inverse, norms[0:1, :])


def media_back(media, grad_kv, norms, w_kv, first, run, into=()):
    images, media_len, width = media.shape
    inner2 = w_kv.shape[1]
    at = lambda i: (i + first, 0, 0)
    return pl.pallas_call(
        media_back_kernel,
        grid=(run,),
        in_specs=[
            pl.BlockSpec((1, media_len, width), at),
            pl.BlockSpec((1, media_len, inner2), at),
            pl.BlockSpec(norms.shape, fixed_at),
            pl.BlockSpec(w_kv.shape, fixed_at),
            *[pl.BlockSpec(memory_space=pl.ANY) for _ in into],
        ],
        out_specs=pl.BlockSpec((1, media_len, width), at),
        out_shape=jax.ShapeDtypeStruct((images, media_len, width), F32),
        input_output_aliases={4 + i: i for i in range(len(into))},
        scratch_shapes=[pltpu.VMEM((media_len, width), F32)],
        compiler_params=params(32),
        cost_estimate=cost(0.5),
        name="media_back",
    )(media, grad_kv, norms, w_kv, *into)


def fold_rows(value):
    half = value.shape[0] // 2
    return jnp.concatenate([value[:half], value[half:]], 1)


def shards(
    dp,
    media_tokens,
    patch_counts,
    latents,
    media_gain,
    media_bias,
    latent_gain,
    latent_bias,
    query_weight,
    keyval_weight,
    outproj_weight,
    ff_gain,
    ff_bias,
    ff_in_weight,
    ff_out_weight,
    cotangent,
):
    me, core = lax.axis_index("dp"), lax.axis_index("rep")
    place = jnp.stack([me, core]).astype(jnp.int32)
    columns = dp // PLANE
    images, _, width = media_tokens.shape
    lat_len = latents.shape[1]
    inner = query_weight.shape[1]
    part = width // dp
    slot = ff_in_weight.shape[1] // dp // 2
    kv_rows, o_rows = part // 2, inner // dp // 2
    flat = (images * lat_len, width)

    def swap(value, bits):
        return lax.ppermute(value, "dp", [(i, i ^ bits) for i in range(dp)])

    def other(value):
        return lax.ppermute(value, "rep", [(0, 1), (1, 0)])

    def mine(value, axis):
        return lax.dynamic_index_in_dim(value, core, axis, keepdims=False)

    def down(value):
        return [value] + [swap(value, c * PLANE) for c in range(1, columns)]

    def across(values):
        return [values[0]] + [swap(values[p], p) for p in range(1, PLANE)]

    def down_sums(values):
        return [values[0]] + [swap(values[c], c * PLANE) for c in range(1, columns)]

    norms = jnp.stack([media_gain, media_bias, latent_gain, latent_bias, ff_gain, ff_bias])
    norms = lax.dynamic_update_slice(jnp.zeros((PAD, width), BF16), norms, (0, me * part))
    attn = [
        mine(keyval_weight.reshape(2, kv_rows, width), 0),
        fold_rows(mine(query_weight.reshape(2, kv_rows, inner), 0)),
        mine(outproj_weight.reshape(2, o_rows, width), 0),
        norms,
    ]
    attn = jnp.stack(down(jnp.concatenate(attn, 0)))
    ffout = mine(ff_out_weight.reshape(2, slot, width), 0)
    ffin = mine(ff_in_weight.reshape(part, dp, 2, slot), 2).reshape(part, dp * slot)
    cut = ffin.shape[1] // 2
    ffin = jnp.concatenate([ffin[:, :cut], ffin[:, cut:]], 0)
    attn, ffout, ffin = tie(attn, ffout, ffin)
    attn = [attn] + [swap(attn, p) for p in range(1, PLANE)]
    w_ffout = lax.all_gather(ffout, "dp", axis=0, tiled=True)
    ffin = jnp.stack([ffin, swap(ffin, 2 * PLANE)])
    got = swap(ffin, PLANE)
    w_kv, w_q, w_o, norms = in_order(place, attn, [other(value) for value in attn], inner)
    lo, hi = [
        jnp.stack([ffin[0, rows], got[0, rows], ffin[1, rows], got[1, rows]])
        for rows in (slice(0, part), slice(part, 2 * part))
    ]
    dout = cotangent.astype(BF16).reshape(flat)
    douts = dout, other(dout)

    w_kv, lo, hi = tie(w_kv, lo, hi)
    lo, hi = {0: lo, 2: swap(lo, 2)}, {0: hi, 1: swap(hi, 1)}
    run = images // 2
    held = attend(patch_counts, media_tokens, latents, norms, w_kv, w_q, 0, run)
    held, lo, hi = tie(held, lo, hi)
    lo[1], lo[3] = swap(lo[0], 1), swap(lo[2], 1)
    hi[2], hi[3] = swap(hi[0], 2), swap(hi[1], 2)
    turned, lat_low, keyvals, queries, mixed = attend(
        patch_counts, media_tokens, latents, norms, w_kv, w_q, run, images - run, held
    )
    mixed = mixed.reshape(-1, inner)
    resid, low = add_branch(mixed, latents.reshape(flat), w_o, norms)
    low, lo, hi = tie(low, lo, hi)
    lo, hi = [lo[p] for p in range(PLANE)], [hi[p] for p in range(PLANE)]

    activ, slope, low_t, dout, w_ffin, *grads = feed_forward(
        place, (low, other(low)), douts, lo, hi, slot
    )
    out_sum = grads[0], swap(grads[1], 1), grads[2], swap(grads[3], 2)
    *grads, kept, sent = feed_back(place, dout, low_t, w_ffin, w_ffout, slope, columns, part)
    kept, out_sum = tie(kept, out_sum)
    grad_resid, grad_mixed, grad_o, ff_vectors = resid_back(
        kept, other(sent), resid, cotangent.reshape(flat), mixed, w_o, norms
    )
    grad_mixed, out_sum = tie(grad_mixed, out_sum)
    out_sum = fold_first(*out_sum)
    grad_mixed, out_sum = tie(grad_mixed, out_sum)
    out_sum = out_sum[0], swap(out_sum[1], 2), out_sum[2], swap(out_sum[3], 1)
    in_sum = grads[0], swap(grads[1], 1), grads[2], swap(grads[3], 2)
    grad_kv, grad_q = attend_back(
        patch_counts, keyvals, queries, grad_mixed.reshape(images, lat_len, inner)
    )
    grad_kv, grad_q, out_sum, in_sum = tie(grad_kv, grad_q, out_sum, in_sum)
    keep, send = fold_second(*out_sum)
    in_sum = fold_first(*in_sum)
    grad_q, keep, send, in_sum = tie(grad_q, keep, send, in_sum)
    out_sum = keep, swap(send, PLANE)
    in_sum = in_sum[0], swap(in_sum[1], 2), in_sum[2], swap(in_sum[3], 1)
    keep, send = weight_back(
        place,
        grad_kv,
        grad_q,
        turned,
        lat_low.reshape(flat),
        w_kv,
        w_q,
        norms,
        grad_o,
        ff_vectors,
        columns,
    )
    keep, send, out_sum, in_sum = tie(keep, send, out_sum, in_sum)
    got = other(send)
    in_keep, in_send = fold_second(*in_sum)
    held, passed = fold_third(*out_sum)
    keep, in_send, passed = tie(keep, in_send, passed)
    in_sum = in_keep, swap(in_send, PLANE)
    out_sum = held, swap(passed, 2 * PLANE)
    attn = add_both(keep, got)
    attn = across(attn)
    grad_kv, attn[0] = tie(grad_kv, attn[0])
    done = media_back(media_tokens, grad_kv, norms, w_kv, 0, run)
    done, in_sum = tie(done, in_sum)
    held, passed = fold_third(*in_sum)
    done, held, passed = tie(done, held, passed)
    in_sum = held, swap(passed, 2 * PLANE)
    media_grad = media_back(media_tokens, grad_kv, norms, w_kv, run, images - run, (done,))
    media_grad, attn = tie(media_grad, attn)
    attn = fold(attn)
    attn, activ, grad_q, in_sum = tie(attn, activ, grad_q, in_sum)
    attn = down_sums(attn)
    latent_grad = latent_back(
        grad_kv, grad_q, latents, grad_resid.reshape(latents.shape), w_kv, w_q, norms
    )
    share, sent = feed_out(activ, w_ffout)
    own_in, own_out = [value[0].astype(F32) + value[1].astype(F32) for value in (in_sum, out_sum)]
    grad_ffin, grad_ffout = final_ff(place, own_in, other(own_in), own_out, other(own_out))
    sent, attn, grad_ffin, latent_grad = tie(sent, attn, grad_ffin, latent_grad)
    own = functools.reduce(jnp.add, [value.astype(F32) for value in attn])
    new_latents = resid + (share + other(sent).astype(F32))
    rows = own.shape[0] - PAD
    vectors = lax.dynamic_slice(own[rows:], (0, me * part), (6, part))
    own = own[:rows]
    grad_wkv, grad_wq, grad_wo = final_attn(place, own, other(own), inner, kv_rows, o_rows)
    return (
        new_latents.reshape(latents.shape),
        media_grad,
        latent_grad,
        vectors[0],
        vectors[1],
        vectors[2],
        vectors[3],
        grad_wq,
        grad_wkv,
        grad_wo,
        vectors[4],
        vectors[5],
        grad_ffin,
        grad_ffout,
    )


def norm_apply(values, gain, bias):
    centre = jnp.mean(values, -1, keepdims=True)
    centred = values - centre
    inverse = lax.rsqrt(jnp.mean(centred * centred, -1, keepdims=True) + EPS)
    unit = centred * inverse
    return (unit * gain.astype(jnp.float32) + bias.astype(jnp.float32), unit, inverse)


def plain_norm_grad(grad_normed, unit, inverse, gain):
    scaled = grad_normed * gain.astype(jnp.float32)
    return inverse * (
        scaled
        - jnp.mean(scaled, -1, keepdims=True)
        - unit * jnp.mean(scaled * unit, -1, keepdims=True)
    )


def row_total(values):
    return jnp.sum(values.reshape(-1, values.shape[-1]), axis=0)


def gelu_exact(values):
    return jax.nn.gelu(values, approximate=False)


def masked_scores(query_heads, key_heads, valid, scale):
    raw = (
        jnp.einsum("iqhe,ikhe->ihqk", query_heads, key_heads, preferred_element_type=jnp.float32)
        * scale
    )
    return jnp.where(valid[:, None, None, :], raw, jnp.float32(-1e30))


def plain_shards(
    media_tokens,
    patch_counts,
    latents,
    media_gain,
    media_bias,
    latent_gain,
    latent_bias,
    query_weight,
    keyval_weight,
    outproj_weight,
    ff_gain,
    ff_bias,
    ff_in_weight,
    ff_out_weight,
    cotangent,
):
    f32 = jnp.float32
    bf16 = jnp.bfloat16
    whole = (
        lax.all_gather(media_gain, "dp", axis=0, tiled=True),
        lax.all_gather(media_bias, "dp", axis=0, tiled=True),
        lax.all_gather(latent_gain, "dp", axis=0, tiled=True),
        lax.all_gather(latent_bias, "dp", axis=0, tiled=True),
        lax.all_gather(query_weight, "dp", axis=0, tiled=True),
        lax.all_gather(keyval_weight, "dp", axis=0, tiled=True),
        lax.all_gather(outproj_weight, "dp", axis=0, tiled=True),
        lax.all_gather(ff_gain, "dp", axis=0, tiled=True),
        lax.all_gather(ff_bias, "dp", axis=0, tiled=True),
        lax.all_gather(ff_in_weight, "dp", axis=0, tiled=True),
        lax.all_gather(ff_out_weight, "dp", axis=0, tiled=True),
    )
    (
        gain_media,
        bias_media,
        gain_latent,
        bias_latent,
        w_query,
        w_keyval,
        w_outproj,
        gain_ff,
        bias_ff,
        w_ffin,
        w_ffout,
    ) = whole
    images, media_len, width = media_tokens.shape
    lat_len = latents.shape[1]
    keys_len = media_len + lat_len
    inner_width = w_query.shape[1]
    head_size = inner_width // HEADS
    scale = 1.0 / math.sqrt(head_size)
    media_f = media_tokens.astype(f32)
    latent_f = latents.astype(f32)
    media_normed, media_unit, media_inv = norm_apply(media_f, gain_media, bias_media)
    latent_normed, latent_unit, latent_inv = norm_apply(latent_f, gain_latent, bias_latent)
    media_low = media_normed.astype(bf16)
    latent_low = latent_normed.astype(bf16)
    queries = jnp.einsum("ild,de->ile", latent_low, w_query, preferred_element_type=f32).astype(
        bf16
    )
    key_input = jnp.concatenate([media_low, latent_low], axis=1)
    keyvals = jnp.einsum("ikd,de->ike", key_input, w_keyval, preferred_element_type=f32).astype(
        bf16
    )
    key_heads = keyvals[:, :, :inner_width].reshape(images, keys_len, HEADS, head_size)
    value_heads = keyvals[:, :, inner_width:].reshape(images, keys_len, HEADS, head_size)
    query_heads = queries.reshape(images, lat_len, HEADS, head_size)
    positions = jnp.arange(keys_len, dtype=jnp.int32)
    valid = (positions[None, :] < patch_counts[:, None]) | (positions[None, :] >= media_len)
    scores = masked_scores(query_heads, key_heads, valid, scale)
    top = jnp.max(scores, -1, keepdims=True)
    expd = jnp.exp(scores - top)
    total = jnp.sum(expd, -1, keepdims=True)
    probs = expd / total
    log_total = top + jnp.log(total)
    mixed = jnp.einsum(
        "ihqk,ikhe->iqhe", probs.astype(bf16), value_heads, preferred_element_type=f32
    )
    mixed = mixed.reshape(images, lat_len, inner_width).astype(bf16)
    branch = jnp.einsum("ile,ed->ild", mixed, w_outproj, preferred_element_type=f32)
    resid = latent_f + branch
    ff_normed, ff_unit, ff_inv = norm_apply(resid, gain_ff, bias_ff)
    ff_low = ff_normed.astype(bf16)
    pre_act = jnp.einsum("ild,df->ilf", ff_low, w_ffin, preferred_element_type=f32)
    activ, gelu_pull = jax.vjp(gelu_exact, pre_act)
    activ_low = activ.astype(bf16)
    new_latents = resid + jnp.einsum("ilf,fd->ild", activ_low, w_ffout, preferred_element_type=f32)
    again = (
        lax.all_gather(media_gain, "dp", axis=0, tiled=True),
        lax.all_gather(media_bias, "dp", axis=0, tiled=True),
        lax.all_gather(latent_gain, "dp", axis=0, tiled=True),
        lax.all_gather(latent_bias, "dp", axis=0, tiled=True),
        lax.all_gather(query_weight, "dp", axis=0, tiled=True),
        lax.all_gather(keyval_weight, "dp", axis=0, tiled=True),
        lax.all_gather(outproj_weight, "dp", axis=0, tiled=True),
        lax.all_gather(ff_gain, "dp", axis=0, tiled=True),
        lax.all_gather(ff_bias, "dp", axis=0, tiled=True),
        lax.all_gather(ff_in_weight, "dp", axis=0, tiled=True),
        lax.all_gather(ff_out_weight, "dp", axis=0, tiled=True),
    )
    (
        gain_media_b,
        bias_media_b,
        gain_latent_b,
        bias_latent_b,
        w_query_b,
        w_keyval_b,
        w_outproj_b,
        gain_ff_b,
        bias_ff_b,
        w_ffin_b,
        w_ffout_b,
    ) = again
    grad_out_low = cotangent.astype(bf16)
    grad_ffout = jnp.einsum("ilf,ild->fd", activ_low, grad_out_low, preferred_element_type=f32)
    grad_activ = jnp.einsum("ild,fd->ilf", grad_out_low, w_ffout_b, preferred_element_type=f32)
    (grad_pre,) = gelu_pull(grad_activ)
    grad_pre_low = grad_pre.astype(bf16)
    grad_ffin = jnp.einsum("ild,ilf->df", ff_low, grad_pre_low, preferred_element_type=f32)
    grad_ffnormed = jnp.einsum("ilf,df->ild", grad_pre_low, w_ffin_b, preferred_element_type=f32)
    grad_gain_ff = row_total(grad_ffnormed * ff_unit)
    grad_bias_ff = row_total(grad_ffnormed)
    grad_resid = cotangent + plain_norm_grad(grad_ffnormed, ff_unit, ff_inv, gain_ff_b)
    grad_resid_low = grad_resid.astype(bf16)
    grad_outproj = jnp.einsum("ile,ild->ed", mixed, grad_resid_low, preferred_element_type=f32)
    grad_mixed = jnp.einsum(
        "ild,ed->ile", grad_resid_low, w_outproj_b, preferred_element_type=f32
    ).astype(bf16)
    grad_mixed_heads = grad_mixed.reshape(images, lat_len, HEADS, head_size)
    scores_again = masked_scores(query_heads, key_heads, valid, scale)
    probs_again = jnp.exp(scores_again - log_total)
    grad_probs = jnp.einsum(
        "iqhe,ikhe->ihqk", grad_mixed_heads, value_heads, preferred_element_type=f32
    )
    grad_scores = probs_again * (grad_probs - jnp.sum(probs_again * grad_probs, -1, keepdims=True))
    grad_scores_low = grad_scores.astype(bf16)
    grad_queries = (
        jnp.einsum("ihqk,ikhe->iqhe", grad_scores_low, key_heads, preferred_element_type=f32)
        * scale
    )
    grad_queries = grad_queries.reshape(images, lat_len, inner_width).astype(bf16)
    grad_keys = (
        jnp.einsum("ihqk,iqhe->ikhe", grad_scores_low, query_heads, preferred_element_type=f32)
        * scale
    )
    grad_values = jnp.einsum(
        "ihqk,iqhe->ikhe", probs_again.astype(bf16), grad_mixed_heads, preferred_element_type=f32
    )
    grad_keyvals = jnp.concatenate(
        [
            grad_keys.reshape(images, keys_len, inner_width),
            grad_values.reshape(images, keys_len, inner_width),
        ],
        axis=-1,
    ).astype(bf16)
    grad_qweight = jnp.einsum("ild,ile->de", latent_low, grad_queries, preferred_element_type=f32)
    grad_kvweight = jnp.einsum("ikd,ike->de", key_input, grad_keyvals, preferred_element_type=f32)
    grad_key_input = jnp.einsum("ike,de->ikd", grad_keyvals, w_keyval_b, preferred_element_type=f32)
    grad_latnormed = jnp.einsum("ile,de->ild", grad_queries, w_query_b, preferred_element_type=f32)
    grad_latnormed = grad_latnormed + grad_key_input[:, media_len:]
    grad_medianormed = grad_key_input[:, :media_len]
    media_grad = plain_norm_grad(grad_medianormed, media_unit, media_inv, gain_media_b)
    latent_grad = grad_resid + plain_norm_grad(grad_latnormed, latent_unit, latent_inv, gain_latent_b)
    grad_gain_media = row_total(grad_medianormed * media_unit)
    grad_bias_media = row_total(grad_medianormed)
    grad_gain_latent = row_total(grad_latnormed * latent_unit)
    grad_bias_latent = row_total(grad_latnormed)
    owned = (
        lax.psum_scatter(
            grad_gain_media.astype(jnp.bfloat16), "dp", scatter_dimension=0, tiled=True
        ).astype(jnp.float32),
        lax.psum_scatter(
            grad_bias_media.astype(jnp.bfloat16), "dp", scatter_dimension=0, tiled=True
        ).astype(jnp.float32),
        lax.psum_scatter(
            grad_gain_latent.astype(jnp.bfloat16), "dp", scatter_dimension=0, tiled=True
        ).astype(jnp.float32),
        lax.psum_scatter(
            grad_bias_latent.astype(jnp.bfloat16), "dp", scatter_dimension=0, tiled=True
        ).astype(jnp.float32),
        lax.psum_scatter(
            grad_qweight.astype(jnp.bfloat16), "dp", scatter_dimension=0, tiled=True
        ).astype(jnp.float32),
        lax.psum_scatter(
            grad_kvweight.astype(jnp.bfloat16), "dp", scatter_dimension=0, tiled=True
        ).astype(jnp.float32),
        lax.psum_scatter(
            grad_outproj.astype(jnp.bfloat16), "dp", scatter_dimension=0, tiled=True
        ).astype(jnp.float32),
        lax.psum_scatter(
            grad_gain_ff.astype(jnp.bfloat16), "dp", scatter_dimension=0, tiled=True
        ).astype(jnp.float32),
        lax.psum_scatter(
            grad_bias_ff.astype(jnp.bfloat16), "dp", scatter_dimension=0, tiled=True
        ).astype(jnp.float32),
        lax.psum_scatter(
            grad_ffin.astype(jnp.bfloat16), "dp", scatter_dimension=0, tiled=True
        ).astype(jnp.float32),
        lax.psum_scatter(
            grad_ffout.astype(jnp.bfloat16), "dp", scatter_dimension=0, tiled=True
        ).astype(jnp.float32),
    )
    summed = (
        lax.psum(owned[0].astype(jnp.bfloat16), "rep").astype(jnp.float32),
        lax.psum(owned[1].astype(jnp.bfloat16), "rep").astype(jnp.float32),
        lax.psum(owned[2].astype(jnp.bfloat16), "rep").astype(jnp.float32),
        lax.psum(owned[3].astype(jnp.bfloat16), "rep").astype(jnp.float32),
        lax.psum(owned[4].astype(jnp.bfloat16), "rep").astype(jnp.float32),
        lax.psum(owned[5].astype(jnp.bfloat16), "rep").astype(jnp.float32),
        lax.psum(owned[6].astype(jnp.bfloat16), "rep").astype(jnp.float32),
        lax.psum(owned[7].astype(jnp.bfloat16), "rep").astype(jnp.float32),
        lax.psum(owned[8].astype(jnp.bfloat16), "rep").astype(jnp.float32),
        lax.psum(owned[9].astype(jnp.bfloat16), "rep").astype(jnp.float32),
        lax.psum(owned[10].astype(jnp.bfloat16), "rep").astype(jnp.float32),
    )
    (
        sum_gain_media,
        sum_bias_media,
        sum_gain_latent,
        sum_bias_latent,
        sum_query,
        sum_keyval,
        sum_outproj,
        sum_gain_ff,
        sum_bias_ff,
        sum_ffin,
        sum_ffout,
    ) = summed
    return (
        new_latents,
        media_grad,
        latent_grad,
        sum_gain_media,
        sum_bias_media,
        sum_gain_latent,
        sum_bias_latent,
        sum_query,
        sum_keyval,
        sum_outproj,
        sum_gain_ff,
        sum_bias_ff,
        sum_ffin,
        sum_ffout,
    )


def solution(mesh):
    dp, rep = mesh.shape["dp"], mesh.shape["rep"]

    def program(*arrays):
        if rep != 2 or dp != PLANE * PLANE:
            return plain_shards(*arrays)
        return shards(dp, *arrays)

    return jax.shard_map(
        program,
        mesh=mesh,
        in_specs=(
            P(("dp", "rep"), None, None),
            P(("dp", "rep")),
            P(("dp", "rep"), None, None),
            P("dp"),
            P("dp"),
            P("dp"),
            P("dp"),
            P("dp", None),
            P("dp", None),
            P("dp", None),
            P("dp"),
            P("dp"),
            P("dp", None),
            P("dp", None),
            P(("dp", "rep"), None, None),
        ),
        out_specs=(
            P(("dp", "rep"), None, None),
            P(("dp", "rep"), None, None),
            P(("dp", "rep"), None, None),
            P("dp"),
            P("dp"),
            P("dp"),
            P("dp"),
            P("dp", None),
            P("dp", None),
            P("dp", None),
            P("dp"),
            P("dp"),
            P("dp", None),
            P("dp", None),
        ),
        check_vma=False,
    )
```

```python
import functools
import math

import jax
import jax.numpy as jnp
from jax import lax
from jax.experimental import pallas as pl
from jax.experimental.pallas import tpu as pltpu
from jax.sharding import PartitionSpec as P

HEADS = 8
GROUP = 4
EPS = 1e-05
NEG = -1e30
ROWS = 64
FF_TILE = 512
PLANE = 4
PAD = 8
F32 = jnp.float32
BF16 = jnp.bfloat16


def cost(us):
    return pl.CostEstimate(flops=int(us * 1.1e9), bytes_accessed=1 << 18, transcendentals=0)


def contract(a, b, over):
    return lax.dot_general(a, b, ((over[:1], over[1:]), ((), ())), preferred_element_type=F32)


def norm_rows(values):
    centred = values - jnp.mean(values, -1, keepdims=True)
    inverse = lax.rsqrt(jnp.mean(centred * centred, -1, keepdims=True) + EPS)
    return centred * inverse, inverse


def norm_back(grad, unit, inverse, gain):
    scaled = grad * gain
    return inverse * (
        scaled
        - jnp.mean(scaled, -1, keepdims=True)
        - unit * jnp.mean(scaled * unit, -1, keepdims=True)
    )


def spread(value, size):
    lane = lax.broadcasted_iota(jnp.int32, value.shape, 1) // size
    value = value.astype(F32)
    return jnp.concatenate([jnp.where(lane == h, value, 0.0) for h in range(GROUP)], 0)


def gathered(value, size):
    rows = value.shape[0] // GROUP
    lane = lax.broadcasted_iota(jnp.int32, (rows, value.shape[1]), 1) // size
    out = jnp.zeros((rows, value.shape[1]), F32)
    for h in range(GROUP):
        out = jnp.where(lane == h, value[h * rows : (h + 1) * rows], out)
    return out


def tie(*values):
    return lax.optimization_barrier(values)


def params(mib):
    return pltpu.CompilerParams(vmem_limit_bytes=mib << 20)


def image_at(i, c):
    return (i, 0, 0)


def fixed_at(*_):
    return (0, 0)


def order_kernel(place, *refs):
    sides = refs[:PLANE], refs[PLANE : 2 * PLANE]
    w_kv, w_q, w_o, norms = refs[2 * PLANE :]
    me, core = place[0], place[1]
    columns = sides[0][0].shape[0]
    chips = columns * PLANE
    kv_rows, o_rows = w_kv.shape[0] // chips // 2, w_o.shape[0] // chips // 2
    q_rows, inner = kv_rows // 2, w_q.shape[1]
    total = jnp.zeros(norms.shape, F32)
    for plane in range(PLANE):
        for column in range(columns):
            chip = me ^ (column * PLANE + plane)
            for side in range(2):
                block = sides[side][plane]
                half = core if side == 0 else 1 - core
                at = pl.multiple_of((chip * 2 + half) * kv_rows, kv_rows)
                w_kv[pl.ds(at, kv_rows), :] = block[column, :kv_rows, :]
                rest = block[column, kv_rows : kv_rows + q_rows, :]
                w_q[pl.ds(at, q_rows), :] = rest[:, :inner]
                w_q[pl.ds(pl.multiple_of(at + q_rows, q_rows), q_rows), :] = rest[:, inner:]
                at = pl.multiple_of((chip * 2 + half) * o_rows, o_rows)
                w_o[pl.ds(at, o_rows), :] = block[
                    column, kv_rows + q_rows : kv_rows + q_rows + o_rows, :
                ]
            total += sides[0][plane][column, kv_rows + q_rows + o_rows :, :].astype(F32)
    norms[...] = total


def in_order(place, own, other, inner):
    columns, _, width = own[0].shape
    return pl.pallas_call(
        order_kernel,
        grid_spec=pltpu.PrefetchScalarGridSpec(
            num_scalar_prefetch=1,
            grid=(1,),
            in_specs=[
                pl.BlockSpec(value.shape, lambda t, c: (0, 0, 0)) for value in (*own, *other)
            ],
            out_specs=[
                pl.BlockSpec((width, 2 * inner), fixed_at),
                pl.BlockSpec((width, inner), fixed_at),
                pl.BlockSpec((inner, width), fixed_at),
                pl.BlockSpec((8, width), fixed_at),
            ],
        ),
        out_shape=[
            jax.ShapeDtypeStruct((width, 2 * inner), BF16),
            jax.ShapeDtypeStruct((width, inner), BF16),
            jax.ShapeDtypeStruct((inner, width), BF16),
            jax.ShapeDtypeStruct((8, width), F32),
        ],
        compiler_params=params(24),
        cost_estimate=cost(1),
        name="in_order",
    )(place, *own, *other)


def whole_at(rank):
    return lambda *_: (0,) * rank


def small(kernel, values, outs, us, name):
    return pl.pallas_call(
        kernel,
        grid=(1,),
        in_specs=[pl.BlockSpec(value.shape, whole_at(value.ndim)) for value in values],
        out_specs=[pl.BlockSpec(shape, whole_at(len(shape))) for shape in outs],
        out_shape=[jax.ShapeDtypeStruct(shape, BF16) for shape in outs],
        compiler_params=params(20),
        cost_estimate=cost(us),
        name=name,
    )(*values)


def added(one, two):
    return (one.astype(F32) + two.astype(F32)).astype(BF16)


def fold_kernel(*refs):
    for column in range(len(refs) - PLANE):
        total = refs[0][column].astype(F32)
        for plane in range(1, PLANE):
            total += refs[plane][column].astype(F32)
        refs[PLANE + column][...] = total.astype(BF16)


def fold(values):
    columns = values[0].shape[0]
    return small(fold_kernel, values, [values[0].shape[1:]] * columns, 2, "fold")


def first_kernel(keep0, got0, keep1, got1, held0, pass0, held1, pass1):
    held0[...] = added(keep0[0], got0[0])
    pass0[...] = added(keep0[1], got0[1])
    held1[...] = added(keep1[0], got1[0])
    pass1[...] = added(keep1[1], got1[1])


def fold_first(keep0, got0, keep1, got1):
    values = keep0, got0, keep1, got1
    return small(first_kernel, values, [keep0.shape[1:]] * 4, 2, "fold_first")


def second_kernel(held0, got0, held1, got1, keep, send):
    half = held0.shape[1]
    for i in range(2):
        for out, column in ((keep, 2 * i), (send, 2 * i + 1)):
            out[i, :half, :] = added(held0[column], got0[column])
            out[i, half:, :] = added(held1[column], got1[column])


def fold_second(held0, got0, held1, got1):
    values = held0, got0, held1, got1
    shape = (2, 2 * held0.shape[1], held0.shape[2])
    return small(second_kernel, values, [shape] * 2, 2, "fold_second")


def third_kernel(keep, got, held, passed):
    held[...] = added(keep[0], got[0])
    passed[...] = added(keep[1], got[1])


def fold_third(keep, got):
    return small(third_kernel, (keep, got), [keep.shape[1:]] * 2, 0.5, "fold_third")


def both_kernel(keep, got, *outs):
    for plane, out in enumerate(outs):
        out[...] = (keep[plane].astype(F32) + got[plane].astype(F32)).astype(BF16)


def add_both(keep, got):
    tail = keep.shape[1:]
    whole = lambda t: (0, 0, 0, 0)
    return pl.pallas_call(
        both_kernel,
        grid=(1,),
        in_specs=[pl.BlockSpec(keep.shape, whole), pl.BlockSpec(keep.shape, whole)],
        out_specs=[pl.BlockSpec(tail, lambda t: (0, 0, 0)) for _ in range(PLANE)],
        out_shape=[jax.ShapeDtypeStruct(tail, BF16) for _ in range(PLANE)],
        compiler_params=params(16),
        cost_estimate=cost(2),
        name="add_both",
    )(keep, got)


def final_ff_kernel(place, own_in, other_in, own_out, other_out, grad_in, grad_out):
    first = place[1] == 0
    slot = own_out.shape[0]
    for chip in range(own_in.shape[1] // slot):
        here = slice(chip * slot, (chip + 1) * slot)
        one, two = own_in[:, here], other_in[:, here]
        at = 2 * chip * slot
        grad_in[:, at : at + slot] = jnp.where(first, one, two)
        grad_in[:, at + slot : at + 2 * slot] = jnp.where(first, two, one)
    grad_out[:slot, :] = jnp.where(first, own_out[...], other_out[...])
    grad_out[slot:, :] = jnp.where(first, other_out[...], own_out[...])


def final_ff(place, own_in, other_in, own_out, other_out):
    values = own_in, other_in, own_out, other_out
    shapes = (own_in.shape[0], 2 * own_in.shape[1]), (2 * own_out.shape[0], own_out.shape[1])
    return pl.pallas_call(
        final_ff_kernel,
        grid_spec=pltpu.PrefetchScalarGridSpec(
            num_scalar_prefetch=1,
            grid=(1,),
            in_specs=[pl.BlockSpec(value.shape, fixed_at) for value in values],
            out_specs=[pl.BlockSpec(shape, fixed_at) for shape in shapes],
        ),
        out_shape=[jax.ShapeDtypeStruct(shape, F32) for shape in shapes],
        compiler_params=params(16),
        cost_estimate=cost(2),
        name="final_ff",
    )(place, *values)


def final_attn_kernel(place, own, other, grad_kv, grad_q, grad_o):
    kv_rows, o_rows = grad_kv.shape[0] // 2, grad_o.shape[0] // 2
    q_rows, inner = kv_rows // 2, grad_q.shape[1]
    first = place[1] == 0
    for half in range(2):
        value = jnp.where(first == (half == 0), own[...], other[...])
        at = half * kv_rows
        grad_kv[at : at + kv_rows, :] = value[:kv_rows]
        rest = value[kv_rows : kv_rows + q_rows]
        grad_q[at : at + q_rows, :] = rest[:, :inner]
        grad_q[at + q_rows : at + kv_rows, :] = rest[:, inner:]
        grad_o[half * o_rows : (half + 1) * o_rows, :] = value[
            kv_rows + q_rows : kv_rows + q_rows + o_rows
        ]


def final_attn(place, own, other, inner, kv_rows, o_rows):
    width = own.shape[1]
    shapes = (2 * kv_rows, width), (2 * kv_rows, inner), (2 * o_rows, width)
    return pl.pallas_call(
        final_attn_kernel,
        grid_spec=pltpu.PrefetchScalarGridSpec(
            num_scalar_prefetch=1,
            grid=(1,),
            in_specs=[pl.BlockSpec(own.shape, fixed_at), pl.BlockSpec(own.shape, fixed_at)],
            out_specs=[pl.BlockSpec(shape, fixed_at) for shape in shapes],
        ),
        out_shape=[jax.ShapeDtypeStruct(shape, F32) for shape in shapes],
        compiler_params=params(16),
        cost_estimate=cost(2),
        name="final_attn",
    )(place, own, other)


def attend_kernel(counts, media, latent, norms, w_kv, w_q, *refs):
    turned, lat_low, keyvals, queries, mixed, key_input = refs[-6:]
    media_len, lat_len = media.shape[1], latent.shape[1]
    keys_len = media_len + lat_len
    inner = w_q.shape[1]
    size = inner // HEADS
    wide = size * GROUP
    for at in range(0, media_len, ROWS):
        unit, _ = norm_rows(media[0, at : at + ROWS, :].astype(F32))
        key_input[at : at + ROWS, :] = (unit * norms[0:1, :] + norms[1:2, :]).astype(BF16)
    unit, _ = norm_rows(latent[0].astype(F32))
    low = (unit * norms[2:3, :] + norms[3:4, :]).astype(BF16)
    key_input[media_len:, :] = low
    lat_low[0] = low
    query = contract(low, w_q[...], (1, 0)).astype(BF16)
    queries[0] = query
    keyvals[0] = contract(key_input[...], w_kv[...], (1, 0)).astype(BF16)
    for side in range(2):

        @pl.when(pl.program_id(0) % 2 == side)
        def _(side=side):
            turned[0, :, side * keys_len : (side + 1) * keys_len] = key_input[...].T

    key_at = lax.broadcasted_iota(jnp.int32, (1, keys_len), 1)
    valid = (key_at < counts[pl.program_id(0)]) | (key_at >= media_len)
    for at in range(0, inner, wide):
        own = spread(query[:, at : at + wide].astype(F32) * (1.0 / math.sqrt(size)), size)
        scores = contract(own.astype(BF16), keyvals[0, :, at : at + wide], (1, 1))
        scores = jnp.where(valid, scores, NEG)
        expd = jnp.exp(scores - jnp.max(scores, -1, keepdims=True))
        probs = (expd * (1.0 / jnp.sum(expd, -1, keepdims=True))).astype(BF16)
        out = contract(probs, keyvals[0, :, inner + at : inner + at + wide], (1, 0))
        mixed[0, :, at : at + wide] = gathered(out, size).astype(BF16)


def attend(counts, media, latent, norms, w_kv, w_q, first, run, into=()):
    images, media_len, width = media.shape
    lat_len, inner = latent.shape[1], w_q.shape[1]
    keys_len = media_len + lat_len
    at = lambda i, c: (i + first, 0, 0)
    shapes = [
        (images, lat_len, width),
        (images, keys_len, 2 * inner),
        (images, lat_len, inner),
        (images, lat_len, inner),
    ]
    return pl.pallas_call(
        attend_kernel,
        grid_spec=pltpu.PrefetchScalarGridSpec(
            num_scalar_prefetch=1,
            grid=(run,),
            in_specs=[
                pl.BlockSpec((1, media_len, width), at),
                pl.BlockSpec((1, lat_len, width), at),
                pl.BlockSpec(norms.shape, fixed_at),
                pl.BlockSpec(w_kv.shape, fixed_at),
                pl.BlockSpec(w_q.shape, fixed_at),
                *[pl.BlockSpec(memory_space=pl.ANY) for _ in into],
            ],
            out_specs=[
                pl.BlockSpec((1, width, 2 * keys_len), lambda i, c: ((i + first) // 2, 0, 0)),
                *[pl.BlockSpec((1,) + shape[1:], at) for shape in shapes],
            ],
            scratch_shapes=[pltpu.VMEM((keys_len, width), BF16)],
        ),
        out_shape=[
            jax.ShapeDtypeStruct((images // 2, width, 2 * keys_len), BF16),
            *[jax.ShapeDtypeStruct(shape, BF16) for shape in shapes],
        ],
        input_output_aliases={6 + i: i for i in range(len(into))},
        compiler_params=params(32),
        cost_estimate=cost(14),
        name="attend",
    )(counts[first : first + run], media, latent, norms, w_kv, w_q, *into)


def resid_kernel(mixed, latent, w_o, norms, resid, low):
    value = latent[...].astype(F32) + contract(mixed[...], w_o[...], (1, 0))
    resid[...] = value
    unit, _ = norm_rows(value)
    low[...] = (unit * norms[4:5, :] + norms[5:6, :]).astype(BF16)


def add_branch(mixed, latent, w_o, norms):
    rows, width = latent.shape
    inner = mixed.shape[1]
    block = rows // 4
    row_at = lambda i: (i, 0)
    return pl.pallas_call(
        resid_kernel,
        grid=(rows // block,),
        in_specs=[
            pl.BlockSpec((block, inner), row_at),
            pl.BlockSpec((block, width), row_at),
            pl.BlockSpec(w_o.shape, fixed_at),
            pl.BlockSpec(norms.shape, fixed_at),
        ],
        out_specs=[pl.BlockSpec((block, width), row_at), pl.BlockSpec((block, width), row_at)],
        out_shape=[
            jax.ShapeDtypeStruct((rows, width), F32),
            jax.ShapeDtypeStruct((rows, width), BF16),
        ],
        compiler_params=params(16),
        cost_estimate=cost(3),
        name="add_branch",
    )(mixed, latent, w_o, norms)


def ff_kernel(place, *refs):
    low0, low1, dout0, dout1 = refs[:4]
    lo, hi = refs[4:8], refs[8:12]
    activ, slope, low_t, dout, w_in = refs[12:17]
    keep0, send0, keep1, send1 = refs[17:21]
    low, grad = refs[21:]
    step, steps = pl.program_id(0), pl.num_programs(0)
    me = place[0]
    half = low0.shape[0]
    part = lo[0].shape[1]
    slot = grad.shape[0] // PLANE
    cut = slot // 2

    @pl.when(step == 0)
    def _():
        low[:half, :] = low0[...]
        low[half:, :] = low1[...]
        dout[:half, :] = dout0[...]
        dout[half:, :] = dout1[...]
        low_t[...] = low[...].T

    def put(pieces):
        for plane in range(PLANE):
            for column in range(pieces[0].shape[0]):
                at = pl.multiple_of((me ^ (column * PLANE + plane)) * part, part)
                w_in[pl.ds(at, part), :] = pieces[plane][column]

    pl.when(step < steps // 2)(lambda: put(lo))
    pl.when(step >= steps // 2)(lambda: put(hi))
    pre = contract(low[...], w_in[...], (1, 0))
    cdf = 0.5 * (1.0 + lax.erf(pre * math.sqrt(0.5)))
    slope[...] = cdf + pre * (jnp.exp(pre * pre * -0.5) * (1.0 / math.sqrt(2.0 * math.pi)))
    value = (pre * cdf).astype(BF16)
    activ[...] = value
    grad[...] = contract(value, dout[...], (0, 0)).astype(BF16)

    def block(plane, at):
        at = pl.multiple_of((plane ^ (me % PLANE)) * slot + at, cut)
        return grad[pl.ds(at, cut), :]

    for i in range(2):
        keep0[i, 0] = block(2 * i, 0)
        send0[i, 0] = block(2 * i + 1, 0)
        keep1[i, 0] = block(i, cut)
        send1[i, 0] = block(2 + i, cut)


def feed_forward(place, lows, douts, lo, hi, slot):
    half, width = lows[0].shape
    rows = 2 * half
    columns, part, cut = lo[0].shape
    tile = PLANE * slot
    steps = 2 * cut // tile
    in_at = lambda t, c: (0, t)
    lo_at = lambda t, c: (0, 0, jnp.minimum(t, steps // 2 - 1))
    hi_at = lambda t, c: (0, 0, jnp.maximum(t - steps // 2, 0))
    once = pl.Buffered(1)
    return pl.pallas_call(
        ff_kernel,
        grid_spec=pltpu.PrefetchScalarGridSpec(
            num_scalar_prefetch=1,
            grid=(steps,),
            in_specs=[
                *[pl.BlockSpec((half, width), fixed_at, pipeline_mode=once) for _ in range(4)],
                *[pl.BlockSpec((columns, part, tile), lo_at) for _ in lo],
                *[pl.BlockSpec((columns, part, tile), hi_at) for _ in hi],
            ],
            out_specs=[
                pl.BlockSpec((rows, tile), in_at),
                pl.BlockSpec((rows, tile), in_at),
                pl.BlockSpec((width, rows), fixed_at),
                pl.BlockSpec((rows, width), fixed_at),
                pl.BlockSpec((width, tile), in_at),
                *[
                    pl.BlockSpec(
                        (2, 1, slot // 2, width), lambda t, c: (0, t ^ (c[0] // PLANE), 0, 0)
                    )
                    for _ in range(4)
                ],
            ],
            scratch_shapes=[pltpu.VMEM((rows, width), BF16), pltpu.VMEM((tile, width), BF16)],
        ),
        out_shape=[
            jax.ShapeDtypeStruct((rows, 2 * cut), BF16),
            jax.ShapeDtypeStruct((rows, 2 * cut), F32),
            jax.ShapeDtypeStruct((width, rows), BF16),
            jax.ShapeDtypeStruct((rows, width), BF16),
            jax.ShapeDtypeStruct((width, 2 * cut), BF16),
            *[
                kind((2, columns, slot // 2, width), BF16)
                for kind in (jax.ShapeDtypeStruct, pltpu.HBM) * 2
            ],
        ],
        compiler_params=params(44),
        cost_estimate=cost(18),
        name="feed_forward",
    )(place, *lows, *douts, *lo, *hi)


def ff_back_kernel(
    place, dout, low_t, w_in, w_out, slope, keep0, send0, keep1, send1, kept, sent, total, grad_in
):
    step, steps = pl.program_id(0), pl.num_programs(0)
    columns, cut = keep0.shape[1:3]

    @pl.when(step == 0)
    def _():
        total[...] = jnp.zeros_like(total)

    grad = (contract(dout[...], w_out[...], (1, 1)) * slope[...]).astype(BF16)
    grad_in[...] = contract(low_t[...], grad, (1, 0)).astype(BF16)

    def block(plane, column, at):
        at = pl.multiple_of((place[0] ^ (column * PLANE + plane)) * 2 * cut + at, cut)
        return grad_in[pl.ds(at, cut), :]

    for column in range(columns):
        for i in range(2):
            keep0[i, column] = block(2 * i, column, 0)
            send0[i, column] = block(2 * i + 1, column, 0)
            keep1[i, column] = block(i, column, cut)
            send1[i, column] = block(2 + i, column, cut)
    total[...] += contract(grad, w_in[...], (1, 1))

    @pl.when(step == steps - 1)
    def _():
        half = kept.shape[0]
        kept[...] = total[:half, :]
        sent[...] = total[half:, :].astype(BF16)


def feed_back(place, dout, low_t, w_in, w_out, slope, columns, part):
    rows, width = dout.shape
    hidden = w_in.shape[1]
    tile = min(FF_TILE, hidden)
    half = rows // 2
    in_at, out_at = (lambda t, c: (0, t)), (lambda t, c: (t, 0))
    once = pl.Buffered(1)
    return pl.pallas_call(
        ff_back_kernel,
        grid_spec=pltpu.PrefetchScalarGridSpec(
            num_scalar_prefetch=1,
            grid=(hidden // tile,),
            in_specs=[
                pl.BlockSpec((rows, width), fixed_at, pipeline_mode=once),
                pl.BlockSpec((width, rows), fixed_at, pipeline_mode=once),
                pl.BlockSpec((width, tile), in_at),
                pl.BlockSpec((tile, width), out_at),
                pl.BlockSpec((rows, tile), in_at),
            ],
            out_specs=[
                *[
                    pl.BlockSpec((2, columns, part // 2, tile), lambda t, c: (0, 0, 0, t))
                    for _ in range(4)
                ],
                pl.BlockSpec((half, width), fixed_at, pipeline_mode=once),
                pl.BlockSpec((half, width), fixed_at, pipeline_mode=once),
            ],
            scratch_shapes=[pltpu.VMEM((rows, width), F32), pltpu.VMEM((width, tile), BF16)],
        ),
        out_shape=[
            *[
                kind((2, columns, part // 2, hidden), BF16)
                for kind in (jax.ShapeDtypeStruct, pltpu.HBM) * 2
            ],
            jax.ShapeDtypeStruct((half, width), F32),
            jax.ShapeDtypeStruct((half, width), BF16),
        ],
        compiler_params=params(48),
        cost_estimate=cost(21),
        name="feed_back",
    )(place, dout, low_t, w_in, w_out, slope)


def ff_out_kernel(activ, w_out, kept, sent, total):
    step = pl.program_id(0)

    @pl.when(step == 0)
    def _():
        total[...] = jnp.zeros_like(total)

    total[...] += contract(activ[...], w_out[...], (1, 0))

    @pl.when(step == pl.num_programs(0) - 1)
    def _():
        half = kept.shape[0]
        kept[...] = total[:half, :]
        sent[...] = total[half:, :].astype(BF16)


def feed_out(activ, w_out):
    rows, hidden = activ.shape
    width = w_out.shape[1]
    tile = min(FF_TILE, hidden)
    half = rows // 2
    once = pl.Buffered(1)
    return pl.pallas_call(
        ff_out_kernel,
        grid=(hidden // tile,),
        in_specs=[
            pl.BlockSpec((rows, tile), lambda t: (0, t)),
            pl.BlockSpec((tile, width), lambda t: (t, 0)),
        ],
        out_specs=[pl.BlockSpec((half, width), fixed_at, pipeline_mode=once)] * 2,
        out_shape=[
            jax.ShapeDtypeStruct((half, width), F32),
            jax.ShapeDtypeStruct((half, width), BF16),
        ],
        scratch_shapes=[pltpu.VMEM((rows, width), F32)],
        compiler_params=params(24),
        cost_estimate=cost(7),
        name="feed_out",
    )(activ, w_out)


def resid_back_kernel(
    kept,
    got,
    resid,
    cotangent,
    mixed,
    w_o,
    norms,
    grad_resid,
    grad_mixed,
    grad_o,
    vectors,
    total,
):
    step = pl.program_id(0)

    @pl.when(step == 0)
    def _():
        vectors[...] = jnp.zeros_like(vectors)
        total[...] = jnp.zeros_like(total)

    grad = kept[...] + got[...].astype(F32)
    unit, inverse = norm_rows(resid[...])
    vectors[0:1, :] += jnp.sum(grad * unit, 0, keepdims=True)
    vectors[1:2, :] += jnp.sum(grad, 0, keepdims=True)
    value = cotangent[...] + norm_back(grad, unit, inverse, norms[4:5, :])
    grad_resid[...] = value
    low = value.astype(BF16)
    grad_mixed[...] = contract(low, w_o[...], (1, 1)).astype(BF16)
    total[...] += contract(mixed[...], low, (0, 0))
    grad_o[...] = total[...].astype(BF16)


def resid_back(kept, got, resid, cotangent, mixed, w_o, norms):
    rows, width = resid.shape
    inner = mixed.shape[1]
    block = rows // 4
    row_at = lambda i: (i, 0)
    wide = pl.BlockSpec((block, width), row_at)
    return pl.pallas_call(
        resid_back_kernel,
        grid=(rows // block,),
        in_specs=[
            *[wide] * 4,
            pl.BlockSpec((block, inner), row_at),
            pl.BlockSpec(w_o.shape, fixed_at),
            pl.BlockSpec(norms.shape, fixed_at),
        ],
        out_specs=[
            wide,
            pl.BlockSpec((block, inner), row_at),
            pl.BlockSpec(w_o.shape, fixed_at),
            pl.BlockSpec((8, width), fixed_at),
        ],
        out_shape=[
            jax.ShapeDtypeStruct((rows, width), F32),
            jax.ShapeDtypeStruct((rows, inner), BF16),
            jax.ShapeDtypeStruct(w_o.shape, BF16),
            jax.ShapeDtypeStruct((8, width), F32),
        ],
        scratch_shapes=[pltpu.VMEM(w_o.shape, F32)],
        compiler_params=params(24),
        cost_estimate=cost(6),
        name="resid_back",
    )(kept, got, resid, cotangent, mixed, w_o, norms)


def as_row(column):
    out = []
    size = 128
    same = lax.broadcasted_iota(jnp.int32, (size, size), 0) == lax.broadcasted_iota(
        jnp.int32, (size, size), 1
    )
    for at in range(0, column.shape[0], size):
        out.append(jnp.sum(jnp.where(same, column[at : at + size, :], 0.0), 0, keepdims=True))
    return jnp.concatenate(out, 1)


def in_bf16(row):
    parts = []
    for _ in range(3):
        parts.append(row.astype(BF16))
        row = row - parts[-1].astype(F32)
    return parts


def attend_back_kernel(counts, keyvals, queries, grad_mixed, grad_kv, grad_q):
    taken, keys_len = keyvals.shape[:2]
    lat_len, inner = queries.shape[1:]
    media_len = keys_len - lat_len
    size = inner // HEADS
    wide = size * GROUP
    scale = 1.0 / math.sqrt(size)
    key_at = lax.broadcasted_iota(jnp.int32, (keys_len, 1), 0)

    def begin(i, at):
        own = spread(queries[i, :, at : at + wide].astype(F32) * scale, size).astype(BF16)
        grad = spread(grad_mixed[i, :, at : at + wide], size).astype(BF16)
        scores = contract(keyvals[i, :, at : at + wide], own, (1, 1))
        grad_probs = contract(keyvals[i, :, inner + at : inner + at + wide], grad, (1, 1))
        return own, grad, scores, grad_probs

    def weigh(i, scores, grad_probs):
        valid = (key_at < counts[pl.program_id(0) * taken + i]) | (key_at >= media_len)
        scores = jnp.where(valid, scores, NEG)
        expd = jnp.exp(scores - jnp.max(scores, 0, keepdims=True))
        probs = expd * (1.0 / jnp.sum(expd, 0, keepdims=True))
        held = jnp.sum(probs * grad_probs, 0, keepdims=True)
        return probs.astype(BF16), (probs * (grad_probs - held)).astype(BF16)

    def end(i, at, own, grad, probs, low):
        grad_v = contract(probs, grad, (1, 0)).astype(BF16)
        grad_kv[i, :, inner + at : inner + at + wide] = grad_v
        grad_kv[i, :, at : at + wide] = contract(low, own, (1, 0)).astype(BF16)
        back = contract(low, keyvals[i, :, at : at + wide], (0, 0))
        grad_q[i, :, at : at + wide] = (gathered(back, size) * scale).astype(BF16)

    items = [(i, at) for i in range(taken) for at in range(0, inner, wide)]
    ahead, behind = begin(*items[0]), None
    for n, item in enumerate(items):
        own, grad, scores, grad_probs = ahead
        if n + 1 < len(items):
            ahead = begin(*items[n + 1])
        weights = weigh(item[0], scores, grad_probs)
        if behind:
            end(*behind)
        behind = (*item, own, grad, *weights)
    end(*behind)


def weight_back_kernel(
    place,
    grad_kv,
    grad_q,
    turned,
    lat_low,
    w_kv,
    w_q,
    norms,
    grad_o,
    ff_vectors,
    keep,
    send,
    total,
    sums,
    lat_kv,
    lat_q,
    total_q,
):
    step, steps = pl.program_id(0), pl.num_programs(0)
    lat_len, inner = grad_q.shape[1:]
    keys_len = grad_kv.shape[1]
    media_len = keys_len - lat_len

    @pl.when(step == 0)
    def _():
        total[...] = jnp.zeros_like(total)
        sums[...] = jnp.zeros_like(sums)

    both = grad_kv[...].reshape(2 * keys_len, 2 * inner)
    total[...] += contract(turned[0], both, (1, 0))
    sums[...] += jnp.sum(both.astype(F32), 0, keepdims=True)
    for side in range(2):
        here = pl.ds(pl.multiple_of((2 * step + side) * lat_len, lat_len), lat_len)
        lat_kv[here, :] = grad_kv[side, media_len:, :]
        lat_q[here, :] = grad_q[side]

    @pl.when(step == steps - 1)
    def _():
        lat_w = contract(lat_low[...], lat_kv[...], (0, 0))
        lat_wq = contract(lat_low[...], lat_q[...], (0, 0))
        weight, weight_q = w_kv[...].astype(F32), w_q[...].astype(F32)
        lat_sum = jnp.sum(lat_kv[...].astype(F32), 0, keepdims=True)
        lat_sum_q = jnp.sum(lat_q[...].astype(F32), 0, keepdims=True)
        rows = in_bf16(sums[0:1, :] - lat_sum) + in_bf16(lat_sum) + [jnp.zeros((2, 2 * inner), BF16)]
        rows_q = in_bf16(lat_sum_q) + [jnp.zeros((5, inner), BF16)]
        biases = contract(jnp.concatenate(rows, 0), w_kv[...], (1, 1))
        biases_q = contract(jnp.concatenate(rows_q, 0), w_q[...], (1, 1))
        media_bias = jnp.sum(biases[0:3], 0, keepdims=True)
        lat_bias = jnp.sum(biases[3:6], 0, keepdims=True) + jnp.sum(biases_q, 0, keepdims=True)
        media_both = as_row(jnp.sum((total[...] - lat_w) * weight, 1, keepdims=True))
        lat_both = as_row(
            jnp.sum(lat_w * weight, 1, keepdims=True)
            + jnp.sum(lat_wq * weight_q, 1, keepdims=True)
        )
        vectors = [
            (media_both - norms[1:2, :] * media_bias) / norms[0:1, :],
            media_bias,
            (lat_both - norms[3:4, :] * lat_bias) / norms[2:3, :],
            lat_bias,
            ff_vectors[0:2, :],
            jnp.zeros((2, ff_vectors.shape[1]), F32),
        ]
        vectors = jnp.concatenate(vectors, 0).astype(BF16)
        total_q[...] = lat_wq
        me, core = place[0], place[1]
        columns = keep.shape[1]
        kv_rows = total.shape[0] // (2 * columns * PLANE)
        o_rows = grad_o.shape[0] // (2 * columns * PLANE)
        q_rows = kv_rows // 2
        for plane in range(PLANE):
            for column in range(columns):
                chip = me ^ (column * PLANE + plane)
                for out, half in ((keep, core), (send, 1 - core)):
                    at = pl.multiple_of((chip * 2 + half) * kv_rows, kv_rows)
                    out[plane, column, :kv_rows, :] = total[pl.ds(at, kv_rows), :].astype(BF16)
                    value = total_q[pl.ds(at, kv_rows), :].astype(BF16)
                    row = kv_rows
                    out[plane, column, row : row + q_rows, :inner] = value[:q_rows]
                    out[plane, column, row : row + q_rows, inner:] = value[q_rows:]
                    row += q_rows
                    at = pl.multiple_of((chip * 2 + half) * o_rows, o_rows)
                    out[plane, column, row : row + o_rows, :] = grad_o[pl.ds(at, o_rows), :]
                    out[plane, column, row + o_rows :, :] = vectors


def attend_back(counts, keyvals, queries, grad_mixed):
    images, keys_len, wide = keyvals.shape
    lat_len, inner = queries.shape[1:]
    taken = 2
    at = lambda i, c: (i, 0, 0)
    return pl.pallas_call(
        attend_back_kernel,
        grid_spec=pltpu.PrefetchScalarGridSpec(
            num_scalar_prefetch=1,
            grid=(images // taken,),
            in_specs=[
                pl.BlockSpec((taken, keys_len, wide), at),
                pl.BlockSpec((taken, lat_len, inner), at),
                pl.BlockSpec((taken, lat_len, inner), at),
            ],
            out_specs=[
                pl.BlockSpec((taken, keys_len, wide), at),
                pl.BlockSpec((taken, lat_len, inner), at),
            ],
        ),
        out_shape=[
            jax.ShapeDtypeStruct((images, keys_len, wide), BF16),
            jax.ShapeDtypeStruct((images, lat_len, inner), BF16),
        ],
        compiler_params=params(58),
        cost_estimate=cost(15),
        name="attend_back",
    )(counts, keyvals, queries, grad_mixed)


def weight_back(
    place, grad_kv, grad_q, turned, lat_low, w_kv, w_q, norms, grad_o, ff_vectors, columns
):
    images, keys_len, _ = grad_kv.shape
    width = turned.shape[1]
    lat_len, inner = grad_q.shape[1:]
    rows = images * lat_len
    chips = columns * PLANE
    kv_rows, o_rows = width // chips // 2, inner // chips // 2
    pack = (PLANE, columns, kv_rows + kv_rows // 2 + o_rows + PAD, width)
    at = lambda i, c: (i, 0, 0)
    once = pl.Buffered(1)
    return pl.pallas_call(
        weight_back_kernel,
        grid_spec=pltpu.PrefetchScalarGridSpec(
            num_scalar_prefetch=1,
            grid=(images // 2,),
            in_specs=[
                pl.BlockSpec((2, keys_len, 2 * inner), at),
                pl.BlockSpec((2, lat_len, inner), at),
                pl.BlockSpec((1, width, 2 * keys_len), at),
                pl.BlockSpec(lat_low.shape, fixed_at, pipeline_mode=once),
                pl.BlockSpec(w_kv.shape, fixed_at, pipeline_mode=once),
                pl.BlockSpec(w_q.shape, fixed_at, pipeline_mode=once),
                pl.BlockSpec(norms.shape, fixed_at),
                pl.BlockSpec(grad_o.shape, fixed_at, pipeline_mode=once),
                pl.BlockSpec(ff_vectors.shape, fixed_at),
            ],
            out_specs=[
                pl.BlockSpec(pack, whole_at(4), pipeline_mode=once),
                pl.BlockSpec(pack, whole_at(4), pipeline_mode=once),
            ],
            scratch_shapes=[
                pltpu.VMEM(w_kv.shape, F32),
                pltpu.VMEM((8, 2 * inner), F32),
                pltpu.VMEM((rows, 2 * inner), BF16),
                pltpu.VMEM((rows, inner), BF16),
                pltpu.VMEM(w_q.shape, F32),
            ],
        ),
        out_shape=[jax.ShapeDtypeStruct(pack, BF16), jax.ShapeDtypeStruct(pack, BF16)],
        compiler_params=params(58),
        cost_estimate=cost(17),
        name="weight_back",
    )(place, grad_kv, grad_q, turned, lat_low, w_kv, w_q, norms, grad_o, ff_vectors)


def latent_back_kernel(grad_kv, grad_q, latent, grad_resid, w_kv, w_q, norms, latent_grad):
    images, lat_len, width = latent.shape
    rows = images * lat_len
    grad = contract(grad_kv[...].reshape(rows, grad_kv.shape[2]), w_kv[...], (1, 1))
    grad += contract(grad_q[...].reshape(rows, grad_q.shape[2]), w_q[...], (1, 1))
    unit, inverse = norm_rows(latent[...].reshape(rows, width).astype(F32))
    back = norm_back(grad, unit, inverse, norms[2:3, :])
    latent_grad[...] = grad_resid[...] + back.reshape(images, lat_len, width)


def latent_back(grad_kv, grad_q, latent, grad_resid, w_kv, w_q, norms):
    images, lat_len, width = latent.shape
    inner = w_q.shape[1]
    tail = grad_kv.shape[1] // lat_len - 1
    block = images // 2
    at = lambda i: (i, 0, 0)
    return pl.pallas_call(
        latent_back_kernel,
        grid=(images // block,),
        in_specs=[
            pl.BlockSpec((block, lat_len, 2 * inner), lambda i: (i, tail, 0)),
            pl.BlockSpec((block, lat_len, inner), at),
            pl.BlockSpec((block, lat_len, width), at),
            pl.BlockSpec((block, lat_len, width), at),
            pl.BlockSpec(w_kv.shape, fixed_at),
            pl.BlockSpec(w_q.shape, fixed_at),
            pl.BlockSpec(norms.shape, fixed_at),
        ],
        out_specs=pl.BlockSpec((block, lat_len, width), at),
        out_shape=jax.ShapeDtypeStruct((images, lat_len, width), F32),
        compiler_params=params(32),
        cost_estimate=cost(4),
        name="latent_back",
    )(grad_kv, grad_q, latent, grad_resid, w_kv, w_q, norms)


def media_back_kernel(media, grad_kv, norms, w_kv, *refs):
    out, grad = refs[-2:]
    grad[...] = contract(grad_kv[0], w_kv[...], (1, 1))
    for at in range(0, media.shape[1], ROWS):
        unit, inverse = norm_rows(media[0, at : at + ROWS, :].astype(F32))
        out[0, at : at + ROWS, :] = norm_back(grad[at : at + ROWS, :], unit, inverse, norms[0:1, :])


def media_back(media, grad_kv, norms, w_kv, first, run, into=()):
    images, media_len, width = media.shape
    inner2 = w_kv.shape[1]
    at = lambda i: (i + first, 0, 0)
    return pl.pallas_call(
        media_back_kernel,
        grid=(run,),
        in_specs=[
            pl.BlockSpec((1, media_len, width), at),
            pl.BlockSpec((1, media_len, inner2), at),
            pl.BlockSpec(norms.shape, fixed_at),
            pl.BlockSpec(w_kv.shape, fixed_at),
            *[pl.BlockSpec(memory_space=pl.ANY) for _ in into],
        ],
        out_specs=pl.BlockSpec((1, media_len, width), at),
        out_shape=jax.ShapeDtypeStruct((images, media_len, width), F32),
        input_output_aliases={4 + i: i for i in range(len(into))},
        scratch_shapes=[pltpu.VMEM((media_len, width), F32)],
        compiler_params=params(32),
        cost_estimate=cost(0.5),
        name="media_back",
    )(media, grad_kv, norms, w_kv, *into)


def fold_rows(value):
    half = value.shape[0] // 2
    return jnp.concatenate([value[:half], value[half:]], 1)


def shards(
    dp,
    media_tokens,
    patch_counts,
    latents,
    media_gain,
    media_bias,
    latent_gain,
    latent_bias,
    query_weight,
    keyval_weight,
    outproj_weight,
    ff_gain,
    ff_bias,
    ff_in_weight,
    ff_out_weight,
    cotangent,
):
    me, core = lax.axis_index("dp"), lax.axis_index("rep")
    place = jnp.stack([me, core]).astype(jnp.int32)
    columns = dp // PLANE
    images, _, width = media_tokens.shape
    lat_len = latents.shape[1]
    inner = query_weight.shape[1]
    part = width // dp
    slot = ff_in_weight.shape[1] // dp // 2
    kv_rows, o_rows = part // 2, inner // dp // 2
    flat = (images * lat_len, width)

    def swap(value, bits):
        return lax.ppermute(value, "dp", [(i, i ^ bits) for i in range(dp)])

    def other(value):
        return lax.ppermute(value, "rep", [(0, 1), (1, 0)])

    def mine(value, axis):
        return lax.dynamic_index_in_dim(value, core, axis, keepdims=False)

    def down(value):
        return [value] + [swap(value, c * PLANE) for c in range(1, columns)]

    def across(values):
        return [values[0]] + [swap(values[p], p) for p in range(1, PLANE)]

    def down_sums(values):
        return [values[0]] + [swap(values[c], c * PLANE) for c in range(1, columns)]

    norms = jnp.stack([media_gain, media_bias, latent_gain, latent_bias, ff_gain, ff_bias])
    norms = lax.dynamic_update_slice(jnp.zeros((PAD, width), BF16), norms, (0, me * part))
    attn = [
        mine(keyval_weight.reshape(2, kv_rows, width), 0),
        fold_rows(mine(query_weight.reshape(2, kv_rows, inner), 0)),
        mine(outproj_weight.reshape(2, o_rows, width), 0),
        norms,
    ]
    attn = jnp.stack(down(jnp.concatenate(attn, 0)))
    ffout = mine(ff_out_weight.reshape(2, slot, width), 0)
    ffin = mine(ff_in_weight.reshape(part, dp, 2, slot), 2).reshape(part, dp * slot)
    cut = ffin.shape[1] // 2
    ffin = jnp.concatenate([ffin[:, :cut], ffin[:, cut:]], 0)
    attn, ffout, ffin = tie(attn, ffout, ffin)
    attn = [attn] + [swap(attn, p) for p in range(1, PLANE)]
    w_ffout = lax.all_gather(ffout, "dp", axis=0, tiled=True)
    ffin = jnp.stack([ffin, swap(ffin, 2 * PLANE)])
    got = swap(ffin, PLANE)
    w_kv, w_q, w_o, norms = in_order(place, attn, [other(value) for value in attn], inner)
    lo, hi = [
        jnp.stack([ffin[0, rows], got[0, rows], ffin[1, rows], got[1, rows]])
        for rows in (slice(0, part), slice(part, 2 * part))
    ]
    dout = cotangent.astype(BF16).reshape(flat)
    douts = dout, other(dout)

    w_kv, lo, hi = tie(w_kv, lo, hi)
    lo, hi = {0: lo, 2: swap(lo, 2)}, {0: hi, 1: swap(hi, 1)}
    run = images // 2
    few = images // 4
    held = attend(patch_counts, media_tokens, latents, norms, w_kv, w_q, 0, few)
    held, lo, hi = tie(held, lo, hi)
    lo[1], lo[3] = swap(lo[0], 1), swap(lo[2], 1)
    hi[2], hi[3] = swap(hi[0], 2), swap(hi[1], 2)
    turned, lat_low, keyvals, queries, mixed = attend(
        patch_counts, media_tokens, latents, norms, w_kv, w_q, few, images - few, held
    )
    mixed = mixed.reshape(-1, inner)
    resid, low = add_branch(mixed, latents.reshape(flat), w_o, norms)
    low, lo, hi = tie(low, lo, hi)
    lo, hi = [lo[p] for p in range(PLANE)], [hi[p] for p in range(PLANE)]

    activ, slope, low_t, dout, w_ffin, *grads = feed_forward(
        place, (low, other(low)), douts, lo, hi, slot
    )
    out_sum = grads[0], swap(grads[1], 1), grads[2], swap(grads[3], 2)
    *grads, kept, sent = feed_back(place, dout, low_t, w_ffin, w_ffout, slope, columns, part)
    kept, out_sum = tie(kept, out_sum)
    grad_resid, grad_mixed, grad_o, ff_vectors = resid_back(
        kept, other(sent), resid, cotangent.reshape(flat), mixed, w_o, norms
    )
    grad_mixed, out_sum = tie(grad_mixed, out_sum)
    out_sum = fold_first(*out_sum)
    grad_mixed, out_sum = tie(grad_mixed, out_sum)
    out_sum = out_sum[0], swap(out_sum[1], 2), out_sum[2], swap(out_sum[3], 1)
    in_sum = grads[0], swap(grads[1], 1), grads[2], swap(grads[3], 2)
    grad_kv, grad_q = attend_back(
        patch_counts, keyvals, queries, grad_mixed.reshape(images, lat_len, inner)
    )
    grad_kv, grad_q, out_sum, in_sum = tie(grad_kv, grad_q, out_sum, in_sum)
    keep, send = fold_second(*out_sum)
    in_sum = fold_first(*in_sum)
    grad_q, keep, send, in_sum = tie(grad_q, keep, send, in_sum)
    out_sum = keep, swap(send, PLANE)
    in_sum = in_sum[0], swap(in_sum[1], 2), in_sum[2], swap(in_sum[3], 1)
    keep, send = weight_back(
        place,
        grad_kv,
        grad_q,
        turned,
        lat_low.reshape(flat),
        w_kv,
        w_q,
        norms,
        grad_o,
        ff_vectors,
        columns,
    )
    keep, send, out_sum, in_sum = tie(keep, send, out_sum, in_sum)
    got = other(send)
    in_keep, in_send = fold_second(*in_sum)
    held, passed = fold_third(*out_sum)
    keep, in_send, passed = tie(keep, in_send, passed)
    in_sum = in_keep, swap(in_send, PLANE)
    out_sum = held, swap(passed, 2 * PLANE)
    attn = add_both(keep, got)
    attn = across(attn)
    grad_kv, attn[0] = tie(grad_kv, attn[0])
    done = media_back(media_tokens, grad_kv, norms, w_kv, 0, run)
    done, in_sum = tie(done, in_sum)
    held, passed = fold_third(*in_sum)
    done, held, passed = tie(done, held, passed)
    in_sum = held, swap(passed, 2 * PLANE)
    media_grad = media_back(media_tokens, grad_kv, norms, w_kv, run, images - run, (done,))
    media_grad, attn = tie(media_grad, attn)
    attn = fold(attn)
    attn, activ, grad_q, in_sum = tie(attn, activ, grad_q, in_sum)
    attn = down_sums(attn)
    latent_grad = latent_back(
        grad_kv, grad_q, latents, grad_resid.reshape(latents.shape), w_kv, w_q, norms
    )
    share, sent = feed_out(activ, w_ffout)
    own_in, own_out = [value[0].astype(F32) + value[1].astype(F32) for value in (in_sum, out_sum)]
    grad_ffin, grad_ffout = final_ff(place, own_in, other(own_in), own_out, other(own_out))
    sent, attn, grad_ffin, latent_grad = tie(sent, attn, grad_ffin, latent_grad)
    own = functools.reduce(jnp.add, [value.astype(F32) for value in attn])
    new_latents = resid + (share + other(sent).astype(F32))
    rows = own.shape[0] - PAD
    vectors = lax.dynamic_slice(own[rows:], (0, me * part), (6, part))
    own = own[:rows]
    grad_wkv, grad_wq, grad_wo = final_attn(place, own, other(own), inner, kv_rows, o_rows)
    return (
        new_latents.reshape(latents.shape),
        media_grad,
        latent_grad,
        vectors[0],
        vectors[1],
        vectors[2],
        vectors[3],
        grad_wq,
        grad_wkv,
        grad_wo,
        vectors[4],
        vectors[5],
        grad_ffin,
        grad_ffout,
    )


def norm_apply(values, gain, bias):
    centre = jnp.mean(values, -1, keepdims=True)
    centred = values - centre
    inverse = lax.rsqrt(jnp.mean(centred * centred, -1, keepdims=True) + EPS)
    unit = centred * inverse
    return (unit * gain.astype(jnp.float32) + bias.astype(jnp.float32), unit, inverse)


def plain_norm_grad(grad_normed, unit, inverse, gain):
    scaled = grad_normed * gain.astype(jnp.float32)
    return inverse * (
        scaled
        - jnp.mean(scaled, -1, keepdims=True)
        - unit * jnp.mean(scaled * unit, -1, keepdims=True)
    )


def row_total(values):
    return jnp.sum(values.reshape(-1, values.shape[-1]), axis=0)


def gelu_exact(values):
    return jax.nn.gelu(values, approximate=False)


def masked_scores(query_heads, key_heads, valid, scale):
    raw = (
        jnp.einsum("iqhe,ikhe->ihqk", query_heads, key_heads, preferred_element_type=jnp.float32)
        * scale
    )
    return jnp.where(valid[:, None, None, :], raw, jnp.float32(-1e30))


def plain_shards(
    media_tokens,
    patch_counts,
    latents,
    media_gain,
    media_bias,
    latent_gain,
    latent_bias,
    query_weight,
    keyval_weight,
    outproj_weight,
    ff_gain,
    ff_bias,
    ff_in_weight,
    ff_out_weight,
    cotangent,
):
    f32 = jnp.float32
    bf16 = jnp.bfloat16
    whole = (
        lax.all_gather(media_gain, "dp", axis=0, tiled=True),
        lax.all_gather(media_bias, "dp", axis=0, tiled=True),
        lax.all_gather(latent_gain, "dp", axis=0, tiled=True),
        lax.all_gather(latent_bias, "dp", axis=0, tiled=True),
        lax.all_gather(query_weight, "dp", axis=0, tiled=True),
        lax.all_gather(keyval_weight, "dp", axis=0, tiled=True),
        lax.all_gather(outproj_weight, "dp", axis=0, tiled=True),
        lax.all_gather(ff_gain, "dp", axis=0, tiled=True),
        lax.all_gather(ff_bias, "dp", axis=0, tiled=True),
        lax.all_gather(ff_in_weight, "dp", axis=0, tiled=True),
        lax.all_gather(ff_out_weight, "dp", axis=0, tiled=True),
    )
    (
        gain_media,
        bias_media,
        gain_latent,
        bias_latent,
        w_query,
        w_keyval,
        w_outproj,
        gain_ff,
        bias_ff,
        w_ffin,
        w_ffout,
    ) = whole
    images, media_len, width = media_tokens.shape
    lat_len = latents.shape[1]
    keys_len = media_len + lat_len
    inner_width = w_query.shape[1]
    head_size = inner_width // HEADS
    scale = 1.0 / math.sqrt(head_size)
    media_f = media_tokens.astype(f32)
    latent_f = latents.astype(f32)
    media_normed, media_unit, media_inv = norm_apply(media_f, gain_media, bias_media)
    latent_normed, latent_unit, latent_inv = norm_apply(latent_f, gain_latent, bias_latent)
    media_low = media_normed.astype(bf16)
    latent_low = latent_normed.astype(bf16)
    queries = jnp.einsum("ild,de->ile", latent_low, w_query, preferred_element_type=f32).astype(
        bf16
    )
    key_input = jnp.concatenate([media_low, latent_low], axis=1)
    keyvals = jnp.einsum("ikd,de->ike", key_input, w_keyval, preferred_element_type=f32).astype(
        bf16
    )
    key_heads = keyvals[:, :, :inner_width].reshape(images, keys_len, HEADS, head_size)
    value_heads = keyvals[:, :, inner_width:].reshape(images, keys_len, HEADS, head_size)
    query_heads = queries.reshape(images, lat_len, HEADS, head_size)
    positions = jnp.arange(keys_len, dtype=jnp.int32)
    valid = (positions[None, :] < patch_counts[:, None]) | (positions[None, :] >= media_len)
    scores = masked_scores(query_heads, key_heads, valid, scale)
    top = jnp.max(scores, -1, keepdims=True)
    expd = jnp.exp(scores - top)
    total = jnp.sum(expd, -1, keepdims=True)
    probs = expd / total
    log_total = top + jnp.log(total)
    mixed = jnp.einsum(
        "ihqk,ikhe->iqhe", probs.astype(bf16), value_heads, preferred_element_type=f32
    )
    mixed = mixed.reshape(images, lat_len, inner_width).astype(bf16)
    branch = jnp.einsum("ile,ed->ild", mixed, w_outproj, preferred_element_type=f32)
    resid = latent_f + branch
    ff_normed, ff_unit, ff_inv = norm_apply(resid, gain_ff, bias_ff)
    ff_low = ff_normed.astype(bf16)
    pre_act = jnp.einsum("ild,df->ilf", ff_low, w_ffin, preferred_element_type=f32)
    activ, gelu_pull = jax.vjp(gelu_exact, pre_act)
    activ_low = activ.astype(bf16)
    new_latents = resid + jnp.einsum("ilf,fd->ild", activ_low, w_ffout, preferred_element_type=f32)
    again = (
        lax.all_gather(media_gain, "dp", axis=0, tiled=True),
        lax.all_gather(media_bias, "dp", axis=0, tiled=True),
        lax.all_gather(latent_gain, "dp", axis=0, tiled=True),
        lax.all_gather(latent_bias, "dp", axis=0, tiled=True),
        lax.all_gather(query_weight, "dp", axis=0, tiled=True),
        lax.all_gather(keyval_weight, "dp", axis=0, tiled=True),
        lax.all_gather(outproj_weight, "dp", axis=0, tiled=True),
        lax.all_gather(ff_gain, "dp", axis=0, tiled=True),
        lax.all_gather(ff_bias, "dp", axis=0, tiled=True),
        lax.all_gather(ff_in_weight, "dp", axis=0, tiled=True),
        lax.all_gather(ff_out_weight, "dp", axis=0, tiled=True),
    )
    (
        gain_media_b,
        bias_media_b,
        gain_latent_b,
        bias_latent_b,
        w_query_b,
        w_keyval_b,
        w_outproj_b,
        gain_ff_b,
        bias_ff_b,
        w_ffin_b,
        w_ffout_b,
    ) = again
    grad_out_low = cotangent.astype(bf16)
    grad_ffout = jnp.einsum("ilf,ild->fd", activ_low, grad_out_low, preferred_element_type=f32)
    grad_activ = jnp.einsum("ild,fd->ilf", grad_out_low, w_ffout_b, preferred_element_type=f32)
    (grad_pre,) = gelu_pull(grad_activ)
    grad_pre_low = grad_pre.astype(bf16)
    grad_ffin = jnp.einsum("ild,ilf->df", ff_low, grad_pre_low, preferred_element_type=f32)
    grad_ffnormed = jnp.einsum("ilf,df->ild", grad_pre_low, w_ffin_b, preferred_element_type=f32)
    grad_gain_ff = row_total(grad_ffnormed * ff_unit)
    grad_bias_ff = row_total(grad_ffnormed)
    grad_resid = cotangent + plain_norm_grad(grad_ffnormed, ff_unit, ff_inv, gain_ff_b)
    grad_resid_low = grad_resid.astype(bf16)
    grad_outproj = jnp.einsum("ile,ild->ed", mixed, grad_resid_low, preferred_element_type=f32)
    grad_mixed = jnp.einsum(
        "ild,ed->ile", grad_resid_low, w_outproj_b, preferred_element_type=f32
    ).astype(bf16)
    grad_mixed_heads = grad_mixed.reshape(images, lat_len, HEADS, head_size)
    scores_again = masked_scores(query_heads, key_heads, valid, scale)
    probs_again = jnp.exp(scores_again - log_total)
    grad_probs = jnp.einsum(
        "iqhe,ikhe->ihqk", grad_mixed_heads, value_heads, preferred_element_type=f32
    )
    grad_scores = probs_again * (grad_probs - jnp.sum(probs_again * grad_probs, -1, keepdims=True))
    grad_scores_low = grad_scores.astype(bf16)
    grad_queries = (
        jnp.einsum("ihqk,ikhe->iqhe", grad_scores_low, key_heads, preferred_element_type=f32)
        * scale
    )
    grad_queries = grad_queries.reshape(images, lat_len, inner_width).astype(bf16)
    grad_keys = (
        jnp.einsum("ihqk,iqhe->ikhe", grad_scores_low, query_heads, preferred_element_type=f32)
        * scale
    )
    grad_values = jnp.einsum(
        "ihqk,iqhe->ikhe", probs_again.astype(bf16), grad_mixed_heads, preferred_element_type=f32
    )
    grad_keyvals = jnp.concatenate(
        [
            grad_keys.reshape(images, keys_len, inner_width),
            grad_values.reshape(images, keys_len, inner_width),
        ],
        axis=-1,
    ).astype(bf16)
    grad_qweight = jnp.einsum("ild,ile->de", latent_low, grad_queries, preferred_element_type=f32)
    grad_kvweight = jnp.einsum("ikd,ike->de", key_input, grad_keyvals, preferred_element_type=f32)
    grad_key_input = jnp.einsum("ike,de->ikd", grad_keyvals, w_keyval_b, preferred_element_type=f32)
    grad_latnormed = jnp.einsum("ile,de->ild", grad_queries, w_query_b, preferred_element_type=f32)
    grad_latnormed = grad_latnormed + grad_key_input[:, media_len:]
    grad_medianormed = grad_key_input[:, :media_len]
    media_grad = plain_norm_grad(grad_medianormed, media_unit, media_inv, gain_media_b)
    latent_grad = grad_resid + plain_norm_grad(grad_latnormed, latent_unit, latent_inv, gain_latent_b)
    grad_gain_media = row_total(grad_medianormed * media_unit)
    grad_bias_media = row_total(grad_medianormed)
    grad_gain_latent = row_total(grad_latnormed * latent_unit)
    grad_bias_latent = row_total(grad_latnormed)
    owned = (
        lax.psum_scatter(
            grad_gain_media.astype(jnp.bfloat16), "dp", scatter_dimension=0, tiled=True
        ).astype(jnp.float32),
        lax.psum_scatter(
            grad_bias_media.astype(jnp.bfloat16), "dp", scatter_dimension=0, tiled=True
        ).astype(jnp.float32),
        lax.psum_scatter(
            grad_gain_latent.astype(jnp.bfloat16), "dp", scatter_dimension=0, tiled=True
        ).astype(jnp.float32),
        lax.psum_scatter(
            grad_bias_latent.astype(jnp.bfloat16), "dp", scatter_dimension=0, tiled=True
        ).astype(jnp.float32),
        lax.psum_scatter(
            grad_qweight.astype(jnp.bfloat16), "dp", scatter_dimension=0, tiled=True
        ).astype(jnp.float32),
        lax.psum_scatter(
            grad_kvweight.astype(jnp.bfloat16), "dp", scatter_dimension=0, tiled=True
        ).astype(jnp.float32),
        lax.psum_scatter(
            grad_outproj.astype(jnp.bfloat16), "dp", scatter_dimension=0, tiled=True
        ).astype(jnp.float32),
        lax.psum_scatter(
            grad_gain_ff.astype(jnp.bfloat16), "dp", scatter_dimension=0, tiled=True
        ).astype(jnp.float32),
        lax.psum_scatter(
            grad_bias_ff.astype(jnp.bfloat16), "dp", scatter_dimension=0, tiled=True
        ).astype(jnp.float32),
        lax.psum_scatter(
            grad_ffin.astype(jnp.bfloat16), "dp", scatter_dimension=0, tiled=True
        ).astype(jnp.float32),
        lax.psum_scatter(
            grad_ffout.astype(jnp.bfloat16), "dp", scatter_dimension=0, tiled=True
        ).astype(jnp.float32),
    )
    summed = (
        lax.psum(owned[0].astype(jnp.bfloat16), "rep").astype(jnp.float32),
        lax.psum(owned[1].astype(jnp.bfloat16), "rep").astype(jnp.float32),
        lax.psum(owned[2].astype(jnp.bfloat16), "rep").astype(jnp.float32),
        lax.psum(owned[3].astype(jnp.bfloat16), "rep").astype(jnp.float32),
        lax.psum(owned[4].astype(jnp.bfloat16), "rep").astype(jnp.float32),
        lax.psum(owned[5].astype(jnp.bfloat16), "rep").astype(jnp.float32),
        lax.psum(owned[6].astype(jnp.bfloat16), "rep").astype(jnp.float32),
        lax.psum(owned[7].astype(jnp.bfloat16), "rep").astype(jnp.float32),
        lax.psum(owned[8].astype(jnp.bfloat16), "rep").astype(jnp.float32),
        lax.psum(owned[9].astype(jnp.bfloat16), "rep").astype(jnp.float32),
        lax.psum(owned[10].astype(jnp.bfloat16), "rep").astype(jnp.float32),
    )
    (
        sum_gain_media,
        sum_bias_media,
        sum_gain_latent,
        sum_bias_latent,
        sum_query,
        sum_keyval,
        sum_outproj,
        sum_gain_ff,
        sum_bias_ff,
        sum_ffin,
        sum_ffout,
    ) = summed
    return (
        new_latents,
        media_grad,
        latent_grad,
        sum_gain_media,
        sum_bias_media,
        sum_gain_latent,
        sum_bias_latent,
        sum_query,
        sum_keyval,
        sum_outproj,
        sum_gain_ff,
        sum_bias_ff,
        sum_ffin,
        sum_ffout,
    )


def solution(mesh):
    dp, rep = mesh.shape["dp"], mesh.shape["rep"]

    def program(*arrays):
        if rep != 2 or dp != PLANE * PLANE:
            return plain_shards(*arrays)
        return shards(dp, *arrays)

    return jax.shard_map(
        program,
        mesh=mesh,
        in_specs=(
            P(("dp", "rep"), None, None),
            P(("dp", "rep")),
            P(("dp", "rep"), None, None),
            P("dp"),
            P("dp"),
            P("dp"),
            P("dp"),
            P("dp", None),
            P("dp", None),
            P("dp", None),
            P("dp"),
            P("dp"),
            P("dp", None),
            P("dp", None),
            P(("dp", "rep"), None, None),
        ),
        out_specs=(
            P(("dp", "rep"), None, None),
            P(("dp", "rep"), None, None),
            P(("dp", "rep"), None, None),
            P("dp"),
            P("dp"),
            P("dp"),
            P("dp"),
            P("dp", None),
            P("dp", None),
            P("dp", None),
            P("dp"),
            P("dp"),
            P("dp", None),
            P("dp", None),
        ),
        check_vma=False,
    )
```
